32 devices in a mesh: dp: 8 (over z, y), tensor: 4 (over x, core).
Axes of the slice: x: 2, y: 2, z: 4, core: 2. Of those that a mesh axis runs over, the one named last changes fastest.
Arguments:
- tokens: bfloat16 [8192, 2048], P(('dp', 'tensor')), may hold values from -6 to 6
- cotangent: bfloat16 [8192, 2048], P(('dp', 'tensor')), may hold values from -6 to 6
- segment_ids: int32 [8, 1024], P('dp'), may hold values from 0 to 15, never falling along the last dimension, each value on 1 to 512 neighbouring positions
- adapter_set: int32 [8], P('dp'), may hold values from 0 to 7
- w_query: bfloat16 [2048, 2048], P(None, 'tensor'), may hold values from -1 to 1
- w_key: bfloat16 [2048, 2048], P(None, 'tensor'), may hold values from -1 to 1
- w_value: bfloat16 [2048, 2048], P(None, 'tensor'), may hold values from -0.125 to 0.125
- w_out: bfloat16 [2048, 2048], P('tensor'), may hold values from -0.5 to 0.5
- w_gate: bfloat16 [2048, 8192], P(None, 'tensor'), may hold values from -0.125 to 0.125
- w_up: bfloat16 [2048, 8192], P(None, 'tensor'), may hold values from -0.125 to 0.125
- w_down: bfloat16 [8192, 2048], P('tensor'), may hold values from -0.0625 to 0.0625
- query_gain: bfloat16 [2048], P('tensor'), may hold values from 0.099609375 to 1.8984375
- key_gain: bfloat16 [2048], P('tensor'), may hold values from 0.099609375 to 1.8984375
- mixer_gain: bfloat16 [2048], replicated, may hold values from 0.099609375 to 1.8984375
- feed_gain: bfloat16 [2048], replicated, may hold values from 0.099609375 to 1.8984375
- shrink_query: bfloat16 [8, 16, 2048], replicated, may hold values from -0.125 to 0.125
- expand_query: bfloat16 [8, 16, 2048], P(None, None, 'tensor'), may hold values from -1.5 to 1.5
- shrink_key: bfloat16 [8, 16, 2048], replicated, may hold values from -0.125 to 0.125
- expand_key: bfloat16 [8, 16, 2048], P(None, None, 'tensor'), may hold values from -1.5 to 1.5
- shrink_value: bfloat16 [8, 16, 2048], replicated, may hold values from -0.125 to 0.125
- expand_value: bfloat16 [8, 16, 2048], P(None, None, 'tensor'), may hold values from -1.5 to 1.5
- shrink_out: bfloat16 [8, 16, 2048], P(None, None, 'tensor'), may hold values from -0.5 to 0.5
- expand_out: bfloat16 [8, 16, 2048], replicated, may hold values from -1.5 to 1.5
- shrink_gate: bfloat16 [8, 16, 2048], replicated, may hold values from -0.125 to 0.125
- expand_gate: bfloat16 [8, 16, 8192], P(None, None, 'tensor'), may hold values from -1.5 to 1.5
- shrink_up: bfloat16 [8, 16, 2048], replicated, may hold values from -0.125 to 0.125
- expand_up: bfloat16 [8, 16, 8192], P(None, None, 'tensor'), may hold values from -1.5 to 1.5
- shrink_down: bfloat16 [8, 16, 8192], P(None, None, 'tensor'), may hold values from -0.0625 to 0.0625
- expand_down: bfloat16 [8, 16, 2048], replicated, may hold values from -1.5 to 1.5
Outputs:
- block_output: bfloat16 [8192, 2048], P(('dp', 'tensor'))
- token_grads: float32 [8192, 2048], P(('dp', 'tensor'))
- grad_shrink_query: float32 [8, 16, 2048], P(None, None, ('dp', 'tensor'))
- grad_expand_query: float32 [8, 16, 2048], P(None, None, 'tensor')
- grad_shrink_key: float32 [8, 16, 2048], P(None, None, ('dp', 'tensor'))
- grad_expand_key: float32 [8, 16, 2048], P(None, None, 'tensor')
- grad_shrink_value: float32 [8, 16, 2048], P(None, None, ('dp', 'tensor'))
- grad_expand_value: float32 [8, 16, 2048], P(None, None, 'tensor')
- grad_shrink_out: float32 [8, 16, 2048], P(None, None, 'tensor')
- grad_expand_out: float32 [8, 16, 2048], P(None, None, ('dp', 'tensor'))
- grad_shrink_gate: float32 [8, 16, 2048], P(None, None, ('dp', 'tensor'))
- grad_expand_gate: float32 [8, 16, 8192], P(None, None, 'tensor')
- grad_shrink_up: float32 [8, 16, 2048], P(None, None, ('dp', 'tensor'))
- grad_expand_up: float32 [8, 16, 8192], P(None, None, 'tensor')
- grad_shrink_down: float32 [8, 16, 8192], P(None, None, 'tensor')
- grad_expand_down: float32 [8, 16, 2048], P(None, None, ('dp', 'tensor'))
The draws below stay inside these ranges and needn't reach their ends.
Inputs may be any that keep to these rules, and one draw needn't show every extreme that they name: `segment_ids`: along each sequence the document numbers never fall; a document has 1 to 512 tokens, and one has exactly 512.
All inputs are finite; a program needn't handle non-finite values.
Results may differ from the reference program's by a relative error of at most 0.022.
Values may be sent and summed in bfloat16 or wider, within the bound.
A program may use at most 256 MiB of HBM per device.

```python
import math
import jax
import jax.numpy as jnp
import numpy as np
from jax import lax

D = 2048
HEADS = 16
HEAD_DIM = 128
FF = 8192
RANK = 16
SETS = 8
SEQ_LEN = 1024
DOCS = 16
DOC_MOST = 512
SEQS = 8
TOKENS = 8192


def rising(key, rows, cols):
    base = jax.random.normal(key, (rows, cols), jnp.float32)
    ramp = 1.0 + 1.2 * jnp.arange(cols, dtype=jnp.float32) / cols
    return (base * ramp[None, :] * rows ** (-0.5)).astype(jnp.bfloat16)


def draw_w_query(key, part):
    return rising(jax.random.fold_in(key, 11), D, D)


def draw_w_key(key, part):
    return rising(jax.random.fold_in(key, 23), D, D)


def set_ends(array, own_key, least, top_value):
    longest = array.shape.index(max(array.shape))
    spots = []
    for shift in (0, 1):
        where = [jax.random.randint(jax.random.fold_in(own_key, axis), (), 0, length) for axis, length in enumerate(array.shape)]
        where[longest] = (where[longest] + shift) % array.shape[longest]
        spots.append(tuple(where))
    return array.at[spots[0]].set(least).at[spots[1]].set(top_value)


def block_scale(key, dims, pieces, least, top_value):
    factor_of = 1.0
    for position, shards_of in pieces:
        steps = jax.random.uniform(jax.random.fold_in(jax.random.fold_in(key, 6), position), (shards_of,), jnp.float32, least / len(pieces), top_value / len(pieces))
        factor_of = factor_of * jnp.repeat(jnp.exp(steps), dims[position] // shards_of).reshape((-1,) + (1,) * (len(dims) - 1 - position))
    return factor_of


def length_profile(count, total, limit, slope):
    portions = [(1 << 20) // math.isqrt(standing ** slope) + 1 for standing in range(2, count + 1)]
    surplus, counts = total - limit - (count - 1), [1] * (count - 1)
    while surplus > 0:
        free = [i for i in range(count - 1) if counts[i] < limit]
        whole, remaining = sum([portions[i] for i in free]), surplus
        for i in free:
            addition = min(limit - counts[i], max(1, remaining * portions[i] // whole), surplus)
            counts[i] = counts[i] + addition
            surplus = surplus - addition
    return np.array([limit] + counts)


def ragged_sizes(rng, number_of, total, limit, lean):
    if number_of == 2:
        one = jax.random.randint(rng, (), max(1, total - limit), min(limit, total - 1) + 1)
        return jnp.stack([one, total - one])
    tallies = jnp.asarray(length_profile(number_of, total, limit, lean), jnp.int32)
    pairs = (number_of - 1) // 2
    giver, taker = tallies[1:1 + 2 * pairs:2], tallies[2:2 + 2 * pairs:2]
    margin = jnp.minimum(giver - 1, limit - taker)
    moved = jax.random.randint(jax.random.fold_in(rng, 1), (pairs,), 0, 1 << 20) % (margin + 1)
    tallies = tallies.at[1:1 + 2 * pairs:2].set(giver - moved).at[2:2 + 2 * pairs:2].set(taker + moved)
    return tallies[jax.random.permutation(jax.random.fold_in(rng, 2), number_of)]


def scatter_about(own_key, dims, deviation, most, shards=(), kind=jnp.bfloat16):
    level = block_scale(own_key, dims, shards, -0.22, 0.18) if shards else 1.0
    values = jax.random.normal(own_key, dims, jnp.float32) * deviation * level
    return jnp.minimum(jnp.maximum(values, -most), most).astype(kind)


def setup_inputs(seed: int = 0) -> dict:
    keys = jax.random.split(jax.random.key(seed), 30)
    return {
        "tokens": scatter_about(keys[0], (TOKENS, D), 1.0, 6.0, ((0, 32),)),
        "cotangent": scatter_about(keys[1], (TOKENS, D), 1.0, 6.0, ((0, 32),)),
        "segment_ids": jax.vmap(lambda own: jnp.searchsorted(jnp.cumsum(ragged_sizes(own, DOCS, SEQ_LEN, DOC_MOST, 2)), jnp.arange(SEQ_LEN), side="right"))(jax.random.split(keys[2], SEQS)).reshape((SEQS, SEQ_LEN)).astype(jnp.int32),
        "adapter_set": set_ends(jax.random.randint(keys[3], (SEQS,), 0, SETS), jax.random.fold_in(keys[3], 1), 0, SETS - 1).astype(jnp.int32),
        "w_query": draw_w_query(jax.random.fold_in(keys[29], 71), 0),
        "w_key": draw_w_key(jax.random.fold_in(keys[29], 71), 0),
        "w_value": scatter_about(keys[6], (D, D), D ** -0.5, 0.125, ((1, 4),)),
        "w_out": scatter_about(keys[7], (D, D), (D // 16) ** -0.5, 0.5, ((0, 4),)),
        "w_gate": scatter_about(keys[8], (D, FF), D ** -0.5, 0.125, ((1, 4),)),
        "w_up": scatter_about(keys[9], (D, FF), D ** -0.5, 0.125, ((1, 4),)),
        "w_down": scatter_about(keys[10], (FF, D), FF ** -0.5, 0.0625, ((0, 4),)),
        "query_gain": jnp.clip(1.0 + 0.18 * jax.random.normal(keys[11], (D,), jnp.float32), 0.099609375, 1.8984375).astype(jnp.bfloat16),
        "key_gain": jnp.clip(1.0 + 0.18 * jax.random.normal(keys[12], (D,), jnp.float32), 0.099609375, 1.8984375).astype(jnp.bfloat16),
        "mixer_gain": jnp.clip(1.0 + 0.18 * jax.random.normal(keys[13], (D,), jnp.float32), 0.099609375, 1.8984375).astype(jnp.bfloat16),
        "feed_gain": jnp.clip(1.0 + 0.18 * jax.random.normal(keys[14], (D,), jnp.float32), 0.099609375, 1.8984375).astype(jnp.bfloat16),
        "shrink_query": scatter_about(keys[15], (SETS, RANK, D), D ** -0.5, 0.125),
        "expand_query": scatter_about(keys[16], (SETS, RANK, D), RANK ** -0.5, 1.5, ((2, 4),)),
        "shrink_key": scatter_about(keys[17], (SETS, RANK, D), D ** -0.5, 0.125),
        "expand_key": scatter_about(keys[18], (SETS, RANK, D), RANK ** -0.5, 1.5, ((2, 4),)),
        "shrink_value": scatter_about(keys[19], (SETS, RANK, D), D ** -0.5, 0.125),
        "expand_value": scatter_about(keys[20], (SETS, RANK, D), RANK ** -0.5, 1.5, ((2, 4),)),
        "shrink_out": scatter_about(keys[21], (SETS, RANK, D), (D // 16) ** -0.5, 0.5, ((2, 4),)),
        "expand_out": scatter_about(keys[22], (SETS, RANK, D), RANK ** -0.5, 1.5),
        "shrink_gate": scatter_about(keys[23], (SETS, RANK, D), D ** -0.5, 0.125),
        "expand_gate": scatter_about(keys[24], (SETS, RANK, FF), RANK ** -0.5, 1.5, ((2, 4),)),
        "shrink_up": scatter_about(keys[25], (SETS, RANK, D), D ** -0.5, 0.125),
        "expand_up": scatter_about(keys[26], (SETS, RANK, FF), RANK ** -0.5, 1.5, ((2, 4),)),
        "shrink_down": scatter_about(keys[27], (SETS, RANK, FF), FF ** -0.5, 0.0625, ((2, 4),)),
        "expand_down": scatter_about(keys[28], (SETS, RANK, D), RANK ** -0.5, 1.5),
    }


epsilon = 1e-06
adapter_scale_factor = 0.5
rotary_base = 500000.0
highest = lax.Precision.HIGHEST

@jax.custom_vjp
def low(v):
    return lax.optimization_barrier(v.astype(jnp.bfloat16)).astype(jnp.float32)

@jax.custom_vjp
def low_back(v):
    return v

def low_keep(v):
    return (low(v), None)

def low_pass(kept, grad):
    return (grad,)

def back_keep(v):
    return (v, None)

def back_low(kept, grad):
    return (low(grad),)
low.defvjp(low_keep, low_pass)
low_back.defvjp(back_keep, back_low)

def matrix_product(left, right):
    return jnp.dot(left, right, precision=highest, preferred_element_type=jnp.float32)

def rms_norm(values, gains):
    factor = lax.rsqrt(lax.optimization_barrier(jnp.mean(values * values, axis=-1, keepdims=True)) + epsilon)
    return values * factor * gains

def rotary_tables(length, head_dim):
    half_dim = head_dim // 2
    frequency = rotary_base ** (-(jnp.arange(half_dim, dtype=jnp.float32) * 2.0 / head_dim))
    angles = jnp.arange(length, dtype=jnp.float32)[:, None] * frequency[None, :]
    return (jnp.cos(angles)[:, None, :], jnp.sin(angles)[:, None, :])

def rotate(values, cosine_table, sine_table):
    half_dim = values.shape[-1] // 2
    leading = values[..., :half_dim]
    trailing = values[..., half_dim:]
    return jnp.concatenate([leading * cosine_table - trailing * sine_table, trailing * cosine_table + leading * sine_table], axis=-1)

def adapted(input_rows, weight_matrix, shrink, widen_factor):
    middle_rows = matrix_product(input_rows, shrink.T)
    return matrix_product(input_rows, weight_matrix) + adapter_scale_factor * matrix_product(middle_rows, widen_factor)

def layer(seq_tokens, adapters, weights, segments, chosen):
    shrink_query, expand_query, shrink_key, expand_key, shrink_value, expand_value, shrink_out, expand_out, shrink_gate, expand_gate, shrink_up, expand_up, shrink_down, expand_down = adapters
    w_query, w_key, w_value, w_out, w_gate, w_up, w_down, query_gain, key_gain, mixer_gain, feed_gain = weights
    length = seq_tokens.shape[0]
    query = low_back(adapted(seq_tokens, w_query, shrink_query[chosen], expand_query[chosen]))
    key_proj = low_back(adapted(seq_tokens, w_key, shrink_key[chosen], expand_key[chosen]))
    value_proj = low(low_back(adapted(seq_tokens, w_value, shrink_value[chosen], expand_value[chosen])))
    cosine_table, sine_table = rotary_tables(length, HEAD_DIM)
    query_rot = low(rotate(rms_norm(query, query_gain).reshape(length, HEADS, HEAD_DIM), cosine_table, sine_table))
    key_rot = low(rotate(rms_norm(key_proj, key_gain).reshape(length, HEADS, HEAD_DIM), cosine_table, sine_table))
    value_heads = value_proj.reshape(length, HEADS, HEAD_DIM)
    raw_scores = low_back(jnp.einsum('qhe,khe->hqk', query_rot, key_rot, precision=highest)) * HEAD_DIM ** (-0.5)
    positions = jnp.arange(length)
    allowed = (positions[None, :] <= positions[:, None]) & (segments[:, None] == segments[None, :])
    masked = jnp.where(allowed[None], raw_scores, -jnp.inf)
    prob_low = low(jax.nn.softmax(masked, axis=-1))
    mixed = low(low_back(jnp.einsum('hqk,khe->qhe', prob_low, value_heads, precision=highest))).reshape(length, D)
    mixer = low_back(adapted(mixed, w_out, shrink_out[chosen], expand_out[chosen]))
    hidden = seq_tokens + rms_norm(mixer, mixer_gain)
    hidden_low = low(hidden)
    gate = low_back(adapted(hidden_low, w_gate, shrink_gate[chosen], expand_gate[chosen]))
    up_proj = low_back(adapted(hidden_low, w_up, shrink_up[chosen], expand_up[chosen]))
    inner_act = low(jax.nn.silu(gate) * up_proj)
    feed = low_back(adapted(inner_act, w_down, shrink_down[chosen], expand_down[chosen]))
    return hidden + rms_norm(feed, feed_gain)

def to_float(array_in):
    return array_in.astype(jnp.float32)

def reference(tokens, cotangent, segment_ids, adapter_set, w_query, w_key, w_value, w_out, w_gate, w_up, w_down, query_gain, key_gain, mixer_gain, feed_gain, shrink_query, expand_query, shrink_key, expand_key, shrink_value, expand_value, shrink_out, expand_out, shrink_gate, expand_gate, shrink_up, expand_up, shrink_down, expand_down):
    weights = jax.tree.map(to_float, (w_query, w_key, w_value, w_out, w_gate, w_up, w_down, query_gain, key_gain, mixer_gain, feed_gain))
    adapters = jax.tree.map(to_float, (shrink_query, expand_query, shrink_key, expand_key, shrink_value, expand_value, shrink_out, expand_out, shrink_gate, expand_gate, shrink_up, expand_up, shrink_down, expand_down))
    seqs_tokens = tokens.reshape(SEQS, SEQ_LEN, D)
    seqs_cot = cotangent.reshape(SEQS, SEQ_LEN, D)

    def one_sequence(running, scanned):
        seq_tokens, seq_cot, segments, chosen = scanned

        def forward(input_rows, adapter_args):
            return layer(input_rows, adapter_args, weights, segments, chosen)
        result, pullback = jax.vjp(forward, seq_tokens.astype(jnp.float32), adapters)
        token_grad, adapter_grad = pullback(seq_cot.astype(jnp.float32))
        return (jax.tree.map(jnp.add, running, adapter_grad), (result.astype(jnp.bfloat16), token_grad))
    zeros = jax.tree.map(jnp.zeros_like, adapters)
    totals, (outputs, token_grads) = lax.scan(one_sequence, zeros, (seqs_tokens, seqs_cot, segment_ids, adapter_set))
    return (outputs.reshape(TOKENS, D), token_grads.reshape(TOKENS, D), totals[0], totals[1], totals[2], totals[3], totals[4], totals[5], totals[6], totals[7], totals[8], totals[9], totals[10], totals[11], totals[12], totals[13])
```

```python
import jax
import jax.numpy as jnp
from jax import lax
from jax.sharding import PartitionSpec as P

HEAD_DIM = 128
QBLOCK = 512


epsilon = 1e-06
adapter_scale_factor = 0.5
rotary_base = 500000.0
highest = lax.Precision.HIGHEST


def rotary_tables(length, head_dim):
    half_dim = head_dim // 2
    frequency = rotary_base ** (-(jnp.arange(half_dim, dtype=jnp.float32) * 2.0 / head_dim))
    angles = jnp.arange(length, dtype=jnp.float32)[:, None] * frequency[None, :]
    return (jnp.cos(angles)[:, None, :], jnp.sin(angles)[:, None, :])


def rotate(values, cosine_table, sine_table):
    half_dim = values.shape[-1] // 2
    leading = values[..., :half_dim]
    trailing = values[..., half_dim:]
    return jnp.concatenate(
        [
            leading * cosine_table - trailing * sine_table,
            trailing * cosine_table + leading * sine_table,
        ],
        axis=-1,
    )


def unrotate(grads, cosine_table, sine_table):
    half_dim = grads.shape[-1] // 2
    leading = grads[..., :half_dim]
    trailing = grads[..., half_dim:]
    return jnp.concatenate(
        [
            leading * cosine_table + trailing * sine_table,
            trailing * cosine_table - leading * sine_table,
        ],
        axis=-1,
    )


def scale_of(values):
    return lax.rsqrt(jnp.mean(values * values, axis=-1, keepdims=True) + epsilon)


def norm_back(values, factor, gains, grads):
    weighted = grads * gains
    return factor * weighted - values * factor**3 * jnp.mean(
        values * weighted, axis=-1, keepdims=True
    )


def rank_reduced(input_rows, shrink):
    return jnp.dot(input_rows, shrink.T, preferred_element_type=jnp.float32)


def widen_from_rank(middle_rows, widen_factor):
    return jnp.dot(
        middle_rows.astype(jnp.bfloat16), widen_factor, preferred_element_type=jnp.float32
    )


def outer_gradient(middle_rows, input_rows):
    return lax.dot_general(
        middle_rows.astype(jnp.bfloat16),
        input_rows,
        (((0,), (0,)), ((), ())),
        preferred_element_type=jnp.float32,
    )


def per_device(
    tokens,
    cotangent,
    segment_ids,
    adapter_set,
    w_query,
    w_key,
    w_value,
    w_out,
    w_gate,
    w_up,
    w_down,
    query_gain,
    key_gain,
    mixer_gain,
    feed_gain,
    shrink_query,
    expand_query,
    shrink_key,
    expand_key,
    shrink_value,
    expand_value,
    shrink_out,
    expand_out,
    shrink_gate,
    expand_gate,
    shrink_up,
    expand_up,
    shrink_down,
    expand_down,
):
    model_width = w_query.shape[0]
    chosen = adapter_set[0]

    def choose_set(adapters):
        return lax.dynamic_index_in_dim(adapters, chosen, 0, keepdims=False)

    query_shrink, query_widened = (choose_set(shrink_query), choose_set(expand_query))
    key_shrink, key_widened = (choose_set(shrink_key), choose_set(expand_key))
    value_shrink, value_widened = (choose_set(shrink_value), choose_set(expand_value))
    out_shrink, output_widened = (choose_set(shrink_out), choose_set(expand_out))
    gate_shrink, gate_widened = (choose_set(shrink_gate), choose_set(expand_gate))
    up_shrink, up_widened = (choose_set(shrink_up), choose_set(expand_up))
    down_shrink, down_widened = (choose_set(shrink_down), choose_set(expand_down))
    full_tokens = lax.all_gather(tokens, "tensor", axis=0, tiled=True)
    length = full_tokens.shape[0]
    query_middle = rank_reduced(full_tokens, query_shrink)
    key_middle = rank_reduced(full_tokens, key_shrink)
    value_middle = rank_reduced(full_tokens, value_shrink)
    query_proj = jnp.dot(
        full_tokens, w_query, preferred_element_type=jnp.float32
    ) + adapter_scale_factor * widen_from_rank(query_middle, query_widened)
    key_proj = jnp.dot(
        full_tokens, w_key, preferred_element_type=jnp.float32
    ) + adapter_scale_factor * widen_from_rank(key_middle, key_widened)
    value_proj = jnp.dot(
        full_tokens, w_value, preferred_element_type=jnp.float32
    ) + adapter_scale_factor * widen_from_rank(value_middle, value_widened)
    totals = lax.psum(
        (jnp.sum(query_proj * query_proj, axis=-1), jnp.sum(key_proj * key_proj, axis=-1)), "tensor"
    )
    query_scale = lax.rsqrt(totals[0] / model_width + epsilon)[:, None]
    key_scale = lax.rsqrt(totals[1] / model_width + epsilon)[:, None]
    query_gains = query_gain.astype(jnp.float32)
    key_gains = key_gain.astype(jnp.float32)
    heads_here = w_query.shape[1] // HEAD_DIM
    cosine_table, sine_table = rotary_tables(length, HEAD_DIM)
    query_rot = rotate(
        (query_proj * query_scale * query_gains).reshape(length, heads_here, HEAD_DIM),
        cosine_table,
        sine_table,
    ).astype(jnp.bfloat16)
    key_rot = rotate(
        (key_proj * key_scale * key_gains).reshape(length, heads_here, HEAD_DIM),
        cosine_table,
        sine_table,
    ).astype(jnp.bfloat16)
    value_heads = value_proj.astype(jnp.bfloat16).reshape(length, heads_here, HEAD_DIM)
    segments = segment_ids[0]
    positions = jnp.arange(length)
    block_rows = min(QBLOCK, length)
    inverse = HEAD_DIM ** (-0.5)

    def scores_of(row_start, row_end):
        raw_scores = (
            jnp.einsum(
                "qhe,khe->hqk",
                query_rot[row_start:row_end],
                key_rot[:row_end],
                preferred_element_type=jnp.float32,
            )
            * inverse
        )
        allowed = (positions[None, :row_end] <= positions[row_start:row_end, None]) & (
            segments[row_start:row_end, None] == segments[None, :row_end]
        )
        return (raw_scores, allowed)

    mixed_parts = []
    lse_parts = []
    for row_start in range(0, length, block_rows):
        row_end = row_start + block_rows
        raw_scores, allowed = scores_of(row_start, row_end)
        masked = jnp.where(allowed[None], raw_scores, -jnp.inf)
        row_top = jnp.max(masked, axis=-1, keepdims=True)
        row_total = jnp.sum(jnp.exp(masked - row_top), axis=-1, keepdims=True)
        log_total = row_top + jnp.log(row_total)
        prob_low = jnp.exp(masked - log_total).astype(jnp.bfloat16)
        head_part = jnp.einsum(
            "hqk,khe->qhe", prob_low, value_heads[:row_end], preferred_element_type=jnp.float32
        )
        mixed_parts.append(head_part.astype(jnp.bfloat16))
        lse_parts.append(log_total)
    mixed = jnp.concatenate(mixed_parts, axis=0).reshape(length, heads_here * HEAD_DIM)
    output_middle = rank_reduced(mixed, out_shrink)
    mixer_rows = lax.psum_scatter(
        (
            jnp.dot(mixed, w_out, preferred_element_type=jnp.float32)
            + adapter_scale_factor * widen_from_rank(output_middle, output_widened)
        ).astype(jnp.bfloat16),
        "tensor",
        scatter_dimension=0,
        tiled=True,
    ).astype(jnp.float32)
    mixer_scale = scale_of(mixer_rows)
    mixer_gains = mixer_gain.astype(jnp.float32)
    hidden = tokens.astype(jnp.float32) + mixer_rows * mixer_scale * mixer_gains
    full_hidden = lax.all_gather(hidden.astype(jnp.bfloat16), "tensor", axis=0, tiled=True)
    gate_middle = rank_reduced(full_hidden, gate_shrink)
    up_middle = rank_reduced(full_hidden, up_shrink)
    gate = jnp.dot(
        full_hidden, w_gate, preferred_element_type=jnp.float32
    ) + adapter_scale_factor * widen_from_rank(gate_middle, gate_widened)
    up_proj = jnp.dot(
        full_hidden, w_up, preferred_element_type=jnp.float32
    ) + adapter_scale_factor * widen_from_rank(up_middle, up_widened)
    sigmoid_gate = jax.nn.sigmoid(gate)
    inner_act = (gate * sigmoid_gate * up_proj).astype(jnp.bfloat16)
    down_middle = rank_reduced(inner_act, down_shrink)
    feed_rows = lax.psum_scatter(
        (
            jnp.dot(inner_act, w_down, preferred_element_type=jnp.float32)
            + adapter_scale_factor * widen_from_rank(down_middle, down_widened)
        ).astype(jnp.bfloat16),
        "tensor",
        scatter_dimension=0,
        tiled=True,
    ).astype(jnp.float32)
    feed_scale = scale_of(feed_rows)
    feed_gains = feed_gain.astype(jnp.float32)
    block_output = (hidden + feed_rows * feed_scale * feed_gains).astype(jnp.bfloat16)
    upstream = cotangent.astype(jnp.float32)
    feed_grad = norm_back(feed_rows, feed_scale, feed_gains, upstream).astype(jnp.bfloat16)
    complete_feed_gradient = lax.all_gather(feed_grad, "tensor", axis=0, tiled=True)
    down_middle_gradient = adapter_scale_factor * rank_reduced(complete_feed_gradient, down_widened)
    inner_grad = jnp.dot(
        complete_feed_gradient, w_down.T, preferred_element_type=jnp.float32
    ) + widen_from_rank(down_middle_gradient, down_shrink)
    grad_down_shrink = outer_gradient(down_middle_gradient, inner_act)
    gate_gradient = (
        inner_grad * up_proj * (sigmoid_gate * (1.0 + gate * (1.0 - sigmoid_gate)))
    ).astype(jnp.bfloat16)
    up_gradient = (inner_grad * gate * sigmoid_gate).astype(jnp.bfloat16)
    gate_middle_gradient = adapter_scale_factor * rank_reduced(gate_gradient, gate_widened)
    up_middle_gradient = adapter_scale_factor * rank_reduced(up_gradient, up_widened)
    gradient_gate_widened = adapter_scale_factor * outer_gradient(gate_middle, gate_gradient)
    gradient_up_widened = adapter_scale_factor * outer_gradient(up_middle, up_gradient)
    hidden_grad = upstream + lax.psum_scatter(
        (
            jnp.dot(gate_gradient, w_gate.T, preferred_element_type=jnp.float32)
            + jnp.dot(up_gradient, w_up.T, preferred_element_type=jnp.float32)
            + widen_from_rank(gate_middle_gradient, gate_shrink)
            + widen_from_rank(up_middle_gradient, up_shrink)
        ).astype(jnp.bfloat16),
        "tensor",
        scatter_dimension=0,
        tiled=True,
    ).astype(jnp.float32)
    mixer_grad = norm_back(mixer_rows, mixer_scale, mixer_gains, hidden_grad).astype(jnp.bfloat16)
    complete_mixer_gradient = lax.all_gather(mixer_grad, "tensor", axis=0, tiled=True)
    output_middle_gradient = adapter_scale_factor * rank_reduced(
        complete_mixer_gradient, output_widened
    )
    mixed_grad = (
        jnp.dot(complete_mixer_gradient, w_out.T, preferred_element_type=jnp.float32)
        + widen_from_rank(output_middle_gradient, out_shrink)
    ).astype(jnp.bfloat16)
    grad_out_shrink = outer_gradient(output_middle_gradient, mixed)
    mixed_grad_heads = mixed_grad.reshape(length, heads_here, HEAD_DIM)
    key_acc = jnp.zeros((length, heads_here, HEAD_DIM), jnp.float32)
    value_acc = jnp.zeros((length, heads_here, HEAD_DIM), jnp.float32)
    query_parts = []
    for row_start, log_total in zip(range(0, length, block_rows), lse_parts):
        row_end = row_start + block_rows
        raw_scores, allowed = scores_of(row_start, row_end)
        probabilities = jnp.where(allowed[None], jnp.exp(raw_scores - log_total), 0.0)
        prob_low = probabilities.astype(jnp.bfloat16)
        grad_block = mixed_grad_heads[row_start:row_end]
        prob_grad = jnp.einsum(
            "qhe,khe->hqk", grad_block, value_heads[:row_end], preferred_element_type=jnp.float32
        )
        row_delta = jnp.sum(probabilities * prob_grad, axis=-1, keepdims=True)
        score_grad = (probabilities * (prob_grad - row_delta) * inverse).astype(jnp.bfloat16)
        query_parts.append(
            jnp.einsum(
                "hqk,khe->qhe", score_grad, key_rot[:row_end], preferred_element_type=jnp.float32
            )
        )
        key_acc = key_acc.at[:row_end].add(
            jnp.einsum(
                "hqk,qhe->khe",
                score_grad,
                query_rot[row_start:row_end],
                preferred_element_type=jnp.float32,
            )
        )
        value_acc = value_acc.at[:row_end].add(
            jnp.einsum("hqk,qhe->khe", prob_low, grad_block, preferred_element_type=jnp.float32)
        )
    query_norm_grad = unrotate(
        jnp.concatenate(query_parts, axis=0), cosine_table, sine_table
    ).reshape(length, -1)
    key_norm_grad = unrotate(key_acc, cosine_table, sine_table).reshape(length, -1)
    back_sums = lax.psum(
        (
            jnp.sum(query_proj * query_gains * query_norm_grad, axis=-1),
            jnp.sum(key_proj * key_gains * key_norm_grad, axis=-1),
        ),
        "tensor",
    )
    query_gradient = (
        query_scale * query_gains * query_norm_grad
        - query_proj * query_scale**3 * back_sums[0][:, None] / model_width
    ).astype(jnp.bfloat16)
    key_gradient = (
        key_scale * key_gains * key_norm_grad
        - key_proj * key_scale**3 * back_sums[1][:, None] / model_width
    ).astype(jnp.bfloat16)
    value_gradient = value_acc.reshape(length, -1).astype(jnp.bfloat16)
    query_middle_gradient = adapter_scale_factor * rank_reduced(query_gradient, query_widened)
    key_middle_gradient = adapter_scale_factor * rank_reduced(key_gradient, key_widened)
    value_middle_gradient = adapter_scale_factor * rank_reduced(value_gradient, value_widened)
    gradient_query_widened = adapter_scale_factor * outer_gradient(query_middle, query_gradient)
    gradient_key_widened = adapter_scale_factor * outer_gradient(key_middle, key_gradient)
    gradient_value_widened = adapter_scale_factor * outer_gradient(value_middle, value_gradient)
    token_grads = hidden_grad + lax.psum_scatter(
        (
            jnp.dot(query_gradient, w_query.T, preferred_element_type=jnp.float32)
            + jnp.dot(key_gradient, w_key.T, preferred_element_type=jnp.float32)
            + jnp.dot(value_gradient, w_value.T, preferred_element_type=jnp.float32)
            + widen_from_rank(query_middle_gradient, query_shrink)
            + widen_from_rank(key_middle_gradient, key_shrink)
            + widen_from_rank(value_middle_gradient, value_shrink)
        ).astype(jnp.bfloat16),
        "tensor",
        scatter_dimension=0,
        tiled=True,
    ).astype(jnp.float32)
    sets_here = shrink_query.shape[0]
    dp_size = lax.axis_size("dp")
    tensor_size = lax.axis_size("tensor")
    rank = query_shrink.shape[0]
    set_of_each = lax.all_gather(chosen, "dp")
    onehot = (jnp.arange(sets_here)[:, None] == set_of_each[None, :]).astype(jnp.bfloat16)

    split = jnp.concatenate(
        [
            gradient_query_widened,
            gradient_key_widened,
            gradient_value_widened,
            grad_out_shrink,
            gradient_gate_widened,
            gradient_up_widened,
            grad_down_shrink,
        ],
        axis=1,
    ).astype(jnp.bfloat16)
    split_all = lax.all_gather(split, "dp")
    split_sums = jnp.einsum("cs,srw->crw", onehot, split_all, preferred_element_type=jnp.float32)
    local_sums = []
    at = 0
    for part in (
        gradient_query_widened,
        gradient_key_widened,
        gradient_value_widened,
        grad_out_shrink,
        gradient_gate_widened,
        gradient_up_widened,
        grad_down_shrink,
    ):
        local_sums.append(split_sums[:, :, at : at + part.shape[1]])
        at += part.shape[1]
    middles = lax.psum(
        jnp.concatenate(
            [
                query_middle_gradient,
                key_middle_gradient,
                value_middle_gradient,
                adapter_scale_factor * output_middle,
                gate_middle_gradient,
                up_middle_gradient,
                adapter_scale_factor * down_middle,
            ],
            axis=1,
        ),
        "tensor",
    ).astype(jnp.bfloat16)
    wide = jnp.concatenate(
        [
            outer_gradient(middles[:, : 3 * rank], full_tokens),
            outer_gradient(middles[:, 3 * rank : 4 * rank], complete_mixer_gradient),
            outer_gradient(middles[:, 4 * rank : 6 * rank], full_hidden),
            outer_gradient(middles[:, 6 * rank :], complete_feed_gradient),
        ],
        axis=0,
    )
    blocks = wide.reshape(7 * rank, dp_size, tensor_size, -1)
    mine = lax.dynamic_index_in_dim(blocks, lax.axis_index("tensor"), 2, keepdims=False)
    swapped = lax.all_to_all(mine.transpose(1, 0, 2), "dp", 0, 0)
    shared_sums = jnp.einsum(
        "cs,srw->crw",
        onehot.astype(jnp.float32),
        swapped,
        precision=highest,
        preferred_element_type=jnp.float32,
    )
    shared = [shared_sums[:, i * rank : (i + 1) * rank] for i in range(7)]
    return (
        block_output,
        token_grads,
        shared[0],
        local_sums[0],
        shared[1],
        local_sums[1],
        shared[2],
        local_sums[2],
        local_sums[3],
        shared[3],
        shared[4],
        local_sums[4],
        shared[5],
        local_sums[5],
        local_sums[6],
        shared[6],
    )


def solution(mesh):
    in_specs = (
        P(("dp", "tensor"), None),
        P(("dp", "tensor"), None),
        P("dp", None),
        P("dp"),
        P(None, "tensor"),
        P(None, "tensor"),
        P(None, "tensor"),
        P("tensor", None),
        P(None, "tensor"),
        P(None, "tensor"),
        P("tensor", None),
        P("tensor"),
        P("tensor"),
        P(),
        P(),
        P(),
        P(None, None, "tensor"),
        P(),
        P(None, None, "tensor"),
        P(),
        P(None, None, "tensor"),
        P(None, None, "tensor"),
        P(),
        P(),
        P(None, None, "tensor"),
        P(),
        P(None, None, "tensor"),
        P(None, None, "tensor"),
        P(),
    )
    out_specs = (
        P(("dp", "tensor"), None),
        P(("dp", "tensor"), None),
        P(None, None, ("dp", "tensor")),
        P(None, None, "tensor"),
        P(None, None, ("dp", "tensor")),
        P(None, None, "tensor"),
        P(None, None, ("dp", "tensor")),
        P(None, None, "tensor"),
        P(None, None, "tensor"),
        P(None, None, ("dp", "tensor")),
        P(None, None, ("dp", "tensor")),
        P(None, None, "tensor"),
        P(None, None, ("dp", "tensor")),
        P(None, None, "tensor"),
        P(None, None, "tensor"),
        P(None, None, ("dp", "tensor")),
    )
    return jax.shard_map(
        per_device, mesh=mesh, in_specs=in_specs, out_specs=out_specs, check_vma=False
    )
```

```python
import functools
import jax
import jax.numpy as jnp
import numpy as np
from jax import lax
from jax.experimental import pallas as pl
from jax.experimental.pallas import tpu as pltpu
from jax.sharding import PartitionSpec as P

HEAD_DIM = 128
DOC_MOST = 512
ATT_ROWS = 256
rotary_base = 500000.0
NEG = -1e30


def rotary_constants(length, head_dim):
    half = head_dim // 2
    frequency = np.float32(rotary_base) ** (
        -(np.arange(half, dtype=np.float32) * np.float32(2.0) / np.float32(head_dim))
    )
    angles = np.arange(length, dtype=np.float32)[:, None] * frequency.astype(np.float32)[None, :]
    cosine = np.cos(angles.astype(np.float64)).astype(np.float32)
    sine = np.sin(angles.astype(np.float64)).astype(np.float32)
    return (
        np.concatenate([cosine, cosine], axis=1),
        np.concatenate([-sine, sine], axis=1),
    )


def key_window(block, rows):
    first = max(0, (block * rows - (DOC_MOST - 1)) // rows) * rows
    return first, (block + 1) * rows


def attention_forward_body(
    query_ref, key_ref, value_ref, qscale_ref, kscale_ref, qgain_ref, kgain_ref,
    cos_ref, sin_ref, seg_col_ref, seg_row_ref, mixed_ref, qrot_ref, krot_ref,
):
    length = query_ref.shape[0]
    half = HEAD_DIM // 2
    for source, scale, gain, target in (
        (query_ref, qscale_ref, qgain_ref, qrot_ref),
        (key_ref, kscale_ref, kgain_ref, krot_ref),
    ):
        normed = source[...] * scale[...] * gain[...]
        turned = normed * cos_ref[...] + pltpu.roll(normed, half, 1) * sin_ref[...]
        target[...] = turned.astype(jnp.bfloat16)
    inverse = HEAD_DIM ** (-0.5)
    rows = min(ATT_ROWS, length)
    for block in range(length // rows):
        low, high = key_window(block, rows)
        here = pl.ds(block * rows, rows)
        keys = pl.ds(low, high - low)
        scores = (
            lax.dot_general(
                qrot_ref[here, :], krot_ref[keys, :], (((1,), (1,)), ((), ())),
                preferred_element_type=jnp.float32,
            )
            * inverse
        )
        qpos = lax.broadcasted_iota(jnp.int32, scores.shape, 0) + block * rows
        kpos = lax.broadcasted_iota(jnp.int32, scores.shape, 1) + low
        allowed = (kpos <= qpos) & (seg_col_ref[here, :] == seg_row_ref[:, keys])
        scores = jnp.where(allowed, scores, NEG)
        top = jnp.max(scores, axis=1, keepdims=True)
        weights = jnp.exp(scores - top)
        total = jnp.sum(weights, axis=1, keepdims=True)
        probs = (weights * (1.0 / total)).astype(jnp.bfloat16)
        mixed_ref[here, :] = jnp.dot(
            probs, value_ref[keys, :], preferred_element_type=jnp.float32
        ).astype(jnp.bfloat16)


def attention_forward(query, key, value, qscale, kscale, qgain, kgain, cos, sin, seg_col, seg_row):
    length, width = query.shape
    heads = width // HEAD_DIM
    column = pl.BlockSpec((length, HEAD_DIM), lambda h: (0, h))
    gain = pl.BlockSpec((1, HEAD_DIM), lambda h: (0, h))
    whole = lambda a: pl.BlockSpec(a.shape, lambda h: (0, 0))
    flops = 4 * length * length * width
    return pl.pallas_call(
        attention_forward_body,
        grid=(heads,),
        in_specs=[
            column, column, column, whole(qscale), whole(kscale), gain, gain,
            whole(cos), whole(sin), whole(seg_col), whole(seg_row),
        ],
        out_specs=[column, column, column],
        out_shape=[jax.ShapeDtypeStruct((length, width), jnp.bfloat16)] * 3,
        cost_estimate=pl.CostEstimate(
            flops=flops, bytes_accessed=14 * length * width, transcendentals=length * length * heads
        ),
        compiler_params=pltpu.CompilerParams(vmem_limit_bytes=48 * 2**20),
        name="attention_forward",
    )(query, key, value, qscale, kscale, qgain, kgain, cos, sin, seg_col, seg_row)


def attention_backward_body(
    qrot_ref, krot_ref, value_ref, grad_ref, query_ref, key_ref, qgain_ref, kgain_ref,
    cos_ref, sin_ref, seg_col_ref, seg_row_ref,
    dquery_ref, dkey_ref, dvalue_ref, qsum_ref, ksum_ref, dk_acc, dv_acc,
):
    length = qrot_ref.shape[0]
    half = HEAD_DIM // 2
    inverse = HEAD_DIM ** (-0.5)
    rows = min(ATT_ROWS, length)

    @pl.when(pl.program_id(0) == 0)
    def _():
        qsum_ref[...] = jnp.zeros_like(qsum_ref)
        ksum_ref[...] = jnp.zeros_like(ksum_ref)

    dk_acc[...] = jnp.zeros_like(dk_acc)
    dv_acc[...] = jnp.zeros_like(dv_acc)
    for block in range(length // rows):
        low, high = key_window(block, rows)
        here = pl.ds(block * rows, rows)
        keys = pl.ds(low, high - low)
        queries = qrot_ref[here, :]
        key_rows = krot_ref[keys, :]
        grads = grad_ref[here, :]
        scores = (
            lax.dot_general(
                key_rows, queries, (((1,), (1,)), ((), ())), preferred_element_type=jnp.float32
            )
            * inverse
        )
        kpos = lax.broadcasted_iota(jnp.int32, scores.shape, 0) + low
        qpos = lax.broadcasted_iota(jnp.int32, scores.shape, 1) + block * rows
        allowed = (kpos <= qpos) & (seg_col_ref[keys, :] == seg_row_ref[:, here])
        scores = jnp.where(allowed, scores, NEG)
        top = jnp.max(scores, axis=0, keepdims=True)
        weights = jnp.exp(scores - top)
        total = jnp.sum(weights, axis=0, keepdims=True)
        probs = weights * (1.0 / total)
        prob_grad = lax.dot_general(
            value_ref[keys, :], grads, (((1,), (1,)), ((), ())), preferred_element_type=jnp.float32
        )
        weighted = probs * prob_grad
        delta = jnp.sum(weighted, axis=0, keepdims=True)
        score_grad = ((weighted - probs * delta) * inverse).astype(jnp.bfloat16)
        dv_acc[keys, :] += jnp.dot(
            probs.astype(jnp.bfloat16), grads, preferred_element_type=jnp.float32
        )
        dk_acc[keys, :] += jnp.dot(score_grad, queries, preferred_element_type=jnp.float32)
        dq = lax.dot_general(
            score_grad, key_rows, (((0,), (0,)), ((), ())), preferred_element_type=jnp.float32
        )
        dq = dq * cos_ref[here, :] - pltpu.roll(dq, half, 1) * sin_ref[here, :]
        dquery_ref[here, :] = dq
        qsum_ref[here, :] += query_ref[here, :] * qgain_ref[...] * dq
    dk = dk_acc[...]
    dk = dk * cos_ref[...] - pltpu.roll(dk, half, 1) * sin_ref[...]
    dkey_ref[...] = dk
    ksum_ref[...] += key_ref[...] * kgain_ref[...] * dk
    dvalue_ref[...] = dv_acc[...].astype(jnp.bfloat16)


def attention_backward(qrot, krot, value, grad, query, key, qgain, kgain, cos, sin, seg_col, seg_row):
    length, width = qrot.shape
    heads = width // HEAD_DIM
    column = pl.BlockSpec((length, HEAD_DIM), lambda h: (0, h))
    gain = pl.BlockSpec((1, HEAD_DIM), lambda h: (0, h))
    whole = lambda a: pl.BlockSpec(a.shape, lambda h: (0, 0))
    sums = pl.BlockSpec((length, HEAD_DIM), lambda h: (0, 0))
    return pl.pallas_call(
        attention_backward_body,
        grid=(heads,),
        in_specs=[
            column, column, column, column, column, column, gain, gain,
            whole(cos), whole(sin), whole(seg_col), whole(seg_row),
        ],
        out_specs=[column, column, column, sums, sums],
        out_shape=[
            jax.ShapeDtypeStruct((length, width), jnp.float32),
            jax.ShapeDtypeStruct((length, width), jnp.float32),
            jax.ShapeDtypeStruct((length, width), jnp.bfloat16),
            jax.ShapeDtypeStruct((length, HEAD_DIM), jnp.float32),
            jax.ShapeDtypeStruct((length, HEAD_DIM), jnp.float32),
        ],
        scratch_shapes=[
            pltpu.VMEM((length, HEAD_DIM), jnp.float32),
            pltpu.VMEM((length, HEAD_DIM), jnp.float32),
        ],
        cost_estimate=pl.CostEstimate(
            flops=10 * length * length * width, bytes_accessed=30 * length * width,
            transcendentals=length * length * heads,
        ),
        compiler_params=pltpu.CompilerParams(vmem_limit_bytes=48 * 2**20),
        name="attention_backward",
    )(qrot, krot, value, grad, query, key, qgain, kgain, cos, sin, seg_col, seg_row)


epsilon = 1e-06
adapter_scale_factor = 0.5
highest = lax.Precision.HIGHEST


def scale_of(values):
    return lax.rsqrt(jnp.mean(values * values, axis=-1, keepdims=True) + epsilon)


def norm_back(values, factor, gains, grads):
    weighted = grads * gains
    return factor * weighted - values * factor**3 * jnp.mean(
        values * weighted, axis=-1, keepdims=True
    )


def rank_reduced(input_rows, shrink):
    return jnp.dot(input_rows, shrink.T, preferred_element_type=jnp.float32)


def widen_from_rank(middle_rows, widen_factor):
    return jnp.dot(
        middle_rows.astype(jnp.bfloat16), widen_factor, preferred_element_type=jnp.float32
    )


def outer_gradient(middle_rows, input_rows):
    return lax.dot_general(
        middle_rows.astype(jnp.bfloat16),
        input_rows,
        (((0,), (0,)), ((), ())),
        preferred_element_type=jnp.float32,
    )


def per_device(
    tokens,
    cotangent,
    segment_ids,
    adapter_set,
    w_query,
    w_key,
    w_value,
    w_out,
    w_gate,
    w_up,
    w_down,
    query_gain,
    key_gain,
    mixer_gain,
    feed_gain,
    shrink_query,
    expand_query,
    shrink_key,
    expand_key,
    shrink_value,
    expand_value,
    shrink_out,
    expand_out,
    shrink_gate,
    expand_gate,
    shrink_up,
    expand_up,
    shrink_down,
    expand_down,
):
    model_width = w_query.shape[0]
    chosen = adapter_set[0]

    def choose_set(adapters):
        return lax.dynamic_index_in_dim(adapters, chosen, 0, keepdims=False)

    query_shrink, query_widened = (choose_set(shrink_query), choose_set(expand_query))
    key_shrink, key_widened = (choose_set(shrink_key), choose_set(expand_key))
    value_shrink, value_widened = (choose_set(shrink_value), choose_set(expand_value))
    out_shrink, output_widened = (choose_set(shrink_out), choose_set(expand_out))
    gate_shrink, gate_widened = (choose_set(shrink_gate), choose_set(expand_gate))
    up_shrink, up_widened = (choose_set(shrink_up), choose_set(expand_up))
    down_shrink, down_widened = (choose_set(shrink_down), choose_set(expand_down))
    full_tokens = lax.all_gather(tokens, "tensor", axis=0, tiled=True)
    length = full_tokens.shape[0]
    query_middle = rank_reduced(full_tokens, query_shrink)
    key_middle = rank_reduced(full_tokens, key_shrink)
    value_middle = rank_reduced(full_tokens, value_shrink)
    query_proj = jnp.dot(
        full_tokens, w_query, preferred_element_type=jnp.float32
    ) + adapter_scale_factor * widen_from_rank(query_middle, query_widened)
    key_proj = jnp.dot(
        full_tokens, w_key, preferred_element_type=jnp.float32
    ) + adapter_scale_factor * widen_from_rank(key_middle, key_widened)
    value_proj = jnp.dot(
        full_tokens, w_value, preferred_element_type=jnp.float32
    ) + adapter_scale_factor * widen_from_rank(value_middle, value_widened)
    totals = lax.psum(
        (jnp.sum(query_proj * query_proj, axis=-1), jnp.sum(key_proj * key_proj, axis=-1)), "tensor"
    )
    query_scale = lax.rsqrt(totals[0] / model_width + epsilon)[:, None]
    key_scale = lax.rsqrt(totals[1] / model_width + epsilon)[:, None]
    query_gains = query_gain.astype(jnp.float32)
    key_gains = key_gain.astype(jnp.float32)
    cosine_table, sine_table = rotary_constants(length, HEAD_DIM)
    cosine_table, sine_table = jnp.asarray(cosine_table), jnp.asarray(sine_table)
    seg_col = segment_ids.reshape(length, 1)
    value_low = value_proj.astype(jnp.bfloat16)
    mixed, query_rot, key_rot = attention_forward(
        query_proj, key_proj, value_low, query_scale, key_scale, query_gains[None], key_gains[None],
        cosine_table, sine_table, seg_col, segment_ids,
    )
    output_middle = rank_reduced(mixed, out_shrink)
    mixer_rows = lax.psum_scatter(
        (
            jnp.dot(mixed, w_out, preferred_element_type=jnp.float32)
            + adapter_scale_factor * widen_from_rank(output_middle, output_widened)
        ).astype(jnp.bfloat16),
        "tensor",
        scatter_dimension=0,
        tiled=True,
    ).astype(jnp.float32)
    mixer_scale = scale_of(mixer_rows)
    mixer_gains = mixer_gain.astype(jnp.float32)
    hidden = tokens.astype(jnp.float32) + mixer_rows * mixer_scale * mixer_gains
    full_hidden = lax.all_gather(hidden.astype(jnp.bfloat16), "tensor", axis=0, tiled=True)
    gate_middle = rank_reduced(full_hidden, gate_shrink)
    up_middle = rank_reduced(full_hidden, up_shrink)
    gate = jnp.dot(
        full_hidden, w_gate, preferred_element_type=jnp.float32
    ) + adapter_scale_factor * widen_from_rank(gate_middle, gate_widened)
    up_proj = jnp.dot(
        full_hidden, w_up, preferred_element_type=jnp.float32
    ) + adapter_scale_factor * widen_from_rank(up_middle, up_widened)
    sigmoid_gate = jax.nn.sigmoid(gate)
    inner_act = (gate * sigmoid_gate * up_proj).astype(jnp.bfloat16)
    down_middle = rank_reduced(inner_act, down_shrink)
    feed_rows = lax.psum_scatter(
        (
            jnp.dot(inner_act, w_down, preferred_element_type=jnp.float32)
            + adapter_scale_factor * widen_from_rank(down_middle, down_widened)
        ).astype(jnp.bfloat16),
        "tensor",
        scatter_dimension=0,
        tiled=True,
    ).astype(jnp.float32)
    feed_scale = scale_of(feed_rows)
    feed_gains = feed_gain.astype(jnp.float32)
    block_output = (hidden + feed_rows * feed_scale * feed_gains).astype(jnp.bfloat16)
    upstream = cotangent.astype(jnp.float32)
    feed_grad = norm_back(feed_rows, feed_scale, feed_gains, upstream).astype(jnp.bfloat16)
    complete_feed_gradient = lax.all_gather(feed_grad, "tensor", axis=0, tiled=True)
    down_middle_gradient = adapter_scale_factor * rank_reduced(complete_feed_gradient, down_widened)
    inner_grad = jnp.dot(
        complete_feed_gradient, w_down.T, preferred_element_type=jnp.float32
    ) + widen_from_rank(down_middle_gradient, down_shrink)
    grad_down_shrink = outer_gradient(down_middle_gradient, inner_act)
    gate_gradient = (
        inner_grad * up_proj * (sigmoid_gate * (1.0 + gate * (1.0 - sigmoid_gate)))
    ).astype(jnp.bfloat16)
    up_gradient = (inner_grad * gate * sigmoid_gate).astype(jnp.bfloat16)
    gate_middle_gradient = adapter_scale_factor * rank_reduced(gate_gradient, gate_widened)
    up_middle_gradient = adapter_scale_factor * rank_reduced(up_gradient, up_widened)
    gradient_gate_widened = adapter_scale_factor * outer_gradient(gate_middle, gate_gradient)
    gradient_up_widened = adapter_scale_factor * outer_gradient(up_middle, up_gradient)
    hidden_grad = upstream + lax.psum_scatter(
        (
            jnp.dot(gate_gradient, w_gate.T, preferred_element_type=jnp.float32)
            + jnp.dot(up_gradient, w_up.T, preferred_element_type=jnp.float32)
            + widen_from_rank(gate_middle_gradient, gate_shrink)
            + widen_from_rank(up_middle_gradient, up_shrink)
        ).astype(jnp.bfloat16),
        "tensor",
        scatter_dimension=0,
        tiled=True,
    ).astype(jnp.float32)
    mixer_grad = norm_back(mixer_rows, mixer_scale, mixer_gains, hidden_grad).astype(jnp.bfloat16)
    complete_mixer_gradient = lax.all_gather(mixer_grad, "tensor", axis=0, tiled=True)
    output_middle_gradient = adapter_scale_factor * rank_reduced(
        complete_mixer_gradient, output_widened
    )
    mixed_grad = (
        jnp.dot(complete_mixer_gradient, w_out.T, preferred_element_type=jnp.float32)
        + widen_from_rank(output_middle_gradient, out_shrink)
    ).astype(jnp.bfloat16)
    grad_out_shrink = outer_gradient(output_middle_gradient, mixed)
    query_norm_grad, key_norm_grad, value_gradient, query_sums, key_sums = attention_backward(
        query_rot, key_rot, value_low, mixed_grad, query_proj, key_proj,
        query_gains[None], key_gains[None], cosine_table, sine_table, seg_col, segment_ids,
    )
    back_sums = lax.psum((jnp.sum(query_sums, axis=-1), jnp.sum(key_sums, axis=-1)), "tensor")
    query_gradient = (
        query_scale * query_gains * query_norm_grad
        - query_proj * query_scale**3 * back_sums[0][:, None] / model_width
    ).astype(jnp.bfloat16)
    key_gradient = (
        key_scale * key_gains * key_norm_grad
        - key_proj * key_scale**3 * back_sums[1][:, None] / model_width
    ).astype(jnp.bfloat16)
    query_middle_gradient = adapter_scale_factor * rank_reduced(query_gradient, query_widened)
    key_middle_gradient = adapter_scale_factor * rank_reduced(key_gradient, key_widened)
    value_middle_gradient = adapter_scale_factor * rank_reduced(value_gradient, value_widened)
    gradient_query_widened = adapter_scale_factor * outer_gradient(query_middle, query_gradient)
    gradient_key_widened = adapter_scale_factor * outer_gradient(key_middle, key_gradient)
    gradient_value_widened = adapter_scale_factor * outer_gradient(value_middle, value_gradient)
    token_grads = hidden_grad + lax.psum_scatter(
        (
            jnp.dot(query_gradient, w_query.T, preferred_element_type=jnp.float32)
            + jnp.dot(key_gradient, w_key.T, preferred_element_type=jnp.float32)
            + jnp.dot(value_gradient, w_value.T, preferred_element_type=jnp.float32)
            + widen_from_rank(query_middle_gradient, query_shrink)
            + widen_from_rank(key_middle_gradient, key_shrink)
            + widen_from_rank(value_middle_gradient, value_shrink)
        ).astype(jnp.bfloat16),
        "tensor",
        scatter_dimension=0,
        tiled=True,
    ).astype(jnp.float32)
    sets_here = shrink_query.shape[0]
    dp_size = lax.axis_size("dp")
    tensor_size = lax.axis_size("tensor")
    rank = query_shrink.shape[0]
    set_of_each = lax.all_gather(chosen, "dp")
    onehot = (jnp.arange(sets_here)[:, None] == set_of_each[None, :]).astype(jnp.bfloat16)

    split = jnp.concatenate(
        [
            gradient_query_widened,
            gradient_key_widened,
            gradient_value_widened,
            grad_out_shrink,
            gradient_gate_widened,
            gradient_up_widened,
            grad_down_shrink,
        ],
        axis=1,
    ).astype(jnp.bfloat16)
    split_all = lax.all_gather(split, "dp")
    split_sums = jnp.einsum("cs,srw->crw", onehot, split_all, preferred_element_type=jnp.float32)
    local_sums = []
    at = 0
    for part in (
        gradient_query_widened,
        gradient_key_widened,
        gradient_value_widened,
        grad_out_shrink,
        gradient_gate_widened,
        gradient_up_widened,
        grad_down_shrink,
    ):
        local_sums.append(split_sums[:, :, at : at + part.shape[1]])
        at += part.shape[1]
    middles = lax.psum(
        jnp.concatenate(
            [
                query_middle_gradient,
                key_middle_gradient,
                value_middle_gradient,
                adapter_scale_factor * output_middle,
                gate_middle_gradient,
                up_middle_gradient,
                adapter_scale_factor * down_middle,
            ],
            axis=1,
        ),
        "tensor",
    ).astype(jnp.bfloat16)
    wide = jnp.concatenate(
        [
            outer_gradient(middles[:, : 3 * rank], full_tokens),
            outer_gradient(middles[:, 3 * rank : 4 * rank], complete_mixer_gradient),
            outer_gradient(middles[:, 4 * rank : 6 * rank], full_hidden),
            outer_gradient(middles[:, 6 * rank :], complete_feed_gradient),
        ],
        axis=0,
    )
    blocks = wide.reshape(7 * rank, dp_size, tensor_size, -1)
    mine = lax.dynamic_index_in_dim(blocks, lax.axis_index("tensor"), 2, keepdims=False)
    swapped = lax.all_to_all(mine.transpose(1, 0, 2), "dp", 0, 0)
    shared_sums = jnp.einsum(
        "cs,srw->crw",
        onehot.astype(jnp.float32),
        swapped,
        precision=highest,
        preferred_element_type=jnp.float32,
    )
    shared = [shared_sums[:, i * rank : (i + 1) * rank] for i in range(7)]
    return (
        block_output,
        token_grads,
        shared[0],
        local_sums[0],
        shared[1],
        local_sums[1],
        shared[2],
        local_sums[2],
        local_sums[3],
        shared[3],
        shared[4],
        local_sums[4],
        shared[5],
        local_sums[5],
        local_sums[6],
        shared[6],
    )


def solution(mesh):
    in_specs = (
        P(("dp", "tensor"), None),
        P(("dp", "tensor"), None),
        P("dp", None),
        P("dp"),
        P(None, "tensor"),
        P(None, "tensor"),
        P(None, "tensor"),
        P("tensor", None),
        P(None, "tensor"),
        P(None, "tensor"),
        P("tensor", None),
        P("tensor"),
        P("tensor"),
        P(),
        P(),
        P(),
        P(None, None, "tensor"),
        P(),
        P(None, None, "tensor"),
        P(),
        P(None, None, "tensor"),
        P(None, None, "tensor"),
        P(),
        P(),
        P(None, None, "tensor"),
        P(),
        P(None, None, "tensor"),
        P(None, None, "tensor"),
        P(),
    )
    out_specs = (
        P(("dp", "tensor"), None),
        P(("dp", "tensor"), None),
        P(None, None, ("dp", "tensor")),
        P(None, None, "tensor"),
        P(None, None, ("dp", "tensor")),
        P(None, None, "tensor"),
        P(None, None, ("dp", "tensor")),
        P(None, None, "tensor"),
        P(None, None, "tensor"),
        P(None, None, ("dp", "tensor")),
        P(None, None, ("dp", "tensor")),
        P(None, None, "tensor"),
        P(None, None, ("dp", "tensor")),
        P(None, None, "tensor"),
        P(None, None, "tensor"),
        P(None, None, ("dp", "tensor")),
    )
    return jax.shard_map(
        per_device, mesh=mesh, in_specs=in_specs, out_specs=out_specs, check_vma=False
    )
```

```python
import functools
import jax
import jax.numpy as jnp
import numpy as np
from jax import lax
from jax.experimental import pallas as pl
from jax.experimental.pallas import tpu as pltpu
from jax.sharding import PartitionSpec as P

HEAD_DIM = 128
DOC_MOST = 512
ATT_ROWS = 256
rotary_base = 500000.0
NEG = -1e30


def rotary_constants(length, head_dim):
    half = head_dim // 2
    frequency = np.float32(rotary_base) ** (
        -(np.arange(half, dtype=np.float32) * np.float32(2.0) / np.float32(head_dim))
    )
    angles = np.arange(length, dtype=np.float32)[:, None] * frequency.astype(np.float32)[None, :]
    cosine = np.cos(angles.astype(np.float64)).astype(np.float32)
    sine = np.sin(angles.astype(np.float64)).astype(np.float32)
    return (
        np.concatenate([cosine, cosine], axis=1),
        np.concatenate([-sine, sine], axis=1),
    )


def key_window(block, rows):
    first = max(0, (block * rows - (DOC_MOST - 1)) // rows) * rows
    return first, (block + 1) * rows


def attention_forward_body(
    query_ref, key_ref, value_ref, qscale_ref, kscale_ref, qgain_ref, kgain_ref,
    cos_ref, sin_ref, seg_col_ref, seg_row_ref, mixed_ref, qrot_ref, krot_ref,
):
    length = query_ref.shape[0]
    half = HEAD_DIM // 2
    for source, scale, gain, target in (
        (query_ref, qscale_ref, qgain_ref, qrot_ref),
        (key_ref, kscale_ref, kgain_ref, krot_ref),
    ):
        normed = source[...] * scale[...] * gain[...]
        turned = normed * cos_ref[...] + pltpu.roll(normed, half, 1) * sin_ref[...]
        target[...] = turned.astype(jnp.bfloat16)
    inverse = HEAD_DIM ** (-0.5)
    rows = min(ATT_ROWS, length)
    for block in range(length // rows):
        low, high = key_window(block, rows)
        here = pl.ds(block * rows, rows)
        keys = pl.ds(low, high - low)
        scores = (
            lax.dot_general(
                qrot_ref[here, :], krot_ref[keys, :], (((1,), (1,)), ((), ())),
                preferred_element_type=jnp.float32,
            )
            * inverse
        )
        qpos = lax.broadcasted_iota(jnp.int32, scores.shape, 0) + block * rows
        kpos = lax.broadcasted_iota(jnp.int32, scores.shape, 1) + low
        allowed = (kpos <= qpos) & (seg_col_ref[here, :] == seg_row_ref[:, keys])
        scores = jnp.where(allowed, scores, NEG)
        top = jnp.max(scores, axis=1, keepdims=True)
        weights = jnp.exp(scores - top)
        total = jnp.sum(weights, axis=1, keepdims=True)
        probs = (weights * (1.0 / total)).astype(jnp.bfloat16)
        mixed_ref[here, :] = jnp.dot(
            probs, value_ref[keys, :], preferred_element_type=jnp.float32
        ).astype(jnp.bfloat16)


def attention_forward(query, key, value, qscale, kscale, qgain, kgain, cos, sin, seg_col, seg_row):
    length, width = query.shape
    heads = width // HEAD_DIM
    column = pl.BlockSpec((length, HEAD_DIM), lambda h: (0, h))
    gain = pl.BlockSpec((1, HEAD_DIM), lambda h: (0, h))
    whole = lambda a: pl.BlockSpec(a.shape, lambda h: (0, 0))
    flops = 4 * length * length * width
    return pl.pallas_call(
        attention_forward_body,
        grid=(heads,),
        in_specs=[
            column, column, column, whole(qscale), whole(kscale), gain, gain,
            whole(cos), whole(sin), whole(seg_col), whole(seg_row),
        ],
        out_specs=[column, column, column],
        out_shape=[jax.ShapeDtypeStruct((length, width), jnp.bfloat16)] * 3,
        cost_estimate=pl.CostEstimate(
            flops=flops, bytes_accessed=14 * length * width, transcendentals=length * length * heads
        ),
        compiler_params=pltpu.CompilerParams(vmem_limit_bytes=48 * 2**20),
        name="attention_forward",
    )(query, key, value, qscale, kscale, qgain, kgain, cos, sin, seg_col, seg_row)


def attention_backward_body(
    qrot_ref, krot_ref, value_ref, grad_ref, query_ref, key_ref, qgain_ref, kgain_ref,
    cos_ref, sin_ref, seg_col_ref, seg_row_ref,
    dquery_ref, dkey_ref, dvalue_ref, qsum_ref, ksum_ref, dk_acc, dv_acc,
):
    length = qrot_ref.shape[0]
    half = HEAD_DIM // 2
    inverse = HEAD_DIM ** (-0.5)
    rows = min(ATT_ROWS, length)

    @pl.when(pl.program_id(0) == 0)
    def _():
        qsum_ref[...] = jnp.zeros_like(qsum_ref)
        ksum_ref[...] = jnp.zeros_like(ksum_ref)

    dk_acc[...] = jnp.zeros_like(dk_acc)
    dv_acc[...] = jnp.zeros_like(dv_acc)
    for block in range(length // rows):
        low, high = key_window(block, rows)
        here = pl.ds(block * rows, rows)
        keys = pl.ds(low, high - low)
        queries = qrot_ref[here, :]
        key_rows = krot_ref[keys, :]
        grads = grad_ref[here, :]
        scores = (
            lax.dot_general(
                key_rows, queries, (((1,), (1,)), ((), ())), preferred_element_type=jnp.float32
            )
            * inverse
        )
        kpos = lax.broadcasted_iota(jnp.int32, scores.shape, 0) + low
        qpos = lax.broadcasted_iota(jnp.int32, scores.shape, 1) + block * rows
        allowed = (kpos <= qpos) & (seg_col_ref[keys, :] == seg_row_ref[:, here])
        scores = jnp.where(allowed, scores, NEG)
        top = jnp.max(scores, axis=0, keepdims=True)
        weights = jnp.exp(scores - top)
        total = jnp.sum(weights, axis=0, keepdims=True)
        probs = weights * (1.0 / total)
        prob_grad = lax.dot_general(
            value_ref[keys, :], grads, (((1,), (1,)), ((), ())), preferred_element_type=jnp.float32
        )
        weighted = probs * prob_grad
        delta = jnp.sum(weighted, axis=0, keepdims=True)
        score_grad = ((weighted - probs * delta) * inverse).astype(jnp.bfloat16)
        dv_acc[keys, :] += jnp.dot(
            probs.astype(jnp.bfloat16), grads, preferred_element_type=jnp.float32
        )
        dk_acc[keys, :] += jnp.dot(score_grad, queries, preferred_element_type=jnp.float32)
        dq = lax.dot_general(
            score_grad, key_rows, (((0,), (0,)), ((), ())), preferred_element_type=jnp.float32
        )
        dq = dq * cos_ref[here, :] - pltpu.roll(dq, half, 1) * sin_ref[here, :]
        dquery_ref[here, :] = dq
        qsum_ref[here, :] += query_ref[here, :] * qgain_ref[...] * dq
    dk = dk_acc[...]
    dk = dk * cos_ref[...] - pltpu.roll(dk, half, 1) * sin_ref[...]
    dkey_ref[...] = dk
    ksum_ref[...] += key_ref[...] * kgain_ref[...] * dk
    dvalue_ref[...] = dv_acc[...].astype(jnp.bfloat16)


def attention_backward(qrot, krot, value, grad, query, key, qgain, kgain, cos, sin, seg_col, seg_row):
    length, width = qrot.shape
    heads = width // HEAD_DIM
    column = pl.BlockSpec((length, HEAD_DIM), lambda h: (0, h))
    gain = pl.BlockSpec((1, HEAD_DIM), lambda h: (0, h))
    whole = lambda a: pl.BlockSpec(a.shape, lambda h: (0, 0))
    sums = pl.BlockSpec((length, HEAD_DIM), lambda h: (0, 0))
    return pl.pallas_call(
        attention_backward_body,
        grid=(heads,),
        in_specs=[
            column, column, column, column, column, column, gain, gain,
            whole(cos), whole(sin), whole(seg_col), whole(seg_row),
        ],
        out_specs=[column, column, column, sums, sums],
        out_shape=[
            jax.ShapeDtypeStruct((length, width), jnp.float32),
            jax.ShapeDtypeStruct((length, width), jnp.float32),
            jax.ShapeDtypeStruct((length, width), jnp.bfloat16),
            jax.ShapeDtypeStruct((length, HEAD_DIM), jnp.float32),
            jax.ShapeDtypeStruct((length, HEAD_DIM), jnp.float32),
        ],
        scratch_shapes=[
            pltpu.VMEM((length, HEAD_DIM), jnp.float32),
            pltpu.VMEM((length, HEAD_DIM), jnp.float32),
        ],
        cost_estimate=pl.CostEstimate(
            flops=10 * length * length * width, bytes_accessed=30 * length * width,
            transcendentals=length * length * heads,
        ),
        compiler_params=pltpu.CompilerParams(vmem_limit_bytes=48 * 2**20),
        name="attention_backward",
    )(qrot, krot, value, grad, query, key, qgain, kgain, cos, sin, seg_col, seg_row)


epsilon = 1e-06
adapter_scale_factor = 0.5
highest = lax.Precision.HIGHEST


def scale_of(values):
    return lax.rsqrt(jnp.mean(values * values, axis=-1, keepdims=True) + epsilon)


def norm_back(values, factor, gains, grads):
    weighted = grads * gains
    return factor * weighted - values * factor**3 * jnp.mean(
        values * weighted, axis=-1, keepdims=True
    )


def rank_reduced(input_rows, shrink):
    return jnp.dot(input_rows, shrink.T, preferred_element_type=jnp.float32)


def widen_from_rank(middle_rows, widen_factor):
    return jnp.dot(
        middle_rows.astype(jnp.bfloat16), widen_factor, preferred_element_type=jnp.float32
    )


def outer_gradient(middle_rows, input_rows):
    return lax.dot_general(
        middle_rows.astype(jnp.bfloat16),
        input_rows,
        (((0,), (0,)), ((), ())),
        preferred_element_type=jnp.float32,
    )


CHUNKS = 4
TILE = 1024
EXTRA = 128
NT = (((1,), (1,)), ((), ()))
TN = (((0,), (0,)), ((), ()))
MESH_ID = pl.DeviceIdType.MESH
MIDDLE_ORDER = (
    ("S2", 4), ("P4", 8), ("S4", 7), ("P0", 1), ("S1", 2), ("S6", 10), ("F3", 6),
    ("F5", 9), ("S5", 8), ("P2", 4), ("S0", 0), ("F1", 3), ("S3", 5),
)


def mm(left, right):
    return jnp.dot(left, right, preferred_element_type=jnp.float32)


def mm_nt(left, right):
    return lax.dot_general(left, right, NT, preferred_element_type=jnp.float32)


def mm_tn(left, right):
    return lax.dot_general(left, right, TN, preferred_element_type=jnp.float32)


def partners():
    me = lax.axis_index("tensor")
    group = lax.axis_index("dp")
    beside = me + 1 - 2 * lax.rem(me, 2)
    across = lax.rem(me + 2, 4)
    return me, group, beside, across


def greet(group, beside, across):
    barrier = pltpu.get_barrier_semaphore()
    for other in (beside, across):
        pl.semaphore_signal(barrier, inc=1, device_id=(group, other), device_id_type=MESH_ID)
    pl.semaphore_wait(barrier, 2)


def middle_body(
    mixed_ref, tokens_ref, cot_ref, w_out_hbm, w_gate_hbm, w_up_hbm, w_down_hbm,
    mgain_ref, fgain_ref, so_ref, eo_ref, sgu_ref, eg_ref, eu_ref, sd_ref, ed_ref,
    out_ref, hgrad_ref, dmixed_ref, gsd_ref, geg_ref, geu_ref, gso_ref, gsgu_ref, geo_ref, ged_ref,
    w_out, w_gate, w_up, w_down, wsem,
    rows_buf, own_buf, xsend, xrecv, bsend, brecv,
    gate_buf, up_buf, temp_a, temp_b, mgu_buf, mixer_buf, hidden_buf, mout_buf,
    xs_sem, xr_sem, bs_sem, br_sem, gxs_sem, gxr_sem, gbs_sem, gbr_sem, fs_sem, fr_sem,
):
    me, group, beside, across = partners()
    chunks, part, width = rows_buf.shape[0], rows_buf.shape[2], rows_buf.shape[3]
    units = w_gate.shape[1]
    heads_width = w_out.shape[0]
    far = lax.rem(beside + 2, 4)
    order = (me, across, beside, far)
    loads = [
        pltpu.make_async_copy(source, target, wsem.at[i])
        for i, (source, target) in enumerate(
            ((w_out_hbm, w_out), (w_gate_hbm, w_gate), (w_up_hbm, w_up), (w_down_hbm, w_down))
        )
    ]
    for load in loads:
        load.start()
    for ref in (gsd_ref, geg_ref, geu_ref, gso_ref, gsgu_ref, geo_ref, ged_ref):
        ref[...] = jnp.zeros_like(ref)
    greet(group, beside, across)

    def remote(source, target, ssem, rsem, other):
        return pltpu.make_async_remote_copy(
            src_ref=source, dst_ref=target, send_sem=ssem, recv_sem=rsem,
            device_id=(group, other), device_id_type=MESH_ID,
        )

    def gather_across(c):
        return remote(rows_buf.at[c, 0], rows_buf.at[c, 1], gxs_sem.at[c], gxr_sem.at[c], across)

    def gather_beside(c):
        return remote(rows_buf.at[c, 0], rows_buf.at[c, 2], gbs_sem.at[c], gbr_sem.at[c], beside)

    def gather_forward(c):
        return remote(rows_buf.at[c, 1], rows_buf.at[c, 3], fs_sem.at[c], fr_sem.at[c], beside)

    def reduce_beside(c):
        return remote(bsend.at[c], brecv.at[c], bs_sem.at[c], br_sem.at[c], beside)

    def reduce_across(c):
        return remote(xsend.at[c], xrecv.at[c], xs_sem.at[c], xr_sem.at[c], across)

    def store_partial(c, columns, value):
        low = value.astype(jnp.bfloat16)
        own_buf[c, :, columns] = low[:part]
        xsend[c, :, columns] = low[part : 2 * part]
        bsend[c, 0, :, columns] = low[2 * part : 3 * part]
        bsend[c, 1, :, columns] = low[3 * part :]

    def gathered(c):
        return rows_buf[c].reshape(4 * part, width)

    def forward_stage(c):
        gather_across(c).wait_recv()
        gather_forward(c).start()

    def pair_stage(c):
        reduce_beside(c).wait_recv()
        own_buf[c] = (
            own_buf[c].astype(jnp.float32) + brecv[c, 0].astype(jnp.float32)
        ).astype(jnp.bfloat16)
        xsend[c] = (
            xsend[c].astype(jnp.float32) + brecv[c, 1].astype(jnp.float32)
        ).astype(jnp.bfloat16)
        reduce_across(c).start()

    def totals(c):
        reduce_across(c).wait_recv()
        main = own_buf[c, :, :width].astype(jnp.float32) + xrecv[c, :, :width].astype(jnp.float32)
        side = own_buf[c, :, width : width + 32].astype(jnp.float32) + xrecv[
            c, :, width : width + 32
        ].astype(jnp.float32)
        return main, side.astype(jnp.bfloat16)

    def own_rows(c):
        return pl.ds(pl.multiple_of(c * part, part), part)

    def send_rows(c, value, again):
        if again:
            gather_across(c).wait_send()
            gather_beside(c).wait_send()
        rows_buf[c, 0] = value
        gather_across(c).start()
        gather_beside(c).start()

    def chunk_rows(c):
        return pl.ds(pl.multiple_of(c * 4 * part, 4 * part), 4 * part)

    def tiles(total, tile, body):
        def step(j, carry):
            body(pl.ds(pl.multiple_of(j * tile, tile), tile))
            return carry

        lax.fori_loop(0, total // tile, step, 0)

    def mixed_chunk(c):
        return jnp.concatenate([mixed_ref[o, c] for o in order], axis=0)

    def stage_mixer(c):
        @pl.when(c == 0)
        def _():
            loads[0].wait()

        rows = mixed_chunk(c)
        store_partial(c, slice(width, width + 16), mm_nt(rows, so_ref[...]))
        tiles(width, TILE, lambda cols: store_partial(c, cols, mm(rows, w_out[:, cols])))
        reduce_beside(c).start()

    def stage_hidden(c):
        main, side = totals(c)
        mid = side[:, :16]
        mout_buf[c] = mid
        mixer = main + mm(mid, eo_ref[...])
        mixer_buf[own_rows(c), :] = mixer
        factor = lax.rsqrt(jnp.mean(mixer * mixer, axis=1, keepdims=True) + epsilon)
        hidden = tokens_ref[own_rows(c), :].astype(jnp.float32) + mixer * factor * mgain_ref[...]
        hidden_buf[own_rows(c), :] = hidden
        send_rows(c, hidden.astype(jnp.bfloat16), False)

    def arrive(c):
        gather_beside(c).wait_recv()
        gather_forward(c).wait_recv()

    def stage_units(c):
        @pl.when(c == 0)
        def _():
            for load in loads[1:]:
                load.wait()

        arrive(c)
        mids = mm_nt(gathered(c), sgu_ref[...]).astype(jnp.bfloat16)
        mgu_buf[c] = mids

        def unit_tile(cols):
            rows = gathered(c)
            gate = mm(rows, w_gate[:, cols]) + mm(mids, eg_ref[:, cols])
            up = mm(rows, w_up[:, cols]) + mm(mids, eu_ref[:, cols])
            gate_buf[chunk_rows(c), cols] = gate.astype(jnp.bfloat16)
            up_buf[chunk_rows(c), cols] = up.astype(jnp.bfloat16)
            sig = 1.0 / (1.0 + jnp.exp(-gate))
            temp_a[:, cols] = (gate * sig * up).astype(jnp.bfloat16)

        tiles(units, TILE // 2, unit_tile)
        gather_forward(c).wait_send()
        reduce_beside(c).wait_send()
        reduce_across(c).wait_send()
        inner = temp_a[...]
        store_partial(c, slice(width, width + 16), mm_nt(inner, sd_ref[...]))
        tiles(width, TILE, lambda cols: store_partial(c, cols, mm(temp_a[...], w_down[:, cols])))
        reduce_beside(c).start()

    def norm_back_rows(values, gains, grads):
        factor = lax.rsqrt(jnp.mean(values * values, axis=1, keepdims=True) + epsilon)
        weighted = grads * gains
        return factor * weighted - values * (
            factor * factor * factor * jnp.mean(values * weighted, axis=1, keepdims=True)
        )

    def stage_feed(c):
        main, side = totals(c)
        mid = side[:, :16]
        feed = main + mm(mid, ed_ref[...])
        factor = lax.rsqrt(jnp.mean(feed * feed, axis=1, keepdims=True) + epsilon)
        gains = fgain_ref[...]
        out_ref[own_rows(c), :] = (hidden_buf[own_rows(c), :] + feed * factor * gains).astype(
            jnp.bfloat16
        )
        grad = norm_back_rows(feed, gains, cot_ref[own_rows(c), :].astype(jnp.float32))
        grad = grad.astype(jnp.bfloat16)
        send_rows(c, grad, True)
        ged_ref[...] += mm_tn(mid, grad)

    def stage_units_back(c):
        arrive(c)
        dmid = mm_nt(gathered(c), ed_ref[...]).astype(jnp.bfloat16)
        mids = mgu_buf[c]

        def unit_tile(cols):
            rows = gathered(c)
            inner_grad = mm_nt(rows, w_down[cols, :]) + mm(dmid, sd_ref[:, cols])
            gate = gate_buf[chunk_rows(c), cols].astype(jnp.float32)
            up = up_buf[chunk_rows(c), cols].astype(jnp.float32)
            sig = 1.0 / (1.0 + jnp.exp(-gate))
            silu = gate * sig
            gate_grad = (inner_grad * up * (sig + silu * (1.0 - sig))).astype(jnp.bfloat16)
            up_grad = (inner_grad * silu).astype(jnp.bfloat16)
            temp_a[:, cols] = gate_grad
            temp_b[:, cols] = up_grad
            gsd_ref[:, cols] += mm_tn(dmid, (silu * up).astype(jnp.bfloat16))
            geg_ref[:, cols] += mm_tn(mids, gate_grad)
            geu_ref[:, cols] += mm_tn(mids, up_grad)

        tiles(units, TILE // 2, unit_tile)
        gather_forward(c).wait_send()
        reduce_beside(c).wait_send()
        reduce_across(c).wait_send()
        store_partial(
            c,
            slice(width, width + 32),
            mm_nt(temp_a[...], eg_ref[...]) + mm_nt(temp_b[...], eu_ref[...]),
        )

        def width_tile(cols):
            store_partial(
                c, cols, mm_nt(temp_a[...], w_gate[cols, :]) + mm_nt(temp_b[...], w_up[cols, :])
            )

        tiles(width, TILE // 2, width_tile)
        reduce_beside(c).start()

    def stage_mixer_grad(c):
        main, side = totals(c)
        grads = cot_ref[own_rows(c), :].astype(jnp.float32) + main + mm(side, sgu_ref[...])
        hgrad_ref[own_rows(c), :] = grads
        mixer_grad = norm_back_rows(mixer_buf[own_rows(c), :], mgain_ref[...], grads)
        mixer_grad = mixer_grad.astype(jnp.bfloat16)
        send_rows(c, mixer_grad, True)
        geo_ref[...] += mm_tn(mout_buf[c], mixer_grad)
        gsgu_ref[...] += mm_tn(side, hidden_buf[own_rows(c), :].astype(jnp.bfloat16))

    def stage_mixed_grad(c):
        arrive(c)
        dmid = mm_nt(gathered(c), eo_ref[...]).astype(jnp.bfloat16)
        grad = (mm_nt(gathered(c), w_out[...]) + mm(dmid, so_ref[...])).astype(jnp.bfloat16)
        for i, o in enumerate(order):
            dmixed_ref[o, c] = grad[i * part : (i + 1) * part]
        gso_ref[...] += mm_tn(dmid, mixed_chunk(c))
        gather_forward(c).wait_send()
        gather_across(c).wait_send()
        gather_beside(c).wait_send()
        reduce_beside(c).wait_send()
        reduce_across(c).wait_send()

    stages = {
        "S0": stage_mixer, "S1": stage_hidden, "S2": stage_units, "S3": stage_feed,
        "S4": stage_units_back, "S5": stage_mixer_grad, "S6": stage_mixed_grad,
        "P0": pair_stage, "P2": pair_stage, "P4": pair_stage,
        "F1": forward_stage, "F3": forward_stage, "F5": forward_stage,
    }

    def step(i, carry):
        for name, delay in MIDDLE_ORDER:

            @pl.when((i >= delay) & (i < delay + chunks))
            def _():
                stages[name](i - delay)

        return carry

    lax.fori_loop(0, chunks + max(delay for _, delay in MIDDLE_ORDER), step, 0)


def middle(mixed, tokens, cot, w_out, w_gate, w_up, w_down, mgain, fgain, so, eo, sgu, eg, eu, sd, ed):
    rows, width = tokens.shape
    heads_width, units = w_out.shape[0], w_gate.shape[1]
    part = rows // CHUNKS
    whole_width = width + EXTRA
    vmem = pl.BlockSpec(memory_space=pltpu.VMEM)
    hbm = pl.BlockSpec(memory_space=pl.ANY)
    low, full = jnp.bfloat16, jnp.float32
    dma = pltpu.SemaphoreType.DMA((CHUNKS,))
    shape = jax.ShapeDtypeStruct
    flops = 2 * 4 * rows * width * (2 * heads_width + 6 * units)
    return pl.pallas_call(
        middle_body,
        in_specs=[vmem] * 3 + [hbm] * 4 + [vmem] * 9,
        out_specs=[vmem] * 10,
        out_shape=[
            shape((rows, width), low), shape((rows, width), full),
            shape((4, CHUNKS, part, heads_width), low),
            shape((16, units), full), shape((32, units), full), shape((32, units), full),
            shape((16, heads_width), full), shape((32, width), full), shape((16, width), full),
            shape((16, width), full),
        ],
        scratch_shapes=[
            pltpu.VMEM(w_out.shape, low), pltpu.VMEM(w_gate.shape, low),
            pltpu.VMEM(w_up.shape, low), pltpu.VMEM(w_down.shape, low),
            pltpu.SemaphoreType.DMA((4,)),
            pltpu.VMEM((CHUNKS, 4, part, width), low),
            pltpu.VMEM((CHUNKS, part, whole_width), low),
            pltpu.VMEM((CHUNKS, part, whole_width), low),
            pltpu.VMEM((CHUNKS, part, whole_width), low),
            pltpu.VMEM((CHUNKS, 2, part, whole_width), low),
            pltpu.VMEM((CHUNKS, 2, part, whole_width), low),
            pltpu.VMEM((4 * rows, units), low), pltpu.VMEM((4 * rows, units), low),
            pltpu.VMEM((4 * part, units), low), pltpu.VMEM((4 * part, units), low),
            pltpu.VMEM((CHUNKS, 4 * part, 32), low),
            pltpu.VMEM((rows, width), full), pltpu.VMEM((rows, width), full),
            pltpu.VMEM((CHUNKS, part, 16), low),
        ] + [dma] * 10,
        cost_estimate=pl.CostEstimate(
            flops=flops, bytes_accessed=2 * width * (heads_width + 3 * units), transcendentals=0
        ),
        compiler_params=pltpu.CompilerParams(
            collective_id=0, has_side_effects=True, vmem_limit_bytes=67043328
        ),
        name="mixer_to_feed",
    )(mixed.reshape(4, CHUNKS, part, heads_width), tokens, cot, w_out, w_gate, w_up, w_down,
      mgain, fgain, so, eo, sgu, eg, eu, sd, ed)


def per_device(
    tokens,
    cotangent,
    segment_ids,
    adapter_set,
    w_query,
    w_key,
    w_value,
    w_out,
    w_gate,
    w_up,
    w_down,
    query_gain,
    key_gain,
    mixer_gain,
    feed_gain,
    shrink_query,
    expand_query,
    shrink_key,
    expand_key,
    shrink_value,
    expand_value,
    shrink_out,
    expand_out,
    shrink_gate,
    expand_gate,
    shrink_up,
    expand_up,
    shrink_down,
    expand_down,
):
    model_width = w_query.shape[0]
    chosen = adapter_set[0]

    def choose_set(adapters):
        return lax.dynamic_index_in_dim(adapters, chosen, 0, keepdims=False)

    query_shrink, query_widened = (choose_set(shrink_query), choose_set(expand_query))
    key_shrink, key_widened = (choose_set(shrink_key), choose_set(expand_key))
    value_shrink, value_widened = (choose_set(shrink_value), choose_set(expand_value))
    out_shrink, output_widened = (choose_set(shrink_out), choose_set(expand_out))
    gate_shrink, gate_widened = (choose_set(shrink_gate), choose_set(expand_gate))
    up_shrink, up_widened = (choose_set(shrink_up), choose_set(expand_up))
    down_shrink, down_widened = (choose_set(shrink_down), choose_set(expand_down))
    full_tokens = lax.all_gather(tokens, "tensor", axis=0, tiled=True)
    length = full_tokens.shape[0]
    query_middle = rank_reduced(full_tokens, query_shrink)
    key_middle = rank_reduced(full_tokens, key_shrink)
    value_middle = rank_reduced(full_tokens, value_shrink)
    query_proj = jnp.dot(
        full_tokens, w_query, preferred_element_type=jnp.float32
    ) + adapter_scale_factor * widen_from_rank(query_middle, query_widened)
    key_proj = jnp.dot(
        full_tokens, w_key, preferred_element_type=jnp.float32
    ) + adapter_scale_factor * widen_from_rank(key_middle, key_widened)
    value_proj = jnp.dot(
        full_tokens, w_value, preferred_element_type=jnp.float32
    ) + adapter_scale_factor * widen_from_rank(value_middle, value_widened)
    totals = lax.psum(
        (jnp.sum(query_proj * query_proj, axis=-1), jnp.sum(key_proj * key_proj, axis=-1)), "tensor"
    )
    query_scale = lax.rsqrt(totals[0] / model_width + epsilon)[:, None]
    key_scale = lax.rsqrt(totals[1] / model_width + epsilon)[:, None]
    query_gains = query_gain.astype(jnp.float32)
    key_gains = key_gain.astype(jnp.float32)
    cosine_table, sine_table = rotary_constants(length, HEAD_DIM)
    cosine_table, sine_table = jnp.asarray(cosine_table), jnp.asarray(sine_table)
    seg_col = segment_ids.reshape(length, 1)
    value_low = value_proj.astype(jnp.bfloat16)
    mixed, query_rot, key_rot = attention_forward(
        query_proj, key_proj, value_low, query_scale, key_scale, query_gains[None], key_gains[None],
        cosine_table, sine_table, seg_col, segment_ids,
    )
    half = jnp.asarray(adapter_scale_factor, jnp.bfloat16)
    nothing = jnp.zeros_like(gate_widened)
    (
        block_output, hidden_grad, mixed_grad, grad_down_shrink, gradient_gate_widened,
        gradient_up_widened, grad_out_shrink, owner_gate_up, owner_out, owner_down,
    ) = middle(
        mixed, tokens, cotangent, w_out, w_gate, w_up, w_down,
        mixer_gain.astype(jnp.float32)[None], feed_gain.astype(jnp.float32)[None],
        out_shrink, half * output_widened, jnp.concatenate([gate_shrink, up_shrink], axis=0),
        jnp.concatenate([half * gate_widened, nothing], axis=0),
        jnp.concatenate([nothing, half * up_widened], axis=0),
        down_shrink, half * down_widened,
    )
    mixed_grad = mixed_grad.reshape(mixed.shape)
    rank = query_shrink.shape[0]
    gradient_gate_widened = adapter_scale_factor * gradient_gate_widened[:rank]
    gradient_up_widened = adapter_scale_factor * gradient_up_widened[rank:]
    owner_wide = jnp.concatenate(
        [adapter_scale_factor * owner_out, owner_gate_up, adapter_scale_factor * owner_down], axis=0
    )
    query_norm_grad, key_norm_grad, value_gradient, query_sums, key_sums = attention_backward(
        query_rot, key_rot, value_low, mixed_grad, query_proj, key_proj,
        query_gains[None], key_gains[None], cosine_table, sine_table, seg_col, segment_ids,
    )
    back_sums = lax.psum((jnp.sum(query_sums, axis=-1), jnp.sum(key_sums, axis=-1)), "tensor")
    query_gradient = (
        query_scale * query_gains * query_norm_grad
        - query_proj * query_scale**3 * back_sums[0][:, None] / model_width
    ).astype(jnp.bfloat16)
    key_gradient = (
        key_scale * key_gains * key_norm_grad
        - key_proj * key_scale**3 * back_sums[1][:, None] / model_width
    ).astype(jnp.bfloat16)
    query_middle_gradient = adapter_scale_factor * rank_reduced(query_gradient, query_widened)
    key_middle_gradient = adapter_scale_factor * rank_reduced(key_gradient, key_widened)
    value_middle_gradient = adapter_scale_factor * rank_reduced(value_gradient, value_widened)
    gradient_query_widened = adapter_scale_factor * outer_gradient(query_middle, query_gradient)
    gradient_key_widened = adapter_scale_factor * outer_gradient(key_middle, key_gradient)
    gradient_value_widened = adapter_scale_factor * outer_gradient(value_middle, value_gradient)
    token_grads = hidden_grad + lax.psum_scatter(
        (
            jnp.dot(query_gradient, w_query.T, preferred_element_type=jnp.float32)
            + jnp.dot(key_gradient, w_key.T, preferred_element_type=jnp.float32)
            + jnp.dot(value_gradient, w_value.T, preferred_element_type=jnp.float32)
            + widen_from_rank(query_middle_gradient, query_shrink)
            + widen_from_rank(key_middle_gradient, key_shrink)
            + widen_from_rank(value_middle_gradient, value_shrink)
        ).astype(jnp.bfloat16),
        "tensor",
        scatter_dimension=0,
        tiled=True,
    ).astype(jnp.float32)
    sets_here = shrink_query.shape[0]
    dp_size = lax.axis_size("dp")
    tensor_size = lax.axis_size("tensor")
    set_of_each = lax.all_gather(chosen, "dp")
    onehot = (jnp.arange(sets_here)[:, None] == set_of_each[None, :]).astype(jnp.bfloat16)

    split = jnp.concatenate(
        [
            gradient_query_widened,
            gradient_key_widened,
            gradient_value_widened,
            grad_out_shrink,
            gradient_gate_widened,
            gradient_up_widened,
            grad_down_shrink,
        ],
        axis=1,
    ).astype(jnp.bfloat16)
    split_all = lax.all_gather(split, "dp")
    split_sums = jnp.einsum("cs,srw->crw", onehot, split_all, preferred_element_type=jnp.float32)
    local_sums = []
    at = 0
    for part in (
        gradient_query_widened,
        gradient_key_widened,
        gradient_value_widened,
        grad_out_shrink,
        gradient_gate_widened,
        gradient_up_widened,
        grad_down_shrink,
    ):
        local_sums.append(split_sums[:, :, at : at + part.shape[1]])
        at += part.shape[1]
    middles = lax.psum(
        jnp.concatenate(
            [
                query_middle_gradient,
                key_middle_gradient,
                value_middle_gradient,
            ],
            axis=1,
        ),
        "tensor",
    ).astype(jnp.bfloat16)
    wide = outer_gradient(middles, full_tokens)
    blocks = wide.reshape(3 * rank, dp_size, tensor_size, -1)
    mine = lax.dynamic_index_in_dim(blocks, lax.axis_index("tensor"), 2, keepdims=False)
    owner_blocks = owner_wide.reshape(4 * rank, dp_size, tensor_size, -1).transpose(2, 0, 1, 3)
    owner_mine = lax.psum_scatter(owner_blocks, "tensor", scatter_dimension=0)
    mine = jnp.concatenate([mine, owner_mine], axis=0)
    swapped = lax.all_to_all(mine.transpose(1, 0, 2), "dp", 0, 0)
    shared_sums = jnp.einsum(
        "cs,srw->crw",
        onehot.astype(jnp.float32),
        swapped,
        precision=highest,
        preferred_element_type=jnp.float32,
    )
    shared = [shared_sums[:, i * rank : (i + 1) * rank] for i in range(7)]
    return (
        block_output,
        token_grads,
        shared[0],
        local_sums[0],
        shared[1],
        local_sums[1],
        shared[2],
        local_sums[2],
        local_sums[3],
        shared[3],
        shared[4],
        local_sums[4],
        shared[5],
        local_sums[5],
        local_sums[6],
        shared[6],
    )


def solution(mesh):
    in_specs = (
        P(("dp", "tensor"), None),
        P(("dp", "tensor"), None),
        P("dp", None),
        P("dp"),
        P(None, "tensor"),
        P(None, "tensor"),
        P(None, "tensor"),
        P("tensor", None),
        P(None, "tensor"),
        P(None, "tensor"),
        P("tensor", None),
        P("tensor"),
        P("tensor"),
        P(),
        P(),
        P(),
        P(None, None, "tensor"),
        P(),
        P(None, None, "tensor"),
        P(),
        P(None, None, "tensor"),
        P(None, None, "tensor"),
        P(),
        P(),
        P(None, None, "tensor"),
        P(),
        P(None, None, "tensor"),
        P(None, None, "tensor"),
        P(),
    )
    out_specs = (
        P(("dp", "tensor"), None),
        P(("dp", "tensor"), None),
        P(None, None, ("dp", "tensor")),
        P(None, None, "tensor"),
        P(None, None, ("dp", "tensor")),
        P(None, None, "tensor"),
        P(None, None, ("dp", "tensor")),
        P(None, None, "tensor"),
        P(None, None, "tensor"),
        P(None, None, ("dp", "tensor")),
        P(None, None, ("dp", "tensor")),
        P(None, None, "tensor"),
        P(None, None, ("dp", "tensor")),
        P(None, None, "tensor"),
        P(None, None, "tensor"),
        P(None, None, ("dp", "tensor")),
    )
    return jax.shard_map(
        per_device, mesh=mesh, in_specs=in_specs, out_specs=out_specs, check_vma=False
    )
```

```python
import functools
import jax
import jax.numpy as jnp
import numpy as np
from jax import lax
from jax.experimental import pallas as pl
from jax.experimental.pallas import tpu as pltpu
from jax.sharding import PartitionSpec as P

HEAD_DIM = 128
DOC_MOST = 512
ATT_ROWS = 256
rotary_base = 500000.0
NEG = -1e30
LOG2E = 1.4426950408889634


def rotary_constants(length, head_dim):
    half = head_dim // 2
    frequency = np.float32(rotary_base) ** (
        -(np.arange(half, dtype=np.float32) * np.float32(2.0) / np.float32(head_dim))
    )
    angles = np.arange(length, dtype=np.float32)[:, None] * frequency.astype(np.float32)[None, :]
    cosine = np.cos(angles.astype(np.float64)).astype(np.float32)
    sine = np.sin(angles.astype(np.float64)).astype(np.float32)
    return (
        np.concatenate([cosine, cosine], axis=1),
        np.concatenate([-sine, sine], axis=1),
    )


def key_window(block, rows):
    first = max(0, (block * rows - (DOC_MOST - 1)) // rows) * rows
    return first, (block + 1) * rows


def attention_backward_body(
    qrot_ref, krot_ref, value_ref, grad_ref, query_ref, key_ref, qgain_ref, kgain_ref,
    cos_ref, sin_ref, seg_col_ref, seg_row_ref,
    dquery_ref, dkey_ref, dvalue_ref, qsum_ref, ksum_ref, dk_acc, dv_acc,
):
    length = qrot_ref.shape[0]
    half = HEAD_DIM // 2
    inverse = HEAD_DIM ** (-0.5)
    rows = min(ATT_ROWS, length)

    @pl.when(pl.program_id(0) == 0)
    def _():
        qsum_ref[...] = jnp.zeros_like(qsum_ref)
        ksum_ref[...] = jnp.zeros_like(ksum_ref)

    dk_acc[...] = jnp.zeros_like(dk_acc)
    dv_acc[...] = jnp.zeros_like(dv_acc)
    for block in range(length // rows):
        low, high = key_window(block, rows)
        here = pl.ds(block * rows, rows)
        keys = pl.ds(low, high - low)
        queries = qrot_ref[here, :]
        key_rows = krot_ref[keys, :]
        grads = grad_ref[here, :]
        scores = (
            lax.dot_general(
                key_rows, queries, (((1,), (1,)), ((), ())), preferred_element_type=jnp.float32
            )
            * inverse
        )
        kpos = lax.broadcasted_iota(jnp.int32, scores.shape, 0) + low
        qpos = lax.broadcasted_iota(jnp.int32, scores.shape, 1) + block * rows
        allowed = (kpos <= qpos) & (seg_col_ref[keys, :] == seg_row_ref[:, here])
        scores = jnp.where(allowed, scores, NEG)
        top = jnp.max(scores, axis=0, keepdims=True)
        weights = jnp.exp(scores - top)
        total = jnp.sum(weights, axis=0, keepdims=True)
        probs = weights * (1.0 / total)
        prob_grad = lax.dot_general(
            value_ref[keys, :], grads, (((1,), (1,)), ((), ())), preferred_element_type=jnp.float32
        )
        weighted = probs * prob_grad
        delta = jnp.sum(weighted, axis=0, keepdims=True)
        score_grad = ((weighted - probs * delta) * inverse).astype(jnp.bfloat16)
        dv_acc[keys, :] += jnp.dot(
            probs.astype(jnp.bfloat16), grads, preferred_element_type=jnp.float32
        )
        dk_acc[keys, :] += jnp.dot(score_grad, queries, preferred_element_type=jnp.float32)
        dq = lax.dot_general(
            score_grad, key_rows, (((0,), (0,)), ((), ())), preferred_element_type=jnp.float32
        )
        dq = dq * cos_ref[here, :] - pltpu.roll(dq, half, 1) * sin_ref[here, :]
        dquery_ref[here, :] = dq
        qsum_ref[here, :] += query_ref[here, :] * qgain_ref[...] * dq
    dk = dk_acc[...]
    dk = dk * cos_ref[...] - pltpu.roll(dk, half, 1) * sin_ref[...]
    dkey_ref[...] = dk
    ksum_ref[...] += key_ref[...] * kgain_ref[...] * dk
    dvalue_ref[...] = dv_acc[...].astype(jnp.bfloat16)


def attention_backward(qrot, krot, value, grad, query, key, qgain, kgain, cos, sin, seg_col, seg_row):
    length, width = qrot.shape
    heads = width // HEAD_DIM
    column = pl.BlockSpec((length, HEAD_DIM), lambda h: (0, h))
    gain = pl.BlockSpec((1, HEAD_DIM), lambda h: (0, h))
    whole = lambda a: pl.BlockSpec(a.shape, lambda h: (0, 0))
    sums = pl.BlockSpec((length, HEAD_DIM), lambda h: (0, 0))
    return pl.pallas_call(
        attention_backward_body,
        grid=(heads,),
        in_specs=[
            column, column, column, column, column, column, gain, gain,
            whole(cos), whole(sin), whole(seg_col), whole(seg_row),
        ],
        out_specs=[column, column, column, sums, sums],
        out_shape=[
            jax.ShapeDtypeStruct((length, width), jnp.float32),
            jax.ShapeDtypeStruct((length, width), jnp.float32),
            jax.ShapeDtypeStruct((length, width), jnp.bfloat16),
            jax.ShapeDtypeStruct((length, HEAD_DIM), jnp.float32),
            jax.ShapeDtypeStruct((length, HEAD_DIM), jnp.float32),
        ],
        scratch_shapes=[
            pltpu.VMEM((length, HEAD_DIM), jnp.float32),
            pltpu.VMEM((length, HEAD_DIM), jnp.float32),
        ],
        cost_estimate=pl.CostEstimate(
            flops=10 * length * length * width, bytes_accessed=30 * length * width,
            transcendentals=length * length * heads,
        ),
        compiler_params=pltpu.CompilerParams(vmem_limit_bytes=48 * 2**20),
        name="attention_backward",
    )(qrot, krot, value, grad, query, key, qgain, kgain, cos, sin, seg_col, seg_row)


epsilon = 1e-06
adapter_scale_factor = 0.5
highest = lax.Precision.HIGHEST


def scale_of(values):
    return lax.rsqrt(jnp.mean(values * values, axis=-1, keepdims=True) + epsilon)


def norm_back(values, factor, gains, grads):
    weighted = grads * gains
    return factor * weighted - values * factor**3 * jnp.mean(
        values * weighted, axis=-1, keepdims=True
    )


def rank_reduced(input_rows, shrink):
    return jnp.dot(input_rows, shrink.T, preferred_element_type=jnp.float32)


def widen_from_rank(middle_rows, widen_factor):
    return jnp.dot(
        middle_rows.astype(jnp.bfloat16), widen_factor, preferred_element_type=jnp.float32
    )


def outer_gradient(middle_rows, input_rows):
    return lax.dot_general(
        middle_rows.astype(jnp.bfloat16),
        input_rows,
        (((0,), (0,)), ((), ())),
        preferred_element_type=jnp.float32,
    )


CHUNKS = 4
TILE = 1024
EXTRA = 128
NT = (((1,), (1,)), ((), ()))
TN = (((0,), (0,)), ((), ()))
MESH_ID = pl.DeviceIdType.MESH
MIDDLE_ORDER = (
    ("S2", 4), ("P4", 8), ("S4", 7), ("P0", 1), ("S1", 2), ("S6", 10), ("F3", 6),
    ("F5", 9), ("S5", 8), ("P2", 4), ("S0", 0), ("F1", 3), ("S3", 5),
)


def mm(left, right):
    return jnp.dot(left, right, preferred_element_type=jnp.float32)


def mm_nt(left, right):
    return lax.dot_general(left, right, NT, preferred_element_type=jnp.float32)


def mm_tn(left, right):
    return lax.dot_general(left, right, TN, preferred_element_type=jnp.float32)


def partners():
    me = lax.axis_index("tensor")
    group = lax.axis_index("dp")
    beside = me + 1 - 2 * lax.rem(me, 2)
    across = lax.rem(me + 2, 4)
    return me, group, beside, across


def greet(group, beside, across):
    barrier = pltpu.get_barrier_semaphore()
    for other in (beside, across):
        pl.semaphore_signal(barrier, inc=1, device_id=(group, other), device_id_type=MESH_ID)
    pl.semaphore_wait(barrier, 2)


def middle_body(
    mixed_ref, tokens_ref, cot_ref, w_out_hbm, w_gate_hbm, w_up_hbm, w_down_hbm,
    mgain_ref, fgain_ref, so_ref, eo_ref, sgu_ref, eg_ref, eu_ref, sd_ref, ed_ref,
    out_ref, hgrad_ref, dmixed_ref, gsd_ref, geg_ref, geu_ref, gso_ref, gsgu_ref, geo_ref, ged_ref,
    w_out, w_gate, w_up, w_down, wsem,
    rows_buf, own_buf, xsend, xrecv, bsend, brecv,
    gate_buf, up_buf, temp_a, temp_b, mgu_buf, mixer_buf, hidden_buf, mout_buf,
    xs_sem, xr_sem, bs_sem, br_sem, gxs_sem, gxr_sem, gbs_sem, gbr_sem, fs_sem, fr_sem,
):
    me, group, beside, across = partners()
    chunks, part, width = rows_buf.shape[0], rows_buf.shape[2], rows_buf.shape[3]
    units = w_gate.shape[1]
    heads_width = w_out.shape[0]
    far = lax.rem(beside + 2, 4)
    order = (me, across, beside, far)
    loads = [
        pltpu.make_async_copy(source, target, wsem.at[i])
        for i, (source, target) in enumerate(
            ((w_out_hbm, w_out), (w_gate_hbm, w_gate), (w_up_hbm, w_up), (w_down_hbm, w_down))
        )
    ]
    for load in loads:
        load.start()
    for ref in (gsd_ref, geg_ref, geu_ref, gso_ref, gsgu_ref, geo_ref, ged_ref):
        ref[...] = jnp.zeros_like(ref)
    greet(group, beside, across)

    def remote(source, target, ssem, rsem, other):
        return pltpu.make_async_remote_copy(
            src_ref=source, dst_ref=target, send_sem=ssem, recv_sem=rsem,
            device_id=(group, other), device_id_type=MESH_ID,
        )

    def gather_across(c):
        return remote(rows_buf.at[c, 0], rows_buf.at[c, 1], gxs_sem.at[c], gxr_sem.at[c], across)

    def gather_beside(c):
        return remote(rows_buf.at[c, 0], rows_buf.at[c, 2], gbs_sem.at[c], gbr_sem.at[c], beside)

    def gather_forward(c):
        return remote(rows_buf.at[c, 1], rows_buf.at[c, 3], fs_sem.at[c], fr_sem.at[c], beside)

    def reduce_beside(c):
        return remote(bsend.at[c], brecv.at[c], bs_sem.at[c], br_sem.at[c], beside)

    def reduce_across(c):
        return remote(xsend.at[c], xrecv.at[c], xs_sem.at[c], xr_sem.at[c], across)

    def store_partial(c, columns, value):
        low = value.astype(jnp.bfloat16)
        own_buf[c, :, columns] = low[:part]
        xsend[c, :, columns] = low[part : 2 * part]
        bsend[c, 0, :, columns] = low[2 * part : 3 * part]
        bsend[c, 1, :, columns] = low[3 * part :]

    def gathered(c):
        return rows_buf[c].reshape(4 * part, width)

    def forward_stage(c):
        gather_across(c).wait_recv()
        gather_forward(c).start()

    def pair_stage(c):
        reduce_beside(c).wait_recv()
        own_buf[c] = (
            own_buf[c].astype(jnp.float32) + brecv[c, 0].astype(jnp.float32)
        ).astype(jnp.bfloat16)
        xsend[c] = (
            xsend[c].astype(jnp.float32) + brecv[c, 1].astype(jnp.float32)
        ).astype(jnp.bfloat16)
        reduce_across(c).start()

    def totals(c):
        reduce_across(c).wait_recv()
        main = own_buf[c, :, :width].astype(jnp.float32) + xrecv[c, :, :width].astype(jnp.float32)
        side = own_buf[c, :, width : width + 32].astype(jnp.float32) + xrecv[
            c, :, width : width + 32
        ].astype(jnp.float32)
        return main, side.astype(jnp.bfloat16)

    def own_rows(c):
        return pl.ds(pl.multiple_of(c * part, part), part)

    def send_rows(c, value, again):
        if again:
            gather_across(c).wait_send()
            gather_beside(c).wait_send()
        rows_buf[c, 0] = value
        gather_across(c).start()
        gather_beside(c).start()

    def chunk_rows(c):
        return pl.ds(pl.multiple_of(c * 4 * part, 4 * part), 4 * part)

    def tiles(total, tile, body):
        def step(j, carry):
            body(pl.ds(pl.multiple_of(j * tile, tile), tile))
            return carry

        lax.fori_loop(0, total // tile, step, 0)

    def mixed_chunk(c):
        return jnp.concatenate([mixed_ref[o, c] for o in order], axis=0)

    def stage_mixer(c):
        @pl.when(c == 0)
        def _():
            loads[0].wait()

        rows = mixed_chunk(c)
        store_partial(c, slice(width, width + 16), mm_nt(rows, so_ref[...]))
        tiles(width, TILE, lambda cols: store_partial(c, cols, mm(rows, w_out[:, cols])))
        reduce_beside(c).start()

    def stage_hidden(c):
        main, side = totals(c)
        mid = side[:, :16]
        mout_buf[c] = mid
        mixer = main + mm(mid, eo_ref[...])
        mixer_buf[own_rows(c), :] = mixer
        factor = lax.rsqrt(jnp.mean(mixer * mixer, axis=1, keepdims=True) + epsilon)
        hidden = tokens_ref[own_rows(c), :].astype(jnp.float32) + mixer * factor * mgain_ref[...]
        hidden_buf[own_rows(c), :] = hidden
        send_rows(c, hidden.astype(jnp.bfloat16), False)

    def arrive(c):
        gather_beside(c).wait_recv()
        gather_forward(c).wait_recv()

    def stage_units(c):
        @pl.when(c == 0)
        def _():
            for load in loads[1:]:
                load.wait()

        arrive(c)
        mids = mm_nt(gathered(c), sgu_ref[...]).astype(jnp.bfloat16)
        mgu_buf[c] = mids

        def unit_tile(cols):
            rows = gathered(c)
            gate = mm(rows, w_gate[:, cols]) + mm(mids, eg_ref[:, cols])
            up = mm(rows, w_up[:, cols]) + mm(mids, eu_ref[:, cols])
            gate_buf[chunk_rows(c), cols] = gate.astype(jnp.bfloat16)
            up_buf[chunk_rows(c), cols] = up.astype(jnp.bfloat16)
            sig = 1.0 / (1.0 + jnp.exp(-gate))
            temp_a[:, cols] = (gate * sig * up).astype(jnp.bfloat16)

        tiles(units, TILE // 2, unit_tile)
        gather_forward(c).wait_send()
        reduce_beside(c).wait_send()
        reduce_across(c).wait_send()
        inner = temp_a[...]
        store_partial(c, slice(width, width + 16), mm_nt(inner, sd_ref[...]))
        tiles(width, TILE, lambda cols: store_partial(c, cols, mm(temp_a[...], w_down[:, cols])))
        reduce_beside(c).start()

    def norm_back_rows(values, gains, grads):
        factor = lax.rsqrt(jnp.mean(values * values, axis=1, keepdims=True) + epsilon)
        weighted = grads * gains
        return factor * weighted - values * (
            factor * factor * factor * jnp.mean(values * weighted, axis=1, keepdims=True)
        )

    def stage_feed(c):
        main, side = totals(c)
        mid = side[:, :16]
        feed = main + mm(mid, ed_ref[...])
        factor = lax.rsqrt(jnp.mean(feed * feed, axis=1, keepdims=True) + epsilon)
        gains = fgain_ref[...]
        out_ref[own_rows(c), :] = (hidden_buf[own_rows(c), :] + feed * factor * gains).astype(
            jnp.bfloat16
        )
        grad = norm_back_rows(feed, gains, cot_ref[own_rows(c), :].astype(jnp.float32))
        grad = grad.astype(jnp.bfloat16)
        send_rows(c, grad, True)
        ged_ref[...] += mm_tn(mid, grad)

    def stage_units_back(c):
        arrive(c)
        dmid = mm_nt(gathered(c), ed_ref[...]).astype(jnp.bfloat16)
        mids = mgu_buf[c]

        def unit_tile(cols):
            rows = gathered(c)
            inner_grad = mm_nt(rows, w_down[cols, :]) + mm(dmid, sd_ref[:, cols])
            gate = gate_buf[chunk_rows(c), cols].astype(jnp.float32)
            up = up_buf[chunk_rows(c), cols].astype(jnp.float32)
            sig = 1.0 / (1.0 + jnp.exp(-gate))
            silu = gate * sig
            gate_grad = (inner_grad * up * (sig + silu * (1.0 - sig))).astype(jnp.bfloat16)
            up_grad = (inner_grad * silu).astype(jnp.bfloat16)
            temp_a[:, cols] = gate_grad
            temp_b[:, cols] = up_grad
            gsd_ref[:, cols] += mm_tn(dmid, (silu * up).astype(jnp.bfloat16))
            geg_ref[:, cols] += mm_tn(mids, gate_grad)
            geu_ref[:, cols] += mm_tn(mids, up_grad)

        tiles(units, TILE // 2, unit_tile)
        gather_forward(c).wait_send()
        reduce_beside(c).wait_send()
        reduce_across(c).wait_send()
        store_partial(
            c,
            slice(width, width + 32),
            mm_nt(temp_a[...], eg_ref[...]) + mm_nt(temp_b[...], eu_ref[...]),
        )

        def width_tile(cols):
            store_partial(
                c, cols, mm_nt(temp_a[...], w_gate[cols, :]) + mm_nt(temp_b[...], w_up[cols, :])
            )

        tiles(width, TILE // 2, width_tile)
        reduce_beside(c).start()

    def stage_mixer_grad(c):
        main, side = totals(c)
        grads = cot_ref[own_rows(c), :].astype(jnp.float32) + main + mm(side, sgu_ref[...])
        hgrad_ref[own_rows(c), :] = grads
        mixer_grad = norm_back_rows(mixer_buf[own_rows(c), :], mgain_ref[...], grads)
        mixer_grad = mixer_grad.astype(jnp.bfloat16)
        send_rows(c, mixer_grad, True)
        geo_ref[...] += mm_tn(mout_buf[c], mixer_grad)
        gsgu_ref[...] += mm_tn(side, hidden_buf[own_rows(c), :].astype(jnp.bfloat16))

    def stage_mixed_grad(c):
        arrive(c)
        dmid = mm_nt(gathered(c), eo_ref[...]).astype(jnp.bfloat16)
        grad = (mm_nt(gathered(c), w_out[...]) + mm(dmid, so_ref[...])).astype(jnp.bfloat16)
        for i, o in enumerate(order):
            dmixed_ref[o, c] = grad[i * part : (i + 1) * part]
        gso_ref[...] += mm_tn(dmid, mixed_chunk(c))
        gather_forward(c).wait_send()
        gather_across(c).wait_send()
        gather_beside(c).wait_send()
        reduce_beside(c).wait_send()
        reduce_across(c).wait_send()

    stages = {
        "S0": stage_mixer, "S1": stage_hidden, "S2": stage_units, "S3": stage_feed,
        "S4": stage_units_back, "S5": stage_mixer_grad, "S6": stage_mixed_grad,
        "P0": pair_stage, "P2": pair_stage, "P4": pair_stage,
        "F1": forward_stage, "F3": forward_stage, "F5": forward_stage,
    }

    def step(i, carry):
        for name, delay in MIDDLE_ORDER:

            @pl.when((i >= delay) & (i < delay + chunks))
            def _():
                stages[name](i - delay)

        return carry

    lax.fori_loop(0, chunks + max(delay for _, delay in MIDDLE_ORDER), step, 0)


def middle(mixed, tokens, cot, w_out, w_gate, w_up, w_down, mgain, fgain, so, eo, sgu, eg, eu, sd, ed):
    rows, width = tokens.shape
    heads_width, units = w_out.shape[0], w_gate.shape[1]
    part = rows // CHUNKS
    whole_width = width + EXTRA
    vmem = pl.BlockSpec(memory_space=pltpu.VMEM)
    hbm = pl.BlockSpec(memory_space=pl.ANY)
    low, full = jnp.bfloat16, jnp.float32
    dma = pltpu.SemaphoreType.DMA((CHUNKS,))
    shape = jax.ShapeDtypeStruct
    flops = 2 * 4 * rows * width * (2 * heads_width + 6 * units)
    return pl.pallas_call(
        middle_body,
        in_specs=[vmem] * 3 + [hbm] * 4 + [vmem] * 9,
        out_specs=[vmem] * 10,
        out_shape=[
            shape((rows, width), low), shape((rows, width), full),
            shape((4, CHUNKS, part, heads_width), low),
            shape((16, units), full), shape((32, units), full), shape((32, units), full),
            shape((16, heads_width), full), shape((32, width), full), shape((16, width), full),
            shape((16, width), full),
        ],
        scratch_shapes=[
            pltpu.VMEM(w_out.shape, low), pltpu.VMEM(w_gate.shape, low),
            pltpu.VMEM(w_up.shape, low), pltpu.VMEM(w_down.shape, low),
            pltpu.SemaphoreType.DMA((4,)),
            pltpu.VMEM((CHUNKS, 4, part, width), low),
            pltpu.VMEM((CHUNKS, part, whole_width), low),
            pltpu.VMEM((CHUNKS, part, whole_width), low),
            pltpu.VMEM((CHUNKS, part, whole_width), low),
            pltpu.VMEM((CHUNKS, 2, part, whole_width), low),
            pltpu.VMEM((CHUNKS, 2, part, whole_width), low),
            pltpu.VMEM((4 * rows, units), low), pltpu.VMEM((4 * rows, units), low),
            pltpu.VMEM((4 * part, units), low), pltpu.VMEM((4 * part, units), low),
            pltpu.VMEM((CHUNKS, 4 * part, 32), low),
            pltpu.VMEM((rows, width), full), pltpu.VMEM((rows, width), full),
            pltpu.VMEM((CHUNKS, part, 16), low),
        ] + [dma] * 10,
        cost_estimate=pl.CostEstimate(
            flops=flops, bytes_accessed=2 * width * (heads_width + 3 * units), transcendentals=0
        ),
        compiler_params=pltpu.CompilerParams(
            collective_id=0, has_side_effects=True, vmem_limit_bytes=67043328
        ),
        name="mixer_to_feed",
    )(mixed.reshape(4, CHUNKS, part, heads_width), tokens, cot, w_out, w_gate, w_up, w_down,
      mgain, fgain, so, eo, sgu, eg, eu, sd, ed)


def attention_scores(first, second, block, rows, low, seg_first, seg_second, query_axis):
    scores = lax.dot_general(first, second, NT, preferred_element_type=jnp.float32)
    kpos = lax.broadcasted_iota(jnp.int32, scores.shape, 1 - query_axis) + low
    qpos = lax.broadcasted_iota(jnp.int32, scores.shape, query_axis) + block * rows
    return jnp.where((kpos <= qpos) & (seg_first == seg_second), scores, NEG)


def front_body(
    tokens_ref, wq_hbm, wk_hbm, wv_hbm, shrink_ref, eq_ref, ek_ref, ev_ref, qgain_ref, kgain_ref,
    cos_ref, sin_ref, seg_col_ref, seg_row_ref,
    mixed_ref, qrot_ref, krot_ref, value_ref, qproj_ref, kproj_ref, scale_ref, mids_ref, full_hbm,
    wq, wk, wv, wsem, full, lhs, squares, ex_send, ex_recv,
    xs_sem, xr_sem, fs_sem, fr_sem, bs_sem, br_sem, es_sem, er_sem, out_sem,
):
    me, group, beside, across = partners()
    far = lax.rem(beside + 2, 4)
    chunks, part, width = full.shape[1:]
    rows = chunks * part
    length = 4 * rows
    loads = [
        pltpu.make_async_copy(source, target, wsem.at[i])
        for i, (source, target) in enumerate(((wq_hbm, wq), (wk_hbm, wk), (wv_hbm, wv)))
    ]
    for load in loads:
        load.start()
    barrier = pltpu.get_barrier_semaphore()
    for other in (beside, across, far):
        pl.semaphore_signal(barrier, inc=1, device_id=(group, other), device_id_type=MESH_ID)
    pl.semaphore_wait(barrier, 3)

    def remote(source, target, ssem, rsem, other):
        return pltpu.make_async_remote_copy(
            src_ref=source, dst_ref=target, send_sem=ssem, recv_sem=rsem,
            device_id=(group, other), device_id_type=MESH_ID,
        )

    def send_across(c):
        return remote(tokens_ref.at[c], full.at[me, c], xs_sem.at[c], xr_sem.at[c], across)

    def forward(c):
        return remote(full.at[across, c], full.at[across, c], fs_sem.at[c], fr_sem.at[c], beside)

    to_beside = remote(tokens_ref, full.at[me], bs_sem, br_sem, beside)
    for c in range(chunks):
        send_across(c).start()
    to_beside.start()
    full[me] = tokens_ref[...]
    for load in loads:
        load.wait()
    pairs = chunks // 2
    half = rows // 2

    def block_step(b, carry):
        @pl.when(b == 0)
        def _():
            lhs[...] = tokens_ref[...].reshape(rows, width)

        @pl.when(b == 1)
        def _():
            to_beside.wait_recv()
            lhs[...] = full[beside].reshape(rows, width)

        @pl.when(b >= 2)
        def _():
            base = (b - 2) * pairs
            for j in range(pairs):
                send_across(base + j).wait_recv()
                forward(base + j).start()
            for j in range(pairs):
                lhs[j * part : (j + 1) * part] = full[across, base + j]
            for j in range(pairs):
                forward(base + j).wait_recv()
                lhs[half + j * part : half + (j + 1) * part] = full[far, base + j]

        mids = mm_nt(lhs[...], shrink_ref[...]).astype(jnp.bfloat16)
        query = mm(lhs[...], wq[...]) + mm(mids, eq_ref[...])
        key = mm(lhs[...], wk[...]) + mm(mids, ek_ref[...])
        value = (mm(lhs[...], wv[...]) + mm(mids, ev_ref[...])).astype(jnp.bfloat16)
        qsum = jnp.sum(query * query, axis=1, keepdims=True)
        ksum = jnp.sum(key * key, axis=1, keepdims=True)
        lane = lax.broadcasted_iota(jnp.int32, (rows, HEAD_DIM), 1)
        both = jnp.where(lane < 4, qsum, ksum)
        first = jnp.where(b == 0, me, jnp.where(b == 1, beside, across)) * rows
        second = jnp.where(b == 0, me, jnp.where(b == 1, beside, far)) * rows
        first = first + jnp.where(b >= 2, (b - 2) * half, 0)
        second = second + jnp.where(b >= 2, (b - 2) * half, half)
        for start, piece in ((first, slice(0, half)), (second, slice(half, rows))):
            there = pl.ds(pl.multiple_of(start, half), half)
            qproj_ref[there, :] = query[piece]
            kproj_ref[there, :] = key[piece]
            value_ref[there, :] = value[piece]
            mids_ref[there, :] = mids[piece]
            squares[there, :] = both[piece]
        return carry

    lax.fori_loop(0, 4, block_step, 0)
    save = pltpu.make_async_copy(full, full_hbm, out_sem)
    save.start()
    ex_send[...] = jnp.transpose(squares[...])[:8]
    swaps = [
        remote(ex_send, ex_recv.at[i], es_sem.at[i], er_sem.at[i], other)
        for i, other in enumerate((beside, across, far))
    ]
    for swap in swaps:
        swap.start()
    for swap in swaps:
        swap.wait_recv()
    total = ex_send[...] + ex_recv[0] + ex_recv[1] + ex_recv[2]
    factor = lax.rsqrt(total / (4 * wq.shape[1]) + epsilon)
    wide = jnp.concatenate(
        [
            jnp.broadcast_to(factor[:1], (HEAD_DIM // 2, length)),
            jnp.broadcast_to(factor[4:5], (HEAD_DIM // 2, length)),
        ],
        axis=0,
    )
    scale_ref[...] = jnp.transpose(wide)
    heads = wq.shape[1] // HEAD_DIM
    exponent = HEAD_DIM ** (-0.5) * LOG2E
    block_rows = min(ATT_ROWS, length)

    def head_step(h, carry):
        cols = pl.ds(pl.multiple_of(h * HEAD_DIM, HEAD_DIM), HEAD_DIM)
        for source, lane, gain, target in (
            (qproj_ref, 0, qgain_ref, qrot_ref),
            (kproj_ref, HEAD_DIM // 2, kgain_ref, krot_ref),
        ):
            normed = source[:, cols] * scale_ref[:, lane : lane + 1] * gain[:, cols].astype(jnp.float32)
            turned = normed * cos_ref[...] + pltpu.roll(normed, HEAD_DIM // 2, 1) * sin_ref[...]
            target[:, cols] = turned.astype(jnp.bfloat16)
        for block in range(length // block_rows):
            low, high = key_window(block, block_rows)
            here = pl.ds(block * block_rows, block_rows)
            keys = pl.ds(low, high - low)
            scores = attention_scores(
                qrot_ref[here, cols], krot_ref[keys, cols], block, block_rows, low,
                seg_col_ref[here, :], seg_row_ref[:, keys], 0,
            )
            top = jnp.max(scores, axis=1, keepdims=True)
            weights = jnp.exp2((scores - top) * exponent)
            total = jnp.sum(weights, axis=1, keepdims=True)
            mix = mm(weights.astype(jnp.bfloat16), value_ref[keys, cols])
            mixed_ref[here, cols] = (mix * (1.0 / total)).astype(jnp.bfloat16)
        return carry

    lax.fori_loop(0, heads, head_step, 0)
    for c in range(chunks):
        send_across(c).wait_send()
        forward(c).wait_send()
    to_beside.wait_send()
    for swap in swaps:
        swap.wait_send()
    save.wait()


def front(tokens, wq, wk, wv, shrink, eq, ek, ev, qgain, kgain, cos, sin, seg_col, seg_row):
    rows, width = tokens.shape
    heads_width = wq.shape[1]
    length = 4 * rows
    part = rows // CHUNKS
    vmem = pl.BlockSpec(memory_space=pltpu.VMEM)
    hbm = pl.BlockSpec(memory_space=pl.ANY)
    low, full = jnp.bfloat16, jnp.float32
    shape = jax.ShapeDtypeStruct
    dma = pltpu.SemaphoreType.DMA
    return pl.pallas_call(
        front_body,
        in_specs=[vmem] + [hbm] * 3 + [vmem] * 10,
        out_specs=[vmem] * 8 + [hbm],
        out_shape=[
            shape((length, heads_width), low), shape((length, heads_width), low),
            shape((length, heads_width), low), shape((length, heads_width), low),
            shape((length, heads_width), full), shape((length, heads_width), full),
            shape((length, HEAD_DIM), full), shape((length, shrink.shape[0]), low),
            shape((4, CHUNKS, part, width), low),
        ],
        scratch_shapes=[
            pltpu.VMEM(wq.shape, low), pltpu.VMEM(wk.shape, low), pltpu.VMEM(wv.shape, low),
            dma((3,)),
            pltpu.VMEM((4, CHUNKS, part, width), low), pltpu.VMEM((rows, width), low),
            pltpu.VMEM((length, HEAD_DIM), full), pltpu.VMEM((8, length), full),
            pltpu.VMEM((3, 8, length), full),
            dma((CHUNKS,)), dma((CHUNKS,)), dma((CHUNKS,)), dma((CHUNKS,)), dma, dma,
            dma((3,)), dma((3,)), dma,
        ],
        cost_estimate=pl.CostEstimate(
            flops=2 * length * heads_width * (3 * width + 2 * length),
            bytes_accessed=2 * width * (3 * heads_width + length), transcendentals=0,
        ),
        compiler_params=pltpu.CompilerParams(
            collective_id=1, has_side_effects=True, vmem_limit_bytes=67043328
        ),
        name="gather_project_attend",
    )(tokens.reshape(CHUNKS, part, width), wq, wk, wv, shrink, eq, ek, ev, qgain, kgain,
      cos, sin, seg_col, seg_row)


def per_device(
    tokens,
    cotangent,
    segment_ids,
    adapter_set,
    w_query,
    w_key,
    w_value,
    w_out,
    w_gate,
    w_up,
    w_down,
    query_gain,
    key_gain,
    mixer_gain,
    feed_gain,
    shrink_query,
    expand_query,
    shrink_key,
    expand_key,
    shrink_value,
    expand_value,
    shrink_out,
    expand_out,
    shrink_gate,
    expand_gate,
    shrink_up,
    expand_up,
    shrink_down,
    expand_down,
):
    model_width = w_query.shape[0]
    chosen = adapter_set[0]

    def choose_set(adapters):
        return lax.dynamic_index_in_dim(adapters, chosen, 0, keepdims=False)

    query_shrink, query_widened = (choose_set(shrink_query), choose_set(expand_query))
    key_shrink, key_widened = (choose_set(shrink_key), choose_set(expand_key))
    value_shrink, value_widened = (choose_set(shrink_value), choose_set(expand_value))
    out_shrink, output_widened = (choose_set(shrink_out), choose_set(expand_out))
    gate_shrink, gate_widened = (choose_set(shrink_gate), choose_set(expand_gate))
    up_shrink, up_widened = (choose_set(shrink_up), choose_set(expand_up))
    down_shrink, down_widened = (choose_set(shrink_down), choose_set(expand_down))
    length = 4 * tokens.shape[0]
    rank = query_shrink.shape[0]
    half = jnp.asarray(adapter_scale_factor, jnp.bfloat16)
    blank = jnp.zeros_like(query_widened)
    cosine_table, sine_table = rotary_constants(length, HEAD_DIM)
    cosine_table, sine_table = jnp.asarray(cosine_table), jnp.asarray(sine_table)
    seg_col = segment_ids.reshape(length, 1)
    (
        mixed, query_rot, key_rot, value_low, query_proj, key_proj, scales, qkv_middle, full_tokens,
    ) = front(
        tokens, w_query, w_key, w_value,
        jnp.concatenate([query_shrink, key_shrink, value_shrink], axis=0),
        jnp.concatenate([half * query_widened, blank, blank], axis=0),
        jnp.concatenate([blank, half * key_widened, blank], axis=0),
        jnp.concatenate([blank, blank, half * value_widened], axis=0),
        query_gain[None], key_gain[None], cosine_table, sine_table, seg_col, segment_ids,
    )
    full_tokens = full_tokens.reshape(length, -1)
    query_scale, key_scale = scales[:, :1], scales[:, HEAD_DIM // 2 : HEAD_DIM // 2 + 1]
    query_gains = query_gain.astype(jnp.float32)
    key_gains = key_gain.astype(jnp.float32)
    query_middle, key_middle, value_middle = (
        qkv_middle[:, :rank], qkv_middle[:, rank : 2 * rank], qkv_middle[:, 2 * rank :]
    )
    nothing = jnp.zeros_like(gate_widened)
    (
        block_output, hidden_grad, mixed_grad, grad_down_shrink, gradient_gate_widened,
        gradient_up_widened, grad_out_shrink, owner_gate_up, owner_out, owner_down,
    ) = middle(
        mixed, tokens, cotangent, w_out, w_gate, w_up, w_down,
        mixer_gain.astype(jnp.float32)[None], feed_gain.astype(jnp.float32)[None],
        out_shrink, half * output_widened, jnp.concatenate([gate_shrink, up_shrink], axis=0),
        jnp.concatenate([half * gate_widened, nothing], axis=0),
        jnp.concatenate([nothing, half * up_widened], axis=0),
        down_shrink, half * down_widened,
    )
    mixed_grad = mixed_grad.reshape(mixed.shape)
    gradient_gate_widened = adapter_scale_factor * gradient_gate_widened[:rank]
    gradient_up_widened = adapter_scale_factor * gradient_up_widened[rank:]
    owner_wide = jnp.concatenate(
        [adapter_scale_factor * owner_out, owner_gate_up, adapter_scale_factor * owner_down], axis=0
    )
    query_norm_grad, key_norm_grad, value_gradient, query_sums, key_sums = attention_backward(
        query_rot, key_rot, value_low, mixed_grad, query_proj, key_proj,
        query_gains[None], key_gains[None], cosine_table, sine_table, seg_col, segment_ids,
    )
    back_sums = lax.psum((jnp.sum(query_sums, axis=-1), jnp.sum(key_sums, axis=-1)), "tensor")
    query_gradient = (
        query_scale * query_gains * query_norm_grad
        - query_proj * query_scale**3 * back_sums[0][:, None] / model_width
    ).astype(jnp.bfloat16)
    key_gradient = (
        key_scale * key_gains * key_norm_grad
        - key_proj * key_scale**3 * back_sums[1][:, None] / model_width
    ).astype(jnp.bfloat16)
    query_middle_gradient = adapter_scale_factor * rank_reduced(query_gradient, query_widened)
    key_middle_gradient = adapter_scale_factor * rank_reduced(key_gradient, key_widened)
    value_middle_gradient = adapter_scale_factor * rank_reduced(value_gradient, value_widened)
    gradient_query_widened = adapter_scale_factor * outer_gradient(query_middle, query_gradient)
    gradient_key_widened = adapter_scale_factor * outer_gradient(key_middle, key_gradient)
    gradient_value_widened = adapter_scale_factor * outer_gradient(value_middle, value_gradient)
    token_grads = hidden_grad + lax.psum_scatter(
        (
            jnp.dot(query_gradient, w_query.T, preferred_element_type=jnp.float32)
            + jnp.dot(key_gradient, w_key.T, preferred_element_type=jnp.float32)
            + jnp.dot(value_gradient, w_value.T, preferred_element_type=jnp.float32)
            + widen_from_rank(query_middle_gradient, query_shrink)
            + widen_from_rank(key_middle_gradient, key_shrink)
            + widen_from_rank(value_middle_gradient, value_shrink)
        ).astype(jnp.bfloat16),
        "tensor",
        scatter_dimension=0,
        tiled=True,
    ).astype(jnp.float32)
    sets_here = shrink_query.shape[0]
    dp_size = lax.axis_size("dp")
    tensor_size = lax.axis_size("tensor")
    set_of_each = lax.all_gather(chosen, "dp")
    onehot = (jnp.arange(sets_here)[:, None] == set_of_each[None, :]).astype(jnp.bfloat16)

    split = jnp.concatenate(
        [
            gradient_query_widened,
            gradient_key_widened,
            gradient_value_widened,
            grad_out_shrink,
            gradient_gate_widened,
            gradient_up_widened,
            grad_down_shrink,
        ],
        axis=1,
    ).astype(jnp.bfloat16)
    split_all = lax.all_gather(split, "dp")
    split_sums = jnp.einsum("cs,srw->crw", onehot, split_all, preferred_element_type=jnp.float32)
    local_sums = []
    at = 0
    for part in (
        gradient_query_widened,
        gradient_key_widened,
        gradient_value_widened,
        grad_out_shrink,
        gradient_gate_widened,
        gradient_up_widened,
        grad_down_shrink,
    ):
        local_sums.append(split_sums[:, :, at : at + part.shape[1]])
        at += part.shape[1]
    middles = lax.psum(
        jnp.concatenate(
            [
                query_middle_gradient,
                key_middle_gradient,
                value_middle_gradient,
            ],
            axis=1,
        ),
        "tensor",
    ).astype(jnp.bfloat16)
    wide = outer_gradient(middles, full_tokens)
    blocks = wide.reshape(3 * rank, dp_size, tensor_size, -1)
    mine = lax.dynamic_index_in_dim(blocks, lax.axis_index("tensor"), 2, keepdims=False)
    owner_blocks = owner_wide.reshape(4 * rank, dp_size, tensor_size, -1).transpose(2, 0, 1, 3)
    owner_mine = lax.psum_scatter(owner_blocks, "tensor", scatter_dimension=0)
    mine = jnp.concatenate([mine, owner_mine], axis=0)
    swapped = lax.all_to_all(mine.transpose(1, 0, 2), "dp", 0, 0)
    shared_sums = jnp.einsum(
        "cs,srw->crw",
        onehot.astype(jnp.float32),
        swapped,
        precision=highest,
        preferred_element_type=jnp.float32,
    )
    shared = [shared_sums[:, i * rank : (i + 1) * rank] for i in range(7)]
    return (
        block_output,
        token_grads,
        shared[0],
        local_sums[0],
        shared[1],
        local_sums[1],
        shared[2],
        local_sums[2],
        local_sums[3],
        shared[3],
        shared[4],
        local_sums[4],
        shared[5],
        local_sums[5],
        local_sums[6],
        shared[6],
    )


def solution(mesh):
    in_specs = (
        P(("dp", "tensor"), None),
        P(("dp", "tensor"), None),
        P("dp", None),
        P("dp"),
        P(None, "tensor"),
        P(None, "tensor"),
        P(None, "tensor"),
        P("tensor", None),
        P(None, "tensor"),
        P(None, "tensor"),
        P("tensor", None),
        P("tensor"),
        P("tensor"),
        P(),
        P(),
        P(),
        P(None, None, "tensor"),
        P(),
        P(None, None, "tensor"),
        P(),
        P(None, None, "tensor"),
        P(None, None, "tensor"),
        P(),
        P(),
        P(None, None, "tensor"),
        P(),
        P(None, None, "tensor"),
        P(None, None, "tensor"),
        P(),
    )
    out_specs = (
        P(("dp", "tensor"), None),
        P(("dp", "tensor"), None),
        P(None, None, ("dp", "tensor")),
        P(None, None, "tensor"),
        P(None, None, ("dp", "tensor")),
        P(None, None, "tensor"),
        P(None, None, ("dp", "tensor")),
        P(None, None, "tensor"),
        P(None, None, "tensor"),
        P(None, None, ("dp", "tensor")),
        P(None, None, ("dp", "tensor")),
        P(None, None, "tensor"),
        P(None, None, ("dp", "tensor")),
        P(None, None, "tensor"),
        P(None, None, "tensor"),
        P(None, None, ("dp", "tensor")),
    )
    return jax.shard_map(
        per_device, mesh=mesh, in_specs=in_specs, out_specs=out_specs, check_vma=False
    )
```

```python
import functools
import jax
import jax.numpy as jnp
import numpy as np
from jax import lax
from jax.experimental import pallas as pl
from jax.experimental.pallas import tpu as pltpu
from jax.sharding import PartitionSpec as P

HEAD_DIM = 128
DOC_MOST = 512
ATT_ROWS = 256
rotary_base = 500000.0
NEG = -1e30
LOG2E = 1.4426950408889634


def rotary_constants(length, head_dim):
    half = head_dim // 2
    frequency = np.float32(rotary_base) ** (
        -(np.arange(half, dtype=np.float32) * np.float32(2.0) / np.float32(head_dim))
    )
    angles = np.arange(length, dtype=np.float32)[:, None] * frequency.astype(np.float32)[None, :]
    cosine = np.cos(angles.astype(np.float64)).astype(np.float32)
    sine = np.sin(angles.astype(np.float64)).astype(np.float32)
    return (
        np.concatenate([cosine, cosine], axis=1),
        np.concatenate([-sine, sine], axis=1),
    )


def key_window(block, rows):
    first = max(0, (block * rows - (DOC_MOST - 1)) // rows) * rows
    return first, (block + 1) * rows


epsilon = 1e-06
adapter_scale_factor = 0.5


CHUNKS = 4
TILE = 1024
EXTRA = 128
NT = (((1,), (1,)), ((), ()))
TN = (((0,), (0,)), ((), ()))
MESH_ID = pl.DeviceIdType.MESH
MIDDLE_ORDER = (
    ("S2", 4), ("P4", 8), ("S4", 7), ("P0", 1), ("S1", 2), ("S6", 10), ("F3", 6),
    ("F5", 9), ("S5", 8), ("P2", 4), ("S0", 0), ("F1", 3), ("S3", 5),
)


def mm(left, right):
    return jnp.dot(left, right, preferred_element_type=jnp.float32)


def mm_nt(left, right):
    return lax.dot_general(left, right, NT, preferred_element_type=jnp.float32)


def mm_tn(left, right):
    return lax.dot_general(left, right, TN, preferred_element_type=jnp.float32)


def partners():
    me = lax.axis_index("tensor")
    group = lax.axis_index("dp")
    beside = me + 1 - 2 * lax.rem(me, 2)
    across = lax.rem(me + 2, 4)
    return me, group, beside, across


def greet(group, beside, across):
    barrier = pltpu.get_barrier_semaphore()
    for other in (beside, across):
        pl.semaphore_signal(barrier, inc=1, device_id=(group, other), device_id_type=MESH_ID)
    pl.semaphore_wait(barrier, 2)


def middle_body(
    mixed_ref, tokens_ref, cot_ref, w_out_hbm, w_gate_hbm, w_up_hbm, w_down_hbm,
    mgain_ref, fgain_ref, so_ref, eo_ref, sgu_ref, eg_ref, eu_ref, sd_ref, ed_ref,
    out_ref, hgrad_ref, dmixed_ref, gsd_ref, geg_ref, geu_ref, gso_ref, gsgu_ref, geo_ref, ged_ref,
    w_out, w_gate, w_up, w_down, wsem,
    rows_buf, own_buf, xsend, xrecv, bsend, brecv,
    gate_buf, up_buf, temp_a, temp_b, mgu_buf, mixer_buf, hidden_buf, mout_buf,
    xs_sem, xr_sem, bs_sem, br_sem, gxs_sem, gxr_sem, gbs_sem, gbr_sem, fs_sem, fr_sem,
):
    me, group, beside, across = partners()
    chunks, part, width = rows_buf.shape[0], rows_buf.shape[2], rows_buf.shape[3]
    units = w_gate.shape[1]
    heads_width = w_out.shape[0]
    far = lax.rem(beside + 2, 4)
    order = (me, across, beside, far)
    loads = [
        pltpu.make_async_copy(source, target, wsem.at[i])
        for i, (source, target) in enumerate(
            ((w_out_hbm, w_out), (w_gate_hbm, w_gate), (w_up_hbm, w_up), (w_down_hbm, w_down))
        )
    ]
    for load in loads:
        load.start()
    for ref in (gsd_ref, geg_ref, geu_ref, gso_ref, gsgu_ref, geo_ref, ged_ref):
        ref[...] = jnp.zeros_like(ref)
    greet(group, beside, across)

    def remote(source, target, ssem, rsem, other):
        return pltpu.make_async_remote_copy(
            src_ref=source, dst_ref=target, send_sem=ssem, recv_sem=rsem,
            device_id=(group, other), device_id_type=MESH_ID,
        )

    def gather_across(c):
        return remote(rows_buf.at[c, 0], rows_buf.at[c, 1], gxs_sem.at[c], gxr_sem.at[c], across)

    def gather_beside(c):
        return remote(rows_buf.at[c, 0], rows_buf.at[c, 2], gbs_sem.at[c], gbr_sem.at[c], beside)

    def gather_forward(c):
        return remote(rows_buf.at[c, 1], rows_buf.at[c, 3], fs_sem.at[c], fr_sem.at[c], beside)

    def reduce_beside(c):
        return remote(bsend.at[c], brecv.at[c], bs_sem.at[c], br_sem.at[c], beside)

    def reduce_across(c):
        return remote(xsend.at[c], xrecv.at[c], xs_sem.at[c], xr_sem.at[c], across)

    def store_partial(c, columns, value):
        low = value.astype(jnp.bfloat16)
        own_buf[c, :, columns] = low[:part]
        xsend[c, :, columns] = low[part : 2 * part]
        bsend[c, 0, :, columns] = low[2 * part : 3 * part]
        bsend[c, 1, :, columns] = low[3 * part :]

    def gathered(c):
        return rows_buf[c].reshape(4 * part, width)

    def forward_stage(c):
        gather_across(c).wait_recv()
        gather_forward(c).start()

    def pair_stage(c):
        reduce_beside(c).wait_recv()
        own_buf[c] = (
            own_buf[c].astype(jnp.float32) + brecv[c, 0].astype(jnp.float32)
        ).astype(jnp.bfloat16)
        xsend[c] = (
            xsend[c].astype(jnp.float32) + brecv[c, 1].astype(jnp.float32)
        ).astype(jnp.bfloat16)
        reduce_across(c).start()

    def totals(c):
        reduce_across(c).wait_recv()
        main = own_buf[c, :, :width].astype(jnp.float32) + xrecv[c, :, :width].astype(jnp.float32)
        side = own_buf[c, :, width : width + 32].astype(jnp.float32) + xrecv[
            c, :, width : width + 32
        ].astype(jnp.float32)
        return main, side.astype(jnp.bfloat16)

    def own_rows(c):
        return pl.ds(pl.multiple_of(c * part, part), part)

    def send_rows(c, value, again):
        if again:
            gather_across(c).wait_send()
            gather_beside(c).wait_send()
        rows_buf[c, 0] = value
        gather_across(c).start()
        gather_beside(c).start()

    def chunk_rows(c):
        return pl.ds(pl.multiple_of(c * 4 * part, 4 * part), 4 * part)

    def tiles(total, tile, body):
        def step(j, carry):
            body(pl.ds(pl.multiple_of(j * tile, tile), tile))
            return carry

        lax.fori_loop(0, total // tile, step, 0)

    def mixed_chunk(c):
        return jnp.concatenate([mixed_ref[o, c] for o in order], axis=0)

    def stage_mixer(c):
        @pl.when(c == 0)
        def _():
            loads[0].wait()

        rows = mixed_chunk(c)
        store_partial(c, slice(width, width + 16), mm_nt(rows, so_ref[...]))
        tiles(width, TILE, lambda cols: store_partial(c, cols, mm(rows, w_out[:, cols])))
        reduce_beside(c).start()

    def stage_hidden(c):
        main, side = totals(c)
        mid = side[:, :16]
        mout_buf[c] = mid
        mixer = main + mm(mid, eo_ref[...])
        mixer_buf[own_rows(c), :] = mixer
        factor = lax.rsqrt(jnp.mean(mixer * mixer, axis=1, keepdims=True) + epsilon)
        hidden = tokens_ref[own_rows(c), :].astype(jnp.float32) + mixer * factor * mgain_ref[...]
        hidden_buf[own_rows(c), :] = hidden
        send_rows(c, hidden.astype(jnp.bfloat16), False)

    def arrive(c):
        gather_beside(c).wait_recv()
        gather_forward(c).wait_recv()

    def stage_units(c):
        @pl.when(c == 0)
        def _():
            for load in loads[1:]:
                load.wait()

        arrive(c)
        mids = mm_nt(gathered(c), sgu_ref[...]).astype(jnp.bfloat16)
        mgu_buf[c] = mids

        def unit_tile(cols):
            rows = gathered(c)
            gate = mm(rows, w_gate[:, cols]) + mm(mids, eg_ref[:, cols])
            up = mm(rows, w_up[:, cols]) + mm(mids, eu_ref[:, cols])
            gate_buf[chunk_rows(c), cols] = gate.astype(jnp.bfloat16)
            up_buf[chunk_rows(c), cols] = up.astype(jnp.bfloat16)
            sig = 1.0 / (1.0 + jnp.exp(-gate))
            temp_a[:, cols] = (gate * sig * up).astype(jnp.bfloat16)

        tiles(units, TILE // 2, unit_tile)
        gather_forward(c).wait_send()
        reduce_beside(c).wait_send()
        reduce_across(c).wait_send()
        inner = temp_a[...]
        store_partial(c, slice(width, width + 16), mm_nt(inner, sd_ref[...]))
        tiles(width, TILE, lambda cols: store_partial(c, cols, mm(temp_a[...], w_down[:, cols])))
        reduce_beside(c).start()

    def norm_back_rows(values, gains, grads):
        factor = lax.rsqrt(jnp.mean(values * values, axis=1, keepdims=True) + epsilon)
        weighted = grads * gains
        return factor * weighted - values * (
            factor * factor * factor * jnp.mean(values * weighted, axis=1, keepdims=True)
        )

    def stage_feed(c):
        main, side = totals(c)
        mid = side[:, :16]
        feed = main + mm(mid, ed_ref[...])
        factor = lax.rsqrt(jnp.mean(feed * feed, axis=1, keepdims=True) + epsilon)
        gains = fgain_ref[...]
        out_ref[own_rows(c), :] = (hidden_buf[own_rows(c), :] + feed * factor * gains).astype(
            jnp.bfloat16
        )
        grad = norm_back_rows(feed, gains, cot_ref[own_rows(c), :].astype(jnp.float32))
        grad = grad.astype(jnp.bfloat16)
        send_rows(c, grad, True)
        ged_ref[...] += mm_tn(mid, grad)

    def stage_units_back(c):
        arrive(c)
        dmid = mm_nt(gathered(c), ed_ref[...]).astype(jnp.bfloat16)
        mids = mgu_buf[c]

        def unit_tile(cols):
            rows = gathered(c)
            inner_grad = mm_nt(rows, w_down[cols, :]) + mm(dmid, sd_ref[:, cols])
            gate = gate_buf[chunk_rows(c), cols].astype(jnp.float32)
            up = up_buf[chunk_rows(c), cols].astype(jnp.float32)
            sig = 1.0 / (1.0 + jnp.exp(-gate))
            silu = gate * sig
            gate_grad = (inner_grad * up * (sig + silu * (1.0 - sig))).astype(jnp.bfloat16)
            up_grad = (inner_grad * silu).astype(jnp.bfloat16)
            temp_a[:, cols] = gate_grad
            temp_b[:, cols] = up_grad
            gsd_ref[:, cols] += mm_tn(dmid, (silu * up).astype(jnp.bfloat16))
            geg_ref[:, cols] += mm_tn(mids, gate_grad)
            geu_ref[:, cols] += mm_tn(mids, up_grad)

        tiles(units, TILE // 2, unit_tile)
        gather_forward(c).wait_send()
        reduce_beside(c).wait_send()
        reduce_across(c).wait_send()
        store_partial(
            c,
            slice(width, width + 32),
            mm_nt(temp_a[...], eg_ref[...]) + mm_nt(temp_b[...], eu_ref[...]),
        )

        def width_tile(cols):
            store_partial(
                c, cols, mm_nt(temp_a[...], w_gate[cols, :]) + mm_nt(temp_b[...], w_up[cols, :])
            )

        tiles(width, TILE // 2, width_tile)
        reduce_beside(c).start()

    def stage_mixer_grad(c):
        main, side = totals(c)
        grads = cot_ref[own_rows(c), :].astype(jnp.float32) + main + mm(side, sgu_ref[...])
        hgrad_ref[own_rows(c), :] = grads
        mixer_grad = norm_back_rows(mixer_buf[own_rows(c), :], mgain_ref[...], grads)
        mixer_grad = mixer_grad.astype(jnp.bfloat16)
        send_rows(c, mixer_grad, True)
        geo_ref[...] += mm_tn(mout_buf[c], mixer_grad)
        gsgu_ref[...] += mm_tn(side, hidden_buf[own_rows(c), :].astype(jnp.bfloat16))

    def stage_mixed_grad(c):
        arrive(c)
        dmid = mm_nt(gathered(c), eo_ref[...]).astype(jnp.bfloat16)
        grad = (mm_nt(gathered(c), w_out[...]) + mm(dmid, so_ref[...])).astype(jnp.bfloat16)
        for i, o in enumerate(order):
            dmixed_ref[o, c] = grad[i * part : (i + 1) * part]
        gso_ref[...] += mm_tn(dmid, mixed_chunk(c))
        gather_forward(c).wait_send()
        gather_across(c).wait_send()
        gather_beside(c).wait_send()
        reduce_beside(c).wait_send()
        reduce_across(c).wait_send()

    stages = {
        "S0": stage_mixer, "S1": stage_hidden, "S2": stage_units, "S3": stage_feed,
        "S4": stage_units_back, "S5": stage_mixer_grad, "S6": stage_mixed_grad,
        "P0": pair_stage, "P2": pair_stage, "P4": pair_stage,
        "F1": forward_stage, "F3": forward_stage, "F5": forward_stage,
    }

    def step(i, carry):
        for name, delay in MIDDLE_ORDER:

            @pl.when((i >= delay) & (i < delay + chunks))
            def _():
                stages[name](i - delay)

        return carry

    lax.fori_loop(0, chunks + max(delay for _, delay in MIDDLE_ORDER), step, 0)


def middle(mixed, tokens, cot, w_out, w_gate, w_up, w_down, mgain, fgain, so, eo, sgu, eg, eu, sd, ed):
    rows, width = tokens.shape
    heads_width, units = w_out.shape[0], w_gate.shape[1]
    part = rows // CHUNKS
    whole_width = width + EXTRA
    vmem = pl.BlockSpec(memory_space=pltpu.VMEM)
    hbm = pl.BlockSpec(memory_space=pl.ANY)
    low, full = jnp.bfloat16, jnp.float32
    dma = pltpu.SemaphoreType.DMA((CHUNKS,))
    shape = jax.ShapeDtypeStruct
    flops = 2 * 4 * rows * width * (2 * heads_width + 6 * units)
    return pl.pallas_call(
        middle_body,
        in_specs=[vmem] * 3 + [hbm] * 4 + [vmem] * 9,
        out_specs=[vmem] * 10,
        out_shape=[
            shape((rows, width), low), shape((rows, width), full),
            shape((4, CHUNKS, part, heads_width), low),
            shape((16, units), full), shape((32, units), full), shape((32, units), full),
            shape((16, heads_width), full), shape((32, width), full), shape((16, width), full),
            shape((16, width), full),
        ],
        scratch_shapes=[
            pltpu.VMEM(w_out.shape, low), pltpu.VMEM(w_gate.shape, low),
            pltpu.VMEM(w_up.shape, low), pltpu.VMEM(w_down.shape, low),
            pltpu.SemaphoreType.DMA((4,)),
            pltpu.VMEM((CHUNKS, 4, part, width), low),
            pltpu.VMEM((CHUNKS, part, whole_width), low),
            pltpu.VMEM((CHUNKS, part, whole_width), low),
            pltpu.VMEM((CHUNKS, part, whole_width), low),
            pltpu.VMEM((CHUNKS, 2, part, whole_width), low),
            pltpu.VMEM((CHUNKS, 2, part, whole_width), low),
            pltpu.VMEM((4 * rows, units), low), pltpu.VMEM((4 * rows, units), low),
            pltpu.VMEM((4 * part, units), low), pltpu.VMEM((4 * part, units), low),
            pltpu.VMEM((CHUNKS, 4 * part, 32), low),
            pltpu.VMEM((rows, width), full), pltpu.VMEM((rows, width), full),
            pltpu.VMEM((CHUNKS, part, 16), low),
        ] + [dma] * 10,
        cost_estimate=pl.CostEstimate(
            flops=flops, bytes_accessed=2 * width * (heads_width + 3 * units), transcendentals=0
        ),
        compiler_params=pltpu.CompilerParams(
            collective_id=0, has_side_effects=True, vmem_limit_bytes=67043328
        ),
        name="mixer_to_feed",
    )(mixed.reshape(4, CHUNKS, part, heads_width), tokens, cot, w_out, w_gate, w_up, w_down,
      mgain, fgain, so, eo, sgu, eg, eu, sd, ed)


def attention_scores(first, second, block, rows, low, seg_first, seg_second, query_axis):
    scores = lax.dot_general(first, second, NT, preferred_element_type=jnp.float32)
    kpos = lax.broadcasted_iota(jnp.int32, scores.shape, 1 - query_axis) + low
    qpos = lax.broadcasted_iota(jnp.int32, scores.shape, query_axis) + block * rows
    return jnp.where((kpos <= qpos) & (seg_first == seg_second), scores, NEG)


def front_body(
    tokens_ref, wq_hbm, wk_hbm, wv_hbm, shrink_ref, eq_ref, ek_ref, ev_ref, qgain_ref, kgain_ref,
    cos_ref, sin_ref, seg_col_ref, seg_row_ref,
    mixed_ref, qrot_ref, krot_ref, value_ref, qproj_ref, kproj_ref, scale_ref, mids_ref, full_hbm,
    wq, wk, wv, wsem, full, lhs, squares, ex_send, ex_recv,
    xs_sem, xr_sem, fs_sem, fr_sem, bs_sem, br_sem, es_sem, er_sem, out_sem,
):
    me, group, beside, across = partners()
    far = lax.rem(beside + 2, 4)
    chunks, part, width = full.shape[1:]
    rows = chunks * part
    length = 4 * rows
    loads = [
        pltpu.make_async_copy(source, target, wsem.at[i])
        for i, (source, target) in enumerate(((wq_hbm, wq), (wk_hbm, wk), (wv_hbm, wv)))
    ]
    for load in loads:
        load.start()
    barrier = pltpu.get_barrier_semaphore()
    for other in (beside, across, far):
        pl.semaphore_signal(barrier, inc=1, device_id=(group, other), device_id_type=MESH_ID)
    pl.semaphore_wait(barrier, 3)

    def remote(source, target, ssem, rsem, other):
        return pltpu.make_async_remote_copy(
            src_ref=source, dst_ref=target, send_sem=ssem, recv_sem=rsem,
            device_id=(group, other), device_id_type=MESH_ID,
        )

    def send_across(c):
        return remote(tokens_ref.at[c], full.at[me, c], xs_sem.at[c], xr_sem.at[c], across)

    def forward(c):
        return remote(full.at[across, c], full.at[across, c], fs_sem.at[c], fr_sem.at[c], beside)

    to_beside = remote(tokens_ref, full.at[me], bs_sem, br_sem, beside)
    for c in range(chunks):
        send_across(c).start()
    to_beside.start()
    full[me] = tokens_ref[...]
    for load in loads:
        load.wait()
    pairs = chunks // 2
    half = rows // 2

    def block_step(b, carry):
        @pl.when(b == 0)
        def _():
            lhs[...] = tokens_ref[...].reshape(rows, width)

        @pl.when(b == 1)
        def _():
            to_beside.wait_recv()
            lhs[...] = full[beside].reshape(rows, width)

        @pl.when(b >= 2)
        def _():
            base = (b - 2) * pairs
            for j in range(pairs):
                send_across(base + j).wait_recv()
                forward(base + j).start()
            for j in range(pairs):
                lhs[j * part : (j + 1) * part] = full[across, base + j]
            for j in range(pairs):
                forward(base + j).wait_recv()
                lhs[half + j * part : half + (j + 1) * part] = full[far, base + j]

        mids = mm_nt(lhs[...], shrink_ref[...]).astype(jnp.bfloat16)
        query = mm(lhs[...], wq[...]) + mm(mids, eq_ref[...])
        key = mm(lhs[...], wk[...]) + mm(mids, ek_ref[...])
        value = (mm(lhs[...], wv[...]) + mm(mids, ev_ref[...])).astype(jnp.bfloat16)
        qsum = jnp.sum(query * query, axis=1, keepdims=True)
        ksum = jnp.sum(key * key, axis=1, keepdims=True)
        lane = lax.broadcasted_iota(jnp.int32, (rows, HEAD_DIM), 1)
        both = jnp.where(lane < 4, qsum, ksum)
        first = jnp.where(b == 0, me, jnp.where(b == 1, beside, across)) * rows
        second = jnp.where(b == 0, me, jnp.where(b == 1, beside, far)) * rows
        first = first + jnp.where(b >= 2, (b - 2) * half, 0)
        second = second + jnp.where(b >= 2, (b - 2) * half, half)
        for start, piece in ((first, slice(0, half)), (second, slice(half, rows))):
            there = pl.ds(pl.multiple_of(start, half), half)
            qproj_ref[there, :] = query[piece]
            kproj_ref[there, :] = key[piece]
            value_ref[there, :] = value[piece]
            mids_ref[there, :] = mids[piece]
            squares[there, :] = both[piece]
        return carry

    lax.fori_loop(0, 4, block_step, 0)
    save = pltpu.make_async_copy(full, full_hbm, out_sem)
    save.start()
    ex_send[...] = jnp.transpose(squares[...])[:8]
    swaps = [
        remote(ex_send, ex_recv.at[i], es_sem.at[i], er_sem.at[i], other)
        for i, other in enumerate((beside, across, far))
    ]
    for swap in swaps:
        swap.start()
    for swap in swaps:
        swap.wait_recv()
    total = ex_send[...] + ex_recv[0] + ex_recv[1] + ex_recv[2]
    factor = lax.rsqrt(total / (4 * wq.shape[1]) + epsilon)
    wide = jnp.concatenate(
        [
            jnp.broadcast_to(factor[:1], (HEAD_DIM // 2, length)),
            jnp.broadcast_to(factor[4:5], (HEAD_DIM // 2, length)),
        ],
        axis=0,
    )
    scale_ref[...] = jnp.transpose(wide)
    heads = wq.shape[1] // HEAD_DIM
    exponent = HEAD_DIM ** (-0.5) * LOG2E
    block_rows = min(ATT_ROWS, length)

    def head_step(h, carry):
        cols = pl.ds(pl.multiple_of(h * HEAD_DIM, HEAD_DIM), HEAD_DIM)
        for source, lane, gain, target in (
            (qproj_ref, 0, qgain_ref, qrot_ref),
            (kproj_ref, HEAD_DIM // 2, kgain_ref, krot_ref),
        ):
            normed = source[:, cols] * scale_ref[:, lane : lane + 1] * gain[:, cols].astype(jnp.float32)
            turned = normed * cos_ref[...] + pltpu.roll(normed, HEAD_DIM // 2, 1) * sin_ref[...]
            target[:, cols] = turned.astype(jnp.bfloat16)
        for block in range(length // block_rows):
            low, high = key_window(block, block_rows)
            here = pl.ds(block * block_rows, block_rows)
            keys = pl.ds(low, high - low)
            scores = attention_scores(
                qrot_ref[here, cols], krot_ref[keys, cols], block, block_rows, low,
                seg_col_ref[here, :], seg_row_ref[:, keys], 0,
            )
            top = jnp.max(scores, axis=1, keepdims=True)
            weights = jnp.exp2((scores - top) * exponent)
            total = jnp.sum(weights, axis=1, keepdims=True)
            mix = mm(weights.astype(jnp.bfloat16), value_ref[keys, cols])
            mixed_ref[here, cols] = (mix * (1.0 / total)).astype(jnp.bfloat16)
        return carry

    lax.fori_loop(0, heads, head_step, 0)
    for c in range(chunks):
        send_across(c).wait_send()
        forward(c).wait_send()
    to_beside.wait_send()
    for swap in swaps:
        swap.wait_send()
    save.wait()


def front(tokens, wq, wk, wv, shrink, eq, ek, ev, qgain, kgain, cos, sin, seg_col, seg_row):
    rows, width = tokens.shape
    heads_width = wq.shape[1]
    length = 4 * rows
    part = rows // CHUNKS
    vmem = pl.BlockSpec(memory_space=pltpu.VMEM)
    hbm = pl.BlockSpec(memory_space=pl.ANY)
    low, full = jnp.bfloat16, jnp.float32
    shape = jax.ShapeDtypeStruct
    dma = pltpu.SemaphoreType.DMA
    return pl.pallas_call(
        front_body,
        in_specs=[vmem] + [hbm] * 3 + [vmem] * 10,
        out_specs=[vmem] * 8 + [hbm],
        out_shape=[
            shape((length, heads_width), low), shape((length, heads_width), low),
            shape((length, heads_width), low), shape((length, heads_width), low),
            shape((length, heads_width), full), shape((length, heads_width), full),
            shape((length, HEAD_DIM), full), shape((length, shrink.shape[0]), low),
            shape((4, CHUNKS, part, width), low),
        ],
        scratch_shapes=[
            pltpu.VMEM(wq.shape, low), pltpu.VMEM(wk.shape, low), pltpu.VMEM(wv.shape, low),
            dma((3,)),
            pltpu.VMEM((4, CHUNKS, part, width), low), pltpu.VMEM((rows, width), low),
            pltpu.VMEM((length, HEAD_DIM), full), pltpu.VMEM((8, length), full),
            pltpu.VMEM((3, 8, length), full),
            dma((CHUNKS,)), dma((CHUNKS,)), dma((CHUNKS,)), dma((CHUNKS,)), dma, dma,
            dma((3,)), dma((3,)), dma,
        ],
        cost_estimate=pl.CostEstimate(
            flops=2 * length * heads_width * (3 * width + 2 * length),
            bytes_accessed=2 * width * (3 * heads_width + length), transcendentals=0,
        ),
        compiler_params=pltpu.CompilerParams(
            collective_id=1, has_side_effects=True, vmem_limit_bytes=67043328
        ),
        name="gather_project_attend",
    )(tokens.reshape(CHUNKS, part, width), wq, wk, wv, shrink, eq, ek, ev, qgain, kgain,
      cos, sin, seg_col, seg_row)


def back_body(
    qrot_ref, krot_ref, value_ref, dmixed_ref, qproj_ref, kproj_ref, scale_ref, qgain_ref, kgain_ref,
    cos_ref, sin_ref, seg_col_ref, seg_row_ref, wq_hbm, wk_hbm, wv_hbm, shrink_ref,
    eq_ref, ek_ref, ev_ref, mids_ref, full_hbm, hgrad_ref, set_ref,
    gso_ref, geg_ref, geu_ref, gsd_ref, gsgu_ref, geo_ref, ged_ref,
    tgrad_ref, split_hbm, heads_hbm, shared_hbm, inward_hbm,
    wq, wk, wv, full, wsem, dq_buf, dk_buf, dq_low, dk_low, dv_low, dk_acc, dv_acc, sums_buf,
    split_send, heads_send, blocks, blocks_recv, blocks_xrecv, shared_send, inward_send,
    ex_send, ex_recv, dmid_send, dmid_recv, dmid_xsend, dmid_xrecv,
    own_buf, xsend, xrecv, bsend, brecv,
    es_sem, er_sem, xs_sem, xr_sem, bs_sem, br_sem, one_s, one_r,
    sp_s, sp_r, hd_s, hd_r, sh_s, sh_r, in_s, in_r, local_sem,
):
    me, group, beside, across = partners()
    far = lax.rem(beside + 2, 4)
    order = (me, across, beside, far)
    groups = split_hbm.shape[0]
    chunks, part, width = own_buf.shape
    rows = chunks * part
    length = 4 * rows
    heads_width = wq.shape[1]
    units = geg_ref.shape[1]
    cols_each = blocks.shape[3]
    loads = [
        pltpu.make_async_copy(source, target, wsem.at[i])
        for i, (source, target) in enumerate(
            ((wq_hbm, wq), (wk_hbm, wk), (wv_hbm, wv), (full_hbm, full))
        )
    ]
    for load in loads:
        load.start()
    barrier = pltpu.get_barrier_semaphore()
    for other in (beside, across, far):
        pl.semaphore_signal(barrier, inc=1, device_id=(group, other), device_id_type=MESH_ID)

    def greet_group(j, carry):
        other = lax.rem(group + j, groups)
        pl.semaphore_signal(barrier, inc=1, device_id=(other, me), device_id_type=MESH_ID)
        return carry

    lax.fori_loop(1, groups, greet_group, 0)
    pl.semaphore_wait(barrier, groups + 2)

    def remote(source, target, ssem, rsem, other):
        return pltpu.make_async_remote_copy(
            src_ref=source, dst_ref=target, send_sem=ssem, recv_sem=rsem,
            device_id=(group, other), device_id_type=MESH_ID,
        )

    def to_group(source, target, ssem, rsem, j):
        other = lax.rem(group + j, groups)
        return pltpu.make_async_remote_copy(
            src_ref=source(other), dst_ref=target.at[group], send_sem=ssem.at[j],
            recv_sem=rsem.at[group], device_id=(other, me), device_id_type=MESH_ID,
        )

    def from_group(source, target, ssem, rsem, j):
        sender = lax.rem(group + j, groups)
        return pltpu.make_async_remote_copy(
            src_ref=source(sender), dst_ref=target.at[sender], send_sem=ssem.at[j],
            recv_sem=rsem.at[sender], device_id=(sender, me), device_id_type=MESH_ID,
        )

    split = (lambda other: split_send, split_hbm, sp_s, sp_r)
    by_heads = (lambda other: heads_send, heads_hbm, hd_s, hd_r)
    shared = (lambda other: shared_send.at[other], shared_hbm, sh_s, sh_r)
    inward = (lambda other: inward_send.at[other, me], inward_hbm, in_s, in_r)
    exchanges = (split, by_heads, shared, inward)

    def start_exchange(number):
        exchange = exchanges[number]

        def one(j, carry):
            to_group(*exchange, j).start()
            return carry

        lax.fori_loop(1, groups, one, 0)
        pltpu.make_async_copy(
            exchange[0](group), exchange[1].at[group], local_sem.at[number]
        ).start()

    def end_exchange(number):
        exchange = exchanges[number]

        def one(j, carry):
            to_group(*exchange, j).wait_send()
            from_group(*exchange, j).wait_recv()
            return carry

        lax.fori_loop(1, groups, one, 0)
        pltpu.make_async_copy(
            exchange[0](group), exchange[1].at[group], local_sem.at[number]
        ).wait()

    low = jnp.bfloat16
    split_send[:, :heads_width] = gso_ref[...].astype(low)
    split_send[:, heads_width : heads_width + units] = (
        adapter_scale_factor * geg_ref[:16]
    ).astype(low)
    split_send[:, heads_width + units : heads_width + 2 * units] = (
        adapter_scale_factor * geu_ref[16:]
    ).astype(low)
    split_send[:, heads_width + 2 * units : heads_width + 3 * units] = gsd_ref[...].astype(low)
    split_send[:, heads_width + 3 * units :] = jnp.broadcast_to(set_ref[...], (16, 128)).astype(low)
    start_exchange(0)
    for t in range(4):
        for g in range(groups):
            at = slice((g * 4 + t) * cols_each, (g * 4 + t + 1) * cols_each)
            blocks[t, g, :16] = (adapter_scale_factor * geo_ref[:, at]).astype(low)
            blocks[t, g, 16:48] = gsgu_ref[:, at].astype(low)
            blocks[t, g, 48:] = (adapter_scale_factor * ged_ref[:, at]).astype(low)
    block_near = remote(blocks.at[beside], blocks_recv.at[0], one_s.at[0], one_r.at[0], beside)
    block_far = remote(blocks.at[far], blocks_recv.at[1], one_s.at[1], one_r.at[1], beside)
    block_across = remote(shared_send, blocks_xrecv, one_s.at[2], one_r.at[2], across)
    block_near.start()
    block_far.start()

    heads = heads_width // HEAD_DIM
    inverse = HEAD_DIM ** (-0.5)
    exponent = inverse * LOG2E
    block_rows = min(ATT_ROWS, length)
    sums_buf[...] = jnp.zeros_like(sums_buf)

    def head_step(h, carry):
        cols = pl.ds(pl.multiple_of(h * HEAD_DIM, HEAD_DIM), HEAD_DIM)
        dk_acc[...] = jnp.zeros_like(dk_acc)
        dv_acc[...] = jnp.zeros_like(dv_acc)
        for block in range(length // block_rows):
            first, last = key_window(block, block_rows)
            here = pl.ds(block * block_rows, block_rows)
            keys = pl.ds(first, last - first)
            queries = qrot_ref[here, cols]
            key_rows = krot_ref[keys, cols]
            grads = dmixed_ref[here, cols]
            scores = attention_scores(
                key_rows, queries, block, block_rows, first,
                seg_col_ref[keys, :], seg_row_ref[:, here], 1,
            )
            top = jnp.max(scores, axis=0, keepdims=True)
            weights = jnp.exp2((scores - top) * exponent)
            total = jnp.sum(weights, axis=0, keepdims=True)
            probs = weights * (1.0 / total)
            prob_grad = mm_nt(value_ref[keys, cols], grads)
            weighted = probs * prob_grad
            delta = jnp.sum(weighted, axis=0, keepdims=True)
            score_grad = (weighted - probs * delta).astype(low)
            dv_acc[keys, :] += mm(probs.astype(low), grads)
            dk_acc[keys, :] += mm(score_grad, queries)
            dq = mm_tn(score_grad, key_rows) * inverse
            dq = dq * cos_ref[here, :] - pltpu.roll(dq, HEAD_DIM // 2, 1) * sin_ref[here, :]
            dq = dq * qgain_ref[:, cols].astype(jnp.float32)
            dq_buf[here, cols] = dq
            sums_buf[0, here, :] += qproj_ref[here, cols] * dq
        dk = dk_acc[...] * inverse
        dk = dk * cos_ref[...] - pltpu.roll(dk, HEAD_DIM // 2, 1) * sin_ref[...]
        dk = dk * kgain_ref[:, cols].astype(jnp.float32)
        dk_buf[:, cols] = dk
        sums_buf[1] += kproj_ref[:, cols] * dk
        dv_low[:, cols] = dv_acc[...].astype(low)

        @pl.when(h == 0)
        def _():
            block_near.wait_recv()
            block_far.wait_recv()
            shared_send[...] = (
                blocks[across].astype(jnp.float32) + blocks_recv[1].astype(jnp.float32)
            ).astype(low)
            block_across.start()

        @pl.when(h == heads - 1)
        def _():
            block_across.wait()
            shared_send[...] = (
                blocks[me].astype(jnp.float32)
                + blocks_recv[0].astype(jnp.float32)
                + blocks_xrecv[...].astype(jnp.float32)
            ).astype(low)
            start_exchange(2)

        return carry

    lax.fori_loop(0, heads, head_step, 0)

    lane = lax.broadcasted_iota(jnp.int32, (length, HEAD_DIM), 1)
    both = jnp.where(
        lane < 4,
        jnp.sum(sums_buf[0], axis=1, keepdims=True),
        jnp.sum(sums_buf[1], axis=1, keepdims=True),
    )
    ex_send[...] = jnp.transpose(both)[:8]
    swaps = [
        remote(ex_send, ex_recv.at[i], es_sem.at[i], er_sem.at[i], other)
        for i, other in enumerate((beside, across, far))
    ]
    for swap in swaps:
        swap.start()
    for load in loads:
        load.wait()
    for swap in swaps:
        swap.wait_recv()
    total = (ex_send[...] + ex_recv[0] + ex_recv[1] + ex_recv[2]) * (1.0 / (4 * heads_width))
    wide = jnp.concatenate(
        [
            jnp.broadcast_to(total[:1], (HEAD_DIM // 2, length)),
            jnp.broadcast_to(total[4:5], (HEAD_DIM // 2, length)),
        ],
        axis=0,
    )
    sums_buf[0] = jnp.transpose(wide)
    for dn, proj, target, at in (
        (dq_buf, qproj_ref, dq_low, 0), (dk_buf, kproj_ref, dk_low, HEAD_DIM // 2),
    ):
        scale = scale_ref[:, at : at + 1]
        means = sums_buf[0, :, at : at + 1]
        target[...] = (scale * dn[...] - proj[...] * (scale * scale * scale * means)).astype(low)

    dmid_part = (
        mm_nt(eq_ref[...], dq_low[...]) + mm_nt(ek_ref[...], dk_low[...])
        + mm_nt(ev_ref[...], dv_low[...])
    )
    dmid_send[...] = dmid_part.astype(low)
    dmid_near = remote(dmid_send, dmid_recv, one_s.at[3], one_r.at[3], beside)
    dmid_across = remote(dmid_xsend, dmid_xrecv, one_s.at[4], one_r.at[4], across)
    dmid_near.start()

    def reduce_beside(c):
        return remote(bsend.at[c], brecv.at[c], bs_sem.at[c], br_sem.at[c], beside)

    def reduce_across(c):
        return remote(xsend.at[c], xrecv.at[c], xs_sem.at[c], xr_sem.at[c], across)

    def chunk_of(buffer, c):
        return jnp.concatenate(
            [buffer[pl.ds(pl.multiple_of(o * rows + c * part, part), part), :] for o in order], axis=0
        )

    def stage_partial(c):
        parts = [chunk_of(buffer, c) for buffer in (dq_low, dk_low, dv_low)]
        tile = TILE

        def one(j, carry):
            at = pl.ds(pl.multiple_of(j * tile, tile), tile)
            value = (
                mm_nt(parts[0], wq[at, :]) + mm_nt(parts[1], wk[at, :]) + mm_nt(parts[2], wv[at, :])
            ).astype(low)
            own_buf[c, :, at] = value[:part]
            xsend[c, :, at] = value[part : 2 * part]
            bsend[c, 0, :, at] = value[2 * part : 3 * part]
            bsend[c, 1, :, at] = value[3 * part :]
            return carry

        lax.fori_loop(0, width // tile, one, 0)
        reduce_beside(c).start()

    def stage_pair(c):
        reduce_beside(c).wait_recv()
        xsend[c] = (xsend[c].astype(jnp.float32) + brecv[c, 1].astype(jnp.float32)).astype(low)
        reduce_across(c).start()
        own_buf[c] = (own_buf[c].astype(jnp.float32) + brecv[c, 0].astype(jnp.float32)).astype(low)

    def partial_step(i, carry):
        @pl.when(i < chunks)
        def _():
            stage_partial(i)

        @pl.when(i == 0)
        def _():
            dmid_near.wait_recv()
            dmid_xsend[...] = (
                dmid_send[...].astype(jnp.float32) + dmid_recv[...].astype(jnp.float32)
            ).astype(low)
            dmid_across.start()

        @pl.when(i > 0)
        def _():
            stage_pair(i - 1)

        return carry

    lax.fori_loop(0, chunks + 1, partial_step, 0)

    mids = mids_ref[...]
    for i, buffer in enumerate((dq_low, dk_low, dv_low)):
        heads_send[:, i * heads_width : (i + 1) * heads_width] = (
            adapter_scale_factor * mm_tn(mids, buffer[...])[i * 16 : (i + 1) * 16]
        ).astype(low)
    start_exchange(1)
    dmid_across.wait_recv()
    dmid = (
        dmid_xsend[...].astype(jnp.float32) + dmid_xrecv[...].astype(jnp.float32)
    ).astype(low)
    inward_grad = mm(dmid, full[...])
    for t in range(4):
        for g in range(groups):
            at = slice((g * 4 + t) * cols_each, (g * 4 + t + 1) * cols_each)
            inward_send[g, t] = inward_grad[:, at]
    start_exchange(3)
    dmid_xsend_ready = dmid
    ex_dmid = dmid_xsend_ready
    dmid_across.wait_send()
    dmid_xsend[...] = ex_dmid

    def finish_step(c, carry):
        reduce_across(c).wait_recv()
        here = pl.ds(pl.multiple_of(c * part, part), part)
        tgrad_ref[here, :] = (
            hgrad_ref[here, :] + own_buf[c].astype(jnp.float32) + xrecv[c].astype(jnp.float32)
        )
        return carry

    mine = pl.ds(pl.multiple_of(me * rows, rows), rows)
    extra = mm_tn(dmid_xsend[:, mine], shrink_ref[...])
    lax.fori_loop(0, chunks, finish_step, 0)
    tgrad_ref[...] += extra
    for c in range(chunks):
        reduce_beside(c).wait_send()
        reduce_across(c).wait_send()
    for copy in (block_near, block_far, dmid_near, *swaps):
        copy.wait_send()
    for number in range(4):
        end_exchange(number)


def back(
    qrot, krot, value, dmixed, qproj, kproj, scale, qgain, kgain, cos, sin, seg_col, seg_row,
    wq, wk, wv, shrink, eq, ek, ev, mids, full, hgrad, chosen, gso, geg, geu, gsd, gsgu, geo, ged,
):
    rows, width = hgrad.shape
    heads_width, units = wq.shape[1], geg.shape[1]
    length = 4 * rows
    part = rows // CHUNKS
    groups = lax.axis_size("dp")
    cols_each = width // (4 * groups)
    split_width = heads_width + 3 * units + 128
    vmem = pl.BlockSpec(memory_space=pltpu.VMEM)
    hbm = pl.BlockSpec(memory_space=pl.ANY)
    low, f32 = jnp.bfloat16, jnp.float32
    shape = jax.ShapeDtypeStruct
    dma = pltpu.SemaphoreType.DMA
    buf = pltpu.VMEM
    return pl.pallas_call(
        back_body,
        in_specs=[vmem] * 13 + [hbm] * 3 + [vmem] * 5 + [hbm] + [vmem] * 9,
        out_specs=[vmem] + [hbm] * 4,
        out_shape=[
            shape((rows, width), f32),
            shape((groups, 16, split_width), low),
            shape((groups, 16, 3 * heads_width), low),
            shape((groups, 64, cols_each), low),
            shape((groups, 48, cols_each), f32),
        ],
        scratch_shapes=[
            buf(wq.shape, low), buf(wk.shape, low), buf(wv.shape, low), buf(full.shape, low),
            dma((4,)),
            buf((length, heads_width), f32), buf((length, heads_width), f32),
            buf((length, heads_width), low), buf((length, heads_width), low),
            buf((length, heads_width), low),
            buf((length, HEAD_DIM), f32), buf((length, HEAD_DIM), f32),
            buf((2, length, HEAD_DIM), f32),
            buf((16, split_width), low), buf((16, 3 * heads_width), low),
            buf((4, groups, 64, cols_each), low), buf((2, groups, 64, cols_each), low),
            buf((groups, 64, cols_each), low), buf((groups, 64, cols_each), low),
            buf((groups, 4, 48, cols_each), f32),
            buf((8, length), f32), buf((3, 8, length), f32),
            buf((48, length), low), buf((48, length), low), buf((48, length), low),
            buf((48, length), low),
            buf((CHUNKS, part, width), low), buf((CHUNKS, part, width), low),
            buf((CHUNKS, part, width), low),
            buf((CHUNKS, 2, part, width), low), buf((CHUNKS, 2, part, width), low),
            dma((3,)), dma((3,)), dma((CHUNKS,)), dma((CHUNKS,)), dma((CHUNKS,)), dma((CHUNKS,)),
            dma((5,)), dma((5,)),
        ] + [dma((groups,))] * 8 + [dma((4,))],
        cost_estimate=pl.CostEstimate(
            flops=2 * length * heads_width * (3 * width + 5 * length),
            bytes_accessed=2 * width * (3 * heads_width + 3 * length), transcendentals=0,
        ),
        compiler_params=pltpu.CompilerParams(
            collective_id=2, has_side_effects=True, vmem_limit_bytes=67043328
        ),
        name="attention_back_to_tokens",
    )(qrot, krot, value, dmixed, qproj, kproj, scale, qgain, kgain, cos, sin, seg_col, seg_row,
      wq, wk, wv, shrink, eq, ek, ev, mids, full, hgrad, chosen, gso, geg, geu, gsd, gsgu, geo, ged)


def finish_body(split_ref, heads_ref, shared_ref, inward_ref, *outs):
    groups = split_ref.shape[0]
    tag = split_ref.shape[2] - 128
    sets = outs[0].shape[0]
    tags = [split_ref[g, :, tag : tag + 1].astype(jnp.float32) for g in range(groups)]

    def add_up(source, target, first, step=512):
        count, high, wide = target.shape
        for at in range(0, wide, step):
            end = min(wide, at + step)
            pieces = [source(g, first + at, first + end).astype(jnp.float32) for g in range(groups)]
            for c in range(count):
                total = jnp.where(tags[0] == c, pieces[0], 0.0)
                for g in range(1, groups):
                    total += jnp.where(tags[g] == c, pieces[g], 0.0)
                target[c, :, at:end] = total

    sq, eq, sk, ek, sv, ev, so, eo, sg, eg, su, eu, sd, ed = outs
    heads_width = eq.shape[2]
    units = eg.shape[2]
    for i, target in enumerate((eq, ek, ev)):
        add_up(lambda g, a, b: heads_ref[g, :, a:b], target, i * heads_width)
    at = 0
    for target in (so, eg, eu, sd):
        add_up(lambda g, a, b: split_ref[g, :, a:b], target, at)
        at += target.shape[2]
    for i, target in enumerate((sq, sk, sv)):
        add_up(lambda g, a, b: inward_ref[g, i * 16 : (i + 1) * 16, a:b], target, 0)
    for i, target in enumerate((eo, sg, su, ed)):
        add_up(lambda g, a, b: shared_ref[g, i * 16 : (i + 1) * 16, a:b], target, 0)


def finish(split, by_heads, shared, inward, sets, heads_width, units):
    cols = shared.shape[2]
    vmem = pl.BlockSpec(memory_space=pltpu.VMEM)
    widths = (
        cols, heads_width, cols, heads_width, cols, heads_width, heads_width, cols,
        cols, units, cols, units, units, cols,
    )
    return pl.pallas_call(
        finish_body,
        in_specs=[vmem] * 4,
        out_specs=[vmem] * 14,
        out_shape=[jax.ShapeDtypeStruct((sets, 16, w), jnp.float32) for w in widths],
        compiler_params=pltpu.CompilerParams(vmem_limit_bytes=48 * 2**20),
        name="sum_by_set",
    )(split, by_heads, shared, inward)


def per_device(
    tokens,
    cotangent,
    segment_ids,
    adapter_set,
    w_query,
    w_key,
    w_value,
    w_out,
    w_gate,
    w_up,
    w_down,
    query_gain,
    key_gain,
    mixer_gain,
    feed_gain,
    shrink_query,
    expand_query,
    shrink_key,
    expand_key,
    shrink_value,
    expand_value,
    shrink_out,
    expand_out,
    shrink_gate,
    expand_gate,
    shrink_up,
    expand_up,
    shrink_down,
    expand_down,
):
    chosen = adapter_set[0]

    def choose_set(adapters):
        return lax.dynamic_index_in_dim(adapters, chosen, 0, keepdims=False)

    query_shrink, query_widened = (choose_set(shrink_query), choose_set(expand_query))
    key_shrink, key_widened = (choose_set(shrink_key), choose_set(expand_key))
    value_shrink, value_widened = (choose_set(shrink_value), choose_set(expand_value))
    out_shrink, output_widened = (choose_set(shrink_out), choose_set(expand_out))
    gate_shrink, gate_widened = (choose_set(shrink_gate), choose_set(expand_gate))
    up_shrink, up_widened = (choose_set(shrink_up), choose_set(expand_up))
    down_shrink, down_widened = (choose_set(shrink_down), choose_set(expand_down))
    length = 4 * tokens.shape[0]
    rank = query_shrink.shape[0]
    half = jnp.asarray(adapter_scale_factor, jnp.bfloat16)
    blank = jnp.zeros_like(query_widened)
    shrink_rows = jnp.concatenate([query_shrink, key_shrink, value_shrink], axis=0)
    expand_query_rows = jnp.concatenate([half * query_widened, blank, blank], axis=0)
    expand_key_rows = jnp.concatenate([blank, half * key_widened, blank], axis=0)
    expand_value_rows = jnp.concatenate([blank, blank, half * value_widened], axis=0)
    cosine_table, sine_table = rotary_constants(length, HEAD_DIM)
    cosine_table, sine_table = jnp.asarray(cosine_table), jnp.asarray(sine_table)
    seg_col = segment_ids.reshape(length, 1)
    (
        mixed, query_rot, key_rot, value_low, query_proj, key_proj, scales, qkv_middle, full_tokens,
    ) = front(
        tokens, w_query, w_key, w_value, shrink_rows,
        expand_query_rows, expand_key_rows, expand_value_rows,
        query_gain[None], key_gain[None], cosine_table, sine_table, seg_col, segment_ids,
    )
    nothing = jnp.zeros_like(gate_widened)
    (
        block_output, hidden_grad, mixed_grad, grad_down_shrink, gradient_gate_widened,
        gradient_up_widened, grad_out_shrink, owner_gate_up, owner_out, owner_down,
    ) = middle(
        mixed, tokens, cotangent, w_out, w_gate, w_up, w_down,
        mixer_gain.astype(jnp.float32)[None], feed_gain.astype(jnp.float32)[None],
        out_shrink, half * output_widened, jnp.concatenate([gate_shrink, up_shrink], axis=0),
        jnp.concatenate([half * gate_widened, nothing], axis=0),
        jnp.concatenate([nothing, half * up_widened], axis=0),
        down_shrink, half * down_widened,
    )
    token_grads, split, by_heads, shared, inward = back(
        query_rot, key_rot, value_low, mixed_grad.reshape(mixed.shape), query_proj, key_proj, scales,
        query_gain[None], key_gain[None], cosine_table, sine_table, seg_col, segment_ids,
        w_query, w_key, w_value, shrink_rows, expand_query_rows, expand_key_rows, expand_value_rows,
        qkv_middle, full_tokens.reshape(length, -1), hidden_grad,
        jnp.broadcast_to(chosen.astype(jnp.float32), (1, 128)),
        grad_out_shrink, gradient_gate_widened, gradient_up_widened, grad_down_shrink,
        owner_gate_up, owner_out, owner_down,
    )
    adapter_grads = finish(
        split, by_heads, shared, inward, shrink_query.shape[0], w_query.shape[1], w_gate.shape[1]
    )
    return (block_output, token_grads, *adapter_grads)


def solution(mesh):
    in_specs = (
        P(("dp", "tensor"), None),
        P(("dp", "tensor"), None),
        P("dp", None),
        P("dp"),
        P(None, "tensor"),
        P(None, "tensor"),
        P(None, "tensor"),
        P("tensor", None),
        P(None, "tensor"),
        P(None, "tensor"),
        P("tensor", None),
        P("tensor"),
        P("tensor"),
        P(),
        P(),
        P(),
        P(None, None, "tensor"),
        P(),
        P(None, None, "tensor"),
        P(),
        P(None, None, "tensor"),
        P(None, None, "tensor"),
        P(),
        P(),
        P(None, None, "tensor"),
        P(),
        P(None, None, "tensor"),
        P(None, None, "tensor"),
        P(),
    )
    out_specs = (
        P(("dp", "tensor"), None),
        P(("dp", "tensor"), None),
        P(None, None, ("dp", "tensor")),
        P(None, None, "tensor"),
        P(None, None, ("dp", "tensor")),
        P(None, None, "tensor"),
        P(None, None, ("dp", "tensor")),
        P(None, None, "tensor"),
        P(None, None, "tensor"),
        P(None, None, ("dp", "tensor")),
        P(None, None, ("dp", "tensor")),
        P(None, None, "tensor"),
        P(None, None, ("dp", "tensor")),
        P(None, None, "tensor"),
        P(None, None, "tensor"),
        P(None, None, ("dp", "tensor")),
    )
    return jax.shard_map(
        per_device, mesh=mesh, in_specs=in_specs, out_specs=out_specs, check_vma=False
    )
```

```python
import functools
import jax
import jax.numpy as jnp
import numpy as np
from jax import lax
from jax.experimental import pallas as pl
from jax.experimental.pallas import tpu as pltpu
from jax.sharding import PartitionSpec as P

HEAD_DIM = 128
DOC_MOST = 512
ATT_ROWS = 256
rotary_base = 500000.0
NEG = -1e30
LOG2E = 1.4426950408889634


def rotary_constants(length, head_dim):
    half = head_dim // 2
    frequency = np.float32(rotary_base) ** (
        -(np.arange(half, dtype=np.float32) * np.float32(2.0) / np.float32(head_dim))
    )
    angles = np.arange(length, dtype=np.float32)[:, None] * frequency.astype(np.float32)[None, :]
    cosine = np.cos(angles.astype(np.float64)).astype(np.float32)
    sine = np.sin(angles.astype(np.float64)).astype(np.float32)
    return (
        np.concatenate([cosine, cosine], axis=1),
        np.concatenate([-sine, sine], axis=1),
    )


def key_window(block, rows):
    first = max(0, (block * rows - (DOC_MOST - 1)) // rows) * rows
    return first, (block + 1) * rows


epsilon = 1e-06
adapter_scale_factor = 0.5


def pick_body(
    set_ref, seg_ref, qgain, kgain, mgain, fgain,
    sq, eq, sk, ek, sv, ev, so, eo, sg, eg, su, eu, sd, ed,
    shrink_out, eq_out, ek_out, ev_out, so_out, eo_out, sgu_out, eg_out, eu_out, sd_out, ed_out,
    qgain_out, kgain_out, mgain_out, fgain_out, start_col, start_row, set_out,
):
    rank = sq.shape[1]

    def scaled(ref):
        return (adapter_scale_factor * ref[0].astype(jnp.float32)).astype(jnp.bfloat16)

    for i, ref in enumerate((sq, sk, sv)):
        shrink_out[i * rank : (i + 1) * rank, :] = ref[0]
    for i, (ref, target) in enumerate(((eq, eq_out), (ek, ek_out), (ev, ev_out))):
        target[...] = jnp.zeros_like(target)
        target[i * rank : (i + 1) * rank, :] = scaled(ref)
    for i, (ref, target) in enumerate(((eg, eg_out), (eu, eu_out))):
        target[...] = jnp.zeros_like(target)
        target[i * rank : (i + 1) * rank, :] = scaled(ref)
    so_out[...] = so[0]
    sd_out[...] = sd[0]
    eo_out[...] = scaled(eo)
    ed_out[...] = scaled(ed)
    sgu_out[:rank, :] = sg[0]
    sgu_out[rank:, :] = su[0]
    for ref, target in ((qgain, qgain_out), (kgain, kgain_out), (mgain, mgain_out), (fgain, fgain_out)):
        target[...] = ref[...].astype(jnp.float32).reshape(target.shape)
    length = seg_ref.shape[1]
    row = seg_ref[...].astype(jnp.float32)
    col = jnp.transpose(jnp.broadcast_to(row, (HEAD_DIM, length)))[:, :1]
    start_col[...] = jnp.sum(
        jnp.where(row < col, 1.0, 0.0), axis=1, keepdims=True
    ).astype(jnp.int32)
    start_row[...] = jnp.sum(
        jnp.where(col < row, 1.0, 0.0), axis=0, keepdims=True
    ).astype(jnp.int32)
    set_out[...] = jnp.full(set_out.shape, set_ref[0], jnp.int32).astype(jnp.float32)


def pick(adapter_set, segment_ids, gains, adapters):
    whole = lambda a: pl.BlockSpec(a.shape, lambda i, s: (0,) * a.ndim)
    chosen = lambda a: pl.BlockSpec((1,) + a.shape[1:], lambda i, s: (s[0], 0, 0))
    length = segment_ids.shape[1]
    rank, width = adapters[0].shape[1:]
    here, units = adapters[1].shape[2], adapters[9].shape[2]
    low, f32 = jnp.bfloat16, jnp.float32
    shapes = [
        ((3 * rank, width), low), ((3 * rank, here), low), ((3 * rank, here), low),
        ((3 * rank, here), low), ((rank, here), low), ((rank, width), low), ((2 * rank, width), low),
        ((2 * rank, units), low), ((2 * rank, units), low), ((rank, units), low), ((rank, width), low),
        ((1, here), f32), ((1, here), f32), ((1, width), f32), ((1, width), f32),
        ((length, 1), jnp.int32), ((1, length), jnp.int32), ((1, 128), f32),
    ]
    return pl.pallas_call(
        pick_body,
        grid_spec=pltpu.PrefetchScalarGridSpec(
            num_scalar_prefetch=1,
            grid=(1,),
            in_specs=[whole(segment_ids)] + [whole(g) for g in gains] + [chosen(a) for a in adapters],
            out_specs=[pl.BlockSpec(s, lambda i, _: (0,) * 2) for s, _ in shapes],
        ),
        out_shape=[jax.ShapeDtypeStruct(s, t) for s, t in shapes],
        compiler_params=pltpu.CompilerParams(vmem_limit_bytes=32 * 2**20),
        name="pick_adapters",
    )(adapter_set, segment_ids, *gains, *adapters)


CHUNKS = 4
TILE = 1024
EXTRA = 128
NT = (((1,), (1,)), ((), ()))
TN = (((0,), (0,)), ((), ()))
MESH_ID = pl.DeviceIdType.MESH
MIDDLE_ORDER = (
    ("S2", 4), ("P4", 8), ("S4", 7), ("P0", 1), ("S1", 2), ("S6", 10), ("F3", 6),
    ("F5", 9), ("S5", 8), ("P2", 4), ("S0", 0), ("F1", 3), ("S3", 5),
)


def mm(left, right):
    return jnp.dot(left, right, preferred_element_type=jnp.float32)


def mm_nt(left, right):
    return lax.dot_general(left, right, NT, preferred_element_type=jnp.float32)


def mm_tn(left, right):
    return lax.dot_general(left, right, TN, preferred_element_type=jnp.float32)


def partners():
    me = lax.axis_index("tensor")
    group = lax.axis_index("dp")
    beside = me + 1 - 2 * lax.rem(me, 2)
    across = lax.rem(me + 2, 4)
    return me, group, beside, across


def greet(group, beside, across):
    barrier = pltpu.get_barrier_semaphore()
    for other in (beside, across):
        pl.semaphore_signal(barrier, inc=1, device_id=(group, other), device_id_type=MESH_ID)
    pl.semaphore_wait(barrier, 2)


def middle_body(
    mixed_ref, tokens_ref, cot_ref, w_out_hbm, w_gate_hbm, w_up_hbm, w_down_hbm,
    mgain_ref, fgain_ref, so_ref, eo_ref, sgu_ref, eg_ref, eu_ref, sd_ref, ed_ref,
    out_ref, hgrad_ref, dmixed_ref, gsd_ref, geg_ref, geu_ref, gso_ref, gsgu_ref, geo_ref, ged_ref,
    w_out, w_gate, w_up, w_down, wsem,
    rows_buf, own_buf, xsend, xrecv, bsend, brecv,
    gate_buf, up_buf, temp_a, temp_b, mgu_buf, mixer_buf, hidden_buf, mout_buf,
    xs_sem, xr_sem, bs_sem, br_sem, gxs_sem, gxr_sem, gbs_sem, gbr_sem, fs_sem, fr_sem,
):
    me, group, beside, across = partners()
    chunks, part, width = rows_buf.shape[0], rows_buf.shape[2], rows_buf.shape[3]
    units = w_gate.shape[1]
    heads_width = w_out.shape[0]
    far = lax.rem(beside + 2, 4)
    order = (me, across, beside, far)
    loads = [
        pltpu.make_async_copy(source, target, wsem.at[i])
        for i, (source, target) in enumerate(
            ((w_out_hbm, w_out), (w_gate_hbm, w_gate), (w_up_hbm, w_up), (w_down_hbm, w_down))
        )
    ]
    for load in loads:
        load.start()
    for ref in (gsd_ref, geg_ref, geu_ref, gso_ref, gsgu_ref, geo_ref, ged_ref):
        ref[...] = jnp.zeros_like(ref)
    greet(group, beside, across)

    def remote(source, target, ssem, rsem, other):
        return pltpu.make_async_remote_copy(
            src_ref=source, dst_ref=target, send_sem=ssem, recv_sem=rsem,
            device_id=(group, other), device_id_type=MESH_ID,
        )

    def gather_across(c):
        return remote(rows_buf.at[c, 0], rows_buf.at[c, 1], gxs_sem.at[c], gxr_sem.at[c], across)

    def gather_beside(c):
        return remote(rows_buf.at[c, 0], rows_buf.at[c, 2], gbs_sem.at[c], gbr_sem.at[c], beside)

    def gather_forward(c):
        return remote(rows_buf.at[c, 1], rows_buf.at[c, 3], fs_sem.at[c], fr_sem.at[c], beside)

    def reduce_beside(c):
        return remote(bsend.at[c], brecv.at[c], bs_sem.at[c], br_sem.at[c], beside)

    def reduce_across(c):
        return remote(xsend.at[c], xrecv.at[c], xs_sem.at[c], xr_sem.at[c], across)

    def store_partial(c, columns, value):
        low = value.astype(jnp.bfloat16)
        own_buf[c, :, columns] = low[:part]
        xsend[c, :, columns] = low[part : 2 * part]
        bsend[c, 0, :, columns] = low[2 * part : 3 * part]
        bsend[c, 1, :, columns] = low[3 * part :]

    def gathered(c):
        return rows_buf[c].reshape(4 * part, width)

    def forward_stage(c):
        gather_across(c).wait_recv()
        gather_forward(c).start()

    def pair_stage(c):
        reduce_beside(c).wait_recv()
        own_buf[c] = (
            own_buf[c].astype(jnp.float32) + brecv[c, 0].astype(jnp.float32)
        ).astype(jnp.bfloat16)
        xsend[c] = (
            xsend[c].astype(jnp.float32) + brecv[c, 1].astype(jnp.float32)
        ).astype(jnp.bfloat16)
        reduce_across(c).start()

    def totals(c):
        reduce_across(c).wait_recv()
        main = own_buf[c, :, :width].astype(jnp.float32) + xrecv[c, :, :width].astype(jnp.float32)
        side = own_buf[c, :, width : width + 32].astype(jnp.float32) + xrecv[
            c, :, width : width + 32
        ].astype(jnp.float32)
        return main, side.astype(jnp.bfloat16)

    def own_rows(c):
        return pl.ds(pl.multiple_of(c * part, part), part)

    def send_rows(c, value, again):
        if again:
            gather_across(c).wait_send()
            gather_beside(c).wait_send()
        rows_buf[c, 0] = value
        gather_across(c).start()
        gather_beside(c).start()

    def chunk_rows(c):
        return pl.ds(pl.multiple_of(c * 4 * part, 4 * part), 4 * part)

    def tiles(total, tile, body):
        def step(j, carry):
            body(pl.ds(pl.multiple_of(j * tile, tile), tile))
            return carry

        lax.fori_loop(0, total // tile, step, 0)

    def mixed_chunk(c):
        return jnp.concatenate([mixed_ref[o, c] for o in order], axis=0)

    def stage_mixer(c):
        @pl.when(c == 0)
        def _():
            loads[0].wait()

        rows = mixed_chunk(c)
        store_partial(c, slice(width, width + 16), mm_nt(rows, so_ref[...]))
        tiles(width, TILE, lambda cols: store_partial(c, cols, mm(rows, w_out[:, cols])))
        reduce_beside(c).start()

    def stage_hidden(c):
        main, side = totals(c)
        mid = side[:, :16]
        mout_buf[c] = mid
        mixer = main + mm(mid, eo_ref[...])
        mixer_buf[own_rows(c), :] = mixer
        factor = lax.rsqrt(jnp.mean(mixer * mixer, axis=1, keepdims=True) + epsilon)
        hidden = tokens_ref[own_rows(c), :].astype(jnp.float32) + mixer * factor * mgain_ref[...]
        hidden_buf[own_rows(c), :] = hidden
        send_rows(c, hidden.astype(jnp.bfloat16), False)

    def arrive(c):
        gather_beside(c).wait_recv()
        gather_forward(c).wait_recv()

    def stage_units(c):
        @pl.when(c == 0)
        def _():
            for load in loads[1:]:
                load.wait()

        arrive(c)
        mids = mm_nt(gathered(c), sgu_ref[...]).astype(jnp.bfloat16)
        mgu_buf[c] = mids

        def unit_tile(cols):
            rows = gathered(c)
            gate = mm(rows, w_gate[:, cols]) + mm(mids, eg_ref[:, cols])
            up = mm(rows, w_up[:, cols]) + mm(mids, eu_ref[:, cols])
            gate_buf[chunk_rows(c), cols] = gate.astype(jnp.bfloat16)
            up_buf[chunk_rows(c), cols] = up.astype(jnp.bfloat16)
            sig = 1.0 / (1.0 + jnp.exp(-gate))
            temp_a[:, cols] = (gate * sig * up).astype(jnp.bfloat16)

        tiles(units, TILE // 2, unit_tile)
        gather_forward(c).wait_send()
        reduce_beside(c).wait_send()
        reduce_across(c).wait_send()
        inner = temp_a[...]
        store_partial(c, slice(width, width + 16), mm_nt(inner, sd_ref[...]))
        tiles(width, TILE, lambda cols: store_partial(c, cols, mm(temp_a[...], w_down[:, cols])))
        reduce_beside(c).start()

    def norm_back_rows(values, gains, grads):
        factor = lax.rsqrt(jnp.mean(values * values, axis=1, keepdims=True) + epsilon)
        weighted = grads * gains
        return factor * weighted - values * (
            factor * factor * factor * jnp.mean(values * weighted, axis=1, keepdims=True)
        )

    def stage_feed(c):
        main, side = totals(c)
        mid = side[:, :16]
        feed = main + mm(mid, ed_ref[...])
        factor = lax.rsqrt(jnp.mean(feed * feed, axis=1, keepdims=True) + epsilon)
        gains = fgain_ref[...]
        out_ref[own_rows(c), :] = (hidden_buf[own_rows(c), :] + feed * factor * gains).astype(
            jnp.bfloat16
        )
        grad = norm_back_rows(feed, gains, cot_ref[own_rows(c), :].astype(jnp.float32))
        grad = grad.astype(jnp.bfloat16)
        send_rows(c, grad, True)
        ged_ref[...] += mm_tn(mid, grad)

    def stage_units_back(c):
        arrive(c)
        dmid = mm_nt(gathered(c), ed_ref[...]).astype(jnp.bfloat16)
        mids = mgu_buf[c]

        def unit_tile(cols):
            rows = gathered(c)
            inner_grad = mm_nt(rows, w_down[cols, :]) + mm(dmid, sd_ref[:, cols])
            gate = gate_buf[chunk_rows(c), cols].astype(jnp.float32)
            up = up_buf[chunk_rows(c), cols].astype(jnp.float32)
            sig = 1.0 / (1.0 + jnp.exp(-gate))
            silu = gate * sig
            gate_grad = (inner_grad * up * (sig + silu * (1.0 - sig))).astype(jnp.bfloat16)
            up_grad = (inner_grad * silu).astype(jnp.bfloat16)
            temp_a[:, cols] = gate_grad
            temp_b[:, cols] = up_grad
            gsd_ref[:, cols] += mm_tn(dmid, (silu * up).astype(jnp.bfloat16))
            geg_ref[:, cols] += mm_tn(mids, gate_grad)
            geu_ref[:, cols] += mm_tn(mids, up_grad)

        tiles(units, TILE // 2, unit_tile)
        gather_forward(c).wait_send()
        reduce_beside(c).wait_send()
        reduce_across(c).wait_send()
        store_partial(
            c,
            slice(width, width + 32),
            mm_nt(temp_a[...], eg_ref[...]) + mm_nt(temp_b[...], eu_ref[...]),
        )

        def width_tile(cols):
            store_partial(
                c, cols, mm_nt(temp_a[...], w_gate[cols, :]) + mm_nt(temp_b[...], w_up[cols, :])
            )

        tiles(width, TILE // 2, width_tile)
        reduce_beside(c).start()

    def stage_mixer_grad(c):
        main, side = totals(c)
        grads = cot_ref[own_rows(c), :].astype(jnp.float32) + main + mm(side, sgu_ref[...])
        hgrad_ref[own_rows(c), :] = grads
        mixer_grad = norm_back_rows(mixer_buf[own_rows(c), :], mgain_ref[...], grads)
        mixer_grad = mixer_grad.astype(jnp.bfloat16)
        send_rows(c, mixer_grad, True)
        geo_ref[...] += mm_tn(mout_buf[c], mixer_grad)
        gsgu_ref[...] += mm_tn(side, hidden_buf[own_rows(c), :].astype(jnp.bfloat16))

    def stage_mixed_grad(c):
        arrive(c)
        dmid = mm_nt(gathered(c), eo_ref[...]).astype(jnp.bfloat16)
        grad = (mm_nt(gathered(c), w_out[...]) + mm(dmid, so_ref[...])).astype(jnp.bfloat16)
        for i, o in enumerate(order):
            dmixed_ref[o, c] = grad[i * part : (i + 1) * part]
        gso_ref[...] += mm_tn(dmid, mixed_chunk(c))
        gather_forward(c).wait_send()
        gather_across(c).wait_send()
        gather_beside(c).wait_send()
        reduce_beside(c).wait_send()
        reduce_across(c).wait_send()

    stages = {
        "S0": stage_mixer, "S1": stage_hidden, "S2": stage_units, "S3": stage_feed,
        "S4": stage_units_back, "S5": stage_mixer_grad, "S6": stage_mixed_grad,
        "P0": pair_stage, "P2": pair_stage, "P4": pair_stage,
        "F1": forward_stage, "F3": forward_stage, "F5": forward_stage,
    }

    def step(i, carry):
        for name, delay in MIDDLE_ORDER:

            @pl.when((i >= delay) & (i < delay + chunks))
            def _():
                stages[name](i - delay)

        return carry

    lax.fori_loop(0, chunks + max(delay for _, delay in MIDDLE_ORDER), step, 0)


def middle(mixed, tokens, cot, w_out, w_gate, w_up, w_down, mgain, fgain, so, eo, sgu, eg, eu, sd, ed):
    rows, width = tokens.shape
    heads_width, units = w_out.shape[0], w_gate.shape[1]
    part = rows // CHUNKS
    whole_width = width + EXTRA
    vmem = pl.BlockSpec(memory_space=pltpu.VMEM)
    hbm = pl.BlockSpec(memory_space=pl.ANY)
    low, full = jnp.bfloat16, jnp.float32
    dma = pltpu.SemaphoreType.DMA((CHUNKS,))
    shape = jax.ShapeDtypeStruct
    flops = 2 * 4 * rows * width * (2 * heads_width + 6 * units)
    return pl.pallas_call(
        middle_body,
        in_specs=[vmem] * 3 + [hbm] * 4 + [vmem] * 9,
        out_specs=[vmem] * 10,
        out_shape=[
            shape((rows, width), low), shape((rows, width), full),
            shape((4, CHUNKS, part, heads_width), low),
            shape((16, units), full), shape((32, units), full), shape((32, units), full),
            shape((16, heads_width), full), shape((32, width), full), shape((16, width), full),
            shape((16, width), full),
        ],
        scratch_shapes=[
            pltpu.VMEM(w_out.shape, low), pltpu.VMEM(w_gate.shape, low),
            pltpu.VMEM(w_up.shape, low), pltpu.VMEM(w_down.shape, low),
            pltpu.SemaphoreType.DMA((4,)),
            pltpu.VMEM((CHUNKS, 4, part, width), low),
            pltpu.VMEM((CHUNKS, part, whole_width), low),
            pltpu.VMEM((CHUNKS, part, whole_width), low),
            pltpu.VMEM((CHUNKS, part, whole_width), low),
            pltpu.VMEM((CHUNKS, 2, part, whole_width), low),
            pltpu.VMEM((CHUNKS, 2, part, whole_width), low),
            pltpu.VMEM((4 * rows, units), low), pltpu.VMEM((4 * rows, units), low),
            pltpu.VMEM((4 * part, units), low), pltpu.VMEM((4 * part, units), low),
            pltpu.VMEM((CHUNKS, 4 * part, 32), low),
            pltpu.VMEM((rows, width), full), pltpu.VMEM((rows, width), full),
            pltpu.VMEM((CHUNKS, part, 16), low),
        ] + [dma] * 10,
        cost_estimate=pl.CostEstimate(
            flops=flops, bytes_accessed=2 * width * (heads_width + 3 * units), transcendentals=0
        ),
        compiler_params=pltpu.CompilerParams(
            collective_id=0, has_side_effects=True, vmem_limit_bytes=67043328
        ),
        name="mixer_to_feed",
    )(mixed.reshape(4, CHUNKS, part, heads_width), tokens, cot, w_out, w_gate, w_up, w_down,
      mgain, fgain, so, eo, sgu, eg, eu, sd, ed)


def attention_scores(first, second, start, first_query, first_key, query_axis):
    scores = lax.dot_general(first, second, NT, preferred_element_type=jnp.float32)
    kpos = lax.broadcasted_iota(jnp.int32, scores.shape, 1 - query_axis) + first_key
    shape = [1, 1]
    shape[query_axis] = scores.shape[query_axis]
    qpos = lax.broadcasted_iota(jnp.int32, shape, query_axis) + first_query
    return jnp.where((kpos <= qpos) & (kpos >= start), scores, NEG)


def front_body(
    tokens_ref, wq_hbm, wk_hbm, wv_hbm, shrink_ref, eq_ref, ek_ref, ev_ref, qgain_ref, kgain_ref,
    cos_ref, sin_ref, start_ref,
    mixed_ref, qrot_ref, krot_ref, value_ref, qproj_ref, kproj_ref, scale_ref, mids_ref, full_hbm,
    wq, wk, wv, wsem, full, lhs, squares, ex_send, ex_recv,
    xs_sem, xr_sem, fs_sem, fr_sem, bs_sem, br_sem, es_sem, er_sem, out_sem,
):
    me, group, beside, across = partners()
    far = lax.rem(beside + 2, 4)
    chunks, part, width = full.shape[1:]
    rows = chunks * part
    length = 4 * rows
    loads = [
        pltpu.make_async_copy(source, target, wsem.at[i])
        for i, (source, target) in enumerate(((wq_hbm, wq), (wk_hbm, wk), (wv_hbm, wv)))
    ]
    for load in loads:
        load.start()
    barrier = pltpu.get_barrier_semaphore()
    for other in (beside, across, far):
        pl.semaphore_signal(barrier, inc=1, device_id=(group, other), device_id_type=MESH_ID)
    pl.semaphore_wait(barrier, 3)

    def remote(source, target, ssem, rsem, other):
        return pltpu.make_async_remote_copy(
            src_ref=source, dst_ref=target, send_sem=ssem, recv_sem=rsem,
            device_id=(group, other), device_id_type=MESH_ID,
        )

    def send_across(c):
        return remote(tokens_ref.at[c], full.at[me, c], xs_sem.at[c], xr_sem.at[c], across)

    def forward(c):
        return remote(full.at[across, c], full.at[across, c], fs_sem.at[c], fr_sem.at[c], beside)

    to_beside = remote(tokens_ref, full.at[me], bs_sem, br_sem, beside)
    for c in range(chunks):
        send_across(c).start()
    to_beside.start()
    full[me] = tokens_ref[...]
    for load in loads:
        load.wait()
    pairs = chunks // 2
    half = rows // 2

    def block_step(b, carry):
        @pl.when(b == 0)
        def _():
            lhs[...] = tokens_ref[...].reshape(rows, width)

        @pl.when(b == 1)
        def _():
            to_beside.wait_recv()
            lhs[...] = full[beside].reshape(rows, width)

        @pl.when(b >= 2)
        def _():
            base = (b - 2) * pairs
            for j in range(pairs):
                send_across(base + j).wait_recv()
                forward(base + j).start()
            for j in range(pairs):
                lhs[j * part : (j + 1) * part] = full[across, base + j]
            for j in range(pairs):
                forward(base + j).wait_recv()
                lhs[half + j * part : half + (j + 1) * part] = full[far, base + j]

        mids = mm_nt(lhs[...], shrink_ref[...]).astype(jnp.bfloat16)
        query = mm(lhs[...], wq[...]) + mm(mids, eq_ref[...])
        key = mm(lhs[...], wk[...]) + mm(mids, ek_ref[...])
        value = (mm(lhs[...], wv[...]) + mm(mids, ev_ref[...])).astype(jnp.bfloat16)
        qsum = jnp.sum(query * query, axis=1, keepdims=True)
        ksum = jnp.sum(key * key, axis=1, keepdims=True)
        lane = lax.broadcasted_iota(jnp.int32, (rows, HEAD_DIM), 1)
        both = jnp.where(lane < 4, qsum, ksum)
        first = jnp.where(b == 0, me, jnp.where(b == 1, beside, across)) * rows
        second = jnp.where(b == 0, me, jnp.where(b == 1, beside, far)) * rows
        first = first + jnp.where(b >= 2, (b - 2) * half, 0)
        second = second + jnp.where(b >= 2, (b - 2) * half, half)
        for start, piece in ((first, slice(0, half)), (second, slice(half, rows))):
            there = pl.ds(pl.multiple_of(start, half), half)
            qproj_ref[there, :] = query[piece]
            kproj_ref[there, :] = key[piece]
            value_ref[there, :] = value[piece]
            mids_ref[there, :] = mids[piece]
            squares[there, :] = both[piece]
        return carry

    lax.fori_loop(0, 4, block_step, 0)
    save = pltpu.make_async_copy(full, full_hbm, out_sem)
    save.start()
    ex_send[...] = jnp.transpose(squares[...])[:8]
    swaps = [
        remote(ex_send, ex_recv.at[i], es_sem.at[i], er_sem.at[i], other)
        for i, other in enumerate((beside, across, far))
    ]
    for swap in swaps:
        swap.start()
    for swap in swaps:
        swap.wait_recv()
    total = ex_send[...] + ex_recv[0] + ex_recv[1] + ex_recv[2]
    factor = lax.rsqrt(total / (4 * wq.shape[1]) + epsilon)
    wide = jnp.concatenate(
        [
            jnp.broadcast_to(factor[:1], (HEAD_DIM // 2, length)),
            jnp.broadcast_to(factor[4:5], (HEAD_DIM // 2, length)),
        ],
        axis=0,
    )
    scale_ref[...] = jnp.transpose(wide)
    heads = wq.shape[1] // HEAD_DIM
    exponent = HEAD_DIM ** (-0.5) * LOG2E
    block_rows = min(ATT_ROWS, length)

    def head_step(h, carry):
        cols = pl.ds(pl.multiple_of(h * HEAD_DIM, HEAD_DIM), HEAD_DIM)
        for source, lane, gain, target in (
            (qproj_ref, 0, qgain_ref, qrot_ref),
            (kproj_ref, HEAD_DIM // 2, kgain_ref, krot_ref),
        ):
            normed = source[:, cols] * scale_ref[:, lane : lane + 1] * gain[:, cols]
            turned = normed * cos_ref[...] + pltpu.roll(normed, HEAD_DIM // 2, 1) * sin_ref[...]
            target[:, cols] = turned.astype(jnp.bfloat16)
        for block in range(length // block_rows):
            low, high = key_window(block, block_rows)
            here = pl.ds(block * block_rows, block_rows)
            keys = pl.ds(low, high - low)
            scores = attention_scores(
                qrot_ref[here, cols], krot_ref[keys, cols], start_ref[here, :],
                block * block_rows, low, 0,
            )
            top = jnp.max(scores, axis=1, keepdims=True)
            weights = jnp.exp2((scores - top) * exponent)
            total = jnp.sum(weights, axis=1, keepdims=True)
            mix = mm(weights.astype(jnp.bfloat16), value_ref[keys, cols])
            mixed_ref[here, cols] = (mix * (1.0 / total)).astype(jnp.bfloat16)
        return carry

    lax.fori_loop(0, heads, head_step, 0)
    for c in range(chunks):
        send_across(c).wait_send()
        forward(c).wait_send()
    to_beside.wait_send()
    for swap in swaps:
        swap.wait_send()
    save.wait()


def front(tokens, wq, wk, wv, shrink, eq, ek, ev, qgain, kgain, cos, sin, start_col):
    rows, width = tokens.shape
    heads_width = wq.shape[1]
    length = 4 * rows
    part = rows // CHUNKS
    vmem = pl.BlockSpec(memory_space=pltpu.VMEM)
    hbm = pl.BlockSpec(memory_space=pl.ANY)
    low, full = jnp.bfloat16, jnp.float32
    shape = jax.ShapeDtypeStruct
    dma = pltpu.SemaphoreType.DMA
    return pl.pallas_call(
        front_body,
        in_specs=[vmem] + [hbm] * 3 + [vmem] * 9,
        out_specs=[vmem] * 8 + [hbm],
        out_shape=[
            shape((length, heads_width), low), shape((length, heads_width), low),
            shape((length, heads_width), low), shape((length, heads_width), low),
            shape((length, heads_width), full), shape((length, heads_width), full),
            shape((length, HEAD_DIM), full), shape((length, shrink.shape[0]), low),
            shape((4, CHUNKS, part, width), low),
        ],
        scratch_shapes=[
            pltpu.VMEM(wq.shape, low), pltpu.VMEM(wk.shape, low), pltpu.VMEM(wv.shape, low),
            dma((3,)),
            pltpu.VMEM((4, CHUNKS, part, width), low), pltpu.VMEM((rows, width), low),
            pltpu.VMEM((length, HEAD_DIM), full), pltpu.VMEM((8, length), full),
            pltpu.VMEM((3, 8, length), full),
            dma((CHUNKS,)), dma((CHUNKS,)), dma((CHUNKS,)), dma((CHUNKS,)), dma, dma,
            dma((3,)), dma((3,)), dma,
        ],
        cost_estimate=pl.CostEstimate(
            flops=2 * length * heads_width * (3 * width + 2 * length),
            bytes_accessed=2 * width * (3 * heads_width + length), transcendentals=0,
        ),
        compiler_params=pltpu.CompilerParams(
            collective_id=1, has_side_effects=True, vmem_limit_bytes=67043328
        ),
        name="gather_project_attend",
    )(tokens.reshape(CHUNKS, part, width), wq, wk, wv, shrink, eq, ek, ev, qgain, kgain,
      cos, sin, start_col)


def back_body(
    qrot_ref, krot_ref, value_ref, dmixed_ref, qproj_ref, kproj_ref, scale_ref, qgain_ref, kgain_ref,
    cos_ref, sin_ref, start_ref, wq_hbm, wk_hbm, wv_hbm, shrink_ref,
    eq_ref, ek_ref, ev_ref, mids_ref, full_hbm, hgrad_ref, set_ref,
    gso_ref, geg_ref, geu_ref, gsd_ref, gsgu_ref, geo_ref, ged_ref,
    tgrad_ref, split_hbm, heads_hbm, shared_hbm, inward_hbm,
    wq, wk, wv, full, wsem, dq_buf, dk_buf, dq_low, dk_low, dv_low, dk_acc, dv_acc, sums_buf,
    split_send, heads_send, blocks, blocks_recv, blocks_xrecv, shared_send, inward_send,
    ex_send, ex_recv, dmid_send, dmid_recv, dmid_xsend, dmid_xrecv,
    own_buf, xsend, xrecv, bsend, brecv,
    es_sem, er_sem, xs_sem, xr_sem, bs_sem, br_sem, one_s, one_r,
    sp_s, sp_r, hd_s, hd_r, sh_s, sh_r, in_s, in_r, local_sem,
):
    me, group, beside, across = partners()
    far = lax.rem(beside + 2, 4)
    order = (me, across, beside, far)
    groups = split_hbm.shape[0]
    chunks, part, width = own_buf.shape
    rows = chunks * part
    length = 4 * rows
    heads_width = wq.shape[1]
    units = geg_ref.shape[1]
    cols_each = blocks.shape[3]
    loads = [
        pltpu.make_async_copy(source, target, wsem.at[i])
        for i, (source, target) in enumerate(
            ((wq_hbm, wq), (wk_hbm, wk), (wv_hbm, wv), (full_hbm, full))
        )
    ]
    for load in loads:
        load.start()
    barrier = pltpu.get_barrier_semaphore()
    for other in (beside, across, far):
        pl.semaphore_signal(barrier, inc=1, device_id=(group, other), device_id_type=MESH_ID)

    def greet_group(j, carry):
        other = lax.rem(group + j, groups)
        pl.semaphore_signal(barrier, inc=1, device_id=(other, me), device_id_type=MESH_ID)
        return carry

    lax.fori_loop(1, groups, greet_group, 0)
    pl.semaphore_wait(barrier, groups + 2)

    def remote(source, target, ssem, rsem, other):
        return pltpu.make_async_remote_copy(
            src_ref=source, dst_ref=target, send_sem=ssem, recv_sem=rsem,
            device_id=(group, other), device_id_type=MESH_ID,
        )

    def to_group(source, target, ssem, rsem, j):
        other = lax.rem(group + j, groups)
        return pltpu.make_async_remote_copy(
            src_ref=source(other), dst_ref=target.at[group], send_sem=ssem.at[j],
            recv_sem=rsem.at[group], device_id=(other, me), device_id_type=MESH_ID,
        )

    def from_group(source, target, ssem, rsem, j):
        sender = lax.rem(group + j, groups)
        return pltpu.make_async_remote_copy(
            src_ref=source(sender), dst_ref=target.at[sender], send_sem=ssem.at[j],
            recv_sem=rsem.at[sender], device_id=(sender, me), device_id_type=MESH_ID,
        )

    split = (lambda other: split_send, split_hbm, sp_s, sp_r)
    by_heads = (lambda other: heads_send, heads_hbm, hd_s, hd_r)
    shared = (lambda other: shared_send.at[other], shared_hbm, sh_s, sh_r)
    inward = (lambda other: inward_send.at[other, me], inward_hbm, in_s, in_r)
    exchanges = (split, by_heads, shared, inward)

    def start_exchange(number):
        exchange = exchanges[number]

        def one(j, carry):
            to_group(*exchange, j).start()
            return carry

        lax.fori_loop(1, groups, one, 0)
        pltpu.make_async_copy(
            exchange[0](group), exchange[1].at[group], local_sem.at[number]
        ).start()

    def end_exchange(number):
        exchange = exchanges[number]

        def one(j, carry):
            to_group(*exchange, j).wait_send()
            from_group(*exchange, j).wait_recv()
            return carry

        lax.fori_loop(1, groups, one, 0)
        pltpu.make_async_copy(
            exchange[0](group), exchange[1].at[group], local_sem.at[number]
        ).wait()

    low = jnp.bfloat16
    split_send[:, :heads_width] = gso_ref[...].astype(low)
    split_send[:, heads_width : heads_width + units] = (
        adapter_scale_factor * geg_ref[:16]
    ).astype(low)
    split_send[:, heads_width + units : heads_width + 2 * units] = (
        adapter_scale_factor * geu_ref[16:]
    ).astype(low)
    split_send[:, heads_width + 2 * units : heads_width + 3 * units] = gsd_ref[...].astype(low)
    split_send[:, heads_width + 3 * units :] = jnp.broadcast_to(set_ref[...], (16, 128)).astype(low)
    start_exchange(0)
    for t in range(4):
        for g in range(groups):
            at = slice((g * 4 + t) * cols_each, (g * 4 + t + 1) * cols_each)
            blocks[t, g, :16] = (adapter_scale_factor * geo_ref[:, at]).astype(low)
            blocks[t, g, 16:48] = gsgu_ref[:, at].astype(low)
            blocks[t, g, 48:] = (adapter_scale_factor * ged_ref[:, at]).astype(low)
    block_near = remote(blocks.at[beside], blocks_recv.at[0], one_s.at[0], one_r.at[0], beside)
    block_far = remote(blocks.at[far], blocks_recv.at[1], one_s.at[1], one_r.at[1], beside)
    block_across = remote(shared_send, blocks_xrecv, one_s.at[2], one_r.at[2], across)
    block_near.start()
    block_far.start()

    heads = heads_width // HEAD_DIM
    inverse = HEAD_DIM ** (-0.5)
    exponent = inverse * LOG2E
    block_rows = min(ATT_ROWS, length)
    sums_buf[...] = jnp.zeros_like(sums_buf)

    def head_step(h, carry):
        cols = pl.ds(pl.multiple_of(h * HEAD_DIM, HEAD_DIM), HEAD_DIM)
        dk_acc[...] = jnp.zeros_like(dk_acc)
        dv_acc[...] = jnp.zeros_like(dv_acc)
        for block in range(length // block_rows):
            first, last = key_window(block, block_rows)
            here = pl.ds(block * block_rows, block_rows)
            keys = pl.ds(first, last - first)
            queries = qrot_ref[here, cols]
            key_rows = krot_ref[keys, cols]
            grads = dmixed_ref[here, cols]
            scores = attention_scores(
                key_rows, queries, start_ref[:, here], block * block_rows, first, 1,
            )
            top = jnp.max(scores, axis=0, keepdims=True)
            weights = jnp.exp2((scores - top) * exponent)
            total = jnp.sum(weights, axis=0, keepdims=True)
            probs = weights * (1.0 / total)
            prob_grad = mm_nt(value_ref[keys, cols], grads)
            weighted = probs * prob_grad
            delta = jnp.sum(weighted, axis=0, keepdims=True)
            score_grad = (weighted - probs * delta).astype(low)
            dv_acc[keys, :] += mm(probs.astype(low), grads)
            dk_acc[keys, :] += mm(score_grad, queries)
            dq = mm_tn(score_grad, key_rows) * inverse
            dq = dq * cos_ref[here, :] - pltpu.roll(dq, HEAD_DIM // 2, 1) * sin_ref[here, :]
            dq = dq * qgain_ref[:, cols]
            dq_buf[here, cols] = dq
            sums_buf[0, here, :] += qproj_ref[here, cols] * dq
        dk = dk_acc[...] * inverse
        dk = dk * cos_ref[...] - pltpu.roll(dk, HEAD_DIM // 2, 1) * sin_ref[...]
        dk = dk * kgain_ref[:, cols]
        dk_buf[:, cols] = dk
        sums_buf[1] += kproj_ref[:, cols] * dk
        dv_low[:, cols] = dv_acc[...].astype(low)

        @pl.when(h == 0)
        def _():
            block_near.wait_recv()
            block_far.wait_recv()
            shared_send[...] = (
                blocks[across].astype(jnp.float32) + blocks_recv[1].astype(jnp.float32)
            ).astype(low)
            block_across.start()

        @pl.when(h == heads - 1)
        def _():
            block_across.wait()
            shared_send[...] = (
                blocks[me].astype(jnp.float32)
                + blocks_recv[0].astype(jnp.float32)
                + blocks_xrecv[...].astype(jnp.float32)
            ).astype(low)
            start_exchange(2)

        return carry

    lax.fori_loop(0, heads, head_step, 0)

    lane = lax.broadcasted_iota(jnp.int32, (length, HEAD_DIM), 1)
    both = jnp.where(
        lane < 4,
        jnp.sum(sums_buf[0], axis=1, keepdims=True),
        jnp.sum(sums_buf[1], axis=1, keepdims=True),
    )
    ex_send[...] = jnp.transpose(both)[:8]
    swaps = [
        remote(ex_send, ex_recv.at[i], es_sem.at[i], er_sem.at[i], other)
        for i, other in enumerate((beside, across, far))
    ]
    for swap in swaps:
        swap.start()
    for load in loads:
        load.wait()
    for swap in swaps:
        swap.wait_recv()
    total = (ex_send[...] + ex_recv[0] + ex_recv[1] + ex_recv[2]) * (1.0 / (4 * heads_width))
    wide = jnp.concatenate(
        [
            jnp.broadcast_to(total[:1], (HEAD_DIM // 2, length)),
            jnp.broadcast_to(total[4:5], (HEAD_DIM // 2, length)),
        ],
        axis=0,
    )
    sums_buf[0] = jnp.transpose(wide)
    for dn, proj, target, at in (
        (dq_buf, qproj_ref, dq_low, 0), (dk_buf, kproj_ref, dk_low, HEAD_DIM // 2),
    ):
        scale = scale_ref[:, at : at + 1]
        means = sums_buf[0, :, at : at + 1]
        target[...] = (scale * dn[...] - proj[...] * (scale * scale * scale * means)).astype(low)

    dmid_part = (
        mm_nt(eq_ref[...], dq_low[...]) + mm_nt(ek_ref[...], dk_low[...])
        + mm_nt(ev_ref[...], dv_low[...])
    )
    dmid_send[...] = dmid_part.astype(low)
    dmid_near = remote(dmid_send, dmid_recv, one_s.at[3], one_r.at[3], beside)
    dmid_across = remote(dmid_xsend, dmid_xrecv, one_s.at[4], one_r.at[4], across)
    dmid_near.start()

    def reduce_beside(c):
        return remote(bsend.at[c], brecv.at[c], bs_sem.at[c], br_sem.at[c], beside)

    def reduce_across(c):
        return remote(xsend.at[c], xrecv.at[c], xs_sem.at[c], xr_sem.at[c], across)

    def chunk_of(buffer, c):
        return jnp.concatenate(
            [buffer[pl.ds(pl.multiple_of(o * rows + c * part, part), part), :] for o in order], axis=0
        )

    def stage_partial(c):
        parts = [chunk_of(buffer, c) for buffer in (dq_low, dk_low, dv_low)]
        tile = TILE

        def one(j, carry):
            at = pl.ds(pl.multiple_of(j * tile, tile), tile)
            value = (
                mm_nt(parts[0], wq[at, :]) + mm_nt(parts[1], wk[at, :]) + mm_nt(parts[2], wv[at, :])
            ).astype(low)
            own_buf[c, :, at] = value[:part]
            xsend[c, :, at] = value[part : 2 * part]
            bsend[c, 0, :, at] = value[2 * part : 3 * part]
            bsend[c, 1, :, at] = value[3 * part :]
            return carry

        lax.fori_loop(0, width // tile, one, 0)
        reduce_beside(c).start()

    def stage_pair(c):
        reduce_beside(c).wait_recv()
        xsend[c] = (xsend[c].astype(jnp.float32) + brecv[c, 1].astype(jnp.float32)).astype(low)
        reduce_across(c).start()
        own_buf[c] = (own_buf[c].astype(jnp.float32) + brecv[c, 0].astype(jnp.float32)).astype(low)

    def partial_step(i, carry):
        @pl.when(i < chunks)
        def _():
            stage_partial(i)

        @pl.when(i == 0)
        def _():
            dmid_near.wait_recv()
            dmid_xsend[...] = (
                dmid_send[...].astype(jnp.float32) + dmid_recv[...].astype(jnp.float32)
            ).astype(low)
            dmid_across.start()

        @pl.when(i > 0)
        def _():
            stage_pair(i - 1)

        return carry

    lax.fori_loop(0, chunks + 1, partial_step, 0)

    mids = mids_ref[...]
    for i, buffer in enumerate((dq_low, dk_low, dv_low)):
        heads_send[:, i * heads_width : (i + 1) * heads_width] = (
            adapter_scale_factor * mm_tn(mids, buffer[...])[i * 16 : (i + 1) * 16]
        ).astype(low)
    start_exchange(1)
    dmid_across.wait_recv()
    dmid = (
        dmid_xsend[...].astype(jnp.float32) + dmid_xrecv[...].astype(jnp.float32)
    ).astype(low)
    inward_grad = mm(dmid, full[...])
    for t in range(4):
        for g in range(groups):
            at = slice((g * 4 + t) * cols_each, (g * 4 + t + 1) * cols_each)
            inward_send[g, t] = inward_grad[:, at]
    start_exchange(3)
    dmid_xsend_ready = dmid
    ex_dmid = dmid_xsend_ready
    dmid_across.wait_send()
    dmid_xsend[...] = ex_dmid

    def finish_step(c, carry):
        reduce_across(c).wait_recv()
        here = pl.ds(pl.multiple_of(c * part, part), part)
        tgrad_ref[here, :] = (
            hgrad_ref[here, :] + own_buf[c].astype(jnp.float32) + xrecv[c].astype(jnp.float32)
        )
        return carry

    mine = pl.ds(pl.multiple_of(me * rows, rows), rows)
    extra = mm_tn(dmid_xsend[:, mine], shrink_ref[...])
    lax.fori_loop(0, chunks, finish_step, 0)
    tgrad_ref[...] += extra
    for c in range(chunks):
        reduce_beside(c).wait_send()
        reduce_across(c).wait_send()
    for copy in (block_near, block_far, dmid_near, *swaps):
        copy.wait_send()
    for number in range(4):
        end_exchange(number)


def back(
    qrot, krot, value, dmixed, qproj, kproj, scale, qgain, kgain, cos, sin, start_row,
    wq, wk, wv, shrink, eq, ek, ev, mids, full, hgrad, chosen, gso, geg, geu, gsd, gsgu, geo, ged,
):
    rows, width = hgrad.shape
    heads_width, units = wq.shape[1], geg.shape[1]
    length = 4 * rows
    part = rows // CHUNKS
    groups = lax.axis_size("dp")
    cols_each = width // (4 * groups)
    split_width = heads_width + 3 * units + 128
    vmem = pl.BlockSpec(memory_space=pltpu.VMEM)
    hbm = pl.BlockSpec(memory_space=pl.ANY)
    low, f32 = jnp.bfloat16, jnp.float32
    shape = jax.ShapeDtypeStruct
    dma = pltpu.SemaphoreType.DMA
    buf = pltpu.VMEM
    return pl.pallas_call(
        back_body,
        in_specs=[vmem] * 12 + [hbm] * 3 + [vmem] * 5 + [hbm] + [vmem] * 9,
        out_specs=[vmem] + [hbm] * 4,
        out_shape=[
            shape((rows, width), f32),
            shape((groups, 16, split_width), low),
            shape((groups, 16, 3 * heads_width), low),
            shape((groups, 64, cols_each), low),
            shape((groups, 48, cols_each), f32),
        ],
        scratch_shapes=[
            buf(wq.shape, low), buf(wk.shape, low), buf(wv.shape, low), buf(full.shape, low),
            dma((4,)),
            buf((length, heads_width), f32), buf((length, heads_width), f32),
            buf((length, heads_width), low), buf((length, heads_width), low),
            buf((length, heads_width), low),
            buf((length, HEAD_DIM), f32), buf((length, HEAD_DIM), f32),
            buf((2, length, HEAD_DIM), f32),
            buf((16, split_width), low), buf((16, 3 * heads_width), low),
            buf((4, groups, 64, cols_each), low), buf((2, groups, 64, cols_each), low),
            buf((groups, 64, cols_each), low), buf((groups, 64, cols_each), low),
            buf((groups, 4, 48, cols_each), f32),
            buf((8, length), f32), buf((3, 8, length), f32),
            buf((48, length), low), buf((48, length), low), buf((48, length), low),
            buf((48, length), low),
            buf((CHUNKS, part, width), low), buf((CHUNKS, part, width), low),
            buf((CHUNKS, part, width), low),
            buf((CHUNKS, 2, part, width), low), buf((CHUNKS, 2, part, width), low),
            dma((3,)), dma((3,)), dma((CHUNKS,)), dma((CHUNKS,)), dma((CHUNKS,)), dma((CHUNKS,)),
            dma((5,)), dma((5,)),
        ] + [dma((groups,))] * 8 + [dma((4,))],
        cost_estimate=pl.CostEstimate(
            flops=2 * length * heads_width * (3 * width + 5 * length),
            bytes_accessed=2 * width * (3 * heads_width + 3 * length), transcendentals=0,
        ),
        compiler_params=pltpu.CompilerParams(
            collective_id=2, has_side_effects=True, vmem_limit_bytes=67043328
        ),
        name="attention_back_to_tokens",
    )(qrot, krot, value, dmixed, qproj, kproj, scale, qgain, kgain, cos, sin, start_row,
      wq, wk, wv, shrink, eq, ek, ev, mids, full, hgrad, chosen, gso, geg, geu, gsd, gsgu, geo, ged)


def finish_body(split_ref, heads_ref, shared_ref, inward_ref, *outs):
    groups = split_ref.shape[0]
    tag = split_ref.shape[2] - 128
    sets = outs[0].shape[0]
    tags = [split_ref[g, :, tag : tag + 1].astype(jnp.float32) for g in range(groups)]

    def add_up(source, target, first, step=512):
        count, high, wide = target.shape
        for at in range(0, wide, step):
            end = min(wide, at + step)
            pieces = [source(g, first + at, first + end).astype(jnp.float32) for g in range(groups)]
            for c in range(count):
                total = jnp.where(tags[0] == c, pieces[0], 0.0)
                for g in range(1, groups):
                    total += jnp.where(tags[g] == c, pieces[g], 0.0)
                target[c, :, at:end] = total

    sq, eq, sk, ek, sv, ev, so, eo, sg, eg, su, eu, sd, ed = outs
    heads_width = eq.shape[2]
    units = eg.shape[2]
    for i, target in enumerate((eq, ek, ev)):
        add_up(lambda g, a, b: heads_ref[g, :, a:b], target, i * heads_width)
    at = 0
    for target in (so, eg, eu, sd):
        add_up(lambda g, a, b: split_ref[g, :, a:b], target, at)
        at += target.shape[2]
    for i, target in enumerate((sq, sk, sv)):
        add_up(lambda g, a, b: inward_ref[g, i * 16 : (i + 1) * 16, a:b], target, 0)
    for i, target in enumerate((eo, sg, su, ed)):
        add_up(lambda g, a, b: shared_ref[g, i * 16 : (i + 1) * 16, a:b], target, 0)


def finish(split, by_heads, shared, inward, sets, heads_width, units):
    cols = shared.shape[2]
    vmem = pl.BlockSpec(memory_space=pltpu.VMEM)
    widths = (
        cols, heads_width, cols, heads_width, cols, heads_width, heads_width, cols,
        cols, units, cols, units, units, cols,
    )
    return pl.pallas_call(
        finish_body,
        in_specs=[vmem] * 4,
        out_specs=[vmem] * 14,
        out_shape=[jax.ShapeDtypeStruct((sets, 16, w), jnp.float32) for w in widths],
        compiler_params=pltpu.CompilerParams(vmem_limit_bytes=48 * 2**20),
        name="sum_by_set",
    )(split, by_heads, shared, inward)


def per_device(
    tokens,
    cotangent,
    segment_ids,
    adapter_set,
    w_query,
    w_key,
    w_value,
    w_out,
    w_gate,
    w_up,
    w_down,
    query_gain,
    key_gain,
    mixer_gain,
    feed_gain,
    shrink_query,
    expand_query,
    shrink_key,
    expand_key,
    shrink_value,
    expand_value,
    shrink_out,
    expand_out,
    shrink_gate,
    expand_gate,
    shrink_up,
    expand_up,
    shrink_down,
    expand_down,
):
    length = 4 * tokens.shape[0]
    (
        shrink_rows, expand_query_rows, expand_key_rows, expand_value_rows, out_shrink, out_expand,
        gate_up_shrink, gate_expand, up_expand, down_shrink, down_expand,
        query_gains, key_gains, mixer_gains, feed_gains, start_col, start_row, set_row,
    ) = pick(
        adapter_set, segment_ids, (query_gain, key_gain, mixer_gain, feed_gain),
        (
            shrink_query, expand_query, shrink_key, expand_key, shrink_value, expand_value,
            shrink_out, expand_out, shrink_gate, expand_gate, shrink_up, expand_up,
            shrink_down, expand_down,
        ),
    )
    cosine_table, sine_table = rotary_constants(length, HEAD_DIM)
    cosine_table, sine_table = jnp.asarray(cosine_table), jnp.asarray(sine_table)
    (
        mixed, query_rot, key_rot, value_low, query_proj, key_proj, scales, qkv_middle, full_tokens,
    ) = front(
        tokens, w_query, w_key, w_value, shrink_rows,
        expand_query_rows, expand_key_rows, expand_value_rows,
        query_gains, key_gains, cosine_table, sine_table, start_col,
    )
    (
        block_output, hidden_grad, mixed_grad, grad_down_shrink, gradient_gate_widened,
        gradient_up_widened, grad_out_shrink, owner_gate_up, owner_out, owner_down,
    ) = middle(
        mixed, tokens, cotangent, w_out, w_gate, w_up, w_down, mixer_gains, feed_gains,
        out_shrink, out_expand, gate_up_shrink, gate_expand, up_expand, down_shrink, down_expand,
    )
    token_grads, split, by_heads, shared, inward = back(
        query_rot, key_rot, value_low, mixed_grad.reshape(mixed.shape), query_proj, key_proj, scales,
        query_gains, key_gains, cosine_table, sine_table, start_row,
        w_query, w_key, w_value, shrink_rows, expand_query_rows, expand_key_rows, expand_value_rows,
        qkv_middle, full_tokens.reshape(length, -1), hidden_grad, set_row,
        grad_out_shrink, gradient_gate_widened, gradient_up_widened, grad_down_shrink,
        owner_gate_up, owner_out, owner_down,
    )
    adapter_grads = finish(
        split, by_heads, shared, inward, shrink_query.shape[0], w_query.shape[1], w_gate.shape[1]
    )
    return (block_output, token_grads, *adapter_grads)


def solution(mesh):
    in_specs = (
        P(("dp", "tensor"), None),
        P(("dp", "tensor"), None),
        P("dp", None),
        P("dp"),
        P(None, "tensor"),
        P(None, "tensor"),
        P(None, "tensor"),
        P("tensor", None),
        P(None, "tensor"),
        P(None, "tensor"),
        P("tensor", None),
        P("tensor"),
        P("tensor"),
        P(),
        P(),
        P(),
        P(None, None, "tensor"),
        P(),
        P(None, None, "tensor"),
        P(),
        P(None, None, "tensor"),
        P(None, None, "tensor"),
        P(),
        P(),
        P(None, None, "tensor"),
        P(),
        P(None, None, "tensor"),
        P(None, None, "tensor"),
        P(),
    )
    out_specs = (
        P(("dp", "tensor"), None),
        P(("dp", "tensor"), None),
        P(None, None, ("dp", "tensor")),
        P(None, None, "tensor"),
        P(None, None, ("dp", "tensor")),
        P(None, None, "tensor"),
        P(None, None, ("dp", "tensor")),
        P(None, None, "tensor"),
        P(None, None, "tensor"),
        P(None, None, ("dp", "tensor")),
        P(None, None, ("dp", "tensor")),
        P(None, None, "tensor"),
        P(None, None, ("dp", "tensor")),
        P(None, None, "tensor"),
        P(None, None, "tensor"),
        P(None, None, ("dp", "tensor")),
    )
    return jax.shard_map(
        per_device, mesh=mesh, in_specs=in_specs, out_specs=out_specs, check_vma=False
    )
```

```python
import functools
import jax
import jax.numpy as jnp
import numpy as np
from jax import lax
from jax.experimental import pallas as pl
from jax.experimental.pallas import tpu as pltpu
from jax.sharding import PartitionSpec as P

HEAD_DIM = 128
DOC_MOST = 512
ATT_ROWS = 256
rotary_base = 500000.0
NEG = -1e30
LOG2E = 1.4426950408889634


def rotary_constants(length, head_dim):
    half = head_dim // 2
    frequency = np.float32(rotary_base) ** (
        -(np.arange(half, dtype=np.float32) * np.float32(2.0) / np.float32(head_dim))
    )
    angles = np.arange(length, dtype=np.float32)[:, None] * frequency.astype(np.float32)[None, :]
    cosine = np.cos(angles.astype(np.float64)).astype(np.float32)
    sine = np.sin(angles.astype(np.float64)).astype(np.float32)
    return (
        np.concatenate([cosine, cosine], axis=1),
        np.concatenate([-sine, sine], axis=1),
    )


def key_window(block, rows):
    first = max(0, (block * rows - (DOC_MOST - 1)) // rows) * rows
    return first, (block + 1) * rows


epsilon = 1e-06
adapter_scale_factor = 0.5


def pick_body(
    set_ref, seg_ref, qgain, kgain, mgain, fgain,
    sq, eq, sk, ek, sv, ev, so, eo, sg, eg, su, eu, sd, ed,
    shrink_out, eq_out, ek_out, ev_out, so_out, eo_out, sgu_out, eg_out, eu_out, sd_out, ed_out,
    qgain_out, kgain_out, mgain_out, fgain_out, start_col, start_row, set_out,
):
    rank = sq.shape[1]

    def scaled(ref):
        return (adapter_scale_factor * ref[0].astype(jnp.float32)).astype(jnp.bfloat16)

    for i, ref in enumerate((sq, sk, sv)):
        shrink_out[i * rank : (i + 1) * rank, :] = ref[0]
    for i, (ref, target) in enumerate(((eq, eq_out), (ek, ek_out), (ev, ev_out))):
        target[...] = jnp.zeros_like(target)
        target[i * rank : (i + 1) * rank, :] = scaled(ref)
    for i, (ref, target) in enumerate(((eg, eg_out), (eu, eu_out))):
        target[...] = jnp.zeros_like(target)
        target[i * rank : (i + 1) * rank, :] = scaled(ref)
    so_out[...] = so[0]
    sd_out[...] = sd[0]
    eo_out[...] = scaled(eo)
    ed_out[...] = scaled(ed)
    sgu_out[:rank, :] = sg[0]
    sgu_out[rank:, :] = su[0]
    for ref, target in ((qgain, qgain_out), (kgain, kgain_out), (mgain, mgain_out), (fgain, fgain_out)):
        target[...] = ref[...].astype(jnp.float32).reshape(target.shape)
    length = seg_ref.shape[1]
    row = seg_ref[...].astype(jnp.float32)
    col = jnp.transpose(jnp.broadcast_to(row, (HEAD_DIM, length)))[:, :1]
    start_col[...] = jnp.sum(
        jnp.where(row < col, 1.0, 0.0), axis=1, keepdims=True
    ).astype(jnp.int32)
    start_row[...] = jnp.sum(
        jnp.where(col < row, 1.0, 0.0), axis=0, keepdims=True
    ).astype(jnp.int32)
    set_out[...] = jnp.full(set_out.shape, set_ref[0], jnp.int32).astype(jnp.float32)


def pick(adapter_set, segment_ids, gains, adapters):
    whole = lambda a: pl.BlockSpec(a.shape, lambda i, s: (0,) * a.ndim)
    chosen = lambda a: pl.BlockSpec((1,) + a.shape[1:], lambda i, s: (s[0], 0, 0))
    length = segment_ids.shape[1]
    rank, width = adapters[0].shape[1:]
    here, units = adapters[1].shape[2], adapters[9].shape[2]
    low, f32 = jnp.bfloat16, jnp.float32
    shapes = [
        ((3 * rank, width), low), ((3 * rank, here), low), ((3 * rank, here), low),
        ((3 * rank, here), low), ((rank, here), low), ((rank, width), low), ((2 * rank, width), low),
        ((2 * rank, units), low), ((2 * rank, units), low), ((rank, units), low), ((rank, width), low),
        ((1, here), f32), ((1, here), f32), ((1, width), f32), ((1, width), f32),
        ((length, 1), jnp.int32), ((1, length), jnp.int32), ((1, 128), f32),
    ]
    return pl.pallas_call(
        pick_body,
        grid_spec=pltpu.PrefetchScalarGridSpec(
            num_scalar_prefetch=1,
            grid=(1,),
            in_specs=[whole(segment_ids)] + [whole(g) for g in gains] + [chosen(a) for a in adapters],
            out_specs=[pl.BlockSpec(s, lambda i, _: (0,) * 2) for s, _ in shapes],
        ),
        out_shape=[jax.ShapeDtypeStruct(s, t) for s, t in shapes],
        compiler_params=pltpu.CompilerParams(vmem_limit_bytes=67043328),
        name="pick_adapters",
    )(adapter_set, segment_ids, *gains, *adapters)


CHUNKS = 4
TILE = 1024
EXTRA = 128
NT = (((1,), (1,)), ((), ()))
TN = (((0,), (0,)), ((), ()))
MESH_ID = pl.DeviceIdType.MESH
MIDDLE_ORDER = (
    ("S2", 4), ("P4", 8), ("S4", 7), ("P0", 1), ("S1", 2), ("S6", 10), ("F3", 6),
    ("F5", 9), ("S5", 8), ("P2", 4), ("S0", 0), ("F1", 3), ("S3", 5),
)


def mm(left, right):
    return jnp.dot(left, right, preferred_element_type=jnp.float32)


def mm_nt(left, right):
    return lax.dot_general(left, right, NT, preferred_element_type=jnp.float32)


def mm_tn(left, right):
    return lax.dot_general(left, right, TN, preferred_element_type=jnp.float32)


def partners():
    me = lax.axis_index("tensor")
    group = lax.axis_index("dp")
    beside = me + 1 - 2 * lax.rem(me, 2)
    across = lax.rem(me + 2, 4)
    return me, group, beside, across


def greet(group, beside, across):
    barrier = pltpu.get_barrier_semaphore()
    for other in (beside, across):
        pl.semaphore_signal(barrier, inc=1, device_id=(group, other), device_id_type=MESH_ID)
    pl.semaphore_wait(barrier, 2)


def middle_body(
    mixed_ref, tokens_ref, cot_ref, w_out_hbm, w_gate_hbm, w_up_hbm, w_down_hbm,
    mgain_ref, fgain_ref, so_ref, eo_ref, sgu_ref, eg_ref, eu_ref, sd_ref, ed_ref,
    out_ref, hgrad_ref, dmixed_ref, gsd_ref, geg_ref, geu_ref, gso_ref, gsgu_ref, geo_ref, ged_ref,
    w_out, w_gate, w_up, w_down, wsem,
    rows_buf, own_buf, xsend, xrecv, bsend, brecv,
    gate_buf, up_buf, temp_a, temp_b, mgu_buf, mixer_buf, hidden_buf, mout_buf,
    xs_sem, xr_sem, bs_sem, br_sem, gxs_sem, gxr_sem, gbs_sem, gbr_sem, fs_sem, fr_sem,
):
    me, group, beside, across = partners()
    chunks, part, width = rows_buf.shape[0], rows_buf.shape[2], rows_buf.shape[3]
    units = w_gate.shape[1]
    heads_width = w_out.shape[0]
    far = lax.rem(beside + 2, 4)
    order = (me, across, beside, far)
    loads = [
        pltpu.make_async_copy(source, target, wsem.at[i])
        for i, (source, target) in enumerate(
            ((w_out_hbm, w_out), (w_gate_hbm, w_gate), (w_up_hbm, w_up), (w_down_hbm, w_down))
        )
    ]
    for load in loads:
        load.start()
    for ref in (gsd_ref, geg_ref, geu_ref, gso_ref, gsgu_ref, geo_ref, ged_ref):
        ref[...] = jnp.zeros_like(ref)
    greet(group, beside, across)

    def remote(source, target, ssem, rsem, other):
        return pltpu.make_async_remote_copy(
            src_ref=source, dst_ref=target, send_sem=ssem, recv_sem=rsem,
            device_id=(group, other), device_id_type=MESH_ID,
        )

    def gather_across(c):
        return remote(rows_buf.at[c, 0], rows_buf.at[c, 1], gxs_sem.at[c], gxr_sem.at[c], across)

    def gather_beside(c):
        return remote(rows_buf.at[c, 0], rows_buf.at[c, 2], gbs_sem.at[c], gbr_sem.at[c], beside)

    def gather_forward(c):
        return remote(rows_buf.at[c, 1], rows_buf.at[c, 3], fs_sem.at[c], fr_sem.at[c], beside)

    def reduce_beside(c):
        return remote(bsend.at[c], brecv.at[c], bs_sem.at[c], br_sem.at[c], beside)

    def reduce_across(c):
        return remote(xsend.at[c], xrecv.at[c], xs_sem.at[c], xr_sem.at[c], across)

    def store_partial(c, columns, value):
        low = value.astype(jnp.bfloat16)
        own_buf[c, :, columns] = low[:part]
        xsend[c, :, columns] = low[part : 2 * part]
        bsend[c, 0, :, columns] = low[2 * part : 3 * part]
        bsend[c, 1, :, columns] = low[3 * part :]

    def gathered(c):
        return rows_buf[c].reshape(4 * part, width)

    def forward_stage(c):
        gather_across(c).wait_recv()
        gather_forward(c).start()

    def pair_stage(c):
        reduce_beside(c).wait_recv()
        own_buf[c] = (
            own_buf[c].astype(jnp.float32) + brecv[c, 0].astype(jnp.float32)
        ).astype(jnp.bfloat16)
        xsend[c] = (
            xsend[c].astype(jnp.float32) + brecv[c, 1].astype(jnp.float32)
        ).astype(jnp.bfloat16)
        reduce_across(c).start()

    def totals(c):
        reduce_across(c).wait_recv()
        main = own_buf[c, :, :width].astype(jnp.float32) + xrecv[c, :, :width].astype(jnp.float32)
        side = own_buf[c, :, width : width + 32].astype(jnp.float32) + xrecv[
            c, :, width : width + 32
        ].astype(jnp.float32)
        return main, side.astype(jnp.bfloat16)

    def own_rows(c):
        return pl.ds(pl.multiple_of(c * part, part), part)

    def send_rows(c, value, again):
        if again:
            gather_across(c).wait_send()
            gather_beside(c).wait_send()
        rows_buf[c, 0] = value
        gather_across(c).start()
        gather_beside(c).start()

    def chunk_rows(c):
        return pl.ds(pl.multiple_of(c * 4 * part, 4 * part), 4 * part)

    def tiles(total, tile, body):
        def step(j, carry):
            body(pl.ds(pl.multiple_of(j * tile, tile), tile))
            return carry

        lax.fori_loop(0, total // tile, step, 0)

    def mixed_chunk(c):
        return jnp.concatenate([mixed_ref[o, c] for o in order], axis=0)

    def stage_mixer(c):
        @pl.when(c == 0)
        def _():
            loads[0].wait()

        rows = mixed_chunk(c)
        store_partial(c, slice(width, width + 16), mm_nt(rows, so_ref[...]))
        tiles(width, TILE, lambda cols: store_partial(c, cols, mm(rows, w_out[:, cols])))
        reduce_beside(c).start()

    def stage_hidden(c):
        main, side = totals(c)
        mid = side[:, :16]
        mout_buf[c] = mid
        mixer = main + mm(mid, eo_ref[...])
        mixer_buf[own_rows(c), :] = mixer
        factor = lax.rsqrt(jnp.mean(mixer * mixer, axis=1, keepdims=True) + epsilon)
        hidden = tokens_ref[own_rows(c), :].astype(jnp.float32) + mixer * factor * mgain_ref[...]
        hidden_buf[own_rows(c), :] = hidden
        send_rows(c, hidden.astype(jnp.bfloat16), False)

    def arrive(c):
        gather_beside(c).wait_recv()
        gather_forward(c).wait_recv()

    def stage_units(c):
        @pl.when(c == 0)
        def _():
            for load in loads[1:]:
                load.wait()

        arrive(c)
        mids = mm_nt(gathered(c), sgu_ref[...]).astype(jnp.bfloat16)
        mgu_buf[c] = mids

        def unit_tile(cols):
            rows = gathered(c)
            gate = mm(rows, w_gate[:, cols]) + mm(mids, eg_ref[:, cols])
            up = mm(rows, w_up[:, cols]) + mm(mids, eu_ref[:, cols])
            gate_buf[chunk_rows(c), cols] = gate.astype(jnp.bfloat16)
            up_buf[chunk_rows(c), cols] = up.astype(jnp.bfloat16)
            sig = 1.0 / (1.0 + jnp.exp(-gate))
            temp_a[:, cols] = (gate * sig * up).astype(jnp.bfloat16)

        tiles(units, TILE // 2, unit_tile)
        gather_forward(c).wait_send()
        reduce_beside(c).wait_send()
        reduce_across(c).wait_send()
        inner = temp_a[...]
        store_partial(c, slice(width, width + 16), mm_nt(inner, sd_ref[...]))
        tiles(width, TILE, lambda cols: store_partial(c, cols, mm(temp_a[...], w_down[:, cols])))
        reduce_beside(c).start()

    def norm_back_rows(values, gains, grads):
        factor = lax.rsqrt(jnp.mean(values * values, axis=1, keepdims=True) + epsilon)
        weighted = grads * gains
        return factor * weighted - values * (
            factor * factor * factor * jnp.mean(values * weighted, axis=1, keepdims=True)
        )

    def stage_feed(c):
        main, side = totals(c)
        mid = side[:, :16]
        feed = main + mm(mid, ed_ref[...])
        factor = lax.rsqrt(jnp.mean(feed * feed, axis=1, keepdims=True) + epsilon)
        gains = fgain_ref[...]
        out_ref[own_rows(c), :] = (hidden_buf[own_rows(c), :] + feed * factor * gains).astype(
            jnp.bfloat16
        )
        grad = norm_back_rows(feed, gains, cot_ref[own_rows(c), :].astype(jnp.float32))
        grad = grad.astype(jnp.bfloat16)
        send_rows(c, grad, True)
        ged_ref[...] += mm_tn(mid, grad)

    def stage_units_back(c):
        arrive(c)
        dmid = mm_nt(gathered(c), ed_ref[...]).astype(jnp.bfloat16)
        mids = mgu_buf[c]

        def unit_tile(cols):
            rows = gathered(c)
            inner_grad = mm_nt(rows, w_down[cols, :]) + mm(dmid, sd_ref[:, cols])
            gate = gate_buf[chunk_rows(c), cols].astype(jnp.float32)
            up = up_buf[chunk_rows(c), cols].astype(jnp.float32)
            sig = 1.0 / (1.0 + jnp.exp(-gate))
            silu = gate * sig
            gate_grad = (inner_grad * up * (sig + silu * (1.0 - sig))).astype(jnp.bfloat16)
            up_grad = (inner_grad * silu).astype(jnp.bfloat16)
            temp_a[:, cols] = gate_grad
            temp_b[:, cols] = up_grad
            gsd_ref[:, cols] += mm_tn(dmid, (silu * up).astype(jnp.bfloat16))
            geg_ref[:, cols] += mm_tn(mids, gate_grad)
            geu_ref[:, cols] += mm_tn(mids, up_grad)

        tiles(units, TILE // 2, unit_tile)
        gather_forward(c).wait_send()
        reduce_beside(c).wait_send()
        reduce_across(c).wait_send()
        store_partial(
            c,
            slice(width, width + 32),
            mm_nt(temp_a[...], eg_ref[...]) + mm_nt(temp_b[...], eu_ref[...]),
        )

        def width_tile(cols):
            store_partial(
                c, cols, mm_nt(temp_a[...], w_gate[cols, :]) + mm_nt(temp_b[...], w_up[cols, :])
            )

        tiles(width, TILE // 2, width_tile)
        reduce_beside(c).start()

    def stage_mixer_grad(c):
        main, side = totals(c)
        grads = cot_ref[own_rows(c), :].astype(jnp.float32) + main + mm(side, sgu_ref[...])
        hgrad_ref[own_rows(c), :] = grads
        mixer_grad = norm_back_rows(mixer_buf[own_rows(c), :], mgain_ref[...], grads)
        mixer_grad = mixer_grad.astype(jnp.bfloat16)
        send_rows(c, mixer_grad, True)
        geo_ref[...] += mm_tn(mout_buf[c], mixer_grad)
        gsgu_ref[...] += mm_tn(side, hidden_buf[own_rows(c), :].astype(jnp.bfloat16))

    def stage_mixed_grad(c):
        arrive(c)
        dmid = mm_nt(gathered(c), eo_ref[...]).astype(jnp.bfloat16)
        grad = (mm_nt(gathered(c), w_out[...]) + mm(dmid, so_ref[...])).astype(jnp.bfloat16)
        for i, o in enumerate(order):
            dmixed_ref[o, c] = grad[i * part : (i + 1) * part]
        gso_ref[...] += mm_tn(dmid, mixed_chunk(c))
        gather_forward(c).wait_send()
        gather_across(c).wait_send()
        gather_beside(c).wait_send()
        reduce_beside(c).wait_send()
        reduce_across(c).wait_send()

    stages = {
        "S0": stage_mixer, "S1": stage_hidden, "S2": stage_units, "S3": stage_feed,
        "S4": stage_units_back, "S5": stage_mixer_grad, "S6": stage_mixed_grad,
        "P0": pair_stage, "P2": pair_stage, "P4": pair_stage,
        "F1": forward_stage, "F3": forward_stage, "F5": forward_stage,
    }

    def step(i, carry):
        for name, delay in MIDDLE_ORDER:

            @pl.when((i >= delay) & (i < delay + chunks))
            def _():
                stages[name](i - delay)

        return carry

    lax.fori_loop(0, chunks + max(delay for _, delay in MIDDLE_ORDER), step, 0)


def middle(mixed, tokens, cot, w_out, w_gate, w_up, w_down, mgain, fgain, so, eo, sgu, eg, eu, sd, ed):
    rows, width = tokens.shape
    heads_width, units = w_out.shape[0], w_gate.shape[1]
    part = rows // CHUNKS
    whole_width = width + EXTRA
    vmem = pl.BlockSpec(memory_space=pltpu.VMEM)
    hbm = pl.BlockSpec(memory_space=pl.ANY)
    low, full = jnp.bfloat16, jnp.float32
    dma = pltpu.SemaphoreType.DMA((CHUNKS,))
    shape = jax.ShapeDtypeStruct
    flops = 2 * 4 * rows * width * (2 * heads_width + 6 * units)
    return pl.pallas_call(
        middle_body,
        in_specs=[vmem] * 3 + [hbm] * 4 + [vmem] * 9,
        out_specs=[vmem] * 10,
        out_shape=[
            shape((rows, width), low), shape((rows, width), full),
            shape((4, CHUNKS, part, heads_width), low),
            shape((16, units), full), shape((32, units), full), shape((32, units), full),
            shape((16, heads_width), full), shape((32, width), full), shape((16, width), full),
            shape((16, width), full),
        ],
        scratch_shapes=[
            pltpu.VMEM(w_out.shape, low), pltpu.VMEM(w_gate.shape, low),
            pltpu.VMEM(w_up.shape, low), pltpu.VMEM(w_down.shape, low),
            pltpu.SemaphoreType.DMA((4,)),
            pltpu.VMEM((CHUNKS, 4, part, width), low),
            pltpu.VMEM((CHUNKS, part, whole_width), low),
            pltpu.VMEM((CHUNKS, part, whole_width), low),
            pltpu.VMEM((CHUNKS, part, whole_width), low),
            pltpu.VMEM((CHUNKS, 2, part, whole_width), low),
            pltpu.VMEM((CHUNKS, 2, part, whole_width), low),
            pltpu.VMEM((4 * rows, units), low), pltpu.VMEM((4 * rows, units), low),
            pltpu.VMEM((4 * part, units), low), pltpu.VMEM((4 * part, units), low),
            pltpu.VMEM((CHUNKS, 4 * part, 32), low),
            pltpu.VMEM((rows, width), full), pltpu.VMEM((rows, width), full),
            pltpu.VMEM((CHUNKS, part, 16), low),
        ] + [dma] * 10,
        cost_estimate=pl.CostEstimate(
            flops=flops, bytes_accessed=2 * width * (heads_width + 3 * units), transcendentals=0
        ),
        compiler_params=pltpu.CompilerParams(
            collective_id=0, has_side_effects=True, vmem_limit_bytes=67043328
        ),
        name="mixer_to_feed",
    )(mixed.reshape(4, CHUNKS, part, heads_width), tokens, cot, w_out, w_gate, w_up, w_down,
      mgain, fgain, so, eo, sgu, eg, eu, sd, ed)


def attention_scores(first, second, start, first_query, first_key, query_axis):
    scores = lax.dot_general(first, second, NT, preferred_element_type=jnp.float32)
    kpos = lax.broadcasted_iota(jnp.int32, scores.shape, 1 - query_axis) + first_key
    shape = [1, 1]
    shape[query_axis] = scores.shape[query_axis]
    qpos = lax.broadcasted_iota(jnp.int32, shape, query_axis) + first_query
    return jnp.where((kpos <= qpos) & (kpos >= start), scores, NEG)


def front_body(
    tokens_ref, wq_hbm, wk_hbm, wv_hbm, shrink_ref, eq_ref, ek_ref, ev_ref, qgain_ref, kgain_ref,
    cos_ref, sin_ref, start_ref,
    mixed_ref, qrot_ref, krot_ref, value_ref, qproj_ref, kproj_ref, scale_ref, mids_ref, full_hbm,
    wq, wk, wv, wsem, full, lhs, squares, ex_send, ex_recv,
    xs_sem, xr_sem, fs_sem, fr_sem, bs_sem, br_sem, es_sem, er_sem, out_sem,
):
    me, group, beside, across = partners()
    far = lax.rem(beside + 2, 4)
    chunks, part, width = full.shape[1:]
    rows = chunks * part
    length = 4 * rows
    loads = [
        pltpu.make_async_copy(source, target, wsem.at[i])
        for i, (source, target) in enumerate(((wq_hbm, wq), (wk_hbm, wk), (wv_hbm, wv)))
    ]
    for load in loads:
        load.start()
    barrier = pltpu.get_barrier_semaphore()
    for other in (beside, across, far):
        pl.semaphore_signal(barrier, inc=1, device_id=(group, other), device_id_type=MESH_ID)
    pl.semaphore_wait(barrier, 3)

    def remote(source, target, ssem, rsem, other):
        return pltpu.make_async_remote_copy(
            src_ref=source, dst_ref=target, send_sem=ssem, recv_sem=rsem,
            device_id=(group, other), device_id_type=MESH_ID,
        )

    def send_across(c):
        return remote(tokens_ref.at[c], full.at[me, c], xs_sem.at[c], xr_sem.at[c], across)

    def forward(c):
        return remote(full.at[across, c], full.at[across, c], fs_sem.at[c], fr_sem.at[c], beside)

    to_beside = remote(tokens_ref, full.at[me], bs_sem, br_sem, beside)
    for c in range(chunks):
        send_across(c).start()
    to_beside.start()
    full[me] = tokens_ref[...]
    for load in loads:
        load.wait()
    pairs = chunks // 2
    half = rows // 2

    def block_step(b, carry):
        @pl.when(b == 0)
        def _():
            lhs[...] = tokens_ref[...].reshape(rows, width)

        @pl.when(b == 1)
        def _():
            to_beside.wait_recv()
            lhs[...] = full[beside].reshape(rows, width)

        @pl.when(b >= 2)
        def _():
            base = (b - 2) * pairs
            for j in range(pairs):
                send_across(base + j).wait_recv()
                forward(base + j).start()
            for j in range(pairs):
                lhs[j * part : (j + 1) * part] = full[across, base + j]
            for j in range(pairs):
                forward(base + j).wait_recv()
                lhs[half + j * part : half + (j + 1) * part] = full[far, base + j]

        mids = mm_nt(lhs[...], shrink_ref[...]).astype(jnp.bfloat16)
        query = mm(lhs[...], wq[...]) + mm(mids, eq_ref[...])
        key = mm(lhs[...], wk[...]) + mm(mids, ek_ref[...])
        value = (mm(lhs[...], wv[...]) + mm(mids, ev_ref[...])).astype(jnp.bfloat16)
        qsum = jnp.sum(query * query, axis=1, keepdims=True)
        ksum = jnp.sum(key * key, axis=1, keepdims=True)
        lane = lax.broadcasted_iota(jnp.int32, (rows, HEAD_DIM), 1)
        both = jnp.where(lane < 4, qsum, ksum)
        first = jnp.where(b == 0, me, jnp.where(b == 1, beside, across)) * rows
        second = jnp.where(b == 0, me, jnp.where(b == 1, beside, far)) * rows
        first = first + jnp.where(b >= 2, (b - 2) * half, 0)
        second = second + jnp.where(b >= 2, (b - 2) * half, half)
        for start, piece in ((first, slice(0, half)), (second, slice(half, rows))):
            there = pl.ds(pl.multiple_of(start, half), half)
            qproj_ref[there, :] = query[piece]
            kproj_ref[there, :] = key[piece]
            value_ref[there, :] = value[piece]
            mids_ref[there, :] = mids[piece]
            squares[there, :] = both[piece]
        return carry

    lax.fori_loop(0, 4, block_step, 0)
    save = pltpu.make_async_copy(full, full_hbm, out_sem)
    save.start()
    ex_send[...] = jnp.transpose(squares[...])[:8]
    swaps = [
        remote(ex_send, ex_recv.at[i], es_sem.at[i], er_sem.at[i], other)
        for i, other in enumerate((beside, across, far))
    ]
    for swap in swaps:
        swap.start()
    for swap in swaps:
        swap.wait_recv()
    total = ex_send[...] + ex_recv[0] + ex_recv[1] + ex_recv[2]
    factor = lax.rsqrt(total / (4 * wq.shape[1]) + epsilon)
    wide = jnp.concatenate(
        [
            jnp.broadcast_to(factor[:1], (HEAD_DIM // 2, length)),
            jnp.broadcast_to(factor[4:5], (HEAD_DIM // 2, length)),
        ],
        axis=0,
    )
    scale_ref[...] = jnp.transpose(wide)
    heads = wq.shape[1] // HEAD_DIM
    exponent = HEAD_DIM ** (-0.5) * LOG2E
    block_rows = min(ATT_ROWS, length)

    def head_step(h, carry):
        cols = pl.ds(pl.multiple_of(h * HEAD_DIM, HEAD_DIM), HEAD_DIM)
        for source, lane, gain, target in (
            (qproj_ref, 0, qgain_ref, qrot_ref),
            (kproj_ref, HEAD_DIM // 2, kgain_ref, krot_ref),
        ):
            normed = source[:, cols] * scale_ref[:, lane : lane + 1] * gain[:, cols]
            turned = normed * cos_ref[...] + pltpu.roll(normed, HEAD_DIM // 2, 1) * sin_ref[...]
            target[:, cols] = turned.astype(jnp.bfloat16)
        for block in range(length // block_rows):
            low, high = key_window(block, block_rows)
            here = pl.ds(block * block_rows, block_rows)
            keys = pl.ds(low, high - low)
            scores = attention_scores(
                qrot_ref[here, cols], krot_ref[keys, cols], start_ref[here, :],
                block * block_rows, low, 0,
            )
            top = jnp.max(scores, axis=1, keepdims=True)
            weights = jnp.exp2((scores - top) * exponent)
            total = jnp.sum(weights, axis=1, keepdims=True)
            mix = mm(weights.astype(jnp.bfloat16), value_ref[keys, cols])
            mixed_ref[here, cols] = (mix * (1.0 / total)).astype(jnp.bfloat16)
        return carry

    lax.fori_loop(0, heads, head_step, 0)
    for c in range(chunks):
        send_across(c).wait_send()
        forward(c).wait_send()
    to_beside.wait_send()
    for swap in swaps:
        swap.wait_send()
    save.wait()


def front(tokens, wq, wk, wv, shrink, eq, ek, ev, qgain, kgain, cos, sin, start_col):
    rows, width = tokens.shape
    heads_width = wq.shape[1]
    length = 4 * rows
    part = rows // CHUNKS
    vmem = pl.BlockSpec(memory_space=pltpu.VMEM)
    hbm = pl.BlockSpec(memory_space=pl.ANY)
    low, full = jnp.bfloat16, jnp.float32
    shape = jax.ShapeDtypeStruct
    dma = pltpu.SemaphoreType.DMA
    return pl.pallas_call(
        front_body,
        in_specs=[vmem] + [hbm] * 3 + [vmem] * 9,
        out_specs=[vmem] * 8 + [hbm],
        out_shape=[
            shape((length, heads_width), low), shape((length, heads_width), low),
            shape((length, heads_width), low), shape((length, heads_width), low),
            shape((length, heads_width), full), shape((length, heads_width), full),
            shape((length, HEAD_DIM), full), shape((length, shrink.shape[0]), low),
            shape((4, CHUNKS, part, width), low),
        ],
        scratch_shapes=[
            pltpu.VMEM(wq.shape, low), pltpu.VMEM(wk.shape, low), pltpu.VMEM(wv.shape, low),
            dma((3,)),
            pltpu.VMEM((4, CHUNKS, part, width), low), pltpu.VMEM((rows, width), low),
            pltpu.VMEM((length, HEAD_DIM), full), pltpu.VMEM((8, length), full),
            pltpu.VMEM((3, 8, length), full),
            dma((CHUNKS,)), dma((CHUNKS,)), dma((CHUNKS,)), dma((CHUNKS,)), dma, dma,
            dma((3,)), dma((3,)), dma,
        ],
        cost_estimate=pl.CostEstimate(
            flops=2 * length * heads_width * (3 * width + 2 * length),
            bytes_accessed=2 * width * (3 * heads_width + length), transcendentals=0,
        ),
        compiler_params=pltpu.CompilerParams(
            collective_id=1, has_side_effects=True, vmem_limit_bytes=67043328
        ),
        name="gather_project_attend",
    )(tokens.reshape(CHUNKS, part, width), wq, wk, wv, shrink, eq, ek, ev, qgain, kgain,
      cos, sin, start_col)


def back_body(
    qrot_ref, krot_ref, value_ref, dmixed_ref, qproj_ref, kproj_ref, scale_ref, qgain_ref, kgain_ref,
    cos_ref, sin_ref, start_ref, wq_hbm, wk_hbm, wv_hbm, shrink_ref,
    eq_ref, ek_ref, ev_ref, mids_ref, full_hbm, hgrad_ref, set_ref,
    gso_ref, geg_ref, geu_ref, gsd_ref, gsgu_ref, geo_ref, ged_ref,
    tgrad_ref, split_hbm, heads_hbm, shared_hbm, inward_hbm,
    wq, wk, wv, full, wsem, dq_buf, dk_buf, dq_low, dk_low, dv_low, dk_acc, dv_acc, sums_buf,
    split_send, heads_send, blocks, blocks_recv, blocks_xrecv, shared_send, inward_send,
    ex_send, ex_recv, dmid_send, dmid_recv, dmid_xsend, dmid_xrecv,
    own_buf, xsend, xrecv, bsend, brecv,
    es_sem, er_sem, xs_sem, xr_sem, bs_sem, br_sem, one_s, one_r,
    sp_s, sp_r, hd_s, hd_r, sh_s, sh_r, in_s, in_r, local_sem,
):
    me, group, beside, across = partners()
    far = lax.rem(beside + 2, 4)
    order = (me, across, beside, far)
    groups = split_hbm.shape[0]
    chunks, part, width = own_buf.shape
    rows = chunks * part
    length = 4 * rows
    heads_width = wq.shape[1]
    units = geg_ref.shape[1]
    cols_each = blocks.shape[3]
    loads = [
        pltpu.make_async_copy(source, target, wsem.at[i])
        for i, (source, target) in enumerate(
            ((wq_hbm, wq), (wk_hbm, wk), (wv_hbm, wv), (full_hbm, full))
        )
    ]
    for load in loads:
        load.start()
    barrier = pltpu.get_barrier_semaphore()
    for other in (beside, across, far):
        pl.semaphore_signal(barrier, inc=1, device_id=(group, other), device_id_type=MESH_ID)

    def greet_group(j, carry):
        other = lax.rem(group + j, groups)
        pl.semaphore_signal(barrier, inc=1, device_id=(other, me), device_id_type=MESH_ID)
        return carry

    lax.fori_loop(1, groups, greet_group, 0)
    pl.semaphore_wait(barrier, groups + 2)

    def remote(source, target, ssem, rsem, other):
        return pltpu.make_async_remote_copy(
            src_ref=source, dst_ref=target, send_sem=ssem, recv_sem=rsem,
            device_id=(group, other), device_id_type=MESH_ID,
        )

    def to_group(source, target, ssem, rsem, j):
        other = lax.rem(group + j, groups)
        return pltpu.make_async_remote_copy(
            src_ref=source(other), dst_ref=target.at[group], send_sem=ssem.at[j],
            recv_sem=rsem.at[group], device_id=(other, me), device_id_type=MESH_ID,
        )

    def from_group(source, target, ssem, rsem, j):
        sender = lax.rem(group + j, groups)
        return pltpu.make_async_remote_copy(
            src_ref=source(sender), dst_ref=target.at[sender], send_sem=ssem.at[j],
            recv_sem=rsem.at[sender], device_id=(sender, me), device_id_type=MESH_ID,
        )

    split = (lambda other: split_send, split_hbm, sp_s, sp_r)
    by_heads = (lambda other: heads_send, heads_hbm, hd_s, hd_r)
    shared = (lambda other: shared_send.at[other], shared_hbm, sh_s, sh_r)
    inward = (lambda other: inward_send.at[other, me], inward_hbm, in_s, in_r)
    exchanges = (split, by_heads, shared, inward)

    def start_exchange(number):
        exchange = exchanges[number]

        def one(j, carry):
            to_group(*exchange, j).start()
            return carry

        lax.fori_loop(1, groups, one, 0)
        pltpu.make_async_copy(
            exchange[0](group), exchange[1].at[group], local_sem.at[number]
        ).start()

    def end_exchange(number):
        exchange = exchanges[number]

        def one(j, carry):
            to_group(*exchange, j).wait_send()
            from_group(*exchange, j).wait_recv()
            return carry

        lax.fori_loop(1, groups, one, 0)
        pltpu.make_async_copy(
            exchange[0](group), exchange[1].at[group], local_sem.at[number]
        ).wait()

    low = jnp.bfloat16
    split_send[:, :heads_width] = gso_ref[...].astype(low)
    split_send[:, heads_width : heads_width + units] = (
        adapter_scale_factor * geg_ref[:16]
    ).astype(low)
    split_send[:, heads_width + units : heads_width + 2 * units] = (
        adapter_scale_factor * geu_ref[16:]
    ).astype(low)
    split_send[:, heads_width + 2 * units : heads_width + 3 * units] = gsd_ref[...].astype(low)
    split_send[:, heads_width + 3 * units :] = jnp.broadcast_to(set_ref[...], (16, 128)).astype(low)
    start_exchange(0)
    for t in range(4):
        for g in range(groups):
            at = slice((g * 4 + t) * cols_each, (g * 4 + t + 1) * cols_each)
            blocks[t, g, :16] = (adapter_scale_factor * geo_ref[:, at]).astype(low)
            blocks[t, g, 16:48] = gsgu_ref[:, at].astype(low)
            blocks[t, g, 48:] = (adapter_scale_factor * ged_ref[:, at]).astype(low)
    block_near = remote(blocks.at[beside], blocks_recv.at[0], one_s.at[0], one_r.at[0], beside)
    block_far = remote(blocks.at[far], blocks_recv.at[1], one_s.at[1], one_r.at[1], beside)
    block_across = remote(shared_send, blocks_xrecv, one_s.at[2], one_r.at[2], across)
    block_near.start()
    block_far.start()

    heads = heads_width // HEAD_DIM
    inverse = HEAD_DIM ** (-0.5)
    exponent = inverse * LOG2E
    block_rows = min(ATT_ROWS, length)
    sums_buf[...] = jnp.zeros_like(sums_buf)

    def head_step(h, carry):
        cols = pl.ds(pl.multiple_of(h * HEAD_DIM, HEAD_DIM), HEAD_DIM)
        dk_acc[...] = jnp.zeros_like(dk_acc)
        dv_acc[...] = jnp.zeros_like(dv_acc)
        for block in range(length // block_rows):
            first, last = key_window(block, block_rows)
            here = pl.ds(block * block_rows, block_rows)
            keys = pl.ds(first, last - first)
            queries = qrot_ref[here, cols]
            key_rows = krot_ref[keys, cols]
            grads = dmixed_ref[here, cols]
            scores = attention_scores(
                key_rows, queries, start_ref[:, here], block * block_rows, first, 1,
            )
            top = jnp.max(scores, axis=0, keepdims=True)
            weights = jnp.exp2((scores - top) * exponent)
            total = jnp.sum(weights, axis=0, keepdims=True)
            probs = weights * (1.0 / total)
            prob_grad = mm_nt(value_ref[keys, cols], grads)
            weighted = probs * prob_grad
            delta = jnp.sum(weighted, axis=0, keepdims=True)
            score_grad = (weighted - probs * delta).astype(low)
            dv_acc[keys, :] += mm(probs.astype(low), grads)
            dk_acc[keys, :] += mm(score_grad, queries)
            dq = mm_tn(score_grad, key_rows) * inverse
            dq = dq * cos_ref[here, :] - pltpu.roll(dq, HEAD_DIM // 2, 1) * sin_ref[here, :]
            dq = dq * qgain_ref[:, cols]
            dq_buf[here, cols] = dq
            sums_buf[0, here, :] += qproj_ref[here, cols] * dq
        dk = dk_acc[...] * inverse
        dk = dk * cos_ref[...] - pltpu.roll(dk, HEAD_DIM // 2, 1) * sin_ref[...]
        dk = dk * kgain_ref[:, cols]
        dk_buf[:, cols] = dk
        sums_buf[1] += kproj_ref[:, cols] * dk
        dv_low[:, cols] = dv_acc[...].astype(low)

        @pl.when(h == 0)
        def _():
            block_near.wait_recv()
            block_far.wait_recv()
            shared_send[...] = (
                blocks[across].astype(jnp.float32) + blocks_recv[1].astype(jnp.float32)
            ).astype(low)
            block_across.start()

        @pl.when(h == heads - 1)
        def _():
            block_across.wait()
            shared_send[...] = (
                blocks[me].astype(jnp.float32)
                + blocks_recv[0].astype(jnp.float32)
                + blocks_xrecv[...].astype(jnp.float32)
            ).astype(low)
            start_exchange(2)

        return carry

    lax.fori_loop(0, heads, head_step, 0)

    lane = lax.broadcasted_iota(jnp.int32, (length, HEAD_DIM), 1)
    both = jnp.where(
        lane < 4,
        jnp.sum(sums_buf[0], axis=1, keepdims=True),
        jnp.sum(sums_buf[1], axis=1, keepdims=True),
    )
    ex_send[...] = jnp.transpose(both)[:8]
    swaps = [
        remote(ex_send, ex_recv.at[i], es_sem.at[i], er_sem.at[i], other)
        for i, other in enumerate((beside, across, far))
    ]
    for swap in swaps:
        swap.start()
    for load in loads:
        load.wait()
    for swap in swaps:
        swap.wait_recv()
    total = (ex_send[...] + ex_recv[0] + ex_recv[1] + ex_recv[2]) * (1.0 / (4 * heads_width))
    wide = jnp.concatenate(
        [
            jnp.broadcast_to(total[:1], (HEAD_DIM // 2, length)),
            jnp.broadcast_to(total[4:5], (HEAD_DIM // 2, length)),
        ],
        axis=0,
    )
    sums_buf[0] = jnp.transpose(wide)
    for dn, proj, target, at in (
        (dq_buf, qproj_ref, dq_low, 0), (dk_buf, kproj_ref, dk_low, HEAD_DIM // 2),
    ):
        scale = scale_ref[:, at : at + 1]
        means = sums_buf[0, :, at : at + 1]
        target[...] = (scale * dn[...] - proj[...] * (scale * scale * scale * means)).astype(low)

    dmid_part = (
        mm_nt(eq_ref[...], dq_low[...]) + mm_nt(ek_ref[...], dk_low[...])
        + mm_nt(ev_ref[...], dv_low[...])
    )
    dmid_send[...] = dmid_part.astype(low)
    dmid_near = remote(dmid_send, dmid_recv, one_s.at[3], one_r.at[3], beside)
    dmid_across = remote(dmid_xsend, dmid_xrecv, one_s.at[4], one_r.at[4], across)
    dmid_near.start()

    def reduce_beside(c):
        return remote(bsend.at[c], brecv.at[c], bs_sem.at[c], br_sem.at[c], beside)

    def reduce_across(c):
        return remote(xsend.at[c], xrecv.at[c], xs_sem.at[c], xr_sem.at[c], across)

    def chunk_of(buffer, c):
        return jnp.concatenate(
            [buffer[pl.ds(pl.multiple_of(o * rows + c * part, part), part), :] for o in order], axis=0
        )

    def stage_partial(c):
        parts = [chunk_of(buffer, c) for buffer in (dq_low, dk_low, dv_low)]
        tile = TILE

        def one(j, carry):
            at = pl.ds(pl.multiple_of(j * tile, tile), tile)
            value = (
                mm_nt(parts[0], wq[at, :]) + mm_nt(parts[1], wk[at, :]) + mm_nt(parts[2], wv[at, :])
            ).astype(low)
            own_buf[c, :, at] = value[:part]
            xsend[c, :, at] = value[part : 2 * part]
            bsend[c, 0, :, at] = value[2 * part : 3 * part]
            bsend[c, 1, :, at] = value[3 * part :]
            return carry

        lax.fori_loop(0, width // tile, one, 0)
        reduce_beside(c).start()

    def stage_pair(c):
        reduce_beside(c).wait_recv()
        xsend[c] = (xsend[c].astype(jnp.float32) + brecv[c, 1].astype(jnp.float32)).astype(low)
        reduce_across(c).start()
        own_buf[c] = (own_buf[c].astype(jnp.float32) + brecv[c, 0].astype(jnp.float32)).astype(low)

    def partial_step(i, carry):
        @pl.when(i < chunks)
        def _():
            stage_partial(i)

        @pl.when(i == 0)
        def _():
            dmid_near.wait_recv()
            dmid_xsend[...] = (
                dmid_send[...].astype(jnp.float32) + dmid_recv[...].astype(jnp.float32)
            ).astype(low)
            dmid_across.start()

        @pl.when(i > 0)
        def _():
            stage_pair(i - 1)

        return carry

    lax.fori_loop(0, chunks + 1, partial_step, 0)

    mids = mids_ref[...]
    for i, buffer in enumerate((dq_low, dk_low, dv_low)):
        heads_send[:, i * heads_width : (i + 1) * heads_width] = (
            adapter_scale_factor * mm_tn(mids, buffer[...])[i * 16 : (i + 1) * 16]
        ).astype(low)
    start_exchange(1)
    dmid_across.wait_recv()
    dmid = (
        dmid_xsend[...].astype(jnp.float32) + dmid_xrecv[...].astype(jnp.float32)
    ).astype(low)
    inward_grad = mm(dmid, full[...])
    for t in range(4):
        for g in range(groups):
            at = slice((g * 4 + t) * cols_each, (g * 4 + t + 1) * cols_each)
            inward_send[g, t] = inward_grad[:, at]
    start_exchange(3)
    dmid_xsend_ready = dmid
    ex_dmid = dmid_xsend_ready
    dmid_across.wait_send()
    dmid_xsend[...] = ex_dmid

    def finish_step(c, carry):
        reduce_across(c).wait_recv()
        here = pl.ds(pl.multiple_of(c * part, part), part)
        tgrad_ref[here, :] = (
            hgrad_ref[here, :] + own_buf[c].astype(jnp.float32) + xrecv[c].astype(jnp.float32)
        )
        return carry

    mine = pl.ds(pl.multiple_of(me * rows, rows), rows)
    extra = mm_tn(dmid_xsend[:, mine], shrink_ref[...])
    lax.fori_loop(0, chunks, finish_step, 0)
    tgrad_ref[...] += extra
    for c in range(chunks):
        reduce_beside(c).wait_send()
        reduce_across(c).wait_send()
    for copy in (block_near, block_far, dmid_near, *swaps):
        copy.wait_send()
    for number in range(4):
        end_exchange(number)


def back(
    qrot, krot, value, dmixed, qproj, kproj, scale, qgain, kgain, cos, sin, start_row,
    wq, wk, wv, shrink, eq, ek, ev, mids, full, hgrad, chosen, gso, geg, geu, gsd, gsgu, geo, ged,
):
    rows, width = hgrad.shape
    heads_width, units = wq.shape[1], geg.shape[1]
    length = 4 * rows
    part = rows // CHUNKS
    groups = lax.axis_size("dp")
    cols_each = width // (4 * groups)
    split_width = heads_width + 3 * units + 128
    vmem = pl.BlockSpec(memory_space=pltpu.VMEM)
    hbm = pl.BlockSpec(memory_space=pl.ANY)
    low, f32 = jnp.bfloat16, jnp.float32
    shape = jax.ShapeDtypeStruct
    dma = pltpu.SemaphoreType.DMA
    buf = pltpu.VMEM
    return pl.pallas_call(
        back_body,
        in_specs=[vmem] * 12 + [hbm] * 3 + [vmem] * 5 + [hbm] + [vmem] * 9,
        out_specs=[vmem] + [hbm] * 4,
        out_shape=[
            shape((rows, width), f32),
            shape((groups, 16, split_width), low),
            shape((groups, 16, 3 * heads_width), low),
            shape((groups, 64, cols_each), low),
            shape((groups, 48, cols_each), f32),
        ],
        scratch_shapes=[
            buf(wq.shape, low), buf(wk.shape, low), buf(wv.shape, low), buf(full.shape, low),
            dma((4,)),
            buf((length, heads_width), f32), buf((length, heads_width), f32),
            buf((length, heads_width), low), buf((length, heads_width), low),
            buf((length, heads_width), low),
            buf((length, HEAD_DIM), f32), buf((length, HEAD_DIM), f32),
            buf((2, length, HEAD_DIM), f32),
            buf((16, split_width), low), buf((16, 3 * heads_width), low),
            buf((4, groups, 64, cols_each), low), buf((2, groups, 64, cols_each), low),
            buf((groups, 64, cols_each), low), buf((groups, 64, cols_each), low),
            buf((groups, 4, 48, cols_each), f32),
            buf((8, length), f32), buf((3, 8, length), f32),
            buf((48, length), low), buf((48, length), low), buf((48, length), low),
            buf((48, length), low),
            buf((CHUNKS, part, width), low), buf((CHUNKS, part, width), low),
            buf((CHUNKS, part, width), low),
            buf((CHUNKS, 2, part, width), low), buf((CHUNKS, 2, part, width), low),
            dma((3,)), dma((3,)), dma((CHUNKS,)), dma((CHUNKS,)), dma((CHUNKS,)), dma((CHUNKS,)),
            dma((5,)), dma((5,)),
        ] + [dma((groups,))] * 8 + [dma((4,))],
        cost_estimate=pl.CostEstimate(
            flops=2 * length * heads_width * (3 * width + 5 * length),
            bytes_accessed=2 * width * (3 * heads_width + 3 * length), transcendentals=0,
        ),
        compiler_params=pltpu.CompilerParams(
            collective_id=2, has_side_effects=True, vmem_limit_bytes=67043328
        ),
        name="attention_back_to_tokens",
    )(qrot, krot, value, dmixed, qproj, kproj, scale, qgain, kgain, cos, sin, start_row,
      wq, wk, wv, shrink, eq, ek, ev, mids, full, hgrad, chosen, gso, geg, geu, gsd, gsgu, geo, ged)


def finish_body(split_ref, heads_ref, shared_ref, inward_ref, *outs):
    groups = split_ref.shape[0]
    tag = split_ref.shape[2] - 128
    sets = outs[0].shape[0]
    tags = [split_ref[g, :, tag : tag + 1].astype(jnp.float32) for g in range(groups)]

    def add_up(source, target, first, step=512):
        count, high, wide = target.shape
        for at in range(0, wide, step):
            end = min(wide, at + step)
            pieces = [source(g, first + at, first + end).astype(jnp.float32) for g in range(groups)]
            for c in range(count):
                total = jnp.where(tags[0] == c, pieces[0], 0.0)
                for g in range(1, groups):
                    total += jnp.where(tags[g] == c, pieces[g], 0.0)
                target[c, :, at:end] = total

    sq, eq, sk, ek, sv, ev, so, eo, sg, eg, su, eu, sd, ed = outs
    heads_width = eq.shape[2]
    units = eg.shape[2]
    for i, target in enumerate((eq, ek, ev)):
        add_up(lambda g, a, b: heads_ref[g, :, a:b], target, i * heads_width)
    at = 0
    for target in (so, eg, eu, sd):
        add_up(lambda g, a, b: split_ref[g, :, a:b], target, at)
        at += target.shape[2]
    for i, target in enumerate((sq, sk, sv)):
        add_up(lambda g, a, b: inward_ref[g, i * 16 : (i + 1) * 16, a:b], target, 0)
    for i, target in enumerate((eo, sg, su, ed)):
        add_up(lambda g, a, b: shared_ref[g, i * 16 : (i + 1) * 16, a:b], target, 0)


def finish(split, by_heads, shared, inward, sets, heads_width, units):
    cols = shared.shape[2]
    vmem = pl.BlockSpec(memory_space=pltpu.VMEM)
    widths = (
        cols, heads_width, cols, heads_width, cols, heads_width, heads_width, cols,
        cols, units, cols, units, units, cols,
    )
    return pl.pallas_call(
        finish_body,
        in_specs=[vmem] * 4,
        out_specs=[vmem] * 14,
        out_shape=[jax.ShapeDtypeStruct((sets, 16, w), jnp.float32) for w in widths],
        compiler_params=pltpu.CompilerParams(vmem_limit_bytes=67043328),
        name="sum_by_set",
    )(split, by_heads, shared, inward)


def per_device(
    tokens,
    cotangent,
    segment_ids,
    adapter_set,
    w_query,
    w_key,
    w_value,
    w_out,
    w_gate,
    w_up,
    w_down,
    query_gain,
    key_gain,
    mixer_gain,
    feed_gain,
    shrink_query,
    expand_query,
    shrink_key,
    expand_key,
    shrink_value,
    expand_value,
    shrink_out,
    expand_out,
    shrink_gate,
    expand_gate,
    shrink_up,
    expand_up,
    shrink_down,
    expand_down,
):
    length = 4 * tokens.shape[0]
    (
        shrink_rows, expand_query_rows, expand_key_rows, expand_value_rows, out_shrink, out_expand,
        gate_up_shrink, gate_expand, up_expand, down_shrink, down_expand,
        query_gains, key_gains, mixer_gains, feed_gains, start_col, start_row, set_row,
    ) = pick(
        adapter_set, segment_ids, (query_gain, key_gain, mixer_gain, feed_gain),
        (
            shrink_query, expand_query, shrink_key, expand_key, shrink_value, expand_value,
            shrink_out, expand_out, shrink_gate, expand_gate, shrink_up, expand_up,
            shrink_down, expand_down,
        ),
    )
    cosine_table, sine_table = rotary_constants(length, HEAD_DIM)
    cosine_table, sine_table = jnp.asarray(cosine_table), jnp.asarray(sine_table)
    (
        mixed, query_rot, key_rot, value_low, query_proj, key_proj, scales, qkv_middle, full_tokens,
    ) = front(
        tokens, w_query, w_key, w_value, shrink_rows,
        expand_query_rows, expand_key_rows, expand_value_rows,
        query_gains, key_gains, cosine_table, sine_table, start_col,
    )
    (
        block_output, hidden_grad, mixed_grad, grad_down_shrink, gradient_gate_widened,
        gradient_up_widened, grad_out_shrink, owner_gate_up, owner_out, owner_down,
    ) = middle(
        mixed, tokens, cotangent, w_out, w_gate, w_up, w_down, mixer_gains, feed_gains,
        out_shrink, out_expand, gate_up_shrink, gate_expand, up_expand, down_shrink, down_expand,
    )
    token_grads, split, by_heads, shared, inward = back(
        query_rot, key_rot, value_low, mixed_grad.reshape(mixed.shape), query_proj, key_proj, scales,
        query_gains, key_gains, cosine_table, sine_table, start_row,
        w_query, w_key, w_value, shrink_rows, expand_query_rows, expand_key_rows, expand_value_rows,
        qkv_middle, full_tokens.reshape(length, -1), hidden_grad, set_row,
        grad_out_shrink, gradient_gate_widened, gradient_up_widened, grad_down_shrink,
        owner_gate_up, owner_out, owner_down,
    )
    adapter_grads = finish(
        split, by_heads, shared, inward, shrink_query.shape[0], w_query.shape[1], w_gate.shape[1]
    )
    return (block_output, token_grads, *adapter_grads)


def solution(mesh):
    in_specs = (
        P(("dp", "tensor"), None),
        P(("dp", "tensor"), None),
        P("dp", None),
        P("dp"),
        P(None, "tensor"),
        P(None, "tensor"),
        P(None, "tensor"),
        P("tensor", None),
        P(None, "tensor"),
        P(None, "tensor"),
        P("tensor", None),
        P("tensor"),
        P("tensor"),
        P(),
        P(),
        P(),
        P(None, None, "tensor"),
        P(),
        P(None, None, "tensor"),
        P(),
        P(None, None, "tensor"),
        P(None, None, "tensor"),
        P(),
        P(),
        P(None, None, "tensor"),
        P(),
        P(None, None, "tensor"),
        P(None, None, "tensor"),
        P(),
    )
    out_specs = (
        P(("dp", "tensor"), None),
        P(("dp", "tensor"), None),
        P(None, None, ("dp", "tensor")),
        P(None, None, "tensor"),
        P(None, None, ("dp", "tensor")),
        P(None, None, "tensor"),
        P(None, None, ("dp", "tensor")),
        P(None, None, "tensor"),
        P(None, None, "tensor"),
        P(None, None, ("dp", "tensor")),
        P(None, None, ("dp", "tensor")),
        P(None, None, "tensor"),
        P(None, None, ("dp", "tensor")),
        P(None, None, "tensor"),
        P(None, None, "tensor"),
        P(None, None, ("dp", "tensor")),
    )
    return jax.shard_map(
        per_device, mesh=mesh, in_specs=in_specs, out_specs=out_specs, check_vma=False
    )
```

```python
import functools
import jax
import jax.numpy as jnp
import numpy as np
from jax import lax
from jax.experimental import pallas as pl
from jax.experimental.pallas import tpu as pltpu
from jax.sharding import PartitionSpec as P

HEAD_DIM = 128
DOC_MOST = 512
ATT_ROWS = 256
rotary_base = 500000.0
NEG = -1e30
LOG2E = 1.4426950408889634


def rotary_constants(length, head_dim):
    half = head_dim // 2
    frequency = np.float32(rotary_base) ** (
        -(np.arange(half, dtype=np.float32) * np.float32(2.0) / np.float32(head_dim))
    )
    angles = np.arange(length, dtype=np.float32)[:, None] * frequency.astype(np.float32)[None, :]
    cosine = np.cos(angles.astype(np.float64)).astype(np.float32)
    sine = np.sin(angles.astype(np.float64)).astype(np.float32)
    return (
        np.concatenate([cosine, cosine], axis=1),
        np.concatenate([-sine, sine], axis=1),
    )


def key_window(block, rows):
    first = max(0, (block * rows - (DOC_MOST - 1)) // rows) * rows
    return first, (block + 1) * rows


epsilon = 1e-06
adapter_scale_factor = 0.5


def pick_body(
    set_ref, seg_ref, qgain, kgain, mgain, fgain,
    sq, eq, sk, ek, sv, ev, so, eo, sg, eg, su, eu, sd, ed,
    shrink_out, eq_out, ek_out, ev_out, so_out, eo_out, sgu_out, eg_out, eu_out, sd_out, ed_out,
    qgain_out, kgain_out, mgain_out, fgain_out, start_col, start_row, set_out,
):
    rank = sq.shape[1]

    def scaled(ref):
        return (adapter_scale_factor * ref[0].astype(jnp.float32)).astype(jnp.bfloat16)

    for i, ref in enumerate((sq, sk, sv)):
        shrink_out[i * rank : (i + 1) * rank, :] = ref[0]
    for i, (ref, target) in enumerate(((eq, eq_out), (ek, ek_out), (ev, ev_out))):
        target[...] = jnp.zeros_like(target)
        target[i * rank : (i + 1) * rank, :] = scaled(ref)
    for i, (ref, target) in enumerate(((eg, eg_out), (eu, eu_out))):
        target[...] = jnp.zeros_like(target)
        target[i * rank : (i + 1) * rank, :] = scaled(ref)
    so_out[...] = so[0]
    sd_out[...] = sd[0]
    eo_out[...] = scaled(eo)
    ed_out[...] = scaled(ed)
    sgu_out[:rank, :] = sg[0]
    sgu_out[rank:, :] = su[0]
    for ref, target in ((qgain, qgain_out), (kgain, kgain_out), (mgain, mgain_out), (fgain, fgain_out)):
        target[...] = ref[...].astype(jnp.float32).reshape(target.shape)
    length = seg_ref.shape[1]
    row = seg_ref[...].astype(jnp.float32)
    col = jnp.transpose(jnp.broadcast_to(row, (HEAD_DIM, length)))[:, :1]
    start_col[...] = jnp.sum(
        jnp.where(row < col, 1.0, 0.0), axis=1, keepdims=True
    ).astype(jnp.int32)
    start_row[...] = jnp.sum(
        jnp.where(col < row, 1.0, 0.0), axis=0, keepdims=True
    ).astype(jnp.int32)
    set_out[...] = jnp.full(set_out.shape, set_ref[0], jnp.int32).astype(jnp.float32)


def pick(adapter_set, segment_ids, gains, adapters):
    whole = lambda a: pl.BlockSpec(a.shape, lambda i, s: (0,) * a.ndim)
    chosen = lambda a: pl.BlockSpec((1,) + a.shape[1:], lambda i, s: (s[0], 0, 0))
    length = segment_ids.shape[1]
    rank, width = adapters[0].shape[1:]
    here, units = adapters[1].shape[2], adapters[9].shape[2]
    low, f32 = jnp.bfloat16, jnp.float32
    shapes = [
        ((3 * rank, width), low), ((3 * rank, here), low), ((3 * rank, here), low),
        ((3 * rank, here), low), ((rank, here), low), ((rank, width), low), ((2 * rank, width), low),
        ((2 * rank, units), low), ((2 * rank, units), low), ((rank, units), low), ((rank, width), low),
        ((1, here), f32), ((1, here), f32), ((1, width), f32), ((1, width), f32),
        ((length, 1), jnp.int32), ((1, length), jnp.int32), ((1, 128), f32),
    ]
    return pl.pallas_call(
        pick_body,
        grid_spec=pltpu.PrefetchScalarGridSpec(
            num_scalar_prefetch=1,
            grid=(1,),
            in_specs=[whole(segment_ids)] + [whole(g) for g in gains] + [chosen(a) for a in adapters],
            out_specs=[pl.BlockSpec(s, lambda i, _: (0,) * 2) for s, _ in shapes],
        ),
        out_shape=[jax.ShapeDtypeStruct(s, t) for s, t in shapes],
        compiler_params=pltpu.CompilerParams(vmem_limit_bytes=67043328),
        name="pick_adapters",
    )(adapter_set, segment_ids, *gains, *adapters)


CHUNKS = 4
TILE = 1024
EXTRA = 128
NT = (((1,), (1,)), ((), ()))
TN = (((0,), (0,)), ((), ()))
MESH_ID = pl.DeviceIdType.MESH
MIDDLE_ORDER = (
    ("S2", 4), ("S4", 7), ("P0", 1), ("P4", 8), ("P2", 4), ("F3", 6), ("F1", 3), ("S3", 5),
    ("S5", 9), ("S1", 2), ("S0", 0),
)


def mm(left, right):
    return jnp.dot(left, right, preferred_element_type=jnp.float32)


def mm_nt(left, right):
    return lax.dot_general(left, right, NT, preferred_element_type=jnp.float32)


def mm_tn(left, right):
    return lax.dot_general(left, right, TN, preferred_element_type=jnp.float32)


def partners():
    me = lax.axis_index("tensor")
    group = lax.axis_index("dp")
    beside = me + 1 - 2 * lax.rem(me, 2)
    across = lax.rem(me + 2, 4)
    return me, group, beside, across


def greet(group, beside, across):
    barrier = pltpu.get_barrier_semaphore()
    for other in (beside, across):
        pl.semaphore_signal(barrier, inc=1, device_id=(group, other), device_id_type=MESH_ID)
    pl.semaphore_wait(barrier, 2)


def middle_body(
    mixed_ref, tokens_ref, cot_ref, w_out_hbm, w_gate_hbm, w_up_hbm, w_down_hbm,
    mgain_ref, fgain_ref, so_ref, eo_ref, sgu_ref, eg_ref, eu_ref, sd_ref, ed_ref,
    out_ref, hgrad_ref, mgrad_ref, gsd_ref, geg_ref, geu_ref, gsgu_ref, geo_ref, ged_ref,
    w_out, w_gate, w_up, w_down, wsem,
    rows_buf, own_buf, xsend, xrecv, bsend, brecv,
    gate_buf, up_buf, temp_a, temp_b, mgu_buf, mixer_buf, hidden_buf, mout_buf,
    xs_sem, xr_sem, bs_sem, br_sem, gxs_sem, gxr_sem, gbs_sem, gbr_sem, fs_sem, fr_sem,
):
    me, group, beside, across = partners()
    chunks, part, width = rows_buf.shape[0], rows_buf.shape[2], rows_buf.shape[3]
    units = w_gate.shape[1]
    heads_width = w_out.shape[0]
    far = lax.rem(beside + 2, 4)
    order = (me, across, beside, far)
    loads = [
        pltpu.make_async_copy(source, target, wsem.at[i])
        for i, (source, target) in enumerate(
            ((w_out_hbm, w_out), (w_gate_hbm, w_gate), (w_up_hbm, w_up), (w_down_hbm, w_down))
        )
    ]
    for load in loads:
        load.start()
    for ref in (gsd_ref, geg_ref, geu_ref, gsgu_ref, geo_ref, ged_ref):
        ref[...] = jnp.zeros_like(ref)
    greet(group, beside, across)

    def remote(source, target, ssem, rsem, other):
        return pltpu.make_async_remote_copy(
            src_ref=source, dst_ref=target, send_sem=ssem, recv_sem=rsem,
            device_id=(group, other), device_id_type=MESH_ID,
        )

    def gather_across(c):
        return remote(rows_buf.at[c, 0], rows_buf.at[c, 1], gxs_sem.at[c], gxr_sem.at[c], across)

    def gather_beside(c):
        return remote(rows_buf.at[c, 0], rows_buf.at[c, 2], gbs_sem.at[c], gbr_sem.at[c], beside)

    def gather_forward(c):
        return remote(rows_buf.at[c, 1], rows_buf.at[c, 3], fs_sem.at[c], fr_sem.at[c], beside)

    def reduce_beside(c):
        return remote(bsend.at[c], brecv.at[c], bs_sem.at[c], br_sem.at[c], beside)

    def reduce_across(c):
        return remote(xsend.at[c], xrecv.at[c], xs_sem.at[c], xr_sem.at[c], across)

    def store_partial(c, columns, value):
        low = value.astype(jnp.bfloat16)
        own_buf[c, :, columns] = low[:part]
        xsend[c, :, columns] = low[part : 2 * part]
        bsend[c, 0, :, columns] = low[2 * part : 3 * part]
        bsend[c, 1, :, columns] = low[3 * part :]

    def gathered(c):
        return rows_buf[c].reshape(4 * part, width)

    def forward_stage(c):
        gather_across(c).wait_recv()
        gather_forward(c).start()

    def pair_stage(c):
        reduce_beside(c).wait_recv()
        own_buf[c] = (
            own_buf[c].astype(jnp.float32) + brecv[c, 0].astype(jnp.float32)
        ).astype(jnp.bfloat16)
        xsend[c] = (
            xsend[c].astype(jnp.float32) + brecv[c, 1].astype(jnp.float32)
        ).astype(jnp.bfloat16)
        reduce_across(c).start()

    def totals(c):
        reduce_across(c).wait_recv()
        main = own_buf[c, :, :width].astype(jnp.float32) + xrecv[c, :, :width].astype(jnp.float32)
        side = own_buf[c, :, width : width + 32].astype(jnp.float32) + xrecv[
            c, :, width : width + 32
        ].astype(jnp.float32)
        return main, side.astype(jnp.bfloat16)

    def own_rows(c):
        return pl.ds(pl.multiple_of(c * part, part), part)

    def send_rows(c, value, again):
        if again:
            gather_across(c).wait_send()
            gather_beside(c).wait_send()
        rows_buf[c, 0] = value
        gather_across(c).start()
        gather_beside(c).start()

    def chunk_rows(c):
        return pl.ds(pl.multiple_of(c * 4 * part, 4 * part), 4 * part)

    def tiles(total, tile, body):
        def step(j, carry):
            body(pl.ds(pl.multiple_of(j * tile, tile), tile))
            return carry

        lax.fori_loop(0, total // tile, step, 0)

    def mixed_chunk(c):
        return jnp.concatenate([mixed_ref[o, c] for o in order], axis=0)

    def stage_mixer(c):
        @pl.when(c == 0)
        def _():
            loads[0].wait()

        rows = mixed_chunk(c)
        store_partial(c, slice(width, width + 16), mm_nt(rows, so_ref[...]))
        tiles(width, TILE, lambda cols: store_partial(c, cols, mm(rows, w_out[:, cols])))
        reduce_beside(c).start()

    def stage_hidden(c):
        main, side = totals(c)
        mid = side[:, :16]
        mout_buf[c] = mid
        mixer = main + mm(mid, eo_ref[...])
        mixer_buf[own_rows(c), :] = mixer
        factor = lax.rsqrt(jnp.mean(mixer * mixer, axis=1, keepdims=True) + epsilon)
        hidden = tokens_ref[own_rows(c), :].astype(jnp.float32) + mixer * factor * mgain_ref[...]
        hidden_buf[own_rows(c), :] = hidden
        send_rows(c, hidden.astype(jnp.bfloat16), False)

    def arrive(c):
        gather_beside(c).wait_recv()
        gather_forward(c).wait_recv()

    def stage_units(c):
        @pl.when(c == 0)
        def _():
            for load in loads[1:]:
                load.wait()

        arrive(c)
        mids = mm_nt(gathered(c), sgu_ref[...]).astype(jnp.bfloat16)
        mgu_buf[c] = mids

        def unit_tile(cols):
            rows = gathered(c)
            gate = mm(rows, w_gate[:, cols]) + mm(mids, eg_ref[:, cols])
            up = mm(rows, w_up[:, cols]) + mm(mids, eu_ref[:, cols])
            gate_buf[chunk_rows(c), cols] = gate.astype(jnp.bfloat16)
            up_buf[chunk_rows(c), cols] = up.astype(jnp.bfloat16)
            sig = 1.0 / (1.0 + jnp.exp(-gate))
            temp_a[:, cols] = (gate * sig * up).astype(jnp.bfloat16)

        tiles(units, TILE // 2, unit_tile)
        gather_forward(c).wait_send()
        reduce_beside(c).wait_send()
        reduce_across(c).wait_send()
        inner = temp_a[...]
        store_partial(c, slice(width, width + 16), mm_nt(inner, sd_ref[...]))
        tiles(width, TILE, lambda cols: store_partial(c, cols, mm(temp_a[...], w_down[:, cols])))
        reduce_beside(c).start()

    def norm_back_rows(values, gains, grads):
        factor = lax.rsqrt(jnp.mean(values * values, axis=1, keepdims=True) + epsilon)
        weighted = grads * gains
        return factor * weighted - values * (
            factor * factor * factor * jnp.mean(values * weighted, axis=1, keepdims=True)
        )

    def stage_feed(c):
        main, side = totals(c)
        mid = side[:, :16]
        feed = main + mm(mid, ed_ref[...])
        factor = lax.rsqrt(jnp.mean(feed * feed, axis=1, keepdims=True) + epsilon)
        gains = fgain_ref[...]
        out_ref[own_rows(c), :] = (hidden_buf[own_rows(c), :] + feed * factor * gains).astype(
            jnp.bfloat16
        )
        grad = norm_back_rows(feed, gains, cot_ref[own_rows(c), :].astype(jnp.float32))
        grad = grad.astype(jnp.bfloat16)
        send_rows(c, grad, True)
        ged_ref[...] += mm_tn(mid, grad)

    def stage_units_back(c):
        arrive(c)
        dmid = mm_nt(gathered(c), ed_ref[...]).astype(jnp.bfloat16)
        mids = mgu_buf[c]

        def unit_tile(cols):
            rows = gathered(c)
            inner_grad = mm_nt(rows, w_down[cols, :]) + mm(dmid, sd_ref[:, cols])
            gate = gate_buf[chunk_rows(c), cols].astype(jnp.float32)
            up = up_buf[chunk_rows(c), cols].astype(jnp.float32)
            sig = 1.0 / (1.0 + jnp.exp(-gate))
            silu = gate * sig
            gate_grad = (inner_grad * up * (sig + silu * (1.0 - sig))).astype(jnp.bfloat16)
            up_grad = (inner_grad * silu).astype(jnp.bfloat16)
            temp_a[:, cols] = gate_grad
            temp_b[:, cols] = up_grad
            gsd_ref[:, cols] += mm_tn(dmid, (silu * up).astype(jnp.bfloat16))
            geg_ref[:, cols] += mm_tn(mids, gate_grad)
            geu_ref[:, cols] += mm_tn(mids, up_grad)

        tiles(units, TILE // 2, unit_tile)
        gather_forward(c).wait_send()
        reduce_beside(c).wait_send()
        reduce_across(c).wait_send()
        store_partial(
            c,
            slice(width, width + 32),
            mm_nt(temp_a[...], eg_ref[...]) + mm_nt(temp_b[...], eu_ref[...]),
        )

        def width_tile(cols):
            store_partial(
                c, cols, mm_nt(temp_a[...], w_gate[cols, :]) + mm_nt(temp_b[...], w_up[cols, :])
            )

        tiles(width, TILE // 2, width_tile)
        reduce_beside(c).start()

    def stage_mixer_grad(c):
        main, side = totals(c)
        grads = cot_ref[own_rows(c), :].astype(jnp.float32) + main + mm(side, sgu_ref[...])
        hgrad_ref[own_rows(c), :] = grads
        mixer_grad = norm_back_rows(mixer_buf[own_rows(c), :], mgain_ref[...], grads)
        mixer_grad = mixer_grad.astype(jnp.bfloat16)
        mgrad_ref[c] = mixer_grad
        geo_ref[...] += mm_tn(mout_buf[c], mixer_grad)
        gsgu_ref[...] += mm_tn(side, hidden_buf[own_rows(c), :].astype(jnp.bfloat16))
        gather_across(c).wait_send()
        gather_beside(c).wait_send()
        reduce_beside(c).wait_send()
        reduce_across(c).wait_send()

    stages = {
        "S0": stage_mixer, "S1": stage_hidden, "S2": stage_units, "S3": stage_feed,
        "S4": stage_units_back, "S5": stage_mixer_grad,
        "P0": pair_stage, "P2": pair_stage, "P4": pair_stage,
        "F1": forward_stage, "F3": forward_stage,
    }

    def step(i, carry):
        for name, delay in MIDDLE_ORDER:

            @pl.when((i >= delay) & (i < delay + chunks))
            def _():
                stages[name](i - delay)

        return carry

    lax.fori_loop(0, chunks + max(delay for _, delay in MIDDLE_ORDER), step, 0)


def middle(mixed, tokens, cot, w_out, w_gate, w_up, w_down, mgain, fgain, so, eo, sgu, eg, eu, sd, ed):
    rows, width = tokens.shape
    heads_width, units = w_out.shape[0], w_gate.shape[1]
    part = rows // CHUNKS
    whole_width = width + EXTRA
    vmem = pl.BlockSpec(memory_space=pltpu.VMEM)
    hbm = pl.BlockSpec(memory_space=pl.ANY)
    low, full = jnp.bfloat16, jnp.float32
    dma = pltpu.SemaphoreType.DMA((CHUNKS,))
    shape = jax.ShapeDtypeStruct
    flops = 2 * 4 * rows * width * (heads_width + 6 * units)
    return pl.pallas_call(
        middle_body,
        in_specs=[vmem] * 3 + [hbm] * 4 + [vmem] * 9,
        out_specs=[vmem] * 9,
        out_shape=[
            shape((rows, width), low), shape((rows, width), full),
            shape((CHUNKS, part, width), low),
            shape((16, units), full), shape((32, units), full), shape((32, units), full),
            shape((32, width), full), shape((16, width), full),
            shape((16, width), full),
        ],
        scratch_shapes=[
            pltpu.VMEM(w_out.shape, low), pltpu.VMEM(w_gate.shape, low),
            pltpu.VMEM(w_up.shape, low), pltpu.VMEM(w_down.shape, low),
            pltpu.SemaphoreType.DMA((4,)),
            pltpu.VMEM((CHUNKS, 4, part, width), low),
            pltpu.VMEM((CHUNKS, part, whole_width), low),
            pltpu.VMEM((CHUNKS, part, whole_width), low),
            pltpu.VMEM((CHUNKS, part, whole_width), low),
            pltpu.VMEM((CHUNKS, 2, part, whole_width), low),
            pltpu.VMEM((CHUNKS, 2, part, whole_width), low),
            pltpu.VMEM((4 * rows, units), low), pltpu.VMEM((4 * rows, units), low),
            pltpu.VMEM((4 * part, units), low), pltpu.VMEM((4 * part, units), low),
            pltpu.VMEM((CHUNKS, 4 * part, 32), low),
            pltpu.VMEM((rows, width), full), pltpu.VMEM((rows, width), full),
            pltpu.VMEM((CHUNKS, part, 16), low),
        ] + [dma] * 10,
        cost_estimate=pl.CostEstimate(
            flops=flops, bytes_accessed=2 * width * (heads_width + 3 * units), transcendentals=0
        ),
        compiler_params=pltpu.CompilerParams(
            collective_id=0, has_side_effects=True, vmem_limit_bytes=67043328
        ),
        name="mixer_to_feed",
    )(mixed.reshape(4, CHUNKS, part, heads_width), tokens, cot, w_out, w_gate, w_up, w_down,
      mgain, fgain, so, eo, sgu, eg, eu, sd, ed)


def attention_scores(first, second, start, first_query, first_key, query_axis):
    scores = lax.dot_general(first, second, NT, preferred_element_type=jnp.float32)
    kpos = lax.broadcasted_iota(jnp.int32, scores.shape, 1 - query_axis) + first_key
    shape = [1, 1]
    shape[query_axis] = scores.shape[query_axis]
    qpos = lax.broadcasted_iota(jnp.int32, shape, query_axis) + first_query
    return jnp.where((kpos <= qpos) & (kpos >= start), scores, NEG)


def front_body(
    tokens_ref, wq_hbm, wk_hbm, wv_hbm, shrink_ref, eq_ref, ek_ref, ev_ref, qgain_ref, kgain_ref,
    cos_ref, sin_ref, start_ref,
    mixed_ref, qrot_ref, krot_ref, value_ref, qproj_ref, kproj_ref, scale_ref, mids_ref, full_hbm,
    wq, wk, wv, wsem, full, lhs, squares, ex_send, ex_recv,
    xs_sem, xr_sem, fs_sem, fr_sem, bs_sem, br_sem, es_sem, er_sem, out_sem,
):
    me, group, beside, across = partners()
    far = lax.rem(beside + 2, 4)
    chunks, part, width = full.shape[1:]
    rows = chunks * part
    length = 4 * rows
    loads = [
        pltpu.make_async_copy(source, target, wsem.at[i])
        for i, (source, target) in enumerate(((wq_hbm, wq), (wk_hbm, wk), (wv_hbm, wv)))
    ]
    for load in loads:
        load.start()
    barrier = pltpu.get_barrier_semaphore()
    for other in (beside, across, far):
        pl.semaphore_signal(barrier, inc=1, device_id=(group, other), device_id_type=MESH_ID)
    pl.semaphore_wait(barrier, 3)

    def remote(source, target, ssem, rsem, other):
        return pltpu.make_async_remote_copy(
            src_ref=source, dst_ref=target, send_sem=ssem, recv_sem=rsem,
            device_id=(group, other), device_id_type=MESH_ID,
        )

    def send_across(c):
        return remote(tokens_ref.at[c], full.at[me, c], xs_sem.at[c], xr_sem.at[c], across)

    def forward(c):
        return remote(full.at[across, c], full.at[across, c], fs_sem.at[c], fr_sem.at[c], beside)

    to_beside = remote(tokens_ref, full.at[me], bs_sem, br_sem, beside)
    for c in range(chunks):
        send_across(c).start()
    to_beside.start()
    full[me] = tokens_ref[...]
    for load in loads:
        load.wait()
    pairs = chunks // 2
    half = rows // 2

    def block_step(b, carry):
        @pl.when(b == 0)
        def _():
            lhs[...] = tokens_ref[...].reshape(rows, width)

        @pl.when(b == 1)
        def _():
            to_beside.wait_recv()
            lhs[...] = full[beside].reshape(rows, width)

        @pl.when(b >= 2)
        def _():
            base = (b - 2) * pairs
            for j in range(pairs):
                send_across(base + j).wait_recv()
                forward(base + j).start()
            for j in range(pairs):
                lhs[j * part : (j + 1) * part] = full[across, base + j]
            for j in range(pairs):
                forward(base + j).wait_recv()
                lhs[half + j * part : half + (j + 1) * part] = full[far, base + j]

        mids = mm_nt(lhs[...], shrink_ref[...]).astype(jnp.bfloat16)
        query = mm(lhs[...], wq[...]) + mm(mids, eq_ref[...])
        key = mm(lhs[...], wk[...]) + mm(mids, ek_ref[...])
        value = (mm(lhs[...], wv[...]) + mm(mids, ev_ref[...])).astype(jnp.bfloat16)
        qsum = jnp.sum(query * query, axis=1, keepdims=True)
        ksum = jnp.sum(key * key, axis=1, keepdims=True)
        lane = lax.broadcasted_iota(jnp.int32, (rows, HEAD_DIM), 1)
        both = jnp.where(lane < 4, qsum, ksum)
        first = jnp.where(b == 0, me, jnp.where(b == 1, beside, across)) * rows
        second = jnp.where(b == 0, me, jnp.where(b == 1, beside, far)) * rows
        first = first + jnp.where(b >= 2, (b - 2) * half, 0)
        second = second + jnp.where(b >= 2, (b - 2) * half, half)
        for start, piece in ((first, slice(0, half)), (second, slice(half, rows))):
            there = pl.ds(pl.multiple_of(start, half), half)
            qproj_ref[there, :] = query[piece]
            kproj_ref[there, :] = key[piece]
            value_ref[there, :] = value[piece]
            mids_ref[there, :] = mids[piece]
            squares[there, :] = both[piece]
        return carry

    lax.fori_loop(0, 4, block_step, 0)
    save = pltpu.make_async_copy(full, full_hbm, out_sem)
    save.start()
    ex_send[...] = jnp.transpose(squares[...])[:8]
    swaps = [
        remote(ex_send, ex_recv.at[i], es_sem.at[i], er_sem.at[i], other)
        for i, other in enumerate((beside, across, far))
    ]
    for swap in swaps:
        swap.start()
    for swap in swaps:
        swap.wait_recv()
    total = ex_send[...] + ex_recv[0] + ex_recv[1] + ex_recv[2]
    factor = lax.rsqrt(total / (4 * wq.shape[1]) + epsilon)
    wide = jnp.concatenate(
        [
            jnp.broadcast_to(factor[:1], (HEAD_DIM // 2, length)),
            jnp.broadcast_to(factor[4:5], (HEAD_DIM // 2, length)),
        ],
        axis=0,
    )
    scale_ref[...] = jnp.transpose(wide)
    heads = wq.shape[1] // HEAD_DIM
    exponent = HEAD_DIM ** (-0.5) * LOG2E
    block_rows = min(ATT_ROWS, length)

    def head_step(h, carry):
        cols = pl.ds(pl.multiple_of(h * HEAD_DIM, HEAD_DIM), HEAD_DIM)
        for source, lane, gain, target in (
            (qproj_ref, 0, qgain_ref, qrot_ref),
            (kproj_ref, HEAD_DIM // 2, kgain_ref, krot_ref),
        ):
            normed = source[:, cols] * scale_ref[:, lane : lane + 1] * gain[:, cols]
            turned = normed * cos_ref[...] + pltpu.roll(normed, HEAD_DIM // 2, 1) * sin_ref[...]
            target[:, cols] = turned.astype(jnp.bfloat16)
        for block in range(length // block_rows):
            low, high = key_window(block, block_rows)
            here = pl.ds(block * block_rows, block_rows)
            keys = pl.ds(low, high - low)
            scores = attention_scores(
                qrot_ref[here, cols], krot_ref[keys, cols], start_ref[here, :],
                block * block_rows, low, 0,
            )
            top = jnp.max(scores, axis=1, keepdims=True)
            weights = jnp.exp2((scores - top) * exponent)
            total = jnp.sum(weights, axis=1, keepdims=True)
            mix = mm(weights.astype(jnp.bfloat16), value_ref[keys, cols])
            mixed_ref[here, cols] = (mix * (1.0 / total)).astype(jnp.bfloat16)
        return carry

    lax.fori_loop(0, heads, head_step, 0)
    for c in range(chunks):
        send_across(c).wait_send()
        forward(c).wait_send()
    to_beside.wait_send()
    for swap in swaps:
        swap.wait_send()
    save.wait()


def front(tokens, wq, wk, wv, shrink, eq, ek, ev, qgain, kgain, cos, sin, start_col):
    rows, width = tokens.shape
    heads_width = wq.shape[1]
    length = 4 * rows
    part = rows // CHUNKS
    vmem = pl.BlockSpec(memory_space=pltpu.VMEM)
    hbm = pl.BlockSpec(memory_space=pl.ANY)
    low, full = jnp.bfloat16, jnp.float32
    shape = jax.ShapeDtypeStruct
    dma = pltpu.SemaphoreType.DMA
    return pl.pallas_call(
        front_body,
        in_specs=[vmem] + [hbm] * 3 + [vmem] * 9,
        out_specs=[vmem] * 8 + [hbm],
        out_shape=[
            shape((length, heads_width), low), shape((length, heads_width), low),
            shape((length, heads_width), low), shape((length, heads_width), low),
            shape((length, heads_width), full), shape((length, heads_width), full),
            shape((length, HEAD_DIM), full), shape((length, shrink.shape[0]), low),
            shape((4, CHUNKS, part, width), low),
        ],
        scratch_shapes=[
            pltpu.VMEM(wq.shape, low), pltpu.VMEM(wk.shape, low), pltpu.VMEM(wv.shape, low),
            dma((3,)),
            pltpu.VMEM((4, CHUNKS, part, width), low), pltpu.VMEM((rows, width), low),
            pltpu.VMEM((length, HEAD_DIM), full), pltpu.VMEM((8, length), full),
            pltpu.VMEM((3, 8, length), full),
            dma((CHUNKS,)), dma((CHUNKS,)), dma((CHUNKS,)), dma((CHUNKS,)), dma, dma,
            dma((3,)), dma((3,)), dma,
        ],
        cost_estimate=pl.CostEstimate(
            flops=2 * length * heads_width * (3 * width + 2 * length),
            bytes_accessed=2 * width * (3 * heads_width + length), transcendentals=0,
        ),
        compiler_params=pltpu.CompilerParams(
            collective_id=1, has_side_effects=True, vmem_limit_bytes=67043328
        ),
        name="gather_project_attend",
    )(tokens.reshape(CHUNKS, part, width), wq, wk, wv, shrink, eq, ek, ev, qgain, kgain,
      cos, sin, start_col)


def back_body(
    qrot_ref, krot_ref, value_ref, mixed_ref, mgrad_ref, qproj_ref, kproj_ref, scale_ref, qgain_ref,
    kgain_ref, cos_ref, sin_ref, start_ref, wq_hbm, wk_hbm, wv_hbm, w_out_hbm, so_ref, eo_ref,
    shrink_ref,
    eq_ref, ek_ref, ev_ref, mids_ref, full_hbm, hgrad_ref, set_ref,
    geg_ref, geu_ref, gsd_ref, gsgu_ref, geo_ref, ged_ref,
    tgrad_ref, split_hbm, heads_hbm, shared_hbm, inward_hbm,
    wq, wk, wv, w_out, full, wsem, rows_in, lhs, dmixed, gso,
    dq_buf, dk_buf, dv_buf, dq_low, dk_low, dv_low, sums_buf,
    split_send, heads_send, blocks, blocks_recv, blocks_xrecv, shared_send, inward_send,
    ex_send, ex_recv, dmid_send, dmid_recv, dmid_xsend, dmid_xrecv,
    own_buf, xsend, xrecv, bsend, brecv,
    gx_s, gx_r, gf_s, gf_r, gb_s, gb_r,
    es_sem, er_sem, xs_sem, xr_sem, bs_sem, br_sem, one_s, one_r,
    sp_s, sp_r, hd_s, hd_r, sh_s, sh_r, in_s, in_r, local_sem,
):
    me, group, beside, across = partners()
    far = lax.rem(beside + 2, 4)
    order = (me, across, beside, far)
    groups = split_hbm.shape[0]
    chunks, part, width = own_buf.shape
    rows = chunks * part
    length = 4 * rows
    heads_width = wq.shape[1]
    units = geg_ref.shape[1]
    cols_each = blocks.shape[3]
    loads = [
        pltpu.make_async_copy(source, target, wsem.at[i])
        for i, (source, target) in enumerate(
            ((w_out_hbm, w_out), (wq_hbm, wq), (wk_hbm, wk), (wv_hbm, wv), (full_hbm, full))
        )
    ]
    for load in loads:
        load.start()
    barrier = pltpu.get_barrier_semaphore()
    for other in (beside, across, far):
        pl.semaphore_signal(barrier, inc=1, device_id=(group, other), device_id_type=MESH_ID)

    def greet_group(j, carry):
        other = lax.rem(group + j, groups)
        pl.semaphore_signal(barrier, inc=1, device_id=(other, me), device_id_type=MESH_ID)
        return carry

    lax.fori_loop(1, groups, greet_group, 0)
    pl.semaphore_wait(barrier, groups + 2)

    def remote(source, target, ssem, rsem, other):
        return pltpu.make_async_remote_copy(
            src_ref=source, dst_ref=target, send_sem=ssem, recv_sem=rsem,
            device_id=(group, other), device_id_type=MESH_ID,
        )

    def to_group(source, target, ssem, rsem, j):
        other = lax.rem(group + j, groups)
        return pltpu.make_async_remote_copy(
            src_ref=source(other), dst_ref=target.at[group], send_sem=ssem.at[j],
            recv_sem=rsem.at[group], device_id=(other, me), device_id_type=MESH_ID,
        )

    def from_group(source, target, ssem, rsem, j):
        sender = lax.rem(group + j, groups)
        return pltpu.make_async_remote_copy(
            src_ref=source(sender), dst_ref=target.at[sender], send_sem=ssem.at[j],
            recv_sem=rsem.at[sender], device_id=(sender, me), device_id_type=MESH_ID,
        )

    def gather_across(c):
        return remote(mgrad_ref.at[c], rows_in.at[me, c], gx_s.at[c], gx_r.at[c], across)

    def gather_forward(c):
        return remote(rows_in.at[across, c], rows_in.at[across, c], gf_s.at[c], gf_r.at[c], beside)

    gather_beside = remote(mgrad_ref, rows_in.at[me], gb_s, gb_r, beside)
    for c in range(chunks):
        gather_across(c).start()
    gather_beside.start()

    split = (lambda other: split_send, split_hbm, sp_s, sp_r)
    by_heads = (lambda other: heads_send, heads_hbm, hd_s, hd_r)
    shared = (lambda other: shared_send.at[other], shared_hbm, sh_s, sh_r)
    inward = (lambda other: inward_send.at[other, me], inward_hbm, in_s, in_r)
    exchanges = (split, by_heads, shared, inward)

    def start_exchange(number):
        exchange = exchanges[number]

        def one(j, carry):
            to_group(*exchange, j).start()
            return carry

        lax.fori_loop(1, groups, one, 0)
        pltpu.make_async_copy(
            exchange[0](group), exchange[1].at[group], local_sem.at[number]
        ).start()

    def end_exchange(number):
        exchange = exchanges[number]

        def one(j, carry):
            to_group(*exchange, j).wait_send()
            from_group(*exchange, j).wait_recv()
            return carry

        lax.fori_loop(1, groups, one, 0)
        pltpu.make_async_copy(
            exchange[0](group), exchange[1].at[group], local_sem.at[number]
        ).wait()

    low = jnp.bfloat16
    split_send[:, :units] = (adapter_scale_factor * geg_ref[:16]).astype(low)
    split_send[:, units : 2 * units] = (adapter_scale_factor * geu_ref[16:]).astype(low)
    split_send[:, 2 * units : 3 * units] = gsd_ref[...].astype(low)
    split_send[:, 3 * units :] = jnp.broadcast_to(set_ref[...], (16, 128)).astype(low)
    start_exchange(0)
    for t in range(4):
        for g in range(groups):
            at = slice((g * 4 + t) * cols_each, (g * 4 + t + 1) * cols_each)
            blocks[t, g, :16] = (adapter_scale_factor * geo_ref[:, at]).astype(low)
            blocks[t, g, 16:48] = gsgu_ref[:, at].astype(low)
            blocks[t, g, 48:] = (adapter_scale_factor * ged_ref[:, at]).astype(low)
    block_near = remote(blocks.at[beside], blocks_recv.at[0], one_s.at[0], one_r.at[0], beside)
    block_far = remote(blocks.at[far], blocks_recv.at[1], one_s.at[1], one_r.at[1], beside)
    block_across = remote(shared_send, blocks_xrecv, one_s.at[2], one_r.at[2], across)
    block_near.start()
    block_far.start()

    heads = heads_width // HEAD_DIM
    inverse = HEAD_DIM ** (-0.5)
    exponent = inverse * LOG2E
    for ref in (sums_buf, dk_buf, dv_buf, gso):
        ref[...] = jnp.zeros_like(ref)
    half = rows // 2
    reach = -(-(DOC_MOST - 1) // half)
    pairs = chunks // 2

    def attend_back(first_query, first_key, size):
        here = pl.ds(pl.multiple_of(first_query, half), half)
        keys = pl.ds(pl.multiple_of(first_key, half), size)

        def head_step(h, carry):
            cols = pl.ds(pl.multiple_of(h * HEAD_DIM, HEAD_DIM), HEAD_DIM)
            queries = qrot_ref[here, cols]
            key_rows = krot_ref[keys, cols]
            grads = dmixed[here, cols]
            scores = attention_scores(
                key_rows, queries, start_ref[:, here], first_query, first_key, 1
            )
            top = jnp.max(scores, axis=0, keepdims=True)
            weights = jnp.exp2((scores - top) * exponent)
            total = jnp.sum(weights, axis=0, keepdims=True)
            probs = weights * (1.0 / total)
            prob_grad = mm_nt(value_ref[keys, cols], grads)
            weighted = probs * prob_grad
            delta = jnp.sum(weighted, axis=0, keepdims=True)
            score_grad = (weighted - probs * delta).astype(low)
            dv_buf[keys, cols] += mm(probs.astype(low), grads)
            dk_buf[keys, cols] += mm(score_grad, queries)
            dq = mm_tn(score_grad, key_rows) * inverse
            dq = dq * cos_ref[here, :] - pltpu.roll(dq, HEAD_DIM // 2, 1) * sin_ref[here, :]
            dq = dq * qgain_ref[:, cols]
            dq_buf[here, cols] = dq
            sums_buf[0, here, :] += qproj_ref[here, cols] * dq
            return carry

        lax.fori_loop(0, heads, head_step, 0)

    loads[0].wait()

    def block_step(b, carry):
        @pl.when(b == 0)
        def _():
            lhs[...] = mgrad_ref[...].reshape(rows, width)

        @pl.when(b == 1)
        def _():
            gather_beside.wait_recv()
            lhs[...] = rows_in[beside].reshape(rows, width)

        @pl.when(b >= 2)
        def _():
            base = (b - 2) * pairs
            for j in range(pairs):
                gather_across(base + j).wait_recv()
                gather_forward(base + j).start()
            for j in range(pairs):
                lhs[j * part : (j + 1) * part] = rows_in[across, base + j]
            for j in range(pairs):
                gather_forward(base + j).wait_recv()
                lhs[half + j * part : half + (j + 1) * part] = rows_in[far, base + j]

        first = jnp.where(b == 0, me, jnp.where(b == 1, beside, across)) * rows
        second = jnp.where(b == 0, me, jnp.where(b == 1, beside, far)) * rows
        first = first + jnp.where(b >= 2, (b - 2) * half, 0)
        second = second + jnp.where(b >= 2, (b - 2) * half, half)
        starts = (pl.multiple_of(first, half), pl.multiple_of(second, half))
        out_dmid = mm_nt(lhs[...], eo_ref[...]).astype(low)
        grad = (mm_nt(lhs[...], w_out[...]) + mm(out_dmid, so_ref[...])).astype(low)
        for i, start in enumerate(starts):
            dmixed[pl.ds(start, half), :] = grad[i * half : (i + 1) * half]
        gso[...] += mm_tn(
            out_dmid, jnp.concatenate([mixed_ref[pl.ds(start, half), :] for start in starts], axis=0)
        )
        for start in starts:

            @pl.when(start < reach * half)
            def _():
                attend_back(start, 0, min(reach * half, length))

            @pl.when(start >= reach * half)
            def _():
                attend_back(start, start - reach * half, min((reach + 1) * half, length))

        @pl.when(b == 0)
        def _():
            block_near.wait_recv()
            block_far.wait_recv()
            shared_send[...] = (
                blocks[across].astype(jnp.float32) + blocks_recv[1].astype(jnp.float32)
            ).astype(low)
            block_across.start()

        return carry

    lax.fori_loop(0, 4, block_step, 0)
    block_across.wait()
    shared_send[...] = (
        blocks[me].astype(jnp.float32)
        + blocks_recv[0].astype(jnp.float32)
        + blocks_xrecv[...].astype(jnp.float32)
    ).astype(low)
    start_exchange(2)

    def head_end(h, carry):
        cols = pl.ds(pl.multiple_of(h * HEAD_DIM, HEAD_DIM), HEAD_DIM)
        dk = dk_buf[:, cols] * inverse
        dk = dk * cos_ref[...] - pltpu.roll(dk, HEAD_DIM // 2, 1) * sin_ref[...]
        dk = dk * kgain_ref[:, cols]
        dk_buf[:, cols] = dk
        sums_buf[1] += kproj_ref[:, cols] * dk
        dv_low[:, cols] = dv_buf[:, cols].astype(low)
        return carry

    lax.fori_loop(0, heads, head_end, 0)

    lane = lax.broadcasted_iota(jnp.int32, (length, HEAD_DIM), 1)
    both = jnp.where(
        lane < 4,
        jnp.sum(sums_buf[0], axis=1, keepdims=True),
        jnp.sum(sums_buf[1], axis=1, keepdims=True),
    )
    ex_send[...] = jnp.transpose(both)[:8]
    swaps = [
        remote(ex_send, ex_recv.at[i], es_sem.at[i], er_sem.at[i], other)
        for i, other in enumerate((beside, across, far))
    ]
    for swap in swaps:
        swap.start()
    for load in loads[1:]:
        load.wait()
    for swap in swaps:
        swap.wait_recv()
    total = (ex_send[...] + ex_recv[0] + ex_recv[1] + ex_recv[2]) * (1.0 / (4 * heads_width))
    wide = jnp.concatenate(
        [
            jnp.broadcast_to(total[:1], (HEAD_DIM // 2, length)),
            jnp.broadcast_to(total[4:5], (HEAD_DIM // 2, length)),
        ],
        axis=0,
    )
    sums_buf[0] = jnp.transpose(wide)
    for dn, proj, target, at in (
        (dq_buf, qproj_ref, dq_low, 0), (dk_buf, kproj_ref, dk_low, HEAD_DIM // 2),
    ):
        scale = scale_ref[:, at : at + 1]
        means = sums_buf[0, :, at : at + 1]
        target[...] = (scale * dn[...] - proj[...] * (scale * scale * scale * means)).astype(low)

    dmid_part = (
        mm_nt(eq_ref[...], dq_low[...]) + mm_nt(ek_ref[...], dk_low[...])
        + mm_nt(ev_ref[...], dv_low[...])
    )
    dmid_send[...] = dmid_part.astype(low)
    dmid_near = remote(dmid_send, dmid_recv, one_s.at[3], one_r.at[3], beside)
    dmid_across = remote(dmid_xsend, dmid_xrecv, one_s.at[4], one_r.at[4], across)
    dmid_near.start()

    def reduce_beside(c):
        return remote(bsend.at[c], brecv.at[c], bs_sem.at[c], br_sem.at[c], beside)

    def reduce_across(c):
        return remote(xsend.at[c], xrecv.at[c], xs_sem.at[c], xr_sem.at[c], across)

    def chunk_of(buffer, c):
        return jnp.concatenate(
            [buffer[pl.ds(pl.multiple_of(o * rows + c * part, part), part), :] for o in order], axis=0
        )

    def stage_partial(c):
        parts = [chunk_of(buffer, c) for buffer in (dq_low, dk_low, dv_low)]
        tile = TILE

        def one(j, carry):
            at = pl.ds(pl.multiple_of(j * tile, tile), tile)
            value = (
                mm_nt(parts[0], wq[at, :]) + mm_nt(parts[1], wk[at, :]) + mm_nt(parts[2], wv[at, :])
            ).astype(low)
            own_buf[c, :, at] = value[:part]
            xsend[c, :, at] = value[part : 2 * part]
            bsend[c, 0, :, at] = value[2 * part : 3 * part]
            bsend[c, 1, :, at] = value[3 * part :]
            return carry

        lax.fori_loop(0, width // tile, one, 0)
        reduce_beside(c).start()

    def stage_pair(c):
        reduce_beside(c).wait_recv()
        xsend[c] = (xsend[c].astype(jnp.float32) + brecv[c, 1].astype(jnp.float32)).astype(low)
        reduce_across(c).start()
        own_buf[c] = (own_buf[c].astype(jnp.float32) + brecv[c, 0].astype(jnp.float32)).astype(low)

    def partial_step(i, carry):
        @pl.when(i < chunks)
        def _():
            stage_partial(i)

        @pl.when(i == 0)
        def _():
            dmid_near.wait_recv()
            dmid_xsend[...] = (
                dmid_send[...].astype(jnp.float32) + dmid_recv[...].astype(jnp.float32)
            ).astype(low)
            dmid_across.start()

        @pl.when(i > 0)
        def _():
            stage_pair(i - 1)

        return carry

    lax.fori_loop(0, chunks + 1, partial_step, 0)

    mids = mids_ref[...]
    for i, buffer in enumerate((dq_low, dk_low, dv_low)):
        heads_send[:, i * heads_width : (i + 1) * heads_width] = (
            adapter_scale_factor * mm_tn(mids, buffer[...])[i * 16 : (i + 1) * 16]
        ).astype(low)
    heads_send[:, 3 * heads_width :] = gso[...].astype(low)
    start_exchange(1)
    dmid_across.wait_recv()
    dmid = (
        dmid_xsend[...].astype(jnp.float32) + dmid_xrecv[...].astype(jnp.float32)
    ).astype(low)
    inward_grad = mm(dmid, full[...])
    for t in range(4):
        for g in range(groups):
            at = slice((g * 4 + t) * cols_each, (g * 4 + t + 1) * cols_each)
            inward_send[g, t] = inward_grad[:, at]
    start_exchange(3)
    dmid_xsend_ready = dmid
    ex_dmid = dmid_xsend_ready
    dmid_across.wait_send()
    dmid_xsend[...] = ex_dmid

    def finish_step(c, carry):
        reduce_across(c).wait_recv()
        here = pl.ds(pl.multiple_of(c * part, part), part)
        tgrad_ref[here, :] = (
            hgrad_ref[here, :] + own_buf[c].astype(jnp.float32) + xrecv[c].astype(jnp.float32)
        )
        return carry

    mine = pl.ds(pl.multiple_of(me * rows, rows), rows)
    extra = mm_tn(dmid_xsend[:, mine], shrink_ref[...])
    lax.fori_loop(0, chunks, finish_step, 0)
    tgrad_ref[...] += extra
    for c in range(chunks):
        reduce_beside(c).wait_send()
        reduce_across(c).wait_send()
    for c in range(chunks):
        gather_across(c).wait_send()
        gather_forward(c).wait_send()
    for copy in (block_near, block_far, dmid_near, gather_beside, *swaps):
        copy.wait_send()
    for number in range(4):
        end_exchange(number)


def back(
    qrot, krot, value, mixed, mgrad, qproj, kproj, scale, qgain, kgain, cos, sin, start_row,
    wq, wk, wv, w_out, so, eo, shrink, eq, ek, ev, mids, full, hgrad, chosen,
    geg, geu, gsd, gsgu, geo, ged,
):
    rows, width = hgrad.shape
    heads_width, units = wq.shape[1], geg.shape[1]
    length = 4 * rows
    part = rows // CHUNKS
    groups = lax.axis_size("dp")
    cols_each = width // (4 * groups)
    split_width = 3 * units + 128
    vmem = pl.BlockSpec(memory_space=pltpu.VMEM)
    hbm = pl.BlockSpec(memory_space=pl.ANY)
    low, f32 = jnp.bfloat16, jnp.float32
    shape = jax.ShapeDtypeStruct
    dma = pltpu.SemaphoreType.DMA
    buf = pltpu.VMEM
    return pl.pallas_call(
        back_body,
        in_specs=[vmem] * 13 + [hbm] * 4 + [vmem] * 7 + [hbm] + [vmem] * 8,
        out_specs=[vmem] + [hbm] * 4,
        out_shape=[
            shape((rows, width), f32),
            shape((groups, 16, split_width), low),
            shape((groups, 16, 4 * heads_width), low),
            shape((groups, 64, cols_each), low),
            shape((groups, 48, cols_each), f32),
        ],
        scratch_shapes=[
            buf(wq.shape, low), buf(wk.shape, low), buf(wv.shape, low), buf(w_out.shape, low),
            buf(full.shape, low), dma((5,)),
            buf((4, CHUNKS, part, width), low), buf((rows, width), low),
            buf((length, heads_width), low), buf((16, heads_width), f32),
            buf((length, heads_width), f32), buf((length, heads_width), f32),
            buf((length, heads_width), f32),
            buf((length, heads_width), low), buf((length, heads_width), low),
            buf((length, heads_width), low),
            buf((2, length, HEAD_DIM), f32),
            buf((16, split_width), low), buf((16, 4 * heads_width), low),
            buf((4, groups, 64, cols_each), low), buf((2, groups, 64, cols_each), low),
            buf((groups, 64, cols_each), low), buf((groups, 64, cols_each), low),
            buf((groups, 4, 48, cols_each), f32),
            buf((8, length), f32), buf((3, 8, length), f32),
            buf((48, length), low), buf((48, length), low), buf((48, length), low),
            buf((48, length), low),
            buf((CHUNKS, part, width), low), buf((CHUNKS, part, width), low),
            buf((CHUNKS, part, width), low),
            buf((CHUNKS, 2, part, width), low), buf((CHUNKS, 2, part, width), low),
            dma((CHUNKS,)), dma((CHUNKS,)), dma((CHUNKS,)), dma((CHUNKS,)), dma, dma,
            dma((3,)), dma((3,)), dma((CHUNKS,)), dma((CHUNKS,)), dma((CHUNKS,)), dma((CHUNKS,)),
            dma((5,)), dma((5,)),
        ] + [dma((groups,))] * 8 + [dma((4,))],
        cost_estimate=pl.CostEstimate(
            flops=2 * length * heads_width * (3 * width + 5 * length),
            bytes_accessed=2 * width * (3 * heads_width + 3 * length), transcendentals=0,
        ),
        compiler_params=pltpu.CompilerParams(
            collective_id=2, has_side_effects=True, vmem_limit_bytes=67043328
        ),
        name="attention_back_to_tokens",
    )(qrot, krot, value, mixed, mgrad, qproj, kproj, scale, qgain, kgain, cos, sin, start_row,
      wq, wk, wv, w_out, so, eo, shrink, eq, ek, ev, mids, full, hgrad, chosen,
      geg, geu, gsd, gsgu, geo, ged)


def finish_body(split_ref, heads_ref, shared_ref, inward_ref, *outs):
    groups = split_ref.shape[0]
    tag = split_ref.shape[2] - 128
    sets = outs[0].shape[0]
    tags = [split_ref[g, :, tag : tag + 1].astype(jnp.float32) for g in range(groups)]

    def add_up(source, target, first, step=512):
        count, high, wide = target.shape
        for at in range(0, wide, step):
            end = min(wide, at + step)
            pieces = [source(g, first + at, first + end).astype(jnp.float32) for g in range(groups)]
            for c in range(count):
                total = jnp.where(tags[0] == c, pieces[0], 0.0)
                for g in range(1, groups):
                    total += jnp.where(tags[g] == c, pieces[g], 0.0)
                target[c, :, at:end] = total

    sq, eq, sk, ek, sv, ev, so, eo, sg, eg, su, eu, sd, ed = outs
    heads_width = eq.shape[2]
    units = eg.shape[2]
    for i, target in enumerate((eq, ek, ev)):
        add_up(lambda g, a, b: heads_ref[g, :, a:b], target, i * heads_width)
    at = 0
    add_up(lambda g, a, b: heads_ref[g, :, a:b], so, 3 * heads_width)
    for target in (eg, eu, sd):
        add_up(lambda g, a, b: split_ref[g, :, a:b], target, at)
        at += target.shape[2]
    for i, target in enumerate((sq, sk, sv)):
        add_up(lambda g, a, b: inward_ref[g, i * 16 : (i + 1) * 16, a:b], target, 0)
    for i, target in enumerate((eo, sg, su, ed)):
        add_up(lambda g, a, b: shared_ref[g, i * 16 : (i + 1) * 16, a:b], target, 0)


def finish(split, by_heads, shared, inward, sets, heads_width, units):
    cols = shared.shape[2]
    vmem = pl.BlockSpec(memory_space=pltpu.VMEM)
    widths = (
        cols, heads_width, cols, heads_width, cols, heads_width, heads_width, cols,
        cols, units, cols, units, units, cols,
    )
    return pl.pallas_call(
        finish_body,
        in_specs=[vmem] * 4,
        out_specs=[vmem] * 14,
        out_shape=[jax.ShapeDtypeStruct((sets, 16, w), jnp.float32) for w in widths],
        compiler_params=pltpu.CompilerParams(vmem_limit_bytes=67043328),
        name="sum_by_set",
    )(split, by_heads, shared, inward)


def per_device(
    tokens,
    cotangent,
    segment_ids,
    adapter_set,
    w_query,
    w_key,
    w_value,
    w_out,
    w_gate,
    w_up,
    w_down,
    query_gain,
    key_gain,
    mixer_gain,
    feed_gain,
    shrink_query,
    expand_query,
    shrink_key,
    expand_key,
    shrink_value,
    expand_value,
    shrink_out,
    expand_out,
    shrink_gate,
    expand_gate,
    shrink_up,
    expand_up,
    shrink_down,
    expand_down,
):
    length = 4 * tokens.shape[0]
    (
        shrink_rows, expand_query_rows, expand_key_rows, expand_value_rows, out_shrink, out_expand,
        gate_up_shrink, gate_expand, up_expand, down_shrink, down_expand,
        query_gains, key_gains, mixer_gains, feed_gains, start_col, start_row, set_row,
    ) = pick(
        adapter_set, segment_ids, (query_gain, key_gain, mixer_gain, feed_gain),
        (
            shrink_query, expand_query, shrink_key, expand_key, shrink_value, expand_value,
            shrink_out, expand_out, shrink_gate, expand_gate, shrink_up, expand_up,
            shrink_down, expand_down,
        ),
    )
    cosine_table, sine_table = rotary_constants(length, HEAD_DIM)
    cosine_table, sine_table = jnp.asarray(cosine_table), jnp.asarray(sine_table)
    (
        mixed, query_rot, key_rot, value_low, query_proj, key_proj, scales, qkv_middle, full_tokens,
    ) = front(
        tokens, w_query, w_key, w_value, shrink_rows,
        expand_query_rows, expand_key_rows, expand_value_rows,
        query_gains, key_gains, cosine_table, sine_table, start_col,
    )
    (
        block_output, hidden_grad, mixer_grad, grad_down_shrink, gradient_gate_widened,
        gradient_up_widened, owner_gate_up, owner_out, owner_down,
    ) = middle(
        mixed, tokens, cotangent, w_out, w_gate, w_up, w_down, mixer_gains, feed_gains,
        out_shrink, out_expand, gate_up_shrink, gate_expand, up_expand, down_shrink, down_expand,
    )
    token_grads, split, by_heads, shared, inward = back(
        query_rot, key_rot, value_low, mixed, mixer_grad, query_proj, key_proj, scales,
        query_gains, key_gains, cosine_table, sine_table, start_row,
        w_query, w_key, w_value, w_out, out_shrink, out_expand,
        shrink_rows, expand_query_rows, expand_key_rows, expand_value_rows,
        qkv_middle, full_tokens.reshape(length, -1), hidden_grad, set_row,
        gradient_gate_widened, gradient_up_widened, grad_down_shrink,
        owner_gate_up, owner_out, owner_down,
    )
    adapter_grads = finish(
        split, by_heads, shared, inward, shrink_query.shape[0], w_query.shape[1], w_gate.shape[1]
    )
    return (block_output, token_grads, *adapter_grads)


def solution(mesh):
    in_specs = (
        P(("dp", "tensor"), None),
        P(("dp", "tensor"), None),
        P("dp", None),
        P("dp"),
        P(None, "tensor"),
        P(None, "tensor"),
        P(None, "tensor"),
        P("tensor", None),
        P(None, "tensor"),
        P(None, "tensor"),
        P("tensor", None),
        P("tensor"),
        P("tensor"),
        P(),
        P(),
        P(),
        P(None, None, "tensor"),
        P(),
        P(None, None, "tensor"),
        P(),
        P(None, None, "tensor"),
        P(None, None, "tensor"),
        P(),
        P(),
        P(None, None, "tensor"),
        P(),
        P(None, None, "tensor"),
        P(None, None, "tensor"),
        P(),
    )
    out_specs = (
        P(("dp", "tensor"), None),
        P(("dp", "tensor"), None),
        P(None, None, ("dp", "tensor")),
        P(None, None, "tensor"),
        P(None, None, ("dp", "tensor")),
        P(None, None, "tensor"),
        P(None, None, ("dp", "tensor")),
        P(None, None, "tensor"),
        P(None, None, "tensor"),
        P(None, None, ("dp", "tensor")),
        P(None, None, ("dp", "tensor")),
        P(None, None, "tensor"),
        P(None, None, ("dp", "tensor")),
        P(None, None, "tensor"),
        P(None, None, "tensor"),
        P(None, None, ("dp", "tensor")),
    )
    return jax.shard_map(
        per_device, mesh=mesh, in_specs=in_specs, out_specs=out_specs, check_vma=False
    )
```

```python
import functools
import jax
import jax.numpy as jnp
import numpy as np
from jax import lax
from jax.experimental import pallas as pl
from jax.experimental.pallas import tpu as pltpu
from jax.sharding import PartitionSpec as P

HEAD_DIM = 128
DOC_MOST = 512
ATT_ROWS = 256
rotary_base = 500000.0
NEG = -1e30
LOG2E = 1.4426950408889634


def rotary_constants(length, head_dim):
    half = head_dim // 2
    frequency = np.float32(rotary_base) ** (
        -(np.arange(half, dtype=np.float32) * np.float32(2.0) / np.float32(head_dim))
    )
    angles = np.arange(length, dtype=np.float32)[:, None] * frequency.astype(np.float32)[None, :]
    cosine = np.cos(angles.astype(np.float64)).astype(np.float32)
    sine = np.sin(angles.astype(np.float64)).astype(np.float32)
    return np.concatenate([cosine, sine], axis=1)


def open_table(cos_ref, sin_ref):
    table = cos_ref[...]
    turned = pltpu.roll(table, HEAD_DIM // 2, 1)
    low_half = lax.broadcasted_iota(jnp.int32, table.shape, 1) < HEAD_DIM // 2
    cos_ref[...] = jnp.where(low_half, table, turned)
    sin_ref[...] = jnp.where(low_half, -turned, table)


def key_window(block, rows):
    first = max(0, (block * rows - (DOC_MOST - 1)) // rows) * rows
    return first, (block + 1) * rows


epsilon = 1e-06
adapter_scale_factor = 0.5


def pick_body(
    set_ref, seg_ref, qgain, kgain, mgain, fgain,
    sq, eq, sk, ek, sv, ev, so, eo, sg, eg, su, eu, sd, ed,
    shrink_out, eq_out, ek_out, ev_out, so_out, eo_out, sgu_out, eg_out, eu_out, sd_out, ed_out,
    qgain_out, kgain_out, mgain_out, fgain_out, start_col, start_row, set_out,
):
    rank = sq.shape[1]

    def scaled(ref):
        return (adapter_scale_factor * ref[0].astype(jnp.float32)).astype(jnp.bfloat16)

    for i, ref in enumerate((sq, sk, sv)):
        shrink_out[i * rank : (i + 1) * rank, :] = ref[0]
    for i, (ref, target) in enumerate(((eq, eq_out), (ek, ek_out), (ev, ev_out))):
        target[...] = jnp.zeros_like(target)
        target[i * rank : (i + 1) * rank, :] = scaled(ref)
    for i, (ref, target) in enumerate(((eg, eg_out), (eu, eu_out))):
        target[...] = jnp.zeros_like(target)
        target[i * rank : (i + 1) * rank, :] = scaled(ref)
    so_out[...] = so[0]
    sd_out[...] = sd[0]
    eo_out[...] = scaled(eo)
    ed_out[...] = scaled(ed)
    sgu_out[:rank, :] = sg[0]
    sgu_out[rank:, :] = su[0]
    for ref, target in ((qgain, qgain_out), (kgain, kgain_out), (mgain, mgain_out), (fgain, fgain_out)):
        target[...] = ref[...].astype(jnp.float32).reshape(target.shape)
    length = seg_ref.shape[1]
    row = seg_ref[...].astype(jnp.float32)
    col = jnp.transpose(jnp.broadcast_to(row, (HEAD_DIM, length)))[:, :1]
    start_col[...] = jnp.sum(
        jnp.where(row < col, 1.0, 0.0), axis=1, keepdims=True
    ).astype(jnp.int32)
    start_row[...] = jnp.sum(
        jnp.where(col < row, 1.0, 0.0), axis=0, keepdims=True
    ).astype(jnp.int32)
    set_out[...] = jnp.full(set_out.shape, set_ref[0], jnp.int32).astype(jnp.float32)


def pick(adapter_set, segment_ids, gains, adapters):
    whole = lambda a: pl.BlockSpec(a.shape, lambda i, s: (0,) * a.ndim)
    chosen = lambda a: pl.BlockSpec((1,) + a.shape[1:], lambda i, s: (s[0], 0, 0))
    length = segment_ids.shape[1]
    rank, width = adapters[0].shape[1:]
    here, units = adapters[1].shape[2], adapters[9].shape[2]
    low, f32 = jnp.bfloat16, jnp.float32
    shapes = [
        ((3 * rank, width), low), ((3 * rank, here), low), ((3 * rank, here), low),
        ((3 * rank, here), low), ((rank, here), low), ((rank, width), low), ((2 * rank, width), low),
        ((2 * rank, units), low), ((2 * rank, units), low), ((rank, units), low), ((rank, width), low),
        ((1, here), f32), ((1, here), f32), ((1, width), f32), ((1, width), f32),
        ((length, 1), jnp.int32), ((1, length), jnp.int32), ((1, 128), f32),
    ]
    return pl.pallas_call(
        pick_body,
        grid_spec=pltpu.PrefetchScalarGridSpec(
            num_scalar_prefetch=1,
            grid=(1,),
            in_specs=[whole(segment_ids)] + [whole(g) for g in gains] + [chosen(a) for a in adapters],
            out_specs=[pl.BlockSpec(s, lambda i, _: (0,) * 2) for s, _ in shapes],
        ),
        out_shape=[jax.ShapeDtypeStruct(s, t) for s, t in shapes],
        compiler_params=pltpu.CompilerParams(vmem_limit_bytes=67043328),
        name="pick_adapters",
    )(adapter_set, segment_ids, *gains, *adapters)


CHUNKS = 4
TILE = 1024
EXTRA = 128
NT = (((1,), (1,)), ((), ()))
TN = (((0,), (0,)), ((), ()))
MESH_ID = pl.DeviceIdType.MESH
MIDDLE_ORDER = (
    ("S2", 4), ("S4", 7), ("P0", 1), ("P4", 8), ("P2", 4), ("F3", 6), ("F1", 3), ("S3", 5),
    ("S5", 9), ("S1", 2), ("S0", 0),
)


def mm(left, right):
    return jnp.dot(left, right, preferred_element_type=jnp.float32)


def mm_nt(left, right):
    return lax.dot_general(left, right, NT, preferred_element_type=jnp.float32)


def mm_tn(left, right):
    return lax.dot_general(left, right, TN, preferred_element_type=jnp.float32)


def partners():
    me = lax.axis_index("tensor")
    group = lax.axis_index("dp")
    beside = me + 1 - 2 * lax.rem(me, 2)
    across = lax.rem(me + 2, 4)
    return me, group, beside, across


def greet(group, beside, across):
    barrier = pltpu.get_barrier_semaphore()
    for other in (beside, across):
        pl.semaphore_signal(barrier, inc=1, device_id=(group, other), device_id_type=MESH_ID)
    pl.semaphore_wait(barrier, 2)


def middle_body(
    mixed_ref, tokens_ref, cot_ref, w_out_hbm, w_gate_hbm, w_up_hbm, w_down_hbm,
    mgain_ref, fgain_ref, so_ref, eo_ref, sgu_ref, eg_ref, eu_ref, sd_ref, ed_ref,
    out_hbm, hgrad_hbm, mgrad_hbm, gsd_ref, geg_ref, geu_ref, gsgu_ref, geo_ref, ged_ref,
    w_out, w_gate, w_up, w_down, wsem, out_ref, mgrad_ref, save_sem,
    rows_buf, own_buf, xsend, xrecv, bsend, brecv,
    gate_buf, up_buf, temp_a, temp_b, mgu_buf, mixer_buf, hidden_buf, mout_buf,
    xs_sem, xr_sem, bs_sem, br_sem, gxs_sem, gxr_sem, gbs_sem, gbr_sem, fs_sem, fr_sem,
):
    me, group, beside, across = partners()
    chunks, part, width = rows_buf.shape[0], rows_buf.shape[2], rows_buf.shape[3]
    units = w_gate.shape[1]
    heads_width = w_out.shape[0]
    far = lax.rem(beside + 2, 4)
    order = (me, across, beside, far)
    loads = [
        pltpu.make_async_copy(source, target, wsem.at[i])
        for i, (source, target) in enumerate(
            ((w_out_hbm, w_out), (w_gate_hbm, w_gate), (w_up_hbm, w_up), (w_down_hbm, w_down))
        )
    ]
    for load in loads:
        load.start()
    for ref in (gsd_ref, geg_ref, geu_ref, gsgu_ref, geo_ref, ged_ref):
        ref[...] = jnp.zeros_like(ref)
    greet(group, beside, across)

    def remote(source, target, ssem, rsem, other):
        return pltpu.make_async_remote_copy(
            src_ref=source, dst_ref=target, send_sem=ssem, recv_sem=rsem,
            device_id=(group, other), device_id_type=MESH_ID,
        )

    def gather_across(c):
        return remote(rows_buf.at[c, 0], rows_buf.at[c, 1], gxs_sem.at[c], gxr_sem.at[c], across)

    def gather_beside(c):
        return remote(rows_buf.at[c, 0], rows_buf.at[c, 2], gbs_sem.at[c], gbr_sem.at[c], beside)

    def gather_forward(c):
        return remote(rows_buf.at[c, 1], rows_buf.at[c, 3], fs_sem.at[c], fr_sem.at[c], beside)

    def reduce_beside(c):
        return remote(bsend.at[c], brecv.at[c], bs_sem.at[c], br_sem.at[c], beside)

    def reduce_across(c):
        return remote(xsend.at[c], xrecv.at[c], xs_sem.at[c], xr_sem.at[c], across)

    def store_partial(c, columns, value):
        low = value.astype(jnp.bfloat16)
        own_buf[c, :, columns] = low[:part]
        xsend[c, :, columns] = low[part : 2 * part]
        bsend[c, 0, :, columns] = low[2 * part : 3 * part]
        bsend[c, 1, :, columns] = low[3 * part :]

    def gathered(c):
        return rows_buf[c].reshape(4 * part, width)

    def forward_stage(c):
        gather_across(c).wait_recv()
        gather_forward(c).start()

    def pair_stage(c):
        reduce_beside(c).wait_recv()
        own_buf[c] = (
            own_buf[c].astype(jnp.float32) + brecv[c, 0].astype(jnp.float32)
        ).astype(jnp.bfloat16)
        xsend[c] = (
            xsend[c].astype(jnp.float32) + brecv[c, 1].astype(jnp.float32)
        ).astype(jnp.bfloat16)
        reduce_across(c).start()

    def totals(c):
        reduce_across(c).wait_recv()
        main = own_buf[c, :, :width].astype(jnp.float32) + xrecv[c, :, :width].astype(jnp.float32)
        side = own_buf[c, :, width : width + 32].astype(jnp.float32) + xrecv[
            c, :, width : width + 32
        ].astype(jnp.float32)
        return main, side.astype(jnp.bfloat16)

    def own_rows(c):
        return pl.ds(pl.multiple_of(c * part, part), part)

    def save(number, c):
        source, target = ((out_ref, out_hbm), (hidden_buf, hgrad_hbm), (mgrad_ref, mgrad_hbm))[number]
        return pltpu.make_async_copy(
            source.at[own_rows(c), :], target.at[own_rows(c), :], save_sem.at[number, c]
        )

    def send_rows(c, value, again):
        if again:
            gather_across(c).wait_send()
            gather_beside(c).wait_send()
        rows_buf[c, 0] = value
        gather_across(c).start()
        gather_beside(c).start()

    def chunk_rows(c):
        return pl.ds(pl.multiple_of(c * 4 * part, 4 * part), 4 * part)

    def tiles(total, tile, body):
        def step(j, carry):
            body(pl.ds(pl.multiple_of(j * tile, tile), tile))
            return carry

        lax.fori_loop(0, total // tile, step, 0)

    def mixed_chunk(c):
        return jnp.concatenate([mixed_ref[o, c] for o in order], axis=0)

    def stage_mixer(c):
        @pl.when(c == 0)
        def _():
            loads[0].wait()

        rows = mixed_chunk(c)
        store_partial(c, slice(width, width + 16), mm_nt(rows, so_ref[...]))
        tiles(width, TILE, lambda cols: store_partial(c, cols, mm(rows, w_out[:, cols])))
        reduce_beside(c).start()

    def stage_hidden(c):
        main, side = totals(c)
        mid = side[:, :16]
        mout_buf[c] = mid
        mixer = main + mm(mid, eo_ref[...])
        mixer_buf[own_rows(c), :] = mixer
        factor = lax.rsqrt(jnp.mean(mixer * mixer, axis=1, keepdims=True) + epsilon)
        hidden = tokens_ref[own_rows(c), :].astype(jnp.float32) + mixer * factor * mgain_ref[...]
        hidden_buf[own_rows(c), :] = hidden
        send_rows(c, hidden.astype(jnp.bfloat16), False)

    def arrive(c):
        gather_beside(c).wait_recv()
        gather_forward(c).wait_recv()

    def stage_units(c):
        @pl.when(c == 0)
        def _():
            for load in loads[1:]:
                load.wait()

        arrive(c)
        mids = mm_nt(gathered(c), sgu_ref[...]).astype(jnp.bfloat16)
        mgu_buf[c] = mids

        def unit_tile(cols):
            rows = gathered(c)
            gate = mm(rows, w_gate[:, cols]) + mm(mids, eg_ref[:, cols])
            up = mm(rows, w_up[:, cols]) + mm(mids, eu_ref[:, cols])
            gate_buf[chunk_rows(c), cols] = gate.astype(jnp.bfloat16)
            up_buf[chunk_rows(c), cols] = up.astype(jnp.bfloat16)
            sig = 1.0 / (1.0 + jnp.exp(-gate))
            temp_a[:, cols] = (gate * sig * up).astype(jnp.bfloat16)

        tiles(units, TILE, unit_tile)
        gather_forward(c).wait_send()
        reduce_beside(c).wait_send()
        reduce_across(c).wait_send()
        inner = temp_a[...]
        store_partial(c, slice(width, width + 16), mm_nt(inner, sd_ref[...]))
        tiles(width, 2 * TILE, lambda cols: store_partial(c, cols, mm(temp_a[...], w_down[:, cols])))
        reduce_beside(c).start()

    def norm_back_rows(values, gains, grads):
        factor = lax.rsqrt(jnp.mean(values * values, axis=1, keepdims=True) + epsilon)
        weighted = grads * gains
        return factor * weighted - values * (
            factor * factor * factor * jnp.mean(values * weighted, axis=1, keepdims=True)
        )

    def stage_feed(c):
        main, side = totals(c)
        mid = side[:, :16]
        feed = main + mm(mid, ed_ref[...])
        factor = lax.rsqrt(jnp.mean(feed * feed, axis=1, keepdims=True) + epsilon)
        gains = fgain_ref[...]
        out_ref[own_rows(c), :] = (hidden_buf[own_rows(c), :] + feed * factor * gains).astype(
            jnp.bfloat16
        )
        save(0, c).start()
        grad = norm_back_rows(feed, gains, cot_ref[own_rows(c), :].astype(jnp.float32))
        grad = grad.astype(jnp.bfloat16)
        send_rows(c, grad, True)
        ged_ref[...] += mm_tn(mid, grad)

    def stage_units_back(c):
        arrive(c)
        dmid = mm_nt(gathered(c), ed_ref[...]).astype(jnp.bfloat16)
        mids = mgu_buf[c]

        def unit_tile(cols):
            rows = gathered(c)
            inner_grad = mm_nt(rows, w_down[cols, :]) + mm(dmid, sd_ref[:, cols])
            gate = gate_buf[chunk_rows(c), cols].astype(jnp.float32)
            up = up_buf[chunk_rows(c), cols].astype(jnp.float32)
            sig = 1.0 / (1.0 + jnp.exp(-gate))
            silu = gate * sig
            gate_grad = (inner_grad * up * (sig + silu * (1.0 - sig))).astype(jnp.bfloat16)
            up_grad = (inner_grad * silu).astype(jnp.bfloat16)
            temp_a[:, cols] = gate_grad
            temp_b[:, cols] = up_grad
            gsd_ref[:, cols] += mm_tn(dmid, (silu * up).astype(jnp.bfloat16))
            geg_ref[:, cols] += mm_tn(mids, gate_grad)
            geu_ref[:, cols] += mm_tn(mids, up_grad)

        tiles(units, TILE, unit_tile)
        gather_forward(c).wait_send()
        reduce_beside(c).wait_send()
        reduce_across(c).wait_send()
        store_partial(
            c,
            slice(width, width + 32),
            mm_nt(temp_a[...], eg_ref[...]) + mm_nt(temp_b[...], eu_ref[...]),
        )

        def width_tile(cols):
            store_partial(
                c, cols, mm_nt(temp_a[...], w_gate[cols, :]) + mm_nt(temp_b[...], w_up[cols, :])
            )

        tiles(width, TILE, width_tile)
        reduce_beside(c).start()

    def stage_mixer_grad(c):
        main, side = totals(c)
        grads = cot_ref[own_rows(c), :].astype(jnp.float32) + main + mm(side, sgu_ref[...])
        mixer_grad = norm_back_rows(mixer_buf[own_rows(c), :], mgain_ref[...], grads)
        mixer_grad = mixer_grad.astype(jnp.bfloat16)
        mgrad_ref[own_rows(c), :] = mixer_grad
        save(2, c).start()
        geo_ref[...] += mm_tn(mout_buf[c], mixer_grad)
        gsgu_ref[...] += mm_tn(side, hidden_buf[own_rows(c), :].astype(jnp.bfloat16))
        hidden_buf[own_rows(c), :] = grads
        save(1, c).start()
        gather_across(c).wait_send()
        gather_beside(c).wait_send()
        reduce_beside(c).wait_send()
        reduce_across(c).wait_send()

    stages = {
        "S0": stage_mixer, "S1": stage_hidden, "S2": stage_units, "S3": stage_feed,
        "S4": stage_units_back, "S5": stage_mixer_grad,
        "P0": pair_stage, "P2": pair_stage, "P4": pair_stage,
        "F1": forward_stage, "F3": forward_stage,
    }

    def step(i, carry):
        for name, delay in MIDDLE_ORDER:

            @pl.when((i >= delay) & (i < delay + chunks))
            def _():
                stages[name](i - delay)

        return carry

    lax.fori_loop(0, chunks + max(delay for _, delay in MIDDLE_ORDER), step, 0)
    for c in range(chunks):
        for number in range(3):
            save(number, c).wait()


def middle(mixed, tokens, cot, w_out, w_gate, w_up, w_down, mgain, fgain, so, eo, sgu, eg, eu, sd, ed):
    rows, width = tokens.shape
    heads_width, units = w_out.shape[0], w_gate.shape[1]
    part = rows // CHUNKS
    whole_width = width + EXTRA
    vmem = pl.BlockSpec(memory_space=pltpu.VMEM)
    hbm = pl.BlockSpec(memory_space=pl.ANY)
    low, full = jnp.bfloat16, jnp.float32
    dma = pltpu.SemaphoreType.DMA((CHUNKS,))
    shape = jax.ShapeDtypeStruct
    flops = 2 * 4 * rows * width * (heads_width + 6 * units)
    return pl.pallas_call(
        middle_body,
        in_specs=[vmem] * 3 + [hbm] * 4 + [vmem] * 9,
        out_specs=[hbm] * 3 + [vmem] * 6,
        out_shape=[
            shape((rows, width), low), shape((rows, width), full), shape((rows, width), low),
            shape((16, units), full), shape((32, units), full), shape((32, units), full),
            shape((32, width), full), shape((16, width), full),
            shape((16, width), full),
        ],
        scratch_shapes=[
            pltpu.VMEM(w_out.shape, low), pltpu.VMEM(w_gate.shape, low),
            pltpu.VMEM(w_up.shape, low), pltpu.VMEM(w_down.shape, low),
            pltpu.SemaphoreType.DMA((4,)),
            pltpu.VMEM((rows, width), low), pltpu.VMEM((rows, width), low),
            pltpu.SemaphoreType.DMA((3, CHUNKS)),
            pltpu.VMEM((CHUNKS, 4, part, width), low),
            pltpu.VMEM((CHUNKS, part, whole_width), low),
            pltpu.VMEM((CHUNKS, part, whole_width), low),
            pltpu.VMEM((CHUNKS, part, whole_width), low),
            pltpu.VMEM((CHUNKS, 2, part, whole_width), low),
            pltpu.VMEM((CHUNKS, 2, part, whole_width), low),
            pltpu.VMEM((4 * rows, units), low), pltpu.VMEM((4 * rows, units), low),
            pltpu.VMEM((4 * part, units), low), pltpu.VMEM((4 * part, units), low),
            pltpu.VMEM((CHUNKS, 4 * part, 32), low),
            pltpu.VMEM((rows, width), full), pltpu.VMEM((rows, width), full),
            pltpu.VMEM((CHUNKS, part, 16), low),
        ] + [dma] * 10,
        cost_estimate=pl.CostEstimate(
            flops=flops, bytes_accessed=2 * width * (heads_width + 3 * units), transcendentals=0
        ),
        compiler_params=pltpu.CompilerParams(
            collective_id=0, has_side_effects=True, vmem_limit_bytes=67043328
        ),
        name="mixer_to_feed",
    )(mixed.reshape(4, CHUNKS, part, heads_width), tokens, cot, w_out, w_gate, w_up, w_down,
      mgain, fgain, so, eo, sgu, eg, eu, sd, ed)


def attention_scores(first, second, start, first_query, first_key, query_axis):
    scores = lax.dot_general(first, second, NT, preferred_element_type=jnp.float32)
    kpos = lax.broadcasted_iota(jnp.int32, scores.shape, 1 - query_axis) + first_key
    shape = [1, 1]
    shape[query_axis] = scores.shape[query_axis]
    qpos = lax.broadcasted_iota(jnp.int32, shape, query_axis) + first_query
    return jnp.where((kpos <= qpos) & (kpos >= start), scores, NEG)


def front_body(
    tokens_ref, wq_hbm, wk_hbm, wv_hbm, shrink_ref, eq_ref, ek_ref, ev_ref, qgain_ref, kgain_ref,
    table_ref, start_ref,
    mixed_hbm, qrot_hbm, krot_hbm, value_hbm, qproj_hbm, kproj_hbm, scale_hbm, mids_hbm, full_hbm,
    mixed_ref, qrot_ref, krot_ref, value_ref, qproj_ref, kproj_ref, scale_ref, mids_ref, cos_ref, sin_ref,
    wq, wk, wv, wsem, full, lhs, squares, ex_send, ex_recv,
    xs_sem, xr_sem, fs_sem, fr_sem, bs_sem, br_sem, es_sem, er_sem, out_sem,
):
    me, group, beside, across = partners()
    far = lax.rem(beside + 2, 4)
    chunks, part, width = full.shape[1:]
    rows = chunks * part
    length = 4 * rows
    loads = [
        pltpu.make_async_copy(source, target, wsem.at[i])
        for i, (source, target) in enumerate(((wq_hbm, wq), (wk_hbm, wk), (wv_hbm, wv)))
    ]
    for load in loads:
        load.start()
    barrier = pltpu.get_barrier_semaphore()
    for other in (beside, across, far):
        pl.semaphore_signal(barrier, inc=1, device_id=(group, other), device_id_type=MESH_ID)
    pl.semaphore_wait(barrier, 3)

    def remote(source, target, ssem, rsem, other):
        return pltpu.make_async_remote_copy(
            src_ref=source, dst_ref=target, send_sem=ssem, recv_sem=rsem,
            device_id=(group, other), device_id_type=MESH_ID,
        )

    def send_across(c):
        return remote(tokens_ref.at[c], full.at[me, c], xs_sem.at[c], xr_sem.at[c], across)

    def forward(c):
        return remote(full.at[across, c], full.at[across, c], fs_sem.at[c], fr_sem.at[c], beside)

    to_beside = remote(tokens_ref, full.at[me], bs_sem, br_sem, beside)
    for c in range(chunks):
        send_across(c).start()
    to_beside.start()
    full[me] = tokens_ref[...]
    cos_ref[...] = table_ref[...]
    open_table(cos_ref, sin_ref)
    for load in loads:
        load.wait()
    pairs = chunks // 2
    half = rows // 2

    def block_step(b, carry):
        @pl.when(b == 0)
        def _():
            lhs[...] = tokens_ref[...].reshape(rows, width)

        @pl.when(b == 1)
        def _():
            to_beside.wait_recv()
            lhs[...] = full[beside].reshape(rows, width)

        @pl.when(b >= 2)
        def _():
            base = (b - 2) * pairs
            for j in range(pairs):
                send_across(base + j).wait_recv()
                forward(base + j).start()
            for j in range(pairs):
                lhs[j * part : (j + 1) * part] = full[across, base + j]
            for j in range(pairs):
                forward(base + j).wait_recv()
                lhs[half + j * part : half + (j + 1) * part] = full[far, base + j]

        mids = mm_nt(lhs[...], shrink_ref[...]).astype(jnp.bfloat16)
        query = mm(lhs[...], wq[...]) + mm(mids, eq_ref[...])
        key = mm(lhs[...], wk[...]) + mm(mids, ek_ref[...])
        value = (mm(lhs[...], wv[...]) + mm(mids, ev_ref[...])).astype(jnp.bfloat16)
        qsum = jnp.sum(query * query, axis=1, keepdims=True)
        ksum = jnp.sum(key * key, axis=1, keepdims=True)
        lane = lax.broadcasted_iota(jnp.int32, (rows, HEAD_DIM), 1)
        both = jnp.where(lane < 4, qsum, ksum)
        first = jnp.where(b == 0, me, jnp.where(b == 1, beside, across)) * rows
        second = jnp.where(b == 0, me, jnp.where(b == 1, beside, far)) * rows
        first = first + jnp.where(b >= 2, (b - 2) * half, 0)
        second = second + jnp.where(b >= 2, (b - 2) * half, half)
        for start, piece in ((first, slice(0, half)), (second, slice(half, rows))):
            there = pl.ds(pl.multiple_of(start, half), half)
            qproj_ref[there, :] = query[piece]
            kproj_ref[there, :] = key[piece]
            value_ref[there, :] = value[piece]
            mids_ref[there, :] = mids[piece]
            squares[there, :] = both[piece]
        return carry

    lax.fori_loop(0, 4, block_step, 0)
    saves = [
        pltpu.make_async_copy(source, target, out_sem.at[i])
        for i, (source, target) in enumerate(
            (
                (full, full_hbm), (value_ref, value_hbm), (qproj_ref, qproj_hbm),
                (kproj_ref, kproj_hbm), (mids_ref, mids_hbm), (scale_ref, scale_hbm),
                (qrot_ref, qrot_hbm), (krot_ref, krot_hbm), (mixed_ref, mixed_hbm),
            )
        )
    ]
    for save in saves[:5]:
        save.start()
    ex_send[...] = jnp.transpose(squares[...])[:8]
    swaps = [
        remote(ex_send, ex_recv.at[i], es_sem.at[i], er_sem.at[i], other)
        for i, other in enumerate((beside, across, far))
    ]
    for swap in swaps:
        swap.start()
    for swap in swaps:
        swap.wait_recv()
    total = ex_send[...] + ex_recv[0] + ex_recv[1] + ex_recv[2]
    factor = lax.rsqrt(total / (4 * wq.shape[1]) + epsilon)
    wide = jnp.concatenate(
        [
            jnp.broadcast_to(factor[:1], (HEAD_DIM // 2, length)),
            jnp.broadcast_to(factor[4:5], (HEAD_DIM // 2, length)),
        ],
        axis=0,
    )
    scale_ref[...] = jnp.transpose(wide)
    heads = wq.shape[1] // HEAD_DIM
    exponent = HEAD_DIM ** (-0.5) * LOG2E
    block_rows = min(ATT_ROWS, length)

    def turn_step(h, carry):
        cols = pl.ds(pl.multiple_of(h * HEAD_DIM, HEAD_DIM), HEAD_DIM)
        for source, lane, gain, target in (
            (qproj_ref, 0, qgain_ref, qrot_ref),
            (kproj_ref, HEAD_DIM // 2, kgain_ref, krot_ref),
        ):
            normed = source[:, cols] * scale_ref[:, lane : lane + 1] * gain[:, cols]
            turned = normed * cos_ref[...] + pltpu.roll(normed, HEAD_DIM // 2, 1) * sin_ref[...]
            target[:, cols] = turned.astype(jnp.bfloat16)
        return carry

    lax.fori_loop(0, heads, turn_step, 0)
    for save in saves[5:8]:
        save.start()

    def head_step(h, carry):
        cols = pl.ds(pl.multiple_of(h * HEAD_DIM, HEAD_DIM), HEAD_DIM)
        for block in range(length // block_rows):
            low, high = key_window(block, block_rows)
            here = pl.ds(block * block_rows, block_rows)
            keys = pl.ds(low, high - low)
            scores = attention_scores(
                qrot_ref[here, cols], krot_ref[keys, cols], start_ref[here, :],
                block * block_rows, low, 0,
            )
            top = jnp.max(scores, axis=1, keepdims=True)
            weights = jnp.exp2((scores - top) * exponent)
            total = jnp.sum(weights, axis=1, keepdims=True)
            mix = mm(weights.astype(jnp.bfloat16), value_ref[keys, cols])
            mixed_ref[here, cols] = (mix * (1.0 / total)).astype(jnp.bfloat16)
        return carry

    lax.fori_loop(0, heads, head_step, 0)
    saves[8].start()
    for c in range(chunks):
        send_across(c).wait_send()
        forward(c).wait_send()
    to_beside.wait_send()
    for swap in swaps:
        swap.wait_send()
    for save in saves:
        save.wait()


def front(tokens, wq, wk, wv, shrink, eq, ek, ev, qgain, kgain, table, start_col):
    rows, width = tokens.shape
    heads_width = wq.shape[1]
    length = 4 * rows
    part = rows // CHUNKS
    vmem = pl.BlockSpec(memory_space=pltpu.VMEM)
    hbm = pl.BlockSpec(memory_space=pl.ANY)
    low, full = jnp.bfloat16, jnp.float32
    shape = jax.ShapeDtypeStruct
    dma = pltpu.SemaphoreType.DMA
    return pl.pallas_call(
        front_body,
        in_specs=[vmem] + [hbm] * 3 + [vmem] * 8,
        out_specs=[hbm] * 9,
        out_shape=[
            shape((length, heads_width), low), shape((length, heads_width), low),
            shape((length, heads_width), low), shape((length, heads_width), low),
            shape((length, heads_width), full), shape((length, heads_width), full),
            shape((length, HEAD_DIM), full), shape((length, shrink.shape[0]), low),
            shape((4, CHUNKS, part, width), low),
        ],
        scratch_shapes=[pltpu.VMEM((length, heads_width), low)] * 4
        + [pltpu.VMEM((length, heads_width), full)] * 2
        + [
            pltpu.VMEM((length, HEAD_DIM), full), pltpu.VMEM((length, shrink.shape[0]), low),
            pltpu.VMEM(table.shape, full), pltpu.VMEM(table.shape, full),
            pltpu.VMEM(wq.shape, low), pltpu.VMEM(wk.shape, low), pltpu.VMEM(wv.shape, low),
            dma((3,)),
            pltpu.VMEM((4, CHUNKS, part, width), low), pltpu.VMEM((rows, width), low),
            pltpu.VMEM((length, HEAD_DIM), full), pltpu.VMEM((8, length), full),
            pltpu.VMEM((3, 8, length), full),
            dma((CHUNKS,)), dma((CHUNKS,)), dma((CHUNKS,)), dma((CHUNKS,)), dma, dma,
            dma((3,)), dma((3,)), dma((9,)),
        ],
        cost_estimate=pl.CostEstimate(
            flops=2 * length * heads_width * (3 * width + 2 * length),
            bytes_accessed=2 * width * (3 * heads_width + length), transcendentals=0,
        ),
        compiler_params=pltpu.CompilerParams(
            collective_id=1, has_side_effects=True, vmem_limit_bytes=67043328
        ),
        name="gather_project_attend",
    )(tokens.reshape(CHUNKS, part, width), wq, wk, wv, shrink, eq, ek, ev, qgain, kgain,
      table, start_col)


def back_body(
    qrot_hbm, krot_hbm, value_hbm, mixed_hbm, mgrad_ref, qproj_hbm, kproj_hbm, scale_hbm, qgain_ref,
    kgain_ref, table_hbm, start_ref, wq_hbm, wk_hbm, wv_hbm, w_out_hbm, so_ref, eo_ref,
    shrink_ref,
    eq_ref, ek_ref, ev_ref, mids_ref, full_hbm, hgrad_hbm, set_ref,
    geg_ref, geu_ref, gsd_ref, gsgu_ref, geo_ref, ged_ref,
    tgrad_hbm, split_hbm, heads_hbm, shared_hbm, inward_hbm,
    wq, wk, wv, w_out, full, qrot_ref, krot_ref, value_ref, mixed_ref, qproj_ref, kproj_ref,
    scale_ref, cos_ref, sin_ref, hgrad_ref, wsem, save_sem, rows_in, lhs, dmixed, gso,
    dq_buf, dk_buf, dv_buf, dq_low, dk_low, dv_low, sums_buf,
    split_send, heads_send, blocks, blocks_recv, blocks_xrecv, shared_send, inward_send,
    ex_send, ex_recv, dmid_send, dmid_recv, dmid_xsend, dmid_xrecv,
    own_buf, xsend, xrecv, bsend, brecv,
    gx_s, gx_r, gf_s, gf_r, gb_s, gb_r,
    es_sem, er_sem, xs_sem, xr_sem, bs_sem, br_sem, one_s, one_r,
    sp_s, sp_r, hd_s, hd_r, sh_s, sh_r, in_s, in_r, local_sem,
):
    me, group, beside, across = partners()
    far = lax.rem(beside + 2, 4)
    order = (me, across, beside, far)
    groups = split_hbm.shape[0]
    chunks, part, width = own_buf.shape
    rows = chunks * part
    length = 4 * rows
    heads_width = wq.shape[1]
    units = geg_ref.shape[1]
    cols_each = blocks.shape[3]
    loads = [
        pltpu.make_async_copy(source, target, wsem.at[i])
        for i, (source, target) in enumerate(
            (
                (w_out_hbm, w_out), (mixed_hbm, mixed_ref), (qrot_hbm, qrot_ref),
                (krot_hbm, krot_ref), (value_hbm, value_ref),
                (table_hbm, cos_ref), (qproj_hbm, qproj_ref), (kproj_hbm, kproj_ref),
                (scale_hbm, scale_ref), (wq_hbm, wq), (wk_hbm, wk), (wv_hbm, wv),
                (hgrad_hbm, hgrad_ref), (full_hbm, full),
            )
        )
    ]
    for load in loads:
        load.start()
    barrier = pltpu.get_barrier_semaphore()
    for other in (beside, across, far):
        pl.semaphore_signal(barrier, inc=1, device_id=(group, other), device_id_type=MESH_ID)

    def greet_group(j, carry):
        other = lax.rem(group + j, groups)
        pl.semaphore_signal(barrier, inc=1, device_id=(other, me), device_id_type=MESH_ID)
        return carry

    lax.fori_loop(1, groups, greet_group, 0)
    pl.semaphore_wait(barrier, groups + 2)

    def remote(source, target, ssem, rsem, other):
        return pltpu.make_async_remote_copy(
            src_ref=source, dst_ref=target, send_sem=ssem, recv_sem=rsem,
            device_id=(group, other), device_id_type=MESH_ID,
        )

    def to_group(source, target, ssem, rsem, j):
        other = lax.rem(group + j, groups)
        return pltpu.make_async_remote_copy(
            src_ref=source(other), dst_ref=target.at[group], send_sem=ssem.at[j],
            recv_sem=rsem.at[group], device_id=(other, me), device_id_type=MESH_ID,
        )

    def from_group(source, target, ssem, rsem, j):
        sender = lax.rem(group + j, groups)
        return pltpu.make_async_remote_copy(
            src_ref=source(sender), dst_ref=target.at[sender], send_sem=ssem.at[j],
            recv_sem=rsem.at[sender], device_id=(sender, me), device_id_type=MESH_ID,
        )

    def gather_across(c):
        return remote(mgrad_ref.at[c], rows_in.at[me, c], gx_s.at[c], gx_r.at[c], across)

    def gather_forward(c):
        return remote(rows_in.at[across, c], rows_in.at[across, c], gf_s.at[c], gf_r.at[c], beside)

    gather_beside = remote(mgrad_ref, rows_in.at[me], gb_s, gb_r, beside)
    for c in range(chunks):
        gather_across(c).start()
    gather_beside.start()

    split = (lambda other: split_send, split_hbm, sp_s, sp_r)
    by_heads = (lambda other: heads_send, heads_hbm, hd_s, hd_r)
    shared = (lambda other: shared_send.at[other], shared_hbm, sh_s, sh_r)
    inward = (lambda other: inward_send.at[other, me], inward_hbm, in_s, in_r)
    exchanges = (split, by_heads, shared, inward)

    def start_exchange(number):
        exchange = exchanges[number]

        def one(j, carry):
            to_group(*exchange, j).start()
            return carry

        lax.fori_loop(1, groups, one, 0)
        pltpu.make_async_copy(
            exchange[0](group), exchange[1].at[group], local_sem.at[number]
        ).start()

    def end_exchange(number):
        exchange = exchanges[number]

        def one(j, carry):
            to_group(*exchange, j).wait_send()
            from_group(*exchange, j).wait_recv()
            return carry

        lax.fori_loop(1, groups, one, 0)
        pltpu.make_async_copy(
            exchange[0](group), exchange[1].at[group], local_sem.at[number]
        ).wait()

    low = jnp.bfloat16
    split_send[:, :units] = (adapter_scale_factor * geg_ref[:16]).astype(low)
    split_send[:, units : 2 * units] = (adapter_scale_factor * geu_ref[16:]).astype(low)
    split_send[:, 2 * units : 3 * units] = gsd_ref[...].astype(low)
    split_send[:, 3 * units :] = jnp.broadcast_to(set_ref[...], (16, 128)).astype(low)
    start_exchange(0)
    for t in range(4):
        for g in range(groups):
            at = slice((g * 4 + t) * cols_each, (g * 4 + t + 1) * cols_each)
            blocks[t, g, :16] = (adapter_scale_factor * geo_ref[:, at]).astype(low)
            blocks[t, g, 16:48] = gsgu_ref[:, at].astype(low)
            blocks[t, g, 48:] = (adapter_scale_factor * ged_ref[:, at]).astype(low)
    block_near = remote(blocks.at[beside], blocks_recv.at[0], one_s.at[0], one_r.at[0], beside)
    block_far = remote(blocks.at[far], blocks_recv.at[1], one_s.at[1], one_r.at[1], beside)
    block_across = remote(shared_send, blocks_xrecv, one_s.at[2], one_r.at[2], across)
    block_near.start()
    block_far.start()

    heads = heads_width // HEAD_DIM
    inverse = HEAD_DIM ** (-0.5)
    exponent = inverse * LOG2E
    for ref in (sums_buf, dk_buf, dv_buf, gso):
        ref[...] = jnp.zeros_like(ref)
    half = rows // 2
    reach = -(-(DOC_MOST - 1) // half)
    pairs = chunks // 2

    def attend_back(first_query, first_key, size):
        here = pl.ds(pl.multiple_of(first_query, half), half)
        keys = pl.ds(pl.multiple_of(first_key, half), size)

        def head_step(h, carry):
            cols = pl.ds(pl.multiple_of(h * HEAD_DIM, HEAD_DIM), HEAD_DIM)
            queries = qrot_ref[here, cols]
            key_rows = krot_ref[keys, cols]
            grads = dmixed[here, cols]
            scores = attention_scores(
                key_rows, queries, start_ref[:, here], first_query, first_key, 1
            )
            top = jnp.max(scores, axis=0, keepdims=True)
            weights = jnp.exp2((scores - top) * exponent)
            total = jnp.sum(weights, axis=0, keepdims=True)
            probs = weights * (1.0 / total)
            prob_grad = mm_nt(value_ref[keys, cols], grads)
            weighted = probs * prob_grad
            delta = jnp.sum(weighted, axis=0, keepdims=True)
            score_grad = (weighted - probs * delta).astype(low)
            dv_buf[keys, cols] += mm(probs.astype(low), grads)
            dk_buf[keys, cols] += mm(score_grad, queries)
            dq = mm_tn(score_grad, key_rows) * inverse
            dq = dq * cos_ref[here, :] - pltpu.roll(dq, HEAD_DIM // 2, 1) * sin_ref[here, :]
            dq = dq * qgain_ref[:, cols]
            dq_buf[here, cols] = dq
            sums_buf[0, here, :] += qproj_ref[here, cols] * dq
            return carry

        lax.fori_loop(0, heads, head_step, 0)

    for load in loads[:7]:
        load.wait()
    open_table(cos_ref, sin_ref)

    def block_step(b, carry):
        @pl.when(b == 0)
        def _():
            lhs[...] = mgrad_ref[...].reshape(rows, width)

        @pl.when(b == 1)
        def _():
            gather_beside.wait_recv()
            lhs[...] = rows_in[beside].reshape(rows, width)

        @pl.when(b >= 2)
        def _():
            base = (b - 2) * pairs
            for j in range(pairs):
                gather_across(base + j).wait_recv()
                gather_forward(base + j).start()
            for j in range(pairs):
                lhs[j * part : (j + 1) * part] = rows_in[across, base + j]
            for j in range(pairs):
                gather_forward(base + j).wait_recv()
                lhs[half + j * part : half + (j + 1) * part] = rows_in[far, base + j]

        first = jnp.where(b == 0, me, jnp.where(b == 1, beside, across)) * rows
        second = jnp.where(b == 0, me, jnp.where(b == 1, beside, far)) * rows
        first = first + jnp.where(b >= 2, (b - 2) * half, 0)
        second = second + jnp.where(b >= 2, (b - 2) * half, half)
        starts = (pl.multiple_of(first, half), pl.multiple_of(second, half))
        out_dmid = mm_nt(lhs[...], eo_ref[...]).astype(low)
        grad = (mm_nt(lhs[...], w_out[...]) + mm(out_dmid, so_ref[...])).astype(low)
        for i, start in enumerate(starts):
            dmixed[pl.ds(start, half), :] = grad[i * half : (i + 1) * half]
        gso[...] += mm_tn(
            out_dmid, jnp.concatenate([mixed_ref[pl.ds(start, half), :] for start in starts], axis=0)
        )
        for start in starts:

            @pl.when(start < reach * half)
            def _():
                attend_back(start, 0, min(reach * half, length))

            @pl.when(start >= reach * half)
            def _():
                attend_back(start, start - reach * half, min((reach + 1) * half, length))

        @pl.when(b == 0)
        def _():
            block_near.wait_recv()
            block_far.wait_recv()
            shared_send[...] = (
                blocks[across].astype(jnp.float32) + blocks_recv[1].astype(jnp.float32)
            ).astype(low)
            block_across.start()

        return carry

    lax.fori_loop(0, 4, block_step, 0)
    block_across.wait()
    shared_send[...] = (
        blocks[me].astype(jnp.float32)
        + blocks_recv[0].astype(jnp.float32)
        + blocks_xrecv[...].astype(jnp.float32)
    ).astype(low)
    start_exchange(2)

    def head_end(h, carry):
        cols = pl.ds(pl.multiple_of(h * HEAD_DIM, HEAD_DIM), HEAD_DIM)
        dk = dk_buf[:, cols] * inverse
        dk = dk * cos_ref[...] - pltpu.roll(dk, HEAD_DIM // 2, 1) * sin_ref[...]
        dk = dk * kgain_ref[:, cols]
        dk_buf[:, cols] = dk
        sums_buf[1] += kproj_ref[:, cols] * dk
        dv_low[:, cols] = dv_buf[:, cols].astype(low)
        return carry

    for load in loads[7:]:
        load.wait()
    lax.fori_loop(0, heads, head_end, 0)

    lane = lax.broadcasted_iota(jnp.int32, (length, HEAD_DIM), 1)
    both = jnp.where(
        lane < 4,
        jnp.sum(sums_buf[0], axis=1, keepdims=True),
        jnp.sum(sums_buf[1], axis=1, keepdims=True),
    )
    ex_send[...] = jnp.transpose(both)[:8]
    swaps = [
        remote(ex_send, ex_recv.at[i], es_sem.at[i], er_sem.at[i], other)
        for i, other in enumerate((beside, across, far))
    ]
    for swap in swaps:
        swap.start()
    for swap in swaps:
        swap.wait_recv()
    total = (ex_send[...] + ex_recv[0] + ex_recv[1] + ex_recv[2]) * (1.0 / (4 * heads_width))
    wide = jnp.concatenate(
        [
            jnp.broadcast_to(total[:1], (HEAD_DIM // 2, length)),
            jnp.broadcast_to(total[4:5], (HEAD_DIM // 2, length)),
        ],
        axis=0,
    )
    sums_buf[0] = jnp.transpose(wide)
    for dn, proj, target, at in (
        (dq_buf, qproj_ref, dq_low, 0), (dk_buf, kproj_ref, dk_low, HEAD_DIM // 2),
    ):
        scale = scale_ref[:, at : at + 1]
        means = sums_buf[0, :, at : at + 1]
        target[...] = (scale * dn[...] - proj[...] * (scale * scale * scale * means)).astype(low)

    dmid_part = (
        mm_nt(eq_ref[...], dq_low[...]) + mm_nt(ek_ref[...], dk_low[...])
        + mm_nt(ev_ref[...], dv_low[...])
    )
    dmid_send[...] = dmid_part.astype(low)
    dmid_near = remote(dmid_send, dmid_recv, one_s.at[3], one_r.at[3], beside)
    dmid_across = remote(dmid_xsend, dmid_xrecv, one_s.at[4], one_r.at[4], across)
    dmid_near.start()

    def reduce_beside(c):
        return remote(bsend.at[c], brecv.at[c], bs_sem.at[c], br_sem.at[c], beside)

    def reduce_across(c):
        return remote(xsend.at[c], xrecv.at[c], xs_sem.at[c], xr_sem.at[c], across)

    def chunk_of(buffer, c):
        return jnp.concatenate(
            [buffer[pl.ds(pl.multiple_of(o * rows + c * part, part), part), :] for o in order], axis=0
        )

    def stage_partial(c):
        parts = [chunk_of(buffer, c) for buffer in (dq_low, dk_low, dv_low)]
        tile = TILE

        def one(j, carry):
            at = pl.ds(pl.multiple_of(j * tile, tile), tile)
            value = (
                mm_nt(parts[0], wq[at, :]) + mm_nt(parts[1], wk[at, :]) + mm_nt(parts[2], wv[at, :])
            ).astype(low)
            own_buf[c, :, at] = value[:part]
            xsend[c, :, at] = value[part : 2 * part]
            bsend[c, 0, :, at] = value[2 * part : 3 * part]
            bsend[c, 1, :, at] = value[3 * part :]
            return carry

        lax.fori_loop(0, width // tile, one, 0)
        reduce_beside(c).start()

    def stage_pair(c):
        reduce_beside(c).wait_recv()
        xsend[c] = (xsend[c].astype(jnp.float32) + brecv[c, 1].astype(jnp.float32)).astype(low)
        reduce_across(c).start()
        own_buf[c] = (own_buf[c].astype(jnp.float32) + brecv[c, 0].astype(jnp.float32)).astype(low)

    def partial_step(i, carry):
        @pl.when(i < chunks)
        def _():
            stage_partial(i)

        @pl.when(i == 0)
        def _():
            dmid_near.wait_recv()
            dmid_xsend[...] = (
                dmid_send[...].astype(jnp.float32) + dmid_recv[...].astype(jnp.float32)
            ).astype(low)
            dmid_across.start()

        @pl.when(i > 0)
        def _():
            stage_pair(i - 1)

        return carry

    lax.fori_loop(0, chunks + 1, partial_step, 0)

    mids = mids_ref[...]
    for i, buffer in enumerate((dq_low, dk_low, dv_low)):
        heads_send[:, i * heads_width : (i + 1) * heads_width] = (
            adapter_scale_factor * mm_tn(mids, buffer[...])[i * 16 : (i + 1) * 16]
        ).astype(low)
    heads_send[:, 3 * heads_width :] = gso[...].astype(low)
    start_exchange(1)
    dmid_across.wait_recv()
    dmid = (
        dmid_xsend[...].astype(jnp.float32) + dmid_xrecv[...].astype(jnp.float32)
    ).astype(low)
    inward_grad = mm(dmid, full[...])
    for t in range(4):
        for g in range(groups):
            at = slice((g * 4 + t) * cols_each, (g * 4 + t + 1) * cols_each)
            inward_send[g, t] = inward_grad[:, at]
    start_exchange(3)
    dmid_across.wait_send()
    dmid_xsend[...] = dmid
    mine = pl.ds(pl.multiple_of(me * rows, rows), rows)
    hgrad_ref[...] += mm_tn(dmid_xsend[:, mine], shrink_ref[...])

    def own_rows(c):
        return pl.ds(pl.multiple_of(c * part, part), part)

    def save(c):
        return pltpu.make_async_copy(
            hgrad_ref.at[own_rows(c), :], tgrad_hbm.at[own_rows(c), :], save_sem.at[c]
        )

    def finish_step(c, carry):
        reduce_across(c).wait_recv()
        hgrad_ref[own_rows(c), :] += own_buf[c].astype(jnp.float32) + xrecv[c].astype(jnp.float32)
        save(c).start()
        return carry

    lax.fori_loop(0, chunks, finish_step, 0)
    for c in range(chunks):
        save(c).wait()
    for c in range(chunks):
        reduce_beside(c).wait_send()
        reduce_across(c).wait_send()
    for c in range(chunks):
        gather_across(c).wait_send()
        gather_forward(c).wait_send()
    for copy in (block_near, block_far, dmid_near, gather_beside, *swaps):
        copy.wait_send()
    for number in range(4):
        end_exchange(number)


def back(
    qrot, krot, value, mixed, mgrad, qproj, kproj, scale, qgain, kgain, table, start_row,
    wq, wk, wv, w_out, so, eo, shrink, eq, ek, ev, mids, full, hgrad, chosen,
    geg, geu, gsd, gsgu, geo, ged,
):
    rows, width = hgrad.shape
    heads_width, units = wq.shape[1], geg.shape[1]
    length = 4 * rows
    part = rows // CHUNKS
    groups = lax.axis_size("dp")
    cols_each = width // (4 * groups)
    split_width = 3 * units + 128
    vmem = pl.BlockSpec(memory_space=pltpu.VMEM)
    hbm = pl.BlockSpec(memory_space=pl.ANY)
    low, f32 = jnp.bfloat16, jnp.float32
    shape = jax.ShapeDtypeStruct
    dma = pltpu.SemaphoreType.DMA
    buf = pltpu.VMEM
    return pl.pallas_call(
        back_body,
        in_specs=[hbm] * 4 + [vmem] + [hbm] * 3 + [vmem] * 2 + [hbm] + [vmem] + [hbm] * 4 + [vmem] * 7
        + [hbm] * 2 + [vmem] * 7,
        out_specs=[hbm] * 5,
        out_shape=[
            shape((rows, width), f32),
            shape((groups, 16, split_width), low),
            shape((groups, 16, 4 * heads_width), low),
            shape((groups, 64, cols_each), low),
            shape((groups, 48, cols_each), f32),
        ],
        scratch_shapes=[
            buf(wq.shape, low), buf(wk.shape, low), buf(wv.shape, low), buf(w_out.shape, low),
            buf(full.shape, low),
            buf(qrot.shape, low), buf(krot.shape, low), buf(value.shape, low), buf(mixed.shape, low),
            buf(qproj.shape, f32), buf(kproj.shape, f32), buf(scale.shape, f32),
            buf(table.shape, f32), buf(table.shape, f32), buf(hgrad.shape, f32),
            dma((14,)), dma((CHUNKS,)),
            buf((4, CHUNKS, part, width), low), buf((rows, width), low),
            buf((length, heads_width), low), buf((16, heads_width), f32),
            buf((length, heads_width), f32), buf((length, heads_width), f32),
            buf((length, heads_width), f32),
            buf((length, heads_width), low), buf((length, heads_width), low),
            buf((length, heads_width), low),
            buf((2, length, HEAD_DIM), f32),
            buf((16, split_width), low), buf((16, 4 * heads_width), low),
            buf((4, groups, 64, cols_each), low), buf((2, groups, 64, cols_each), low),
            buf((groups, 64, cols_each), low), buf((groups, 64, cols_each), low),
            buf((groups, 4, 48, cols_each), f32),
            buf((8, length), f32), buf((3, 8, length), f32),
            buf((48, length), low), buf((48, length), low), buf((48, length), low),
            buf((48, length), low),
            buf((CHUNKS, part, width), low), buf((CHUNKS, part, width), low),
            buf((CHUNKS, part, width), low),
            buf((CHUNKS, 2, part, width), low), buf((CHUNKS, 2, part, width), low),
            dma((CHUNKS,)), dma((CHUNKS,)), dma((CHUNKS,)), dma((CHUNKS,)), dma, dma,
            dma((3,)), dma((3,)), dma((CHUNKS,)), dma((CHUNKS,)), dma((CHUNKS,)), dma((CHUNKS,)),
            dma((5,)), dma((5,)),
        ] + [dma((groups,))] * 8 + [dma((4,))],
        cost_estimate=pl.CostEstimate(
            flops=2 * length * heads_width * (3 * width + 5 * length),
            bytes_accessed=2 * width * (3 * heads_width + 3 * length), transcendentals=0,
        ),
        compiler_params=pltpu.CompilerParams(
            collective_id=2, has_side_effects=True, vmem_limit_bytes=67043328
        ),
        name="attention_back_to_tokens",
    )(qrot, krot, value, mixed, mgrad.reshape(CHUNKS, part, width), qproj, kproj, scale, qgain, kgain, table, start_row,
      wq, wk, wv, w_out, so, eo, shrink, eq, ek, ev, mids, full, hgrad, chosen,
      geg, geu, gsd, gsgu, geo, ged)


def finish_body(split_ref, heads_ref, shared_ref, inward_ref, block_ref, tokens_ref, *outs):
    block_out, tokens_out, *outs, which = outs
    groups = split_ref.shape[0]
    tag = split_ref.shape[2] - 128
    chosen = pl.program_id(0)

    @pl.when(chosen == 0)
    def _():
        for g in range(groups):
            which[g] = jnp.max(split_ref[g, :, tag:].astype(jnp.float32)).astype(jnp.int32)

    sq, eq, sk, ek, sv, ev, so, eo, sg, eg, su, eu, sd, ed = outs
    here = eq.shape[2]
    units = eg.shape[2]
    sources = []
    for i, target in enumerate((eq, ek, ev, so)):
        sources.append((target, lambda g, i=i: heads_ref[g, :, i * here : (i + 1) * here]))
    for i, target in enumerate((eg, eu, sd)):
        sources.append((target, lambda g, i=i: split_ref[g, :, i * units : (i + 1) * units]))
    for i, target in enumerate((sq, sk, sv)):
        sources.append((target, lambda g, i=i: inward_ref[g, i * 16 : (i + 1) * 16, :]))
    for i, target in enumerate((eo, sg, su, ed)):
        sources.append((target, lambda g, i=i: shared_ref[g, i * 16 : (i + 1) * 16, :]))
    for target, _ in sources:
        target[...] = jnp.zeros_like(target)

    def one(g, carry):
        @pl.when(which[g] == chosen)
        def _():
            for target, source in sources:
                target[0] += source(g).astype(jnp.float32)

        return carry

    lax.fori_loop(0, groups, one, 0)
    block_out[...] = block_ref[...]
    tokens_out[...] = tokens_ref[...]


def finish(split, by_heads, shared, inward, block, tokens, sets, here, units):
    cols = shared.shape[2]
    rows, width = block.shape
    part = rows // sets
    whole = lambda a: pl.BlockSpec(a.shape, lambda i: (0,) * a.ndim)
    strip = pl.BlockSpec((part, width), lambda i: (i, 0))
    widths = (cols, here, cols, here, cols, here, here, cols, cols, units, cols, units, units, cols)
    return pl.pallas_call(
        finish_body,
        grid=(sets,),
        in_specs=[whole(split), whole(by_heads), whole(shared), whole(inward), strip, strip],
        out_specs=[strip, strip] + [pl.BlockSpec((1, 16, w), lambda i: (i, 0, 0)) for w in widths],
        out_shape=[
            jax.ShapeDtypeStruct(block.shape, block.dtype),
            jax.ShapeDtypeStruct(tokens.shape, tokens.dtype),
        ] + [jax.ShapeDtypeStruct((sets, 16, w), jnp.float32) for w in widths],
        scratch_shapes=[pltpu.SMEM((split.shape[0],), jnp.int32)],
        compiler_params=pltpu.CompilerParams(vmem_limit_bytes=67043328),
        name="sum_by_set",
    )(split, by_heads, shared, inward, block, tokens)


def per_device(
    tokens,
    cotangent,
    segment_ids,
    adapter_set,
    w_query,
    w_key,
    w_value,
    w_out,
    w_gate,
    w_up,
    w_down,
    query_gain,
    key_gain,
    mixer_gain,
    feed_gain,
    shrink_query,
    expand_query,
    shrink_key,
    expand_key,
    shrink_value,
    expand_value,
    shrink_out,
    expand_out,
    shrink_gate,
    expand_gate,
    shrink_up,
    expand_up,
    shrink_down,
    expand_down,
):
    length = 4 * tokens.shape[0]
    (
        shrink_rows, expand_query_rows, expand_key_rows, expand_value_rows, out_shrink, out_expand,
        gate_up_shrink, gate_expand, up_expand, down_shrink, down_expand,
        query_gains, key_gains, mixer_gains, feed_gains, start_col, start_row, set_row,
    ) = pick(
        adapter_set, segment_ids, (query_gain, key_gain, mixer_gain, feed_gain),
        (
            shrink_query, expand_query, shrink_key, expand_key, shrink_value, expand_value,
            shrink_out, expand_out, shrink_gate, expand_gate, shrink_up, expand_up,
            shrink_down, expand_down,
        ),
    )
    table = jnp.asarray(rotary_constants(length, HEAD_DIM))
    (
        mixed, query_rot, key_rot, value_low, query_proj, key_proj, scales, qkv_middle, full_tokens,
    ) = front(
        tokens, w_query, w_key, w_value, shrink_rows,
        expand_query_rows, expand_key_rows, expand_value_rows,
        query_gains, key_gains, table, start_col,
    )
    (
        block_output, hidden_grad, mixer_grad, grad_down_shrink, gradient_gate_widened,
        gradient_up_widened, owner_gate_up, owner_out, owner_down,
    ) = middle(
        mixed, tokens, cotangent, w_out, w_gate, w_up, w_down, mixer_gains, feed_gains,
        out_shrink, out_expand, gate_up_shrink, gate_expand, up_expand, down_shrink, down_expand,
    )
    token_grads, split, by_heads, shared, inward = back(
        query_rot, key_rot, value_low, mixed, mixer_grad, query_proj, key_proj, scales,
        query_gains, key_gains, table, start_row,
        w_query, w_key, w_value, w_out, out_shrink, out_expand,
        shrink_rows, expand_query_rows, expand_key_rows, expand_value_rows,
        qkv_middle, full_tokens.reshape(length, -1), hidden_grad, set_row,
        gradient_gate_widened, gradient_up_widened, grad_down_shrink,
        owner_gate_up, owner_out, owner_down,
    )
    return finish(
        split, by_heads, shared, inward, block_output, token_grads,
        shrink_query.shape[0], w_query.shape[1], w_gate.shape[1],
    )


def solution(mesh):
    in_specs = (
        P(("dp", "tensor"), None),
        P(("dp", "tensor"), None),
        P("dp", None),
        P("dp"),
        P(None, "tensor"),
        P(None, "tensor"),
        P(None, "tensor"),
        P("tensor", None),
        P(None, "tensor"),
        P(None, "tensor"),
        P("tensor", None),
        P("tensor"),
        P("tensor"),
        P(),
        P(),
        P(),
        P(None, None, "tensor"),
        P(),
        P(None, None, "tensor"),
        P(),
        P(None, None, "tensor"),
        P(None, None, "tensor"),
        P(),
        P(),
        P(None, None, "tensor"),
        P(),
        P(None, None, "tensor"),
        P(None, None, "tensor"),
        P(),
    )
    out_specs = (
        P(("dp", "tensor"), None),
        P(("dp", "tensor"), None),
        P(None, None, ("dp", "tensor")),
        P(None, None, "tensor"),
        P(None, None, ("dp", "tensor")),
        P(None, None, "tensor"),
        P(None, None, ("dp", "tensor")),
        P(None, None, "tensor"),
        P(None, None, "tensor"),
        P(None, None, ("dp", "tensor")),
        P(None, None, ("dp", "tensor")),
        P(None, None, "tensor"),
        P(None, None, ("dp", "tensor")),
        P(None, None, "tensor"),
        P(None, None, "tensor"),
        P(None, None, ("dp", "tensor")),
    )
    return jax.shard_map(
        per_device, mesh=mesh, in_specs=in_specs, out_specs=out_specs, check_vma=False
    )
```

```python
import functools
import jax
import jax.numpy as jnp
import numpy as np
from jax import lax
from jax.experimental import pallas as pl
from jax.experimental.pallas import tpu as pltpu
from jax.sharding import PartitionSpec as P

HEAD_DIM = 128
DOC_MOST = 512
ATT_ROWS = 256
rotary_base = 500000.0
NEG = -1e30
LOG2E = 1.4426950408889634


def rotary_constants(length, head_dim):
    half = head_dim // 2
    frequency = np.float32(rotary_base) ** (
        -(np.arange(half, dtype=np.float32) * np.float32(2.0) / np.float32(head_dim))
    )
    angles = np.arange(length, dtype=np.float32)[:, None] * frequency.astype(np.float32)[None, :]
    cosine = np.cos(angles.astype(np.float64)).astype(np.float32)
    sine = np.sin(angles.astype(np.float64)).astype(np.float32)
    return np.concatenate([cosine, sine], axis=1)


def open_table(cos_ref, sin_ref):
    table = cos_ref[...]
    turned = pltpu.roll(table, HEAD_DIM // 2, 1)
    low_half = lax.broadcasted_iota(jnp.int32, table.shape, 1) < HEAD_DIM // 2
    cos_ref[...] = jnp.where(low_half, table, turned)
    sin_ref[...] = jnp.where(low_half, -turned, table)


def key_window(block, rows):
    first = max(0, (block * rows - (DOC_MOST - 1)) // rows) * rows
    return first, (block + 1) * rows


epsilon = 1e-06
adapter_scale_factor = 0.5


CHUNKS = 4
FINISH_STEPS = 2
TILE = 1024
EXTRA = 128
NT = (((1,), (1,)), ((), ()))
TN = (((0,), (0,)), ((), ()))
MESH_ID = pl.DeviceIdType.MESH
MIDDLE_STAGES = ("S0", "P0", "S1", "F1", "S2", "P2", "S3", "F3", "S4", "P4", "S5", "F5", "S6")
MIDDLE_ORDER = (
    0, 1, 2, 4, 3, 5, 6, 7, 8, 9, 10, 11, 12,
    16, 13, 14, 17, 20, 18, 21, 15, 24, 19, 22, 25, 23,
    28, 32, 26, 29, 36, 33, 27, 30, 37, 34, 40, 31, 38,
    35, 41, 44, 39, 48, 42, 45, 49, 43, 46, 50, 47, 51,
)


def mm(left, right):
    return jnp.dot(left, right, preferred_element_type=jnp.float32)


def mm_nt(left, right):
    return lax.dot_general(left, right, NT, preferred_element_type=jnp.float32)


def mm_tn(left, right):
    return lax.dot_general(left, right, TN, preferred_element_type=jnp.float32)


def partners():
    me = lax.axis_index("tensor")
    group = lax.axis_index("dp")
    beside = me + 1 - 2 * lax.rem(me, 2)
    across = lax.rem(me + 2, 4)
    return me, group, beside, across


def greet(group, beside, across):
    barrier = pltpu.get_barrier_semaphore()
    for other in (beside, across):
        pl.semaphore_signal(barrier, inc=1, device_id=(group, other), device_id_type=MESH_ID)
    pl.semaphore_wait(barrier, 2)


def middle_body(
    mixed_ref, tokens_ref, cot_ref, w_out_hbm, w_gate_hbm, w_up_hbm, w_down_hbm,
    mgain_ref, fgain_ref, so_ref, eo_ref, sgu_ref, eg_ref, eu_ref, sd_ref, ed_ref,
    out_hbm, hgrad_hbm, dmixed_hbm, gsd_ref, geg_ref, geu_ref, gso_ref, gsgu_ref, geo_ref, ged_ref,
    w_out, w_gate, w_up, w_down, wsem, out_ref, dmixed_ref, save_sem,
    rows_buf, own_buf, xsend, xrecv, bsend, brecv,
    gate_buf, up_buf, temp_a, temp_b, mgu_buf, mixer_buf, hidden_buf, mout_buf,
    xs_sem, xr_sem, bs_sem, br_sem, gxs_sem, gxr_sem, gbs_sem, gbr_sem, fs_sem, fr_sem,
):
    me, group, beside, across = partners()
    chunks, part, width = rows_buf.shape[0], rows_buf.shape[2], rows_buf.shape[3]
    units = w_gate.shape[1]
    heads_width = w_out.shape[0]
    far = lax.rem(beside + 2, 4)
    order = (me, across, beside, far)
    loads = [
        pltpu.make_async_copy(source, target, wsem.at[i])
        for i, (source, target) in enumerate(
            ((w_out_hbm, w_out), (w_gate_hbm, w_gate), (w_up_hbm, w_up), (w_down_hbm, w_down))
        )
    ]
    for load in loads:
        load.start()
    for ref in (gsd_ref, geg_ref, geu_ref, gso_ref, gsgu_ref, geo_ref, ged_ref):
        ref[...] = jnp.zeros_like(ref)
    greet(group, beside, across)

    def remote(source, target, ssem, rsem, other):
        return pltpu.make_async_remote_copy(
            src_ref=source, dst_ref=target, send_sem=ssem, recv_sem=rsem,
            device_id=(group, other), device_id_type=MESH_ID,
        )

    def gather_across(c):
        return remote(rows_buf.at[c, 0], rows_buf.at[c, 1], gxs_sem.at[c], gxr_sem.at[c], across)

    def gather_beside(c):
        return remote(rows_buf.at[c, 0], rows_buf.at[c, 2], gbs_sem.at[c], gbr_sem.at[c], beside)

    def gather_forward(c):
        return remote(rows_buf.at[c, 1], rows_buf.at[c, 3], fs_sem.at[c], fr_sem.at[c], beside)

    def reduce_beside(c):
        return remote(bsend.at[c], brecv.at[c], bs_sem.at[c], br_sem.at[c], beside)

    def reduce_across(c):
        return remote(xsend.at[c], xrecv.at[c], xs_sem.at[c], xr_sem.at[c], across)

    def store_partial(c, columns, value):
        low = value.astype(jnp.bfloat16)
        own_buf[c, :, columns] = low[:part]
        xsend[c, :, columns] = low[part : 2 * part]
        bsend[c, 0, :, columns] = low[2 * part : 3 * part]
        bsend[c, 1, :, columns] = low[3 * part :]

    def gathered(c):
        return rows_buf[c].reshape(4 * part, width)

    def forward_stage(c):
        gather_across(c).wait_recv()
        gather_forward(c).start()

    def pair_stage(c):
        reduce_beside(c).wait_recv()
        own_buf[c] = (
            own_buf[c].astype(jnp.float32) + brecv[c, 0].astype(jnp.float32)
        ).astype(jnp.bfloat16)
        xsend[c] = (
            xsend[c].astype(jnp.float32) + brecv[c, 1].astype(jnp.float32)
        ).astype(jnp.bfloat16)
        reduce_across(c).start()

    def totals(c):
        reduce_across(c).wait_recv()
        main = own_buf[c, :, :width].astype(jnp.float32) + xrecv[c, :, :width].astype(jnp.float32)
        side = own_buf[c, :, width : width + 32].astype(jnp.float32) + xrecv[
            c, :, width : width + 32
        ].astype(jnp.float32)
        return main, side.astype(jnp.bfloat16)

    def own_rows(c):
        return pl.ds(pl.multiple_of(c * part, part), part)

    def save(number, c):
        source, target = ((out_ref, out_hbm), (hidden_buf, hgrad_hbm))[number]
        return pltpu.make_async_copy(
            source.at[own_rows(c), :], target.at[own_rows(c), :], save_sem.at[number, c]
        )

    def send_rows(c, value, again):
        if again:
            gather_across(c).wait_send()
            gather_beside(c).wait_send()
        rows_buf[c, 0] = value
        gather_across(c).start()
        gather_beside(c).start()

    def chunk_rows(c):
        return pl.ds(pl.multiple_of(c * 4 * part, 4 * part), 4 * part)

    def tiles(total, tile, body):
        def step(j, carry):
            body(pl.ds(pl.multiple_of(j * tile, tile), tile))
            return carry

        lax.fori_loop(0, total // tile, step, 0)

    def mixed_chunk(c):
        return jnp.concatenate([mixed_ref[o, c] for o in order], axis=0)

    def stage_mixer(c):
        @pl.when(c == 0)
        def _():
            loads[0].wait()

        rows = mixed_chunk(c)
        store_partial(c, slice(width, width + 16), mm_nt(rows, so_ref[...]))
        tiles(width, TILE, lambda cols: store_partial(c, cols, mm(rows, w_out[:, cols])))
        reduce_beside(c).start()

    def stage_hidden(c):
        main, side = totals(c)
        mid = side[:, :16]
        mout_buf[c] = mid
        mixer = main + mm(mid, eo_ref[...])
        mixer_buf[own_rows(c), :] = mixer
        factor = lax.rsqrt(jnp.mean(mixer * mixer, axis=1, keepdims=True) + epsilon)
        hidden = tokens_ref[own_rows(c), :].astype(jnp.float32) + mixer * factor * mgain_ref[...]
        hidden_buf[own_rows(c), :] = hidden
        send_rows(c, hidden.astype(jnp.bfloat16), False)

    def arrive(c):
        gather_beside(c).wait_recv()
        gather_forward(c).wait_recv()

    def stage_units(c):
        @pl.when(c == 0)
        def _():
            for load in loads[1:]:
                load.wait()

        arrive(c)
        mids = mm_nt(gathered(c), sgu_ref[...]).astype(jnp.bfloat16)
        mgu_buf[c] = mids

        def unit_tile(cols):
            rows = gathered(c)
            gate = mm(rows, w_gate[:, cols]) + mm(mids, eg_ref[:, cols])
            up = mm(rows, w_up[:, cols]) + mm(mids, eu_ref[:, cols])
            gate_buf[chunk_rows(c), cols] = gate.astype(jnp.bfloat16)
            up_buf[chunk_rows(c), cols] = up.astype(jnp.bfloat16)
            sig = 1.0 / (1.0 + jnp.exp(-gate))
            temp_a[:, cols] = (gate * sig * up).astype(jnp.bfloat16)

        tiles(units, TILE, unit_tile)
        gather_forward(c).wait_send()
        reduce_beside(c).wait_send()
        reduce_across(c).wait_send()
        inner = temp_a[...]
        store_partial(c, slice(width, width + 16), mm_nt(inner, sd_ref[...]))
        tiles(width, 2 * TILE, lambda cols: store_partial(c, cols, mm(temp_a[...], w_down[:, cols])))
        reduce_beside(c).start()

    def norm_back_rows(values, gains, grads):
        factor = lax.rsqrt(jnp.mean(values * values, axis=1, keepdims=True) + epsilon)
        weighted = grads * gains
        return factor * weighted - values * (
            factor * factor * factor * jnp.mean(values * weighted, axis=1, keepdims=True)
        )

    def stage_feed(c):
        main, side = totals(c)
        mid = side[:, :16]
        feed = main + mm(mid, ed_ref[...])
        factor = lax.rsqrt(jnp.mean(feed * feed, axis=1, keepdims=True) + epsilon)
        gains = fgain_ref[...]
        out_ref[own_rows(c), :] = (hidden_buf[own_rows(c), :] + feed * factor * gains).astype(
            jnp.bfloat16
        )
        save(0, c).start()
        grad = norm_back_rows(feed, gains, cot_ref[own_rows(c), :].astype(jnp.float32))
        grad = grad.astype(jnp.bfloat16)
        send_rows(c, grad, True)
        ged_ref[...] += mm_tn(mid, grad)

    def stage_units_back(c):
        arrive(c)
        dmid = mm_nt(gathered(c), ed_ref[...]).astype(jnp.bfloat16)
        mids = mgu_buf[c]

        def unit_tile(cols):
            rows = gathered(c)
            inner_grad = mm_nt(rows, w_down[cols, :]) + mm(dmid, sd_ref[:, cols])
            gate = gate_buf[chunk_rows(c), cols].astype(jnp.float32)
            up = up_buf[chunk_rows(c), cols].astype(jnp.float32)
            sig = 1.0 / (1.0 + jnp.exp(-gate))
            silu = gate * sig
            gate_grad = (inner_grad * up * (sig + silu * (1.0 - sig))).astype(jnp.bfloat16)
            up_grad = (inner_grad * silu).astype(jnp.bfloat16)
            temp_a[:, cols] = gate_grad
            temp_b[:, cols] = up_grad
            gsd_ref[:, cols] += mm_tn(dmid, (silu * up).astype(jnp.bfloat16))
            geg_ref[:, cols] += mm_tn(mids, gate_grad)
            geu_ref[:, cols] += mm_tn(mids, up_grad)

        tiles(units, TILE, unit_tile)
        gather_forward(c).wait_send()
        reduce_beside(c).wait_send()
        reduce_across(c).wait_send()
        store_partial(
            c,
            slice(width, width + 32),
            mm_nt(temp_a[...], eg_ref[...]) + mm_nt(temp_b[...], eu_ref[...]),
        )

        def width_tile(cols):
            store_partial(
                c, cols, mm_nt(temp_a[...], w_gate[cols, :]) + mm_nt(temp_b[...], w_up[cols, :])
            )

        tiles(width, TILE, width_tile)
        reduce_beside(c).start()

    def stage_mixer_grad(c):
        main, side = totals(c)
        grads = cot_ref[own_rows(c), :].astype(jnp.float32) + main + mm(side, sgu_ref[...])
        mixer_grad = norm_back_rows(mixer_buf[own_rows(c), :], mgain_ref[...], grads)
        mixer_grad = mixer_grad.astype(jnp.bfloat16)
        send_rows(c, mixer_grad, True)
        geo_ref[...] += mm_tn(mout_buf[c], mixer_grad)
        gsgu_ref[...] += mm_tn(side, hidden_buf[own_rows(c), :].astype(jnp.bfloat16))
        hidden_buf[own_rows(c), :] = grads
        save(1, c).start()

    def stage_mixed_grad(c):
        arrive(c)
        dmid = mm_nt(gathered(c), eo_ref[...]).astype(jnp.bfloat16)
        grad = (mm_nt(gathered(c), w_out[...]) + mm(dmid, so_ref[...])).astype(jnp.bfloat16)
        for i, o in enumerate(order):
            dmixed_ref[o, c] = grad[i * part : (i + 1) * part]
        gso_ref[...] += mm_tn(dmid, mixed_chunk(c))
        gather_forward(c).wait_send()
        gather_across(c).wait_send()
        gather_beside(c).wait_send()
        reduce_beside(c).wait_send()
        reduce_across(c).wait_send()

    stages = {
        "S0": stage_mixer, "S1": stage_hidden, "S2": stage_units, "S3": stage_feed,
        "S4": stage_units_back, "S5": stage_mixer_grad, "S6": stage_mixed_grad,
        "P0": pair_stage, "P2": pair_stage, "P4": pair_stage,
        "F1": forward_stage, "F3": forward_stage, "F5": forward_stage,
    }

    packed = [
        sum(code << (6 * j) for j, code in enumerate(MIDDLE_ORDER[at : at + 5]))
        for at in range(0, len(MIDDLE_ORDER), 5)
    ]

    def step(i, carry):
        word = jnp.int32(packed[0])
        for k in range(1, len(packed)):
            word = jnp.where(i >= 5 * k, jnp.int32(packed[k]), word)
        place = lax.rem(i, 5)
        unit = jnp.int32(1)
        for k in range(1, 5):
            unit = jnp.where(place == k, jnp.int32(64**k), unit)
        code = lax.rem(lax.div(word, unit), 64)
        stage, c = lax.div(code, chunks), lax.rem(code, chunks)
        for k, name in enumerate(MIDDLE_STAGES):

            @pl.when(stage == k)
            def _():
                stages[name](c)

        return carry

    lax.fori_loop(0, len(MIDDLE_ORDER), step, 0)
    save_mixture = pltpu.make_async_copy(dmixed_ref, dmixed_hbm, save_sem.at[2, 0])
    save_mixture.start()
    for c in range(chunks):
        for number in range(2):
            save(number, c).wait()
    save_mixture.wait()


def middle(mixed, tokens, cot, w_out, w_gate, w_up, w_down, mgain, fgain, so, eo, sgu, eg, eu, sd, ed):
    rows, width = tokens.shape
    heads_width, units = w_out.shape[0], w_gate.shape[1]
    part = rows // CHUNKS
    whole_width = width + EXTRA
    vmem = pl.BlockSpec(memory_space=pltpu.VMEM)
    hbm = pl.BlockSpec(memory_space=pl.ANY)
    low, full = jnp.bfloat16, jnp.float32
    dma = pltpu.SemaphoreType.DMA((CHUNKS,))
    shape = jax.ShapeDtypeStruct
    flops = 2 * 4 * rows * width * (2 * heads_width + 6 * units)
    return pl.pallas_call(
        middle_body,
        in_specs=[vmem] * 3 + [hbm] * 4 + [vmem] * 9,
        out_specs=[hbm] * 3 + [vmem] * 7,
        out_shape=[
            shape((rows, width), low), shape((rows, width), full),
            shape((4, CHUNKS, part, heads_width), low),
            shape((16, units), full), shape((32, units), full), shape((32, units), full),
            shape((16, heads_width), full), shape((32, width), full), shape((16, width), full),
            shape((16, width), full),
        ],
        scratch_shapes=[
            pltpu.VMEM(w_out.shape, low), pltpu.VMEM(w_gate.shape, low),
            pltpu.VMEM(w_up.shape, low), pltpu.VMEM(w_down.shape, low),
            pltpu.SemaphoreType.DMA((4,)),
            pltpu.VMEM((rows, width), low), pltpu.VMEM((4, CHUNKS, part, heads_width), low),
            pltpu.SemaphoreType.DMA((3, CHUNKS)),
            pltpu.VMEM((CHUNKS, 4, part, width), low),
            pltpu.VMEM((CHUNKS, part, whole_width), low),
            pltpu.VMEM((CHUNKS, part, whole_width), low),
            pltpu.VMEM((CHUNKS, part, whole_width), low),
            pltpu.VMEM((CHUNKS, 2, part, whole_width), low),
            pltpu.VMEM((CHUNKS, 2, part, whole_width), low),
            pltpu.VMEM((4 * rows, units), low), pltpu.VMEM((4 * rows, units), low),
            pltpu.VMEM((4 * part, units), low), pltpu.VMEM((4 * part, units), low),
            pltpu.VMEM((CHUNKS, 4 * part, 32), low),
            pltpu.VMEM((rows, width), full), pltpu.VMEM((rows, width), full),
            pltpu.VMEM((CHUNKS, part, 16), low),
        ] + [dma] * 10,
        cost_estimate=pl.CostEstimate(
            flops=flops, bytes_accessed=2 * width * (heads_width + 3 * units), transcendentals=0
        ),
        compiler_params=pltpu.CompilerParams(
            collective_id=0, has_side_effects=True, vmem_limit_bytes=67043328
        ),
        name="mixer_to_feed",
    )(mixed.reshape(4, CHUNKS, part, heads_width), tokens, cot, w_out, w_gate, w_up, w_down,
      mgain, fgain, so, eo, sgu, eg, eu, sd, ed)


def attention_scores(first, second, start, first_query, first_key, query_axis):
    scores = lax.dot_general(first, second, NT, preferred_element_type=jnp.float32)
    kpos = lax.broadcasted_iota(jnp.int32, scores.shape, 1 - query_axis) + first_key
    shape = [1, 1]
    shape[query_axis] = scores.shape[query_axis]
    qpos = lax.broadcasted_iota(jnp.int32, shape, query_axis) + first_query
    return jnp.where((kpos <= qpos) & (kpos >= start), scores, NEG)


def pick_body(
    at, seg_ref, qgain, kgain, mgain, fgain,
    sq, eq, sk, ek, sv, ev, so, eo, sg, eg, su, eu, sd, ed,
    shrink_out, eq_out, ek_out, ev_out, so_out, eo_out, sgu_out, eg_out, eu_out, sd_out, ed_out,
    qgain_out, kgain_out, mgain_out, fgain_out, start_col, start_row, set_out,
):
    rank = sq.shape[1]

    def scaled(ref):
        return (adapter_scale_factor * ref[at].astype(jnp.float32)).astype(jnp.bfloat16)

    for i, ref in enumerate((sq, sk, sv)):
        shrink_out[i * rank : (i + 1) * rank, :] = ref[at]
    for i, (ref, target) in enumerate(((eq, eq_out), (ek, ek_out), (ev, ev_out))):
        target[...] = jnp.zeros_like(target)
        target[i * rank : (i + 1) * rank, :] = scaled(ref)
    for i, (ref, target) in enumerate(((eg, eg_out), (eu, eu_out))):
        target[...] = jnp.zeros_like(target)
        target[i * rank : (i + 1) * rank, :] = scaled(ref)
    so_out[...] = so[at]
    sd_out[...] = sd[at]
    eo_out[...] = scaled(eo)
    ed_out[...] = scaled(ed)
    sgu_out[:rank, :] = sg[at]
    sgu_out[rank:, :] = su[at]
    for ref, target in ((qgain, qgain_out), (kgain, kgain_out), (mgain, mgain_out), (fgain, fgain_out)):
        target[...] = ref[...].astype(jnp.float32).reshape(target.shape)
    length = seg_ref.shape[1]
    row = seg_ref[...].astype(jnp.float32)
    col = jnp.transpose(jnp.broadcast_to(row, (HEAD_DIM, length)))[:, :1]
    start_col[...] = jnp.sum(
        jnp.where(row < col, 1.0, 0.0), axis=1, keepdims=True
    ).astype(jnp.int32)
    start_row[...] = jnp.sum(
        jnp.where(col < row, 1.0, 0.0), axis=0, keepdims=True
    ).astype(jnp.int32)
    set_out[...] = jnp.full(set_out.shape, at, jnp.int32).astype(jnp.float32)


def front_body(
    set_ref, tokens_ref, wq_hbm, wk_hbm, wv_hbm, table_ref, seg_ref, qg_ref, kg_ref, mg_ref, fg_ref,
    *refs,
):
    adapters_hbm, refs = refs[:14], refs[14:]
    picked, refs = refs[:18], refs[18:]
    adapters, adapter_sem, refs = refs[-15:-1], refs[-1], refs[:-15]
    shrink_ref, eq_ref, ek_ref, ev_ref = picked[:4]
    qgain_ref, kgain_ref, start_ref = picked[11], picked[12], picked[15]
    front_steps(
        set_ref, tokens_ref, wq_hbm, wk_hbm, wv_hbm, table_ref,
        (seg_ref, qg_ref, kg_ref, mg_ref, fg_ref), adapters_hbm, adapters, adapter_sem, picked,
        shrink_ref, eq_ref, ek_ref, ev_ref, qgain_ref, kgain_ref, start_ref, *refs,
    )


def front_steps(
    set_ref, tokens_ref, wq_hbm, wk_hbm, wv_hbm, table_ref, small, adapters_hbm, adapters,
    adapter_sem, picked, shrink_ref, eq_ref, ek_ref, ev_ref, qgain_ref, kgain_ref, start_ref,
    mixed_hbm, qrot_hbm, krot_hbm, value_hbm, qproj_hbm, kproj_hbm, scale_hbm, mids_hbm, full_hbm,
    mixed_ref, qrot_ref, krot_ref, value_ref, qproj_ref, kproj_ref, scale_ref, mids_ref, cos_ref, sin_ref,
    wq, wk, wv, wsem, full, lhs, squares, ex_send, ex_recv,
    xs_sem, xr_sem, fs_sem, fr_sem, bs_sem, br_sem, es_sem, er_sem, out_sem,
):
    me, group, beside, across = partners()
    far = lax.rem(beside + 2, 4)
    chunks, part, width = full.shape[1:]
    rows = chunks * part
    length = 4 * rows
    loads = [
        pltpu.make_async_copy(source, target, wsem.at[i])
        for i, (source, target) in enumerate(((wq_hbm, wq), (wk_hbm, wk), (wv_hbm, wv)))
    ]
    barrier = pltpu.get_barrier_semaphore()
    for other in (beside, across, far):
        pl.semaphore_signal(barrier, inc=1, device_id=(group, other), device_id_type=MESH_ID)
    fetches = [
        pltpu.make_async_copy(source, target, adapter_sem.at[i])
        for i, (source, target) in enumerate(zip(adapters_hbm, adapters))
    ]
    for load in (*fetches, *loads):
        load.start()
    pl.semaphore_wait(barrier, 3)

    def remote(source, target, ssem, rsem, other):
        return pltpu.make_async_remote_copy(
            src_ref=source, dst_ref=target, send_sem=ssem, recv_sem=rsem,
            device_id=(group, other), device_id_type=MESH_ID,
        )

    def send_across(c):
        return remote(tokens_ref.at[c], full.at[me, c], xs_sem.at[c], xr_sem.at[c], across)

    def forward(c):
        return remote(full.at[across, c], full.at[across, c], fs_sem.at[c], fr_sem.at[c], beside)

    to_beside = remote(tokens_ref, full.at[me], bs_sem, br_sem, beside)
    for c in range(chunks):
        send_across(c).start()
    to_beside.start()
    full[me] = tokens_ref[...]
    cos_ref[...] = table_ref[...]
    open_table(cos_ref, sin_ref)
    for fetch in fetches:
        fetch.wait()
    pick_body(set_ref[0], *small, *adapters, *picked)
    for load in loads:
        load.wait()
    pairs = chunks // 2
    half = rows // 2

    def block_step(b, carry):
        @pl.when(b == 0)
        def _():
            lhs[...] = tokens_ref[...].reshape(rows, width)

        @pl.when(b == 1)
        def _():
            to_beside.wait_recv()
            lhs[...] = full[beside].reshape(rows, width)

        @pl.when(b >= 2)
        def _():
            base = (b - 2) * pairs
            for j in range(pairs):
                send_across(base + j).wait_recv()
                forward(base + j).start()
            for j in range(pairs):
                lhs[j * part : (j + 1) * part] = full[across, base + j]
            for j in range(pairs):
                forward(base + j).wait_recv()
                lhs[half + j * part : half + (j + 1) * part] = full[far, base + j]

        mids = mm_nt(lhs[...], shrink_ref[...]).astype(jnp.bfloat16)
        query = mm(lhs[...], wq[...]) + mm(mids, eq_ref[...])
        key = mm(lhs[...], wk[...]) + mm(mids, ek_ref[...])
        value = (mm(lhs[...], wv[...]) + mm(mids, ev_ref[...])).astype(jnp.bfloat16)
        qsum = jnp.sum(query * query, axis=1, keepdims=True)
        ksum = jnp.sum(key * key, axis=1, keepdims=True)
        lane = lax.broadcasted_iota(jnp.int32, (rows, HEAD_DIM), 1)
        both = jnp.where(lane < 4, qsum, ksum)
        first = jnp.where(b == 0, me, jnp.where(b == 1, beside, across)) * rows
        second = jnp.where(b == 0, me, jnp.where(b == 1, beside, far)) * rows
        first = first + jnp.where(b >= 2, (b - 2) * half, 0)
        second = second + jnp.where(b >= 2, (b - 2) * half, half)
        for start, piece in ((first, slice(0, half)), (second, slice(half, rows))):
            there = pl.ds(pl.multiple_of(start, half), half)
            qproj_ref[there, :] = query[piece]
            kproj_ref[there, :] = key[piece]
            value_ref[there, :] = value[piece]
            mids_ref[there, :] = mids[piece]
            squares[there, :] = both[piece]
        return carry

    lax.fori_loop(0, 4, block_step, 0)
    saves = [
        pltpu.make_async_copy(source, target, out_sem.at[i])
        for i, (source, target) in enumerate(
            (
                (full, full_hbm), (value_ref, value_hbm), (qproj_ref, qproj_hbm),
                (kproj_ref, kproj_hbm), (mids_ref, mids_hbm), (scale_ref, scale_hbm),
                (qrot_ref, qrot_hbm), (krot_ref, krot_hbm), (mixed_ref, mixed_hbm),
            )
        )
    ]
    for save in saves[:5]:
        save.start()
    ex_send[...] = jnp.transpose(squares[...])[:8]
    swaps = [
        remote(ex_send, ex_recv.at[i], es_sem.at[i], er_sem.at[i], other)
        for i, other in enumerate((beside, across, far))
    ]
    for swap in swaps:
        swap.start()
    for swap in swaps:
        swap.wait_recv()
    total = ex_send[...] + ex_recv[0] + ex_recv[1] + ex_recv[2]
    factor = lax.rsqrt(total / (4 * wq.shape[1]) + epsilon)
    wide = jnp.concatenate(
        [
            jnp.broadcast_to(factor[:1], (HEAD_DIM // 2, length)),
            jnp.broadcast_to(factor[4:5], (HEAD_DIM // 2, length)),
        ],
        axis=0,
    )
    scale_ref[...] = jnp.transpose(wide)
    heads = wq.shape[1] // HEAD_DIM
    exponent = HEAD_DIM ** (-0.5) * LOG2E
    block_rows = min(ATT_ROWS, length)

    def turn_step(h, carry):
        cols = pl.ds(pl.multiple_of(h * HEAD_DIM, HEAD_DIM), HEAD_DIM)
        for source, lane, gain, target in (
            (qproj_ref, 0, qgain_ref, qrot_ref),
            (kproj_ref, HEAD_DIM // 2, kgain_ref, krot_ref),
        ):
            normed = source[:, cols] * scale_ref[:, lane : lane + 1] * gain[:, cols]
            turned = normed * cos_ref[...] + pltpu.roll(normed, HEAD_DIM // 2, 1) * sin_ref[...]
            target[:, cols] = turned.astype(jnp.bfloat16)
        return carry

    lax.fori_loop(0, heads, turn_step, 0)
    for save in saves[5:8]:
        save.start()

    def head_step(h, carry):
        cols = pl.ds(pl.multiple_of(h * HEAD_DIM, HEAD_DIM), HEAD_DIM)
        for block in range(length // block_rows):
            low, high = key_window(block, block_rows)
            here = pl.ds(block * block_rows, block_rows)
            keys = pl.ds(low, high - low)
            scores = attention_scores(
                qrot_ref[here, cols], krot_ref[keys, cols], start_ref[here, :],
                block * block_rows, low, 0,
            )
            top = jnp.max(scores, axis=1, keepdims=True)
            weights = jnp.exp2((scores - top) * exponent)
            total = jnp.sum(weights, axis=1, keepdims=True)
            mix = mm(weights.astype(jnp.bfloat16), value_ref[keys, cols])
            mixed_ref[here, cols] = (mix * (1.0 / total)).astype(jnp.bfloat16)
        return carry

    lax.fori_loop(0, heads, head_step, 0)
    saves[8].start()
    for c in range(chunks):
        send_across(c).wait_send()
        forward(c).wait_send()
    to_beside.wait_send()
    for swap in swaps:
        swap.wait_send()
    for save in saves:
        save.wait()


def front(adapter_set, tokens, wq, wk, wv, table, segment_ids, gains, adapters):
    rows, width = tokens.shape
    heads_width = wq.shape[1]
    length = 4 * rows
    part = rows // CHUNKS
    rank = adapters[0].shape[1]
    units = adapters[9].shape[2]
    vmem = pl.BlockSpec(memory_space=pltpu.VMEM)
    hbm = pl.BlockSpec(memory_space=pl.ANY)
    low, full = jnp.bfloat16, jnp.float32
    shape = jax.ShapeDtypeStruct
    dma = pltpu.SemaphoreType.DMA
    return pl.pallas_call(
        front_body,
        in_specs=[pl.BlockSpec(memory_space=pltpu.SMEM), vmem] + [hbm] * 3 + [vmem] * 6 + [hbm] * 14,
        out_specs=[vmem] * 18 + [hbm] * 9,
        out_shape=[
            shape((3 * rank, width), low), shape((3 * rank, heads_width), low),
            shape((3 * rank, heads_width), low), shape((3 * rank, heads_width), low),
            shape((rank, heads_width), low), shape((rank, width), low), shape((2 * rank, width), low),
            shape((2 * rank, units), low), shape((2 * rank, units), low), shape((rank, units), low),
            shape((rank, width), low), shape((1, heads_width), full), shape((1, heads_width), full),
            shape((1, width), full), shape((1, width), full),
            shape((length, 1), jnp.int32), shape((1, length), jnp.int32), shape((1, 128), full),
            shape((length, heads_width), low), shape((length, heads_width), low),
            shape((length, heads_width), low), shape((length, heads_width), low),
            shape((length, heads_width), full), shape((length, heads_width), full),
            shape((length, HEAD_DIM), full), shape((length, 3 * rank), low),
            shape((4, CHUNKS, part, width), low),
        ],
        scratch_shapes=[pltpu.VMEM((length, heads_width), low)] * 4
        + [pltpu.VMEM((length, heads_width), full)] * 2
        + [
            pltpu.VMEM((length, HEAD_DIM), full), pltpu.VMEM((length, 3 * rank), low),
            pltpu.VMEM(table.shape, full), pltpu.VMEM(table.shape, full),
            pltpu.VMEM(wq.shape, low), pltpu.VMEM(wk.shape, low), pltpu.VMEM(wv.shape, low),
            dma((3,)),
            pltpu.VMEM((4, CHUNKS, part, width), low), pltpu.VMEM((rows, width), low),
            pltpu.VMEM((length, HEAD_DIM), full), pltpu.VMEM((8, length), full),
            pltpu.VMEM((3, 8, length), full),
            dma((CHUNKS,)), dma((CHUNKS,)), dma((CHUNKS,)), dma((CHUNKS,)), dma, dma,
            dma((3,)), dma((3,)), dma((9,)),
        ] + [pltpu.VMEM(a.shape, low) for a in adapters] + [dma((14,))],
        cost_estimate=pl.CostEstimate(
            flops=2 * length * heads_width * (3 * width + 2 * length),
            bytes_accessed=2 * width * (3 * heads_width + length), transcendentals=0,
        ),
        compiler_params=pltpu.CompilerParams(
            collective_id=1, has_side_effects=True, vmem_limit_bytes=67043328
        ),
        name="gather_project_attend",
    )(adapter_set, tokens.reshape(CHUNKS, part, width), wq, wk, wv, table, segment_ids, *gains,
      *adapters)


def back_body(
    qrot_hbm, krot_hbm, value_hbm, dmixed_hbm, qproj_hbm, kproj_hbm, scale_hbm, qgain_ref,
    kgain_ref, table_hbm, start_ref, wq_hbm, wk_hbm, wv_hbm, shrink_ref,
    eq_ref, ek_ref, ev_ref, mids_ref, full_hbm, hgrad_hbm, set_ref,
    gso_ref, geg_ref, geu_ref, gsd_ref, gsgu_ref, geo_ref, ged_ref,
    tgrad_hbm, split_hbm, heads_hbm, shared_hbm, inward_hbm,
    wq, wk, wv, full, qrot_ref, krot_ref, value_ref, dmixed, qproj_ref, kproj_ref,
    scale_ref, cos_ref, sin_ref, hgrad_ref, wsem, save_sem,
    dq_buf, dk_buf, dv_buf, dq_low, dk_low, dv_low, sums_buf,
    split_send, heads_send, blocks, blocks_recv, blocks_xrecv, shared_send, inward_send,
    ex_send, ex_recv, dmid_send, dmid_recv, dmid_xsend, dmid_xrecv,
    own_buf, xsend, xrecv, bsend, brecv,
    es_sem, er_sem, xs_sem, xr_sem, bs_sem, br_sem, one_s, one_r,
    sp_s, sp_r, hd_s, hd_r, sh_s, sh_r, in_s, in_r, local_sem,
):
    me, group, beside, across = partners()
    far = lax.rem(beside + 2, 4)
    order = (me, across, beside, far)
    groups = split_hbm.shape[0]
    chunks, part, width = own_buf.shape
    rows = chunks * part
    length = 4 * rows
    heads_width = wq.shape[1]
    units = geg_ref.shape[1]
    cols_each = blocks.shape[3]
    loads = [
        pltpu.make_async_copy(source, target, wsem.at[i])
        for i, (source, target) in enumerate(
            (
                (dmixed_hbm, dmixed), (qrot_hbm, qrot_ref),
                (krot_hbm, krot_ref), (value_hbm, value_ref),
                (table_hbm, cos_ref), (qproj_hbm, qproj_ref), (kproj_hbm, kproj_ref),
                (scale_hbm, scale_ref), (wq_hbm, wq), (wk_hbm, wk), (wv_hbm, wv),
                (hgrad_hbm, hgrad_ref), (full_hbm, full),
            )
        )
    ]
    for load in loads:
        load.start()
    barrier = pltpu.get_barrier_semaphore()
    for other in (beside, across, far):
        pl.semaphore_signal(barrier, inc=1, device_id=(group, other), device_id_type=MESH_ID)

    def greet_group(j, carry):
        other = lax.rem(group + j, groups)
        pl.semaphore_signal(barrier, inc=1, device_id=(other, me), device_id_type=MESH_ID)
        return carry

    lax.fori_loop(1, groups, greet_group, 0)
    pl.semaphore_wait(barrier, groups + 2)

    def remote(source, target, ssem, rsem, other):
        return pltpu.make_async_remote_copy(
            src_ref=source, dst_ref=target, send_sem=ssem, recv_sem=rsem,
            device_id=(group, other), device_id_type=MESH_ID,
        )

    def to_group(source, target, ssem, rsem, j):
        other = lax.rem(group + j, groups)
        return pltpu.make_async_remote_copy(
            src_ref=source(other), dst_ref=target.at[group], send_sem=ssem.at[j],
            recv_sem=rsem.at[group], device_id=(other, me), device_id_type=MESH_ID,
        )

    def from_group(source, target, ssem, rsem, j):
        sender = lax.rem(group + j, groups)
        return pltpu.make_async_remote_copy(
            src_ref=source(sender), dst_ref=target.at[sender], send_sem=ssem.at[j],
            recv_sem=rsem.at[sender], device_id=(sender, me), device_id_type=MESH_ID,
        )

    split = (lambda other: split_send, split_hbm, sp_s, sp_r)
    by_heads = (lambda other: heads_send, heads_hbm, hd_s, hd_r)
    shared = (lambda other: shared_send.at[other], shared_hbm, sh_s, sh_r)
    inward = (lambda other: inward_send.at[other, me], inward_hbm, in_s, in_r)
    exchanges = (split, by_heads, shared, inward)

    def start_exchange(number):
        exchange = exchanges[number]

        def one(j, carry):
            to_group(*exchange, j).start()
            return carry

        lax.fori_loop(1, groups, one, 0)
        pltpu.make_async_copy(
            exchange[0](group), exchange[1].at[group], local_sem.at[number]
        ).start()

    def end_exchange(number):
        exchange = exchanges[number]

        def one(j, carry):
            to_group(*exchange, j).wait_send()
            from_group(*exchange, j).wait_recv()
            return carry

        lax.fori_loop(1, groups, one, 0)
        pltpu.make_async_copy(
            exchange[0](group), exchange[1].at[group], local_sem.at[number]
        ).wait()

    low = jnp.bfloat16
    split_send[:, :units] = (adapter_scale_factor * geg_ref[:16]).astype(low)
    split_send[:, units : 2 * units] = (adapter_scale_factor * geu_ref[16:]).astype(low)
    split_send[:, 2 * units : 3 * units] = gsd_ref[...].astype(low)
    split_send[:, 3 * units :] = jnp.broadcast_to(set_ref[...], (16, 128)).astype(low)
    start_exchange(0)
    for t in range(4):
        for g in range(groups):
            at = slice((g * 4 + t) * cols_each, (g * 4 + t + 1) * cols_each)
            blocks[t, g, :16] = (adapter_scale_factor * geo_ref[:, at]).astype(low)
            blocks[t, g, 16:48] = gsgu_ref[:, at].astype(low)
            blocks[t, g, 48:] = (adapter_scale_factor * ged_ref[:, at]).astype(low)
    block_near = remote(blocks.at[beside], blocks_recv.at[0], one_s.at[0], one_r.at[0], beside)
    block_far = remote(blocks.at[far], blocks_recv.at[1], one_s.at[1], one_r.at[1], beside)
    block_across = remote(shared_send, blocks_xrecv, one_s.at[2], one_r.at[2], across)
    block_near.start()
    block_far.start()

    heads = heads_width // HEAD_DIM
    inverse = HEAD_DIM ** (-0.5)
    exponent = inverse * LOG2E
    for ref in (sums_buf, dk_buf, dv_buf):
        ref[...] = jnp.zeros_like(ref)
    block_rows = min(ATT_ROWS, length)

    def attend_back(first_query, first_key, size):
        here = pl.ds(first_query, block_rows)
        keys = pl.ds(first_key, size)

        def head_step(h, carry):
            cols = pl.ds(pl.multiple_of(h * HEAD_DIM, HEAD_DIM), HEAD_DIM)
            queries = qrot_ref[here, cols]
            key_rows = krot_ref[keys, cols]
            grads = dmixed[here, cols]
            scores = attention_scores(
                key_rows, queries, start_ref[:, here], first_query, first_key, 1
            )
            top = jnp.max(scores, axis=0, keepdims=True)
            weights = jnp.exp2((scores - top) * exponent)
            total = jnp.sum(weights, axis=0, keepdims=True)
            probs = weights * (1.0 / total)
            prob_grad = mm_nt(value_ref[keys, cols], grads)
            weighted = probs * prob_grad
            delta = jnp.sum(weighted, axis=0, keepdims=True)
            score_grad = (weighted - probs * delta).astype(low)
            dv_buf[keys, cols] += mm(probs.astype(low), grads)
            dk_buf[keys, cols] += mm(score_grad, queries)
            dq = mm_tn(score_grad, key_rows) * inverse
            dq = dq * cos_ref[here, :] - pltpu.roll(dq, HEAD_DIM // 2, 1) * sin_ref[here, :]
            dq = dq * qgain_ref[:, cols]
            dq_buf[here, cols] = dq
            sums_buf[0, here, :] += qproj_ref[here, cols] * dq
            return carry

        lax.fori_loop(0, heads, head_step, 0, unroll=2)

    for load in loads[:6]:
        load.wait()
    open_table(cos_ref, sin_ref)
    for block in range(length // block_rows):
        first, last = key_window(block, block_rows)
        attend_back(block * block_rows, first, last - first)
        if block == 0:
            block_near.wait_recv()
            block_far.wait_recv()
            shared_send[...] = (
                blocks[across].astype(jnp.float32) + blocks_recv[1].astype(jnp.float32)
            ).astype(low)
            block_across.start()
        if block == 1:
            block_across.wait()
            shared_send[...] = (
                blocks[me].astype(jnp.float32)
                + blocks_recv[0].astype(jnp.float32)
                + blocks_xrecv[...].astype(jnp.float32)
            ).astype(low)
            start_exchange(2)

    def head_end(h, carry):
        cols = pl.ds(pl.multiple_of(h * HEAD_DIM, HEAD_DIM), HEAD_DIM)
        dk = dk_buf[:, cols] * inverse
        dk = dk * cos_ref[...] - pltpu.roll(dk, HEAD_DIM // 2, 1) * sin_ref[...]
        dk = dk * kgain_ref[:, cols]
        dk_buf[:, cols] = dk
        sums_buf[1] += kproj_ref[:, cols] * dk
        dv_low[:, cols] = dv_buf[:, cols].astype(low)
        return carry

    for load in loads[6:]:
        load.wait()
    lax.fori_loop(0, heads, head_end, 0)

    lane = lax.broadcasted_iota(jnp.int32, (length, HEAD_DIM), 1)
    both = jnp.where(
        lane < 4,
        jnp.sum(sums_buf[0], axis=1, keepdims=True),
        jnp.sum(sums_buf[1], axis=1, keepdims=True),
    )
    ex_send[...] = jnp.transpose(both)[:8]
    swaps = [
        remote(ex_send, ex_recv.at[i], es_sem.at[i], er_sem.at[i], other)
        for i, other in enumerate((beside, across, far))
    ]
    for swap in swaps:
        swap.start()
    for swap in swaps:
        swap.wait_recv()
    total = (ex_send[...] + ex_recv[0] + ex_recv[1] + ex_recv[2]) * (1.0 / (4 * heads_width))
    wide = jnp.concatenate(
        [
            jnp.broadcast_to(total[:1], (HEAD_DIM // 2, length)),
            jnp.broadcast_to(total[4:5], (HEAD_DIM // 2, length)),
        ],
        axis=0,
    )
    sums_buf[0] = jnp.transpose(wide)
    for dn, proj, target, at in (
        (dq_buf, qproj_ref, dq_low, 0), (dk_buf, kproj_ref, dk_low, HEAD_DIM // 2),
    ):
        scale = scale_ref[:, at : at + 1]
        means = sums_buf[0, :, at : at + 1]
        target[...] = (scale * dn[...] - proj[...] * (scale * scale * scale * means)).astype(low)

    dmid_part = (
        mm_nt(eq_ref[...], dq_low[...]) + mm_nt(ek_ref[...], dk_low[...])
        + mm_nt(ev_ref[...], dv_low[...])
    )
    dmid_send[...] = dmid_part.astype(low)
    dmid_near = remote(dmid_send, dmid_recv, one_s.at[3], one_r.at[3], beside)
    dmid_across = remote(dmid_xsend, dmid_xrecv, one_s.at[4], one_r.at[4], across)
    dmid_near.start()

    def reduce_beside(c):
        return remote(bsend.at[c], brecv.at[c], bs_sem.at[c], br_sem.at[c], beside)

    def reduce_across(c):
        return remote(xsend.at[c], xrecv.at[c], xs_sem.at[c], xr_sem.at[c], across)

    def chunk_of(buffer, c):
        return jnp.concatenate(
            [buffer[pl.ds(pl.multiple_of(o * rows + c * part, part), part), :] for o in order], axis=0
        )

    def stage_partial(c):
        parts = [chunk_of(buffer, c) for buffer in (dq_low, dk_low, dv_low)]
        tile = TILE

        def one(j, carry):
            at = pl.ds(pl.multiple_of(j * tile, tile), tile)
            value = (
                mm_nt(parts[0], wq[at, :]) + mm_nt(parts[1], wk[at, :]) + mm_nt(parts[2], wv[at, :])
            ).astype(low)
            own_buf[c, :, at] = value[:part]
            xsend[c, :, at] = value[part : 2 * part]
            bsend[c, 0, :, at] = value[2 * part : 3 * part]
            bsend[c, 1, :, at] = value[3 * part :]
            return carry

        lax.fori_loop(0, width // tile, one, 0)
        reduce_beside(c).start()

    def stage_pair(c):
        reduce_beside(c).wait_recv()
        xsend[c] = (xsend[c].astype(jnp.float32) + brecv[c, 1].astype(jnp.float32)).astype(low)
        reduce_across(c).start()
        own_buf[c] = (own_buf[c].astype(jnp.float32) + brecv[c, 0].astype(jnp.float32)).astype(low)

    def partial_step(i, carry):
        @pl.when(i < chunks)
        def _():
            stage_partial(i)

        @pl.when(i == 0)
        def _():
            dmid_near.wait_recv()
            dmid_xsend[...] = (
                dmid_send[...].astype(jnp.float32) + dmid_recv[...].astype(jnp.float32)
            ).astype(low)
            dmid_across.start()

        @pl.when(i > 0)
        def _():
            stage_pair(i - 1)

        return carry

    lax.fori_loop(0, chunks + 1, partial_step, 0)

    mids = mids_ref[...]
    for i, buffer in enumerate((dq_low, dk_low, dv_low)):
        heads_send[:, i * heads_width : (i + 1) * heads_width] = (
            adapter_scale_factor * mm_tn(mids, buffer[...])[i * 16 : (i + 1) * 16]
        ).astype(low)
    heads_send[:, 3 * heads_width :] = gso_ref[...].astype(low)
    start_exchange(1)
    dmid_across.wait_recv()
    dmid = (
        dmid_xsend[...].astype(jnp.float32) + dmid_xrecv[...].astype(jnp.float32)
    ).astype(low)
    inward_grad = mm(dmid, full[...])
    for t in range(4):
        for g in range(groups):
            at = slice((g * 4 + t) * cols_each, (g * 4 + t + 1) * cols_each)
            inward_send[g, t] = inward_grad[:, at]
    start_exchange(3)
    dmid_across.wait_send()
    dmid_xsend[...] = dmid
    mine = pl.ds(pl.multiple_of(me * rows, rows), rows)
    hgrad_ref[...] += mm_tn(dmid_xsend[:, mine], shrink_ref[...])

    def own_rows(c):
        return pl.ds(pl.multiple_of(c * part, part), part)

    def save(c):
        return pltpu.make_async_copy(
            hgrad_ref.at[own_rows(c), :], tgrad_hbm.at[own_rows(c), :], save_sem.at[c]
        )

    def finish_step(c, carry):
        reduce_across(c).wait_recv()
        hgrad_ref[own_rows(c), :] += own_buf[c].astype(jnp.float32) + xrecv[c].astype(jnp.float32)
        save(c).start()
        return carry

    lax.fori_loop(0, chunks, finish_step, 0)
    for c in range(chunks):
        save(c).wait()
    for c in range(chunks):
        reduce_beside(c).wait_send()
        reduce_across(c).wait_send()
    for copy in (block_near, block_far, dmid_near, *swaps):
        copy.wait_send()
    for number in range(4):
        end_exchange(number)


def back(
    qrot, krot, value, dmixed, qproj, kproj, scale, qgain, kgain, table, start_row,
    wq, wk, wv, shrink, eq, ek, ev, mids, full, hgrad, chosen,
    gso, geg, geu, gsd, gsgu, geo, ged,
):
    rows, width = hgrad.shape
    heads_width, units = wq.shape[1], geg.shape[1]
    length = 4 * rows
    part = rows // CHUNKS
    groups = lax.axis_size("dp")
    cols_each = width // (4 * groups)
    split_width = 3 * units + 128
    vmem = pl.BlockSpec(memory_space=pltpu.VMEM)
    hbm = pl.BlockSpec(memory_space=pl.ANY)
    low, f32 = jnp.bfloat16, jnp.float32
    shape = jax.ShapeDtypeStruct
    dma = pltpu.SemaphoreType.DMA
    buf = pltpu.VMEM
    return pl.pallas_call(
        back_body,
        in_specs=[hbm] * 7 + [vmem] * 2 + [hbm] + [vmem] + [hbm] * 3 + [vmem] * 5 + [hbm] * 2 + [vmem] * 8,
        out_specs=[hbm] * 5,
        out_shape=[
            shape((rows, width), f32),
            shape((groups, 16, split_width), low),
            shape((groups, 16, 4 * heads_width), low),
            shape((groups, 64, cols_each), low),
            shape((groups, 48, cols_each), f32),
        ],
        scratch_shapes=[
            buf(wq.shape, low), buf(wk.shape, low), buf(wv.shape, low),
            buf(full.shape, low),
            buf(qrot.shape, low), buf(krot.shape, low), buf(value.shape, low), buf(dmixed.shape, low),
            buf(qproj.shape, f32), buf(kproj.shape, f32), buf(scale.shape, f32),
            buf(table.shape, f32), buf(table.shape, f32), buf(hgrad.shape, f32),
            dma((13,)), dma((CHUNKS,)),
            buf((length, heads_width), f32), buf((length, heads_width), f32),
            buf((length, heads_width), f32),
            buf((length, heads_width), low), buf((length, heads_width), low),
            buf((length, heads_width), low),
            buf((2, length, HEAD_DIM), f32),
            buf((16, split_width), low), buf((16, 4 * heads_width), low),
            buf((4, groups, 64, cols_each), low), buf((2, groups, 64, cols_each), low),
            buf((groups, 64, cols_each), low), buf((groups, 64, cols_each), low),
            buf((groups, 4, 48, cols_each), f32),
            buf((8, length), f32), buf((3, 8, length), f32),
            buf((48, length), low), buf((48, length), low), buf((48, length), low),
            buf((48, length), low),
            buf((CHUNKS, part, width), low), buf((CHUNKS, part, width), low),
            buf((CHUNKS, part, width), low),
            buf((CHUNKS, 2, part, width), low), buf((CHUNKS, 2, part, width), low),
            dma((3,)), dma((3,)), dma((CHUNKS,)), dma((CHUNKS,)), dma((CHUNKS,)), dma((CHUNKS,)),
            dma((5,)), dma((5,)),
        ] + [dma((groups,))] * 8 + [dma((4,))],
        cost_estimate=pl.CostEstimate(
            flops=2 * length * heads_width * (3 * width + 5 * length),
            bytes_accessed=2 * width * (3 * heads_width + 3 * length), transcendentals=0,
        ),
        compiler_params=pltpu.CompilerParams(
            collective_id=2, has_side_effects=True, vmem_limit_bytes=67043328
        ),
        name="attention_back_to_tokens",
    )(qrot, krot, value, dmixed, qproj, kproj, scale, qgain, kgain, table, start_row,
      wq, wk, wv, shrink, eq, ek, ev, mids, full, hgrad, chosen,
      gso, geg, geu, gsd, gsgu, geo, ged)


def finish_body(split_ref, heads_ref, shared_ref, inward_ref, block_ref, tokens_ref, *outs):
    block_out, tokens_out, *outs, which = outs
    groups = split_ref.shape[0]
    tag = split_ref.shape[2] - 128
    together = outs[0].shape[0]
    first = pl.program_id(0) * together

    @pl.when(first == 0)
    def _():
        for g in range(groups):
            which[g] = jnp.max(split_ref[g, :, tag:].astype(jnp.float32)).astype(jnp.int32)

    sq, eq, sk, ek, sv, ev, so, eo, sg, eg, su, eu, sd, ed = outs
    here = eq.shape[2]
    units = eg.shape[2]
    sources = []
    for i, target in enumerate((eq, ek, ev, so)):
        sources.append((target, lambda g, i=i: heads_ref[g, :, i * here : (i + 1) * here]))
    for i, target in enumerate((eg, eu, sd)):
        sources.append((target, lambda g, i=i: split_ref[g, :, i * units : (i + 1) * units]))
    for i, target in enumerate((sq, sk, sv)):
        sources.append((target, lambda g, i=i: inward_ref[g, i * 16 : (i + 1) * 16, :]))
    for i, target in enumerate((eo, sg, su, ed)):
        sources.append((target, lambda g, i=i: shared_ref[g, i * 16 : (i + 1) * 16, :]))
    for target, _ in sources:
        target[...] = jnp.zeros_like(target)

    def one(g, carry):
        at = which[g] - first

        @pl.when((at >= 0) & (at < together))
        def _():
            for target, source in sources:
                target[at] += source(g).astype(jnp.float32)

        return carry

    lax.fori_loop(0, groups, one, 0)
    block_out[...] = block_ref[...]
    tokens_out[...] = tokens_ref[...]


def finish(split, by_heads, shared, inward, block, tokens, sets, here, units):
    cols = shared.shape[2]
    rows, width = block.shape
    steps = min(FINISH_STEPS, sets)
    together = sets // steps
    part = rows // steps
    whole = lambda a: pl.BlockSpec(a.shape, lambda i: (0,) * a.ndim)
    strip = pl.BlockSpec((part, width), lambda i: (i, 0))
    widths = (cols, here, cols, here, cols, here, here, cols, cols, units, cols, units, units, cols)
    return pl.pallas_call(
        finish_body,
        grid=(steps,),
        in_specs=[whole(split), whole(by_heads), whole(shared), whole(inward), strip, strip],
        out_specs=[strip, strip] + [pl.BlockSpec((together, 16, w), lambda i: (i, 0, 0)) for w in widths],
        out_shape=[
            jax.ShapeDtypeStruct(block.shape, block.dtype),
            jax.ShapeDtypeStruct(tokens.shape, tokens.dtype),
        ] + [jax.ShapeDtypeStruct((sets, 16, w), jnp.float32) for w in widths],
        scratch_shapes=[pltpu.SMEM((split.shape[0],), jnp.int32)],
        compiler_params=pltpu.CompilerParams(vmem_limit_bytes=67043328),
        name="sum_by_set",
    )(split, by_heads, shared, inward, block, tokens)


def per_device(
    tokens,
    cotangent,
    segment_ids,
    adapter_set,
    w_query,
    w_key,
    w_value,
    w_out,
    w_gate,
    w_up,
    w_down,
    query_gain,
    key_gain,
    mixer_gain,
    feed_gain,
    shrink_query,
    expand_query,
    shrink_key,
    expand_key,
    shrink_value,
    expand_value,
    shrink_out,
    expand_out,
    shrink_gate,
    expand_gate,
    shrink_up,
    expand_up,
    shrink_down,
    expand_down,
):
    length = 4 * tokens.shape[0]
    table = jnp.asarray(rotary_constants(length, HEAD_DIM))
    (
        shrink_rows, expand_query_rows, expand_key_rows, expand_value_rows, out_shrink, out_expand,
        gate_up_shrink, gate_expand, up_expand, down_shrink, down_expand,
        query_gains, key_gains, mixer_gains, feed_gains, start_col, start_row, set_row,
        mixed, query_rot, key_rot, value_low, query_proj, key_proj, scales, qkv_middle, full_tokens,
    ) = front(
        adapter_set, tokens, w_query, w_key, w_value, table, segment_ids,
        (query_gain, key_gain, mixer_gain, feed_gain),
        (
            shrink_query, expand_query, shrink_key, expand_key, shrink_value, expand_value,
            shrink_out, expand_out, shrink_gate, expand_gate, shrink_up, expand_up,
            shrink_down, expand_down,
        ),
    )
    (
        block_output, hidden_grad, mixed_grad, grad_down_shrink, gradient_gate_widened,
        gradient_up_widened, grad_out_shrink, owner_gate_up, owner_out, owner_down,
    ) = middle(
        mixed, tokens, cotangent, w_out, w_gate, w_up, w_down, mixer_gains, feed_gains,
        out_shrink, out_expand, gate_up_shrink, gate_expand, up_expand, down_shrink, down_expand,
    )
    token_grads, split, by_heads, shared, inward = back(
        query_rot, key_rot, value_low, mixed_grad.reshape(mixed.shape), query_proj, key_proj, scales,
        query_gains, key_gains, table, start_row,
        w_query, w_key, w_value, shrink_rows, expand_query_rows, expand_key_rows, expand_value_rows,
        qkv_middle, full_tokens.reshape(length, -1), hidden_grad, set_row,
        grad_out_shrink, gradient_gate_widened, gradient_up_widened, grad_down_shrink,
        owner_gate_up, owner_out, owner_down,
    )
    return finish(
        split, by_heads, shared, inward, block_output, token_grads,
        shrink_query.shape[0], w_query.shape[1], w_gate.shape[1],
    )


def solution(mesh):
    in_specs = (
        P(("dp", "tensor"), None),
        P(("dp", "tensor"), None),
        P("dp", None),
        P("dp"),
        P(None, "tensor"),
        P(None, "tensor"),
        P(None, "tensor"),
        P("tensor", None),
        P(None, "tensor"),
        P(None, "tensor"),
        P("tensor", None),
        P("tensor"),
        P("tensor"),
        P(),
        P(),
        P(),
        P(None, None, "tensor"),
        P(),
        P(None, None, "tensor"),
        P(),
        P(None, None, "tensor"),
        P(None, None, "tensor"),
        P(),
        P(),
        P(None, None, "tensor"),
        P(),
        P(None, None, "tensor"),
        P(None, None, "tensor"),
        P(),
    )
    out_specs = (
        P(("dp", "tensor"), None),
        P(("dp", "tensor"), None),
        P(None, None, ("dp", "tensor")),
        P(None, None, "tensor"),
        P(None, None, ("dp", "tensor")),
        P(None, None, "tensor"),
        P(None, None, ("dp", "tensor")),
        P(None, None, "tensor"),
        P(None, None, "tensor"),
        P(None, None, ("dp", "tensor")),
        P(None, None, ("dp", "tensor")),
        P(None, None, "tensor"),
        P(None, None, ("dp", "tensor")),
        P(None, None, "tensor"),
        P(None, None, "tensor"),
        P(None, None, ("dp", "tensor")),
    )
    return jax.shard_map(
        per_device, mesh=mesh, in_specs=in_specs, out_specs=out_specs, check_vma=False
    )
```

```python
import functools
import jax
import jax.numpy as jnp
import numpy as np
from jax import lax
from jax.experimental import pallas as pl
from jax.experimental.pallas import tpu as pltpu
from jax.sharding import PartitionSpec as P

HEAD_DIM = 128
DOC_MOST = 512
ATT_ROWS = 256
rotary_base = 500000.0
NEG = -1e30
LOG2E = 1.4426950408889634


def rotary_constants(length, head_dim):
    half = head_dim // 2
    frequency = np.float32(rotary_base) ** (
        -(np.arange(half, dtype=np.float32) * np.float32(2.0) / np.float32(head_dim))
    )
    angles = np.arange(length, dtype=np.float32)[:, None] * frequency.astype(np.float32)[None, :]
    cosine = np.cos(angles.astype(np.float64)).astype(np.float32)
    sine = np.sin(angles.astype(np.float64)).astype(np.float32)
    return np.concatenate([cosine, sine], axis=1)


def open_table(cos_ref, sin_ref):
    table = cos_ref[...]
    turned = pltpu.roll(table, HEAD_DIM // 2, 1)
    low_half = lax.broadcasted_iota(jnp.int32, table.shape, 1) < HEAD_DIM // 2
    cos_ref[...] = jnp.where(low_half, table, turned)
    sin_ref[...] = jnp.where(low_half, -turned, table)


def key_window(block, rows):
    first = max(0, (block * rows - (DOC_MOST - 1)) // rows) * rows
    return first, (block + 1) * rows


epsilon = 1e-06
adapter_scale_factor = 0.5


CHUNKS = 4
FINISH_STEPS = 2
TILE = 1024
EXTRA = 128
NT = (((1,), (1,)), ((), ()))
TN = (((0,), (0,)), ((), ()))
MESH_ID = pl.DeviceIdType.MESH
MIDDLE_STAGES = ("S0", "P0", "S1", "F1", "S2", "P2", "S3", "F3", "S4", "P4", "S5", "F5", "S6")
MIDDLE_ORDER = (
    0, 1, 2, 4, 3, 5, 6, 7, 8, 9, 10, 11, 12,
    16, 13, 14, 17, 20, 18, 21, 15, 24, 19, 22, 25, 23,
    28, 32, 26, 29, 36, 33, 27, 30, 37, 34, 40, 31, 38,
    35, 41, 44, 39, 48, 42, 45, 49, 43, 46, 50, 47, 51,
)


def mm(left, right):
    return jnp.dot(left, right, preferred_element_type=jnp.float32)


def mm_nt(left, right):
    return lax.dot_general(left, right, NT, preferred_element_type=jnp.float32)


def mm_tn(left, right):
    return lax.dot_general(left, right, TN, preferred_element_type=jnp.float32)


def partners():
    me = lax.axis_index("tensor")
    group = lax.axis_index("dp")
    beside = me + 1 - 2 * lax.rem(me, 2)
    across = lax.rem(me + 2, 4)
    return me, group, beside, across


def greet(group, beside, across):
    barrier = pltpu.get_barrier_semaphore()
    for other in (beside, across):
        pl.semaphore_signal(barrier, inc=1, device_id=(group, other), device_id_type=MESH_ID)
    pl.semaphore_wait(barrier, 2)


def middle_body(
    mixed_ref, tokens_ref, cot_ref, w_out_hbm, w_gate_hbm, w_up_hbm, w_down_hbm,
    mgain_ref, fgain_ref, so_ref, eo_ref, sgu_ref, eg_ref, eu_ref, sd_ref, ed_ref,
    out_hbm, hgrad_hbm, dmixed_hbm, gsd_ref, geg_ref, geu_ref, gso_ref, gsgu_ref, geo_ref, ged_ref,
    w_out, w_gate, w_up, w_down, wsem, out_ref, dmixed_ref, save_sem,
    rows_buf, own_buf, xsend, xrecv, bsend, brecv,
    gate_buf, up_buf, temp_a, temp_b, mgu_buf, mixer_buf, hidden_buf, mout_buf,
    xs_sem, xr_sem, bs_sem, br_sem, gxs_sem, gxr_sem, gbs_sem, gbr_sem, fs_sem, fr_sem,
):
    me, group, beside, across = partners()
    chunks, part, width = rows_buf.shape[0], rows_buf.shape[2], rows_buf.shape[3]
    units = w_gate.shape[1]
    heads_width = w_out.shape[0]
    far = lax.rem(beside + 2, 4)
    order = (me, across, beside, far)
    loads = [
        pltpu.make_async_copy(source, target, wsem.at[i])
        for i, (source, target) in enumerate(
            ((w_out_hbm, w_out), (w_gate_hbm, w_gate), (w_up_hbm, w_up), (w_down_hbm, w_down))
        )
    ]
    for load in loads:
        load.start()
    for ref in (gsd_ref, geg_ref, geu_ref, gso_ref, gsgu_ref, geo_ref, ged_ref):
        ref[...] = jnp.zeros_like(ref)
    greet(group, beside, across)

    def remote(source, target, ssem, rsem, other):
        return pltpu.make_async_remote_copy(
            src_ref=source, dst_ref=target, send_sem=ssem, recv_sem=rsem,
            device_id=(group, other), device_id_type=MESH_ID,
        )

    def gather_across(c):
        return remote(rows_buf.at[c, 0], rows_buf.at[c, 1], gxs_sem.at[c], gxr_sem.at[c], across)

    def gather_beside(c):
        return remote(rows_buf.at[c, 0], rows_buf.at[c, 2], gbs_sem.at[c], gbr_sem.at[c], beside)

    def gather_forward(c):
        return remote(rows_buf.at[c, 1], rows_buf.at[c, 3], fs_sem.at[c], fr_sem.at[c], beside)

    def reduce_beside(c):
        return remote(bsend.at[c], brecv.at[c], bs_sem.at[c], br_sem.at[c], beside)

    def reduce_across(c):
        return remote(xsend.at[c], xrecv.at[c], xs_sem.at[c], xr_sem.at[c], across)

    def store_partial(c, columns, value):
        low = value.astype(jnp.bfloat16)
        own_buf[c, :, columns] = low[:part]
        xsend[c, :, columns] = low[part : 2 * part]
        bsend[c, 0, :, columns] = low[2 * part : 3 * part]
        bsend[c, 1, :, columns] = low[3 * part :]

    def gathered(c):
        return rows_buf[c].reshape(4 * part, width)

    def forward_stage(c):
        gather_across(c).wait_recv()
        gather_forward(c).start()

    def pair_stage(c):
        reduce_beside(c).wait_recv()
        own_buf[c] = (
            own_buf[c].astype(jnp.float32) + brecv[c, 0].astype(jnp.float32)
        ).astype(jnp.bfloat16)
        xsend[c] = (
            xsend[c].astype(jnp.float32) + brecv[c, 1].astype(jnp.float32)
        ).astype(jnp.bfloat16)
        reduce_across(c).start()

    def totals(c):
        reduce_across(c).wait_recv()
        main = own_buf[c, :, :width].astype(jnp.float32) + xrecv[c, :, :width].astype(jnp.float32)
        side = own_buf[c, :, width : width + 32].astype(jnp.float32) + xrecv[
            c, :, width : width + 32
        ].astype(jnp.float32)
        return main, side.astype(jnp.bfloat16)

    def own_rows(c):
        return pl.ds(pl.multiple_of(c * part, part), part)

    def save(number, c):
        source, target = ((out_ref, out_hbm), (hidden_buf, hgrad_hbm))[number]
        return pltpu.make_async_copy(
            source.at[own_rows(c), :], target.at[own_rows(c), :], save_sem.at[number, c]
        )

    def send_rows(c, value, again):
        if again:
            gather_across(c).wait_send()
            gather_beside(c).wait_send()
        rows_buf[c, 0] = value
        gather_across(c).start()
        gather_beside(c).start()

    def chunk_rows(c):
        return pl.ds(pl.multiple_of(c * 4 * part, 4 * part), 4 * part)

    def tiles(total, tile, body):
        def step(j, carry):
            body(pl.ds(pl.multiple_of(j * tile, tile), tile))
            return carry

        lax.fori_loop(0, total // tile, step, 0)

    def mixed_chunk(c):
        return jnp.concatenate([mixed_ref[o, c] for o in order], axis=0)

    def stage_mixer(c):
        @pl.when(c == 0)
        def _():
            loads[0].wait()

        rows = mixed_chunk(c)
        store_partial(c, slice(width, width + 16), mm_nt(rows, so_ref[...]))
        tiles(width, TILE, lambda cols: store_partial(c, cols, mm(rows, w_out[:, cols])))
        reduce_beside(c).start()

    def stage_hidden(c):
        main, side = totals(c)
        mid = side[:, :16]
        mout_buf[c] = mid
        mixer = main + mm(mid, eo_ref[...])
        mixer_buf[own_rows(c), :] = mixer
        factor = lax.rsqrt(jnp.mean(mixer * mixer, axis=1, keepdims=True) + epsilon)
        hidden = tokens_ref[own_rows(c), :].astype(jnp.float32) + mixer * factor * mgain_ref[...]
        hidden_buf[own_rows(c), :] = hidden
        send_rows(c, hidden.astype(jnp.bfloat16), False)

    def arrive(c):
        gather_beside(c).wait_recv()
        gather_forward(c).wait_recv()

    def stage_units(c):
        @pl.when(c == 0)
        def _():
            for load in loads[1:]:
                load.wait()

        arrive(c)
        mids = mm_nt(gathered(c), sgu_ref[...]).astype(jnp.bfloat16)
        mgu_buf[c] = mids

        def unit_tile(cols):
            rows = gathered(c)
            gate = mm(rows, w_gate[:, cols]) + mm(mids, eg_ref[:, cols])
            up = mm(rows, w_up[:, cols]) + mm(mids, eu_ref[:, cols])
            gate_buf[chunk_rows(c), cols] = gate.astype(jnp.bfloat16)
            up_buf[chunk_rows(c), cols] = up.astype(jnp.bfloat16)
            sig = 1.0 / (1.0 + jnp.exp(-gate))
            temp_a[:, cols] = (gate * sig * up).astype(jnp.bfloat16)

        tiles(units, TILE, unit_tile)
        gather_forward(c).wait_send()
        reduce_beside(c).wait_send()
        reduce_across(c).wait_send()
        inner = temp_a[...]
        store_partial(c, slice(width, width + 16), mm_nt(inner, sd_ref[...]))
        tiles(width, 2 * TILE, lambda cols: store_partial(c, cols, mm(temp_a[...], w_down[:, cols])))
        reduce_beside(c).start()

    def norm_back_rows(values, gains, grads):
        factor = lax.rsqrt(jnp.mean(values * values, axis=1, keepdims=True) + epsilon)
        weighted = grads * gains
        return factor * weighted - values * (
            factor * factor * factor * jnp.mean(values * weighted, axis=1, keepdims=True)
        )

    def stage_feed(c):
        main, side = totals(c)
        mid = side[:, :16]
        feed = main + mm(mid, ed_ref[...])
        factor = lax.rsqrt(jnp.mean(feed * feed, axis=1, keepdims=True) + epsilon)
        gains = fgain_ref[...]
        out_ref[own_rows(c), :] = (hidden_buf[own_rows(c), :] + feed * factor * gains).astype(
            jnp.bfloat16
        )
        save(0, c).start()
        grad = norm_back_rows(feed, gains, cot_ref[own_rows(c), :].astype(jnp.float32))
        grad = grad.astype(jnp.bfloat16)
        send_rows(c, grad, True)
        ged_ref[...] += mm_tn(mid, grad)

    def stage_units_back(c):
        arrive(c)
        dmid = mm_nt(gathered(c), ed_ref[...]).astype(jnp.bfloat16)
        mids = mgu_buf[c]

        def unit_tile(cols):
            rows = gathered(c)
            inner_grad = mm_nt(rows, w_down[cols, :]) + mm(dmid, sd_ref[:, cols])
            gate = gate_buf[chunk_rows(c), cols].astype(jnp.float32)
            up = up_buf[chunk_rows(c), cols].astype(jnp.float32)
            sig = 1.0 / (1.0 + jnp.exp(-gate))
            silu = gate * sig
            gate_grad = (inner_grad * up * (sig + silu * (1.0 - sig))).astype(jnp.bfloat16)
            up_grad = (inner_grad * silu).astype(jnp.bfloat16)
            temp_a[:, cols] = gate_grad
            temp_b[:, cols] = up_grad
            gsd_ref[:, cols] += mm_tn(dmid, (silu * up).astype(jnp.bfloat16))
            geg_ref[:, cols] += mm_tn(mids, gate_grad)
            geu_ref[:, cols] += mm_tn(mids, up_grad)

        tiles(units, TILE, unit_tile)
        gather_forward(c).wait_send()
        reduce_beside(c).wait_send()
        reduce_across(c).wait_send()
        store_partial(
            c,
            slice(width, width + 32),
            mm_nt(temp_a[...], eg_ref[...]) + mm_nt(temp_b[...], eu_ref[...]),
        )

        def width_tile(cols):
            store_partial(
                c, cols, mm_nt(temp_a[...], w_gate[cols, :]) + mm_nt(temp_b[...], w_up[cols, :])
            )

        tiles(width, TILE, width_tile)
        reduce_beside(c).start()

    def stage_mixer_grad(c):
        main, side = totals(c)
        grads = cot_ref[own_rows(c), :].astype(jnp.float32) + main + mm(side, sgu_ref[...])
        mixer_grad = norm_back_rows(mixer_buf[own_rows(c), :], mgain_ref[...], grads)
        mixer_grad = mixer_grad.astype(jnp.bfloat16)
        send_rows(c, mixer_grad, True)
        geo_ref[...] += mm_tn(mout_buf[c], mixer_grad)
        gsgu_ref[...] += mm_tn(side, hidden_buf[own_rows(c), :].astype(jnp.bfloat16))
        hidden_buf[own_rows(c), :] = grads
        save(1, c).start()

    def stage_mixed_grad(c):
        arrive(c)
        dmid = mm_nt(gathered(c), eo_ref[...]).astype(jnp.bfloat16)
        grad = (mm_nt(gathered(c), w_out[...]) + mm(dmid, so_ref[...])).astype(jnp.bfloat16)
        for i, o in enumerate(order):
            dmixed_ref[o, c] = grad[i * part : (i + 1) * part]
        gso_ref[...] += mm_tn(dmid, mixed_chunk(c))
        gather_forward(c).wait_send()
        gather_across(c).wait_send()
        gather_beside(c).wait_send()
        reduce_beside(c).wait_send()
        reduce_across(c).wait_send()

    stages = {
        "S0": stage_mixer, "S1": stage_hidden, "S2": stage_units, "S3": stage_feed,
        "S4": stage_units_back, "S5": stage_mixer_grad, "S6": stage_mixed_grad,
        "P0": pair_stage, "P2": pair_stage, "P4": pair_stage,
        "F1": forward_stage, "F3": forward_stage, "F5": forward_stage,
    }

    packed = [
        sum(code << (6 * j) for j, code in enumerate(MIDDLE_ORDER[at : at + 5]))
        for at in range(0, len(MIDDLE_ORDER), 5)
    ]

    def step(i, carry):
        word = jnp.int32(packed[0])
        for k in range(1, len(packed)):
            word = jnp.where(i >= 5 * k, jnp.int32(packed[k]), word)
        place = lax.rem(i, 5)
        unit = jnp.int32(1)
        for k in range(1, 5):
            unit = jnp.where(place == k, jnp.int32(64**k), unit)
        code = lax.rem(lax.div(word, unit), 64)
        stage, c = lax.div(code, chunks), lax.rem(code, chunks)
        for k, name in enumerate(MIDDLE_STAGES):

            @pl.when(stage == k)
            def _():
                stages[name](c)

        return carry

    lax.fori_loop(0, len(MIDDLE_ORDER), step, 0)
    save_mixture = pltpu.make_async_copy(dmixed_ref, dmixed_hbm, save_sem.at[2, 0])
    save_mixture.start()
    for c in range(chunks):
        for number in range(2):
            save(number, c).wait()
    save_mixture.wait()


def middle(mixed, tokens, cot, w_out, w_gate, w_up, w_down, mgain, fgain, so, eo, sgu, eg, eu, sd, ed):
    rows, width = tokens.shape
    heads_width, units = w_out.shape[0], w_gate.shape[1]
    part = rows // CHUNKS
    whole_width = width + EXTRA
    vmem = pl.BlockSpec(memory_space=pltpu.VMEM)
    hbm = pl.BlockSpec(memory_space=pl.ANY)
    low, full = jnp.bfloat16, jnp.float32
    dma = pltpu.SemaphoreType.DMA((CHUNKS,))
    shape = jax.ShapeDtypeStruct
    flops = 2 * 4 * rows * width * (2 * heads_width + 6 * units)
    return pl.pallas_call(
        middle_body,
        in_specs=[vmem] * 3 + [hbm] * 4 + [vmem] * 9,
        out_specs=[hbm] * 3 + [vmem] * 7,
        out_shape=[
            shape((rows, width), low), shape((rows, width), full),
            shape((4, CHUNKS, part, heads_width), low),
            shape((16, units), full), shape((32, units), full), shape((32, units), full),
            shape((16, heads_width), full), shape((32, width), full), shape((16, width), full),
            shape((16, width), full),
        ],
        scratch_shapes=[
            pltpu.VMEM(w_out.shape, low), pltpu.VMEM(w_gate.shape, low),
            pltpu.VMEM(w_up.shape, low), pltpu.VMEM(w_down.shape, low),
            pltpu.SemaphoreType.DMA((4,)),
            pltpu.VMEM((rows, width), low), pltpu.VMEM((4, CHUNKS, part, heads_width), low),
            pltpu.SemaphoreType.DMA((3, CHUNKS)),
            pltpu.VMEM((CHUNKS, 4, part, width), low),
            pltpu.VMEM((CHUNKS, part, whole_width), low),
            pltpu.VMEM((CHUNKS, part, whole_width), low),
            pltpu.VMEM((CHUNKS, part, whole_width), low),
            pltpu.VMEM((CHUNKS, 2, part, whole_width), low),
            pltpu.VMEM((CHUNKS, 2, part, whole_width), low),
            pltpu.VMEM((4 * rows, units), low), pltpu.VMEM((4 * rows, units), low),
            pltpu.VMEM((4 * part, units), low), pltpu.VMEM((4 * part, units), low),
            pltpu.VMEM((CHUNKS, 4 * part, 32), low),
            pltpu.VMEM((rows, width), full), pltpu.VMEM((rows, width), full),
            pltpu.VMEM((CHUNKS, part, 16), low),
        ] + [dma] * 10,
        cost_estimate=pl.CostEstimate(
            flops=flops, bytes_accessed=2 * width * (heads_width + 3 * units), transcendentals=0
        ),
        compiler_params=pltpu.CompilerParams(
            collective_id=0, has_side_effects=True, vmem_limit_bytes=67043328
        ),
        name="mixer_to_feed",
    )(mixed.reshape(4, CHUNKS, part, heads_width), tokens, cot, w_out, w_gate, w_up, w_down,
      mgain, fgain, so, eo, sgu, eg, eu, sd, ed)


def probs_space(length, heads_width):
    rows = min(ATT_ROWS, length)
    blocks = length // rows
    longest = max(high - low for low, high in (key_window(b, rows) for b in range(blocks)))
    return (blocks, heads_width // HEAD_DIM, longest, rows)


def attention_scores(first, second, start, first_query, first_key, query_axis):
    scores = lax.dot_general(first, second, NT, preferred_element_type=jnp.float32)
    kpos = lax.broadcasted_iota(jnp.int32, scores.shape, 1 - query_axis) + first_key
    shape = [1, 1]
    shape[query_axis] = scores.shape[query_axis]
    qpos = lax.broadcasted_iota(jnp.int32, shape, query_axis) + first_query
    return jnp.where((kpos <= qpos) & (kpos >= start), scores, NEG)


def pick_body(
    at, seg_ref, qgain, kgain, mgain, fgain,
    sq, eq, sk, ek, sv, ev, so, eo, sg, eg, su, eu, sd, ed,
    shrink_out, eq_out, ek_out, ev_out, so_out, eo_out, sgu_out, eg_out, eu_out, sd_out, ed_out,
    qgain_out, kgain_out, mgain_out, fgain_out, start_row, set_out,
):
    rank = sq.shape[1]

    def scaled(ref):
        return (adapter_scale_factor * ref[at].astype(jnp.float32)).astype(jnp.bfloat16)

    for i, ref in enumerate((sq, sk, sv)):
        shrink_out[i * rank : (i + 1) * rank, :] = ref[at]
    for i, (ref, target) in enumerate(((eq, eq_out), (ek, ek_out), (ev, ev_out))):
        target[...] = jnp.zeros_like(target)
        target[i * rank : (i + 1) * rank, :] = scaled(ref)
    for i, (ref, target) in enumerate(((eg, eg_out), (eu, eu_out))):
        target[...] = jnp.zeros_like(target)
        target[i * rank : (i + 1) * rank, :] = scaled(ref)
    so_out[...] = so[at]
    sd_out[...] = sd[at]
    eo_out[...] = scaled(eo)
    ed_out[...] = scaled(ed)
    sgu_out[:rank, :] = sg[at]
    sgu_out[rank:, :] = su[at]
    for ref, target in ((qgain, qgain_out), (kgain, kgain_out), (mgain, mgain_out), (fgain, fgain_out)):
        target[...] = ref[...].astype(jnp.float32).reshape(target.shape)
    length = seg_ref.shape[1]
    row = seg_ref[...].astype(jnp.float32)
    col = jnp.transpose(jnp.broadcast_to(row, (HEAD_DIM, length)))[:, :1]
    start_row[...] = jnp.sum(
        jnp.where(col < row, 1.0, 0.0), axis=0, keepdims=True
    ).astype(jnp.int32)
    set_out[...] = jnp.full(set_out.shape, at, jnp.int32).astype(jnp.float32)


def front_body(
    set_ref, tokens_ref, wq_hbm, wk_hbm, wv_hbm, table_ref, seg_ref, qg_ref, kg_ref, mg_ref, fg_ref,
    *refs,
):
    adapters_hbm, refs = refs[:14], refs[14:]
    picked, refs = refs[:17], refs[17:]
    adapters, adapter_sem, refs = refs[-15:-1], refs[-1], refs[:-15]
    shrink_ref, eq_ref, ek_ref, ev_ref = picked[:4]
    qgain_ref, kgain_ref, start_ref = picked[11], picked[12], picked[15]
    front_steps(
        set_ref, tokens_ref, wq_hbm, wk_hbm, wv_hbm, table_ref,
        (seg_ref, qg_ref, kg_ref, mg_ref, fg_ref), adapters_hbm, adapters, adapter_sem, picked,
        shrink_ref, eq_ref, ek_ref, ev_ref, qgain_ref, kgain_ref, start_ref, *refs,
    )


def front_steps(
    set_ref, tokens_ref, wq_hbm, wk_hbm, wv_hbm, table_ref, small, adapters_hbm, adapters,
    adapter_sem, picked, shrink_ref, eq_ref, ek_ref, ev_ref, qgain_ref, kgain_ref, start_ref,
    mixed_hbm, qrot_hbm, krot_hbm, value_hbm, qproj_hbm, kproj_hbm, scale_hbm, mids_hbm, full_hbm,
    probs_hbm, probs_ref, mixed_ref, qrot_ref, krot_ref, value_ref, qproj_ref, kproj_ref, scale_ref, mids_ref, cos_ref, sin_ref,
    wq, wk, wv, wsem, full, lhs, squares, ex_send, ex_recv,
    xs_sem, xr_sem, fs_sem, fr_sem, bs_sem, br_sem, es_sem, er_sem, out_sem,
):
    me, group, beside, across = partners()
    far = lax.rem(beside + 2, 4)
    chunks, part, width = full.shape[1:]
    rows = chunks * part
    length = 4 * rows
    loads = [
        pltpu.make_async_copy(source, target, wsem.at[i])
        for i, (source, target) in enumerate(((wq_hbm, wq), (wk_hbm, wk), (wv_hbm, wv)))
    ]
    barrier = pltpu.get_barrier_semaphore()
    for other in (beside, across, far):
        pl.semaphore_signal(barrier, inc=1, device_id=(group, other), device_id_type=MESH_ID)
    fetches = [
        pltpu.make_async_copy(source, target, adapter_sem.at[i])
        for i, (source, target) in enumerate(zip(adapters_hbm, adapters))
    ]
    for load in (*fetches, *loads):
        load.start()
    pl.semaphore_wait(barrier, 3)

    def remote(source, target, ssem, rsem, other):
        return pltpu.make_async_remote_copy(
            src_ref=source, dst_ref=target, send_sem=ssem, recv_sem=rsem,
            device_id=(group, other), device_id_type=MESH_ID,
        )

    def send_across(c):
        return remote(tokens_ref.at[c], full.at[me, c], xs_sem.at[c], xr_sem.at[c], across)

    def forward(c):
        return remote(full.at[across, c], full.at[across, c], fs_sem.at[c], fr_sem.at[c], beside)

    to_beside = remote(tokens_ref, full.at[me], bs_sem, br_sem, beside)
    for c in range(chunks):
        send_across(c).start()
    to_beside.start()
    full[me] = tokens_ref[...]
    cos_ref[...] = table_ref[...]
    open_table(cos_ref, sin_ref)
    for fetch in fetches:
        fetch.wait()
    pick_body(set_ref[0], *small, *adapters, *picked)
    for load in loads:
        load.wait()
    pairs = chunks // 2
    half = rows // 2

    def block_step(b, carry):
        @pl.when(b == 0)
        def _():
            lhs[...] = tokens_ref[...].reshape(rows, width)

        @pl.when(b == 1)
        def _():
            to_beside.wait_recv()
            lhs[...] = full[beside].reshape(rows, width)

        @pl.when(b >= 2)
        def _():
            base = (b - 2) * pairs
            for j in range(pairs):
                send_across(base + j).wait_recv()
                forward(base + j).start()
            for j in range(pairs):
                lhs[j * part : (j + 1) * part] = full[across, base + j]
            for j in range(pairs):
                forward(base + j).wait_recv()
                lhs[half + j * part : half + (j + 1) * part] = full[far, base + j]

        mids = mm_nt(lhs[...], shrink_ref[...]).astype(jnp.bfloat16)
        query = mm(lhs[...], wq[...]) + mm(mids, eq_ref[...])
        key = mm(lhs[...], wk[...]) + mm(mids, ek_ref[...])
        value = (mm(lhs[...], wv[...]) + mm(mids, ev_ref[...])).astype(jnp.bfloat16)
        qsum = jnp.sum(query * query, axis=1, keepdims=True)
        ksum = jnp.sum(key * key, axis=1, keepdims=True)
        lane = lax.broadcasted_iota(jnp.int32, (rows, HEAD_DIM), 1)
        both = jnp.where(lane < 4, qsum, ksum)
        first = jnp.where(b == 0, me, jnp.where(b == 1, beside, across)) * rows
        second = jnp.where(b == 0, me, jnp.where(b == 1, beside, far)) * rows
        first = first + jnp.where(b >= 2, (b - 2) * half, 0)
        second = second + jnp.where(b >= 2, (b - 2) * half, half)
        for start, piece in ((first, slice(0, half)), (second, slice(half, rows))):
            there = pl.ds(pl.multiple_of(start, half), half)
            qproj_ref[there, :] = query[piece]
            kproj_ref[there, :] = key[piece]
            value_ref[there, :] = value[piece]
            mids_ref[there, :] = mids[piece]
            squares[there, :] = both[piece]
        return carry

    lax.fori_loop(0, 4, block_step, 0)
    saves = [
        pltpu.make_async_copy(source, target, out_sem.at[i])
        for i, (source, target) in enumerate(
            (
                (full, full_hbm), (value_ref, value_hbm), (qproj_ref, qproj_hbm),
                (kproj_ref, kproj_hbm), (mids_ref, mids_hbm), (scale_ref, scale_hbm),
                (qrot_ref, qrot_hbm), (krot_ref, krot_hbm), (mixed_ref, mixed_hbm),
                (probs_ref, probs_hbm),
            )
        )
    ]
    for save in saves[:5]:
        save.start()
    ex_send[...] = jnp.transpose(squares[...])[:8]
    swaps = [
        remote(ex_send, ex_recv.at[i], es_sem.at[i], er_sem.at[i], other)
        for i, other in enumerate((beside, across, far))
    ]
    for swap in swaps:
        swap.start()
    for swap in swaps:
        swap.wait_recv()
    total = ex_send[...] + ex_recv[0] + ex_recv[1] + ex_recv[2]
    factor = lax.rsqrt(total / (4 * wq.shape[1]) + epsilon)
    wide = jnp.concatenate(
        [
            jnp.broadcast_to(factor[:1], (HEAD_DIM // 2, length)),
            jnp.broadcast_to(factor[4:5], (HEAD_DIM // 2, length)),
        ],
        axis=0,
    )
    scale_ref[...] = jnp.transpose(wide)
    heads = wq.shape[1] // HEAD_DIM
    exponent = HEAD_DIM ** (-0.5) * LOG2E
    block_rows = min(ATT_ROWS, length)

    def turn_step(h, carry):
        cols = pl.ds(pl.multiple_of(h * HEAD_DIM, HEAD_DIM), HEAD_DIM)
        for source, lane, gain, target in (
            (qproj_ref, 0, qgain_ref, qrot_ref),
            (kproj_ref, HEAD_DIM // 2, kgain_ref, krot_ref),
        ):
            normed = source[:, cols] * scale_ref[:, lane : lane + 1] * gain[:, cols]
            turned = normed * cos_ref[...] + pltpu.roll(normed, HEAD_DIM // 2, 1) * sin_ref[...]
            target[:, cols] = turned.astype(jnp.bfloat16)
        return carry

    lax.fori_loop(0, heads, turn_step, 0)
    for save in saves[5:8]:
        save.start()

    def head_step(h, carry):
        cols = pl.ds(pl.multiple_of(h * HEAD_DIM, HEAD_DIM), HEAD_DIM)
        for block in range(length // block_rows):
            low, high = key_window(block, block_rows)
            here = pl.ds(block * block_rows, block_rows)
            keys = pl.ds(low, high - low)
            scores = attention_scores(
                krot_ref[keys, cols], qrot_ref[here, cols], start_ref[:, here],
                block * block_rows, low, 1,
            )
            top = jnp.max(scores, axis=0, keepdims=True)
            weights = jnp.exp2((scores - top) * exponent)
            total = jnp.sum(weights, axis=0, keepdims=True)
            probs = (weights * (1.0 / total)).astype(jnp.bfloat16)
            probs_ref[block, h, : high - low, :] = probs
            mixed_ref[here, cols] = mm_tn(probs, value_ref[keys, cols]).astype(jnp.bfloat16)
        return carry

    lax.fori_loop(0, heads, head_step, 0)
    for save in saves[8:]:
        save.start()
    for c in range(chunks):
        send_across(c).wait_send()
        forward(c).wait_send()
    to_beside.wait_send()
    for swap in swaps:
        swap.wait_send()
    for save in saves:
        save.wait()


def front(adapter_set, tokens, wq, wk, wv, table, segment_ids, gains, adapters):
    rows, width = tokens.shape
    heads_width = wq.shape[1]
    length = 4 * rows
    part = rows // CHUNKS
    rank = adapters[0].shape[1]
    units = adapters[9].shape[2]
    probs_shape = probs_space(length, heads_width)
    vmem = pl.BlockSpec(memory_space=pltpu.VMEM)
    hbm = pl.BlockSpec(memory_space=pl.ANY)
    low, full = jnp.bfloat16, jnp.float32
    shape = jax.ShapeDtypeStruct
    dma = pltpu.SemaphoreType.DMA
    return pl.pallas_call(
        front_body,
        in_specs=[pl.BlockSpec(memory_space=pltpu.SMEM), vmem] + [hbm] * 3 + [vmem] * 6 + [hbm] * 14,
        out_specs=[vmem] * 17 + [hbm] * 10,
        out_shape=[
            shape((3 * rank, width), low), shape((3 * rank, heads_width), low),
            shape((3 * rank, heads_width), low), shape((3 * rank, heads_width), low),
            shape((rank, heads_width), low), shape((rank, width), low), shape((2 * rank, width), low),
            shape((2 * rank, units), low), shape((2 * rank, units), low), shape((rank, units), low),
            shape((rank, width), low), shape((1, heads_width), full), shape((1, heads_width), full),
            shape((1, width), full), shape((1, width), full),
            shape((1, length), jnp.int32), shape((1, 128), full),
            shape((length, heads_width), low), shape((length, heads_width), low),
            shape((length, heads_width), low), shape((length, heads_width), low),
            shape((length, heads_width), full), shape((length, heads_width), full),
            shape((length, HEAD_DIM), full), shape((length, 3 * rank), low),
            shape((4, CHUNKS, part, width), low), shape(probs_shape, low),
        ],
        scratch_shapes=[pltpu.VMEM(probs_shape, low)]
        + [pltpu.VMEM((length, heads_width), low)] * 4
        + [pltpu.VMEM((length, heads_width), full)] * 2
        + [
            pltpu.VMEM((length, HEAD_DIM), full), pltpu.VMEM((length, 3 * rank), low),
            pltpu.VMEM(table.shape, full), pltpu.VMEM(table.shape, full),
            pltpu.VMEM(wq.shape, low), pltpu.VMEM(wk.shape, low), pltpu.VMEM(wv.shape, low),
            dma((3,)),
            pltpu.VMEM((4, CHUNKS, part, width), low), pltpu.VMEM((rows, width), low),
            pltpu.VMEM((length, HEAD_DIM), full), pltpu.VMEM((8, length), full),
            pltpu.VMEM((3, 8, length), full),
            dma((CHUNKS,)), dma((CHUNKS,)), dma((CHUNKS,)), dma((CHUNKS,)), dma, dma,
            dma((3,)), dma((3,)), dma((10,)),
        ] + [pltpu.VMEM(a.shape, low) for a in adapters] + [dma((14,))],
        cost_estimate=pl.CostEstimate(
            flops=2 * length * heads_width * (3 * width + 2 * length),
            bytes_accessed=2 * width * (3 * heads_width + length), transcendentals=0,
        ),
        compiler_params=pltpu.CompilerParams(
            collective_id=1, has_side_effects=True, vmem_limit_bytes=67043328
        ),
        name="gather_project_attend",
    )(adapter_set, tokens.reshape(CHUNKS, part, width), wq, wk, wv, table, segment_ids, *gains,
      *adapters)


def back_body(
    qrot_hbm, krot_hbm, value_hbm, dmixed_hbm, qproj_hbm, kproj_hbm, scale_hbm, qgain_ref,
    kgain_ref, table_hbm, probs_hbm, wq_hbm, wk_hbm, wv_hbm, shrink_ref,
    eq_ref, ek_ref, ev_ref, mids_ref, full_hbm, hgrad_hbm, set_ref,
    gso_ref, geg_ref, geu_ref, gsd_ref, gsgu_ref, geo_ref, ged_ref,
    tgrad_hbm, split_hbm, heads_hbm, shared_hbm, inward_hbm,
    wq, wk, wv, full, qrot_ref, krot_ref, value_ref, dmixed, qproj_ref, kproj_ref,
    scale_ref, cos_ref, sin_ref, hgrad_ref, probs_ref, probs_sem, wsem, save_sem,
    dq_buf, dk_buf, dv_buf, dq_low, dk_low, dv_low, sums_buf,
    split_send, heads_send, blocks, blocks_recv, blocks_xrecv, shared_send, inward_send,
    ex_send, ex_recv, dmid_send, dmid_recv, dmid_xsend, dmid_xrecv,
    own_buf, xsend, xrecv, bsend, brecv,
    es_sem, er_sem, xs_sem, xr_sem, bs_sem, br_sem, one_s, one_r,
    sp_s, sp_f, sp_r, hd_s, hd_r, sh_s, sh_r, in_s, in_r, local_sem,
):
    me, group, beside, across = partners()
    far = lax.rem(beside + 2, 4)
    order = (me, across, beside, far)
    groups = split_hbm.shape[0]
    chunks, part, width = own_buf.shape
    rows = chunks * part
    length = 4 * rows
    heads_width = wq.shape[1]
    units = geg_ref.shape[1]
    cols_each = blocks.shape[3]
    loads = [
        pltpu.make_async_copy(source, target, wsem.at[i])
        for i, (source, target) in enumerate(
            (
                (dmixed_hbm, dmixed), (qrot_hbm, qrot_ref),
                (krot_hbm, krot_ref), (value_hbm, value_ref),
                (table_hbm, cos_ref), (qproj_hbm, qproj_ref), (kproj_hbm, kproj_ref),
                (scale_hbm, scale_ref), (wq_hbm, wq), (wk_hbm, wk), (wv_hbm, wv),
                (hgrad_hbm, hgrad_ref), (full_hbm, full),
            )
        )
    ]
    probs_loads = [
        pltpu.make_async_copy(probs_hbm.at[i], probs_ref.at[i], probs_sem.at[i])
        for i in range(probs_hbm.shape[0])
    ]
    for load in (*loads[:6], *probs_loads, *loads[6:]):
        load.start()
    barrier = pltpu.get_barrier_semaphore()
    for other in (beside, across, far):
        pl.semaphore_signal(barrier, inc=1, device_id=(group, other), device_id_type=MESH_ID)

    def greet_group(j, carry):
        other = lax.rem(group + j, groups)
        pl.semaphore_signal(barrier, inc=1, device_id=(other, me), device_id_type=MESH_ID)
        return carry

    lax.fori_loop(1, groups, greet_group, 0)

    def remote(source, target, ssem, rsem, other):
        return pltpu.make_async_remote_copy(
            src_ref=source, dst_ref=target, send_sem=ssem, recv_sem=rsem,
            device_id=(group, other), device_id_type=MESH_ID,
        )

    def to_group(source, target, ssem, rsem, j):
        other = lax.rem(group + j, groups)
        return pltpu.make_async_remote_copy(
            src_ref=source(other), dst_ref=target.at[group], send_sem=ssem.at[j],
            recv_sem=rsem.at[group], device_id=(other, me), device_id_type=MESH_ID,
        )

    def from_group(source, target, ssem, rsem, j):
        sender = lax.rem(group + j, groups)
        return pltpu.make_async_remote_copy(
            src_ref=source(sender), dst_ref=target.at[sender], send_sem=ssem.at[j],
            recv_sem=rsem.at[sender], device_id=(sender, me), device_id_type=MESH_ID,
        )

    by_heads = (lambda other: heads_send, heads_hbm, hd_s, hd_r)
    shared = (lambda other: shared_send.at[other], shared_hbm, sh_s, sh_r)
    inward = (lambda other: inward_send.at[other, me], inward_hbm, in_s, in_r)
    exchanges = (None, by_heads, shared, inward)

    def start_exchange(number):
        exchange = exchanges[number]

        def one(j, carry):
            to_group(*exchange, j).start()
            return carry

        lax.fori_loop(1, groups, one, 0)
        pltpu.make_async_copy(
            exchange[0](group), exchange[1].at[group], local_sem.at[number]
        ).start()

    def end_exchange(number):
        exchange = exchanges[number]

        def one(j, carry):
            to_group(*exchange, j).wait_send()
            from_group(*exchange, j).wait_recv()
            return carry

        lax.fori_loop(1, groups, one, 0)
        pltpu.make_async_copy(
            exchange[0](group), exchange[1].at[group], local_sem.at[number]
        ).wait()

    neighbour = group + 1 - 2 * lax.rem(group, 2)

    def split_copy(source, slot, ssem, other):
        return pltpu.make_async_remote_copy(
            src_ref=source, dst_ref=split_hbm.at[slot], send_sem=ssem, recv_sem=sp_r.at[slot],
            device_id=(other, me), device_id_type=MESH_ID,
        )

    def split_direct(k):
        return split_copy(split_send, group, sp_s.at[2 * k], lax.rem(group + 2 * k, groups))

    def split_passed(k):
        slot = lax.rem(group + 2 * k, groups)
        return split_copy(split_hbm.at[slot], slot, sp_f.at[2 * k], neighbour)

    def split_arrival(slot):
        return split_copy(split_send, slot, sp_s.at[0], neighbour)

    split_near = split_copy(split_send, group, sp_s.at[0], neighbour)
    split_own = pltpu.make_async_copy(split_send, split_hbm.at[group], local_sem.at[0])

    def over_parity(body):
        def one(k, carry):
            body(k)
            return carry

        lax.fori_loop(1, groups // 2, one, 0)

    def start_split():
        over_parity(lambda k: split_direct(k).start())
        split_near.start()
        split_own.start()

    def pass_split(k):
        split_arrival(lax.rem(group + 2 * k, groups)).wait_recv()
        split_passed(k).start()

    def end_split_one(k):
        split_direct(k).wait_send()
        split_passed(k).wait_send()
        split_arrival(lax.rem(neighbour + 2 * k, groups)).wait_recv()

    def end_split():
        over_parity(end_split_one)
        split_near.wait_send()
        split_arrival(neighbour).wait_recv()
        split_own.wait()

    low = jnp.bfloat16
    heads = heads_width // HEAD_DIM
    inverse = HEAD_DIM ** (-0.5)
    for ref in (sums_buf, dk_buf, dv_buf):
        ref[...] = jnp.zeros_like(ref)
    block_rows = min(ATT_ROWS, length)

    def attend_back(block, first_query, first_key, size):
        here = pl.ds(first_query, block_rows)
        keys = pl.ds(first_key, size)

        def head_step(h, carry):
            cols = pl.ds(pl.multiple_of(h * HEAD_DIM, HEAD_DIM), HEAD_DIM)
            queries = qrot_ref[here, cols]
            key_rows = krot_ref[keys, cols]
            grads = dmixed[here, cols]
            prob_low = probs_ref[block, h, :size, :]
            probs = prob_low.astype(jnp.float32)
            prob_grad = mm_nt(value_ref[keys, cols], grads)
            weighted = probs * prob_grad
            delta = jnp.sum(weighted, axis=0, keepdims=True)
            score_grad = (weighted - probs * delta).astype(low)
            dv_buf[keys, cols] += mm(prob_low, grads)
            dk_buf[keys, cols] += mm(score_grad, queries)
            dq = mm_tn(score_grad, key_rows) * inverse
            dq = dq * cos_ref[here, :] - pltpu.roll(dq, HEAD_DIM // 2, 1) * sin_ref[here, :]
            dq = dq * qgain_ref[:, cols]
            dq_buf[here, cols] = dq
            sums_buf[0, here, :] += qproj_ref[here, cols] * dq
            return carry

        lax.fori_loop(0, heads, head_step, 0, unroll=2)

    pl.semaphore_wait(barrier, groups + 2)
    split_send[:, :units] = (adapter_scale_factor * geg_ref[:16]).astype(low)
    split_send[:, units : 2 * units] = (adapter_scale_factor * geu_ref[16:]).astype(low)
    split_send[:, 2 * units : 3 * units] = gsd_ref[...].astype(low)
    split_send[:, 3 * units : 3 * units + heads_width] = gso_ref[...].astype(low)
    split_send[:, 3 * units + heads_width :] = jnp.broadcast_to(set_ref[...], (16, 128)).astype(low)
    start_split()
    for t in range(4):
        for g in range(groups):
            at = slice((g * 4 + t) * cols_each, (g * 4 + t + 1) * cols_each)
            blocks[t, g, :16] = (adapter_scale_factor * geo_ref[:, at]).astype(low)
            blocks[t, g, 16:48] = gsgu_ref[:, at].astype(low)
            blocks[t, g, 48:] = (adapter_scale_factor * ged_ref[:, at]).astype(low)
    block_near = remote(blocks.at[beside], blocks_recv.at[0], one_s.at[0], one_r.at[0], beside)
    block_far = remote(blocks.at[far], blocks_recv.at[1], one_s.at[1], one_r.at[1], beside)
    block_across = remote(shared_send, blocks_xrecv, one_s.at[2], one_r.at[2], across)
    block_near.start()
    block_far.start()
    for load in loads[:6]:
        load.wait()
    open_table(cos_ref, sin_ref)

    for block in range(length // block_rows):
        first, last = key_window(block, block_rows)
        if True:
            probs_loads[block].wait()
            attend_back(block, block * block_rows, first, last - first)
        if block == 1:
            block_near.wait_recv()
            block_far.wait_recv()
            shared_send[...] = (
                blocks[across].astype(jnp.float32) + blocks_recv[1].astype(jnp.float32)
            ).astype(low)
            block_across.start()
        if block == length // block_rows - 1:
            block_across.wait()
            shared_send[...] = (
                blocks[me].astype(jnp.float32)
                + blocks_recv[0].astype(jnp.float32)
                + blocks_xrecv[...].astype(jnp.float32)
            ).astype(low)
            start_exchange(2)

    def head_end(h, carry):
        cols = pl.ds(pl.multiple_of(h * HEAD_DIM, HEAD_DIM), HEAD_DIM)
        dk = dk_buf[:, cols] * inverse
        dk = dk * cos_ref[...] - pltpu.roll(dk, HEAD_DIM // 2, 1) * sin_ref[...]
        dk = dk * kgain_ref[:, cols]
        dk_buf[:, cols] = dk
        sums_buf[1] += kproj_ref[:, cols] * dk
        dv_low[:, cols] = dv_buf[:, cols].astype(low)
        return carry

    for load in loads[6:]:
        load.wait()
    lax.fori_loop(0, heads, head_end, 0)

    lane = lax.broadcasted_iota(jnp.int32, (length, HEAD_DIM), 1)
    both = jnp.where(
        lane < 4,
        jnp.sum(sums_buf[0], axis=1, keepdims=True),
        jnp.sum(sums_buf[1], axis=1, keepdims=True),
    )
    ex_send[...] = jnp.transpose(both)[:8]
    swaps = [
        remote(ex_send, ex_recv.at[i], es_sem.at[i], er_sem.at[i], other)
        for i, other in enumerate((beside, across, far))
    ]
    for swap in swaps:
        swap.start()
    for swap in swaps:
        swap.wait_recv()
    total = (ex_send[...] + ex_recv[0] + ex_recv[1] + ex_recv[2]) * (1.0 / (4 * heads_width))
    wide = jnp.concatenate(
        [
            jnp.broadcast_to(total[:1], (HEAD_DIM // 2, length)),
            jnp.broadcast_to(total[4:5], (HEAD_DIM // 2, length)),
        ],
        axis=0,
    )
    sums_buf[0] = jnp.transpose(wide)
    for dn, proj, target, at in (
        (dq_buf, qproj_ref, dq_low, 0), (dk_buf, kproj_ref, dk_low, HEAD_DIM // 2),
    ):
        scale = scale_ref[:, at : at + 1]
        means = sums_buf[0, :, at : at + 1]
        target[...] = (scale * dn[...] - proj[...] * (scale * scale * scale * means)).astype(low)

    dmid_near = remote(dmid_send, dmid_recv, one_s.at[3], one_r.at[3], beside)
    dmid_across = remote(dmid_xsend, dmid_xrecv, one_s.at[4], one_r.at[4], across)

    def reduce_beside(c):
        return remote(bsend.at[c], brecv.at[c], bs_sem.at[c], br_sem.at[c], beside)

    def reduce_across(c):
        return remote(xsend.at[c], xrecv.at[c], xs_sem.at[c], xr_sem.at[c], across)

    def chunk_of(buffer, c):
        return jnp.concatenate(
            [buffer[pl.ds(pl.multiple_of(o * rows + c * part, part), part), :] for o in order], axis=0
        )

    def stage_partial(c):
        parts = [chunk_of(buffer, c) for buffer in (dq_low, dk_low, dv_low)]
        tile = TILE

        def one(j, carry):
            at = pl.ds(pl.multiple_of(j * tile, tile), tile)
            value = (
                mm_nt(parts[0], wq[at, :]) + mm_nt(parts[1], wk[at, :]) + mm_nt(parts[2], wv[at, :])
            ).astype(low)
            own_buf[c, :, at] = value[:part]
            xsend[c, :, at] = value[part : 2 * part]
            bsend[c, 0, :, at] = value[2 * part : 3 * part]
            bsend[c, 1, :, at] = value[3 * part :]
            return carry

        lax.fori_loop(0, width // tile, one, 0)
        reduce_beside(c).start()

    def stage_pair(c):
        reduce_beside(c).wait_recv()
        xsend[c] = (xsend[c].astype(jnp.float32) + brecv[c, 1].astype(jnp.float32)).astype(low)
        reduce_across(c).start()
        own_buf[c] = (own_buf[c].astype(jnp.float32) + brecv[c, 0].astype(jnp.float32)).astype(low)

    def rank_sums_start():
        dmid_part = (
            mm_nt(eq_ref[...], dq_low[...]) + mm_nt(ek_ref[...], dk_low[...])
            + mm_nt(ev_ref[...], dv_low[...])
        )
        dmid_send[...] = dmid_part.astype(low)
        dmid_near.start()

    def rank_sums_cross():
        dmid_near.wait_recv()
        dmid_xsend[...] = (
            dmid_send[...].astype(jnp.float32) + dmid_recv[...].astype(jnp.float32)
        ).astype(low)
        dmid_across.start()

    def expand_gradients():
        mids = mids_ref[...]
        for i, buffer in enumerate((dq_low, dk_low, dv_low)):
            heads_send[:, i * heads_width : (i + 1) * heads_width] = (
                adapter_scale_factor * mm_tn(mids, buffer[...])[i * 16 : (i + 1) * 16]
            ).astype(low)
        start_exchange(1)

    def partial_step(i, carry):
        stage_partial(i)
        for k, extra in (
            (0, rank_sums_start), (1, rank_sums_cross), (1, lambda: over_parity(pass_split)),
        ):

            @pl.when(i == k)
            def _():
                extra()

        @pl.when(i == 2)
        def _():
            expand_gradients()

        stage_pair(i)
        return carry

    lax.fori_loop(0, chunks, partial_step, 0)
    dmid_across.wait_recv()
    dmid = (
        dmid_xsend[...].astype(jnp.float32) + dmid_xrecv[...].astype(jnp.float32)
    ).astype(low)
    inward_grad = mm(dmid, full[...])
    for t in range(4):
        for g in range(groups):
            at = slice((g * 4 + t) * cols_each, (g * 4 + t + 1) * cols_each)
            inward_send[g, t] = inward_grad[:, at].astype(low)
    start_exchange(3)
    dmid_across.wait_send()
    dmid_xsend[...] = dmid
    mine = pl.ds(pl.multiple_of(me * rows, rows), rows)
    hgrad_ref[...] += mm_tn(dmid_xsend[:, mine], shrink_ref[...])

    def own_rows(c):
        return pl.ds(pl.multiple_of(c * part, part), part)

    def save(c):
        return pltpu.make_async_copy(
            hgrad_ref.at[own_rows(c), :], tgrad_hbm.at[own_rows(c), :], save_sem.at[c]
        )

    def finish_step(c, carry):
        reduce_across(c).wait_recv()
        hgrad_ref[own_rows(c), :] += own_buf[c].astype(jnp.float32) + xrecv[c].astype(jnp.float32)
        save(c).start()
        return carry

    lax.fori_loop(0, chunks, finish_step, 0)
    for c in range(chunks):
        save(c).wait()
    for c in range(chunks):
        reduce_beside(c).wait_send()
        reduce_across(c).wait_send()
    for copy in (block_near, block_far, dmid_near, *swaps):
        copy.wait_send()
    end_split()
    for number in range(1, 4):
        end_exchange(number)


def back(
    qrot, krot, value, dmixed, qproj, kproj, scale, qgain, kgain, table, probs,
    wq, wk, wv, shrink, eq, ek, ev, mids, full, hgrad, chosen,
    gso, geg, geu, gsd, gsgu, geo, ged,
):
    rows, width = hgrad.shape
    heads_width, units = wq.shape[1], geg.shape[1]
    length = 4 * rows
    part = rows // CHUNKS
    groups = lax.axis_size("dp")
    cols_each = width // (4 * groups)
    split_width = 3 * units + heads_width + 128
    vmem = pl.BlockSpec(memory_space=pltpu.VMEM)
    hbm = pl.BlockSpec(memory_space=pl.ANY)
    low, f32 = jnp.bfloat16, jnp.float32
    shape = jax.ShapeDtypeStruct
    dma = pltpu.SemaphoreType.DMA
    buf = pltpu.VMEM
    return pl.pallas_call(
        back_body,
        in_specs=[hbm] * 7 + [vmem] * 2 + [hbm] * 5 + [vmem] * 5 + [hbm] * 2 + [vmem] * 8,
        out_specs=[hbm] * 5,
        out_shape=[
            shape((rows, width), f32),
            shape((groups, 16, split_width), low),
            shape((groups, 16, 3 * heads_width), low),
            shape((groups, 64, cols_each), low),
            shape((groups, 48, cols_each), low),
        ],
        scratch_shapes=[
            buf(wq.shape, low), buf(wk.shape, low), buf(wv.shape, low),
            buf(full.shape, low),
            buf(qrot.shape, low), buf(krot.shape, low), buf(value.shape, low), buf(dmixed.shape, low),
            buf(qproj.shape, f32), buf(kproj.shape, f32), buf(scale.shape, f32),
            buf(table.shape, f32), buf(table.shape, f32), buf(hgrad.shape, f32),
            buf(probs.shape, low), dma((probs.shape[0],)), dma((13,)), dma((CHUNKS,)),
            buf((length, heads_width), f32), buf((length, heads_width), f32),
            buf((length, heads_width), f32),
            buf((length, heads_width), low), buf((length, heads_width), low),
            buf((length, heads_width), low),
            buf((2, length, HEAD_DIM), f32),
            buf((16, split_width), low), buf((16, 3 * heads_width), low),
            buf((4, groups, 64, cols_each), low), buf((2, groups, 64, cols_each), low),
            buf((groups, 64, cols_each), low), buf((groups, 64, cols_each), low),
            buf((groups, 4, 48, cols_each), low),
            buf((8, length), f32), buf((3, 8, length), f32),
            buf((48, length), low), buf((48, length), low), buf((48, length), low),
            buf((48, length), low),
            buf((CHUNKS, part, width), low), buf((CHUNKS, part, width), low),
            buf((CHUNKS, part, width), low),
            buf((CHUNKS, 2, part, width), low), buf((CHUNKS, 2, part, width), low),
            dma((3,)), dma((3,)), dma((CHUNKS,)), dma((CHUNKS,)), dma((CHUNKS,)), dma((CHUNKS,)),
            dma((5,)), dma((5,)),
        ] + [dma((groups,))] * 9 + [dma((4,))],
        cost_estimate=pl.CostEstimate(
            flops=2 * length * heads_width * (3 * width + 5 * length),
            bytes_accessed=2 * width * (3 * heads_width + 3 * length), transcendentals=0,
        ),
        compiler_params=pltpu.CompilerParams(
            collective_id=2, has_side_effects=True, vmem_limit_bytes=67043328
        ),
        name="attention_back_to_tokens",
    )(qrot, krot, value, dmixed, qproj, kproj, scale, qgain, kgain, table, probs,
      wq, wk, wv, shrink, eq, ek, ev, mids, full, hgrad, chosen,
      gso, geg, geu, gsd, gsgu, geo, ged)


def finish_body(split_ref, heads_ref, shared_ref, inward_ref, block_ref, tokens_ref, *outs):
    block_out, tokens_out, *outs, which = outs
    groups = split_ref.shape[0]
    tag = split_ref.shape[2] - 128
    together = outs[0].shape[0]
    first = pl.program_id(0) * together

    @pl.when(first == 0)
    def _():
        for g in range(groups):
            which[g] = jnp.max(split_ref[g, :, tag:].astype(jnp.float32)).astype(jnp.int32)

    sq, eq, sk, ek, sv, ev, so, eo, sg, eg, su, eu, sd, ed = outs
    here = eq.shape[2]
    units = eg.shape[2]
    sources = []
    for i, target in enumerate((eq, ek, ev)):
        sources.append((target, lambda g, i=i: heads_ref[g, :, i * here : (i + 1) * here]))
    for i, target in enumerate((eg, eu, sd)):
        sources.append((target, lambda g, i=i: split_ref[g, :, i * units : (i + 1) * units]))
    sources.append((so, lambda g: split_ref[g, :, 3 * units : 3 * units + here]))
    for i, target in enumerate((sq, sk, sv)):
        sources.append((target, lambda g, i=i: inward_ref[g, i * 16 : (i + 1) * 16, :]))
    for i, target in enumerate((eo, sg, su, ed)):
        sources.append((target, lambda g, i=i: shared_ref[g, i * 16 : (i + 1) * 16, :]))
    for target, _ in sources:
        target[...] = jnp.zeros_like(target)

    def one(g, carry):
        at = which[g] - first

        @pl.when((at >= 0) & (at < together))
        def _():
            for target, source in sources:
                target[at] += source(g).astype(jnp.float32)

        return carry

    lax.fori_loop(0, groups, one, 0)
    block_out[...] = block_ref[...]
    tokens_out[...] = tokens_ref[...]


def finish(split, by_heads, shared, inward, block, tokens, sets, here, units):
    cols = shared.shape[2]
    rows, width = block.shape
    steps = min(FINISH_STEPS, sets)
    together = sets // steps
    part = rows // steps
    whole = lambda a: pl.BlockSpec(a.shape, lambda i: (0,) * a.ndim)
    strip = pl.BlockSpec((part, width), lambda i: (i, 0))
    widths = (cols, here, cols, here, cols, here, here, cols, cols, units, cols, units, units, cols)
    return pl.pallas_call(
        finish_body,
        grid=(steps,),
        in_specs=[whole(split), whole(by_heads), whole(shared), whole(inward), strip, strip],
        out_specs=[strip, strip] + [pl.BlockSpec((together, 16, w), lambda i: (i, 0, 0)) for w in widths],
        out_shape=[
            jax.ShapeDtypeStruct(block.shape, block.dtype),
            jax.ShapeDtypeStruct(tokens.shape, tokens.dtype),
        ] + [jax.ShapeDtypeStruct((sets, 16, w), jnp.float32) for w in widths],
        scratch_shapes=[pltpu.SMEM((split.shape[0],), jnp.int32)],
        compiler_params=pltpu.CompilerParams(vmem_limit_bytes=67043328),
        name="sum_by_set",
    )(split, by_heads, shared, inward, block, tokens)


def per_device(
    tokens,
    cotangent,
    segment_ids,
    adapter_set,
    w_query,
    w_key,
    w_value,
    w_out,
    w_gate,
    w_up,
    w_down,
    query_gain,
    key_gain,
    mixer_gain,
    feed_gain,
    shrink_query,
    expand_query,
    shrink_key,
    expand_key,
    shrink_value,
    expand_value,
    shrink_out,
    expand_out,
    shrink_gate,
    expand_gate,
    shrink_up,
    expand_up,
    shrink_down,
    expand_down,
):
    length = 4 * tokens.shape[0]
    table = jnp.asarray(rotary_constants(length, HEAD_DIM))
    (
        shrink_rows, expand_query_rows, expand_key_rows, expand_value_rows, out_shrink, out_expand,
        gate_up_shrink, gate_expand, up_expand, down_shrink, down_expand,
        query_gains, key_gains, mixer_gains, feed_gains, _, set_row,
        mixed, query_rot, key_rot, value_low, query_proj, key_proj, scales, qkv_middle, full_tokens,
        probs,
    ) = front(
        adapter_set, tokens, w_query, w_key, w_value, table, segment_ids,
        (query_gain, key_gain, mixer_gain, feed_gain),
        (
            shrink_query, expand_query, shrink_key, expand_key, shrink_value, expand_value,
            shrink_out, expand_out, shrink_gate, expand_gate, shrink_up, expand_up,
            shrink_down, expand_down,
        ),
    )
    (
        block_output, hidden_grad, mixed_grad, grad_down_shrink, gradient_gate_widened,
        gradient_up_widened, grad_out_shrink, owner_gate_up, owner_out, owner_down,
    ) = middle(
        mixed, tokens, cotangent, w_out, w_gate, w_up, w_down, mixer_gains, feed_gains,
        out_shrink, out_expand, gate_up_shrink, gate_expand, up_expand, down_shrink, down_expand,
    )
    token_grads, split, by_heads, shared, inward = back(
        query_rot, key_rot, value_low, mixed_grad.reshape(mixed.shape), query_proj, key_proj, scales,
        query_gains, key_gains, table, probs,
        w_query, w_key, w_value, shrink_rows, expand_query_rows, expand_key_rows, expand_value_rows,
        qkv_middle, full_tokens.reshape(length, -1), hidden_grad, set_row,
        grad_out_shrink, gradient_gate_widened, gradient_up_widened, grad_down_shrink,
        owner_gate_up, owner_out, owner_down,
    )
    return finish(
        split, by_heads, shared, inward, block_output, token_grads,
        shrink_query.shape[0], w_query.shape[1], w_gate.shape[1],
    )


def solution(mesh):
    in_specs = (
        P(("dp", "tensor"), None),
        P(("dp", "tensor"), None),
        P("dp", None),
        P("dp"),
        P(None, "tensor"),
        P(None, "tensor"),
        P(None, "tensor"),
        P("tensor", None),
        P(None, "tensor"),
        P(None, "tensor"),
        P("tensor", None),
        P("tensor"),
        P("tensor"),
        P(),
        P(),
        P(),
        P(None, None, "tensor"),
        P(),
        P(None, None, "tensor"),
        P(),
        P(None, None, "tensor"),
        P(None, None, "tensor"),
        P(),
        P(),
        P(None, None, "tensor"),
        P(),
        P(None, None, "tensor"),
        P(None, None, "tensor"),
        P(),
    )
    out_specs = (
        P(("dp", "tensor"), None),
        P(("dp", "tensor"), None),
        P(None, None, ("dp", "tensor")),
        P(None, None, "tensor"),
        P(None, None, ("dp", "tensor")),
        P(None, None, "tensor"),
        P(None, None, ("dp", "tensor")),
        P(None, None, "tensor"),
        P(None, None, "tensor"),
        P(None, None, ("dp", "tensor")),
        P(None, None, ("dp", "tensor")),
        P(None, None, "tensor"),
        P(None, None, ("dp", "tensor")),
        P(None, None, "tensor"),
        P(None, None, "tensor"),
        P(None, None, ("dp", "tensor")),
    )
    return jax.shard_map(
        per_device, mesh=mesh, in_specs=in_specs, out_specs=out_specs, check_vma=False
    )
```

```python
import functools
import jax
import jax.numpy as jnp
import numpy as np
from jax import lax
from jax.experimental import pallas as pl
from jax.experimental.pallas import tpu as pltpu
from jax.sharding import PartitionSpec as P

HEAD_DIM = 128
DOC_MOST = 512
ATT_ROWS = 256
rotary_base = 500000.0
NEG = -1e30
LOG2E = 1.4426950408889634


def rotary_constants(length, head_dim):
    half = head_dim // 2
    frequency = np.float32(rotary_base) ** (
        -(np.arange(half, dtype=np.float32) * np.float32(2.0) / np.float32(head_dim))
    )
    angles = np.arange(length, dtype=np.float32)[:, None] * frequency.astype(np.float32)[None, :]
    cosine = np.cos(angles.astype(np.float64)).astype(np.float32)
    sine = np.sin(angles.astype(np.float64)).astype(np.float32)
    return np.concatenate([cosine, sine], axis=1)


def open_table(cos_ref, sin_ref):
    table = cos_ref[...]
    turned = pltpu.roll(table, HEAD_DIM // 2, 1)
    low_half = lax.broadcasted_iota(jnp.int32, table.shape, 1) < HEAD_DIM // 2
    cos_ref[...] = jnp.where(low_half, table, turned)
    sin_ref[...] = jnp.where(low_half, -turned, table)


def key_window(block, rows):
    first = max(0, (block * rows - (DOC_MOST - 1)) // rows) * rows
    return first, (block + 1) * rows


epsilon = 1e-06
adapter_scale_factor = 0.5


CHUNKS = 4
FINISH_STEPS = 2
TILE = 1024
EXTRA = 128
NT = (((1,), (1,)), ((), ()))
TN = (((0,), (0,)), ((), ()))
MESH_ID = pl.DeviceIdType.MESH
MIDDLE_STAGES = ("S0", "P0", "S1", "F1", "S2", "P2", "S3", "F3", "S4", "P4", "S5", "F5", "S6")
MIDDLE_ORDER = (
    0, 1, 2, 4, 3, 5, 6, 7, 8, 9, 10, 11, 12,
    16, 13, 14, 17, 20, 18, 21, 15, 24, 19, 25, 22, 23,
    28, 32, 26, 29, 36, 33, 27, 30, 37, 34, 40, 31, 41,
    38, 35, 44, 45, 48, 39, 49, 42, 43, 46, 50, 47, 51,
)


def mm(left, right):
    return jnp.dot(left, right, preferred_element_type=jnp.float32)


def mm_nt(left, right):
    return lax.dot_general(left, right, NT, preferred_element_type=jnp.float32)


def mm_tn(left, right):
    return lax.dot_general(left, right, TN, preferred_element_type=jnp.float32)


def partners():
    me = lax.axis_index("tensor")
    group = lax.axis_index("dp")
    beside = me + 1 - 2 * lax.rem(me, 2)
    across = lax.rem(me + 2, 4)
    return me, group, beside, across


def greet(group, beside, across):
    barrier = pltpu.get_barrier_semaphore()
    for other in (beside, across):
        pl.semaphore_signal(barrier, inc=1, device_id=(group, other), device_id_type=MESH_ID)
    pl.semaphore_wait(barrier, 2)


def middle_body(
    mixed_ref, tokens_ref, cot_ref, w_out_hbm, w_gate_hbm, w_up_hbm, w_down_hbm,
    mgain_ref, fgain_ref, so_ref, eo_ref, sgu_ref, eg_ref, eu_ref, sd_ref, ed_ref,
    out_hbm, hgrad_hbm, dmixed_hbm, gsd_ref, geg_ref, geu_ref, gso_ref, gsgu_ref, geo_ref, ged_ref,
    w_out, w_gate, w_up, w_down, wsem, out_ref, dmixed_ref, save_sem,
    rows_buf, own_buf, xsend, xrecv, bsend, brecv,
    gate_buf, up_buf, temp_a, temp_b, mgu_buf, mixer_buf, hidden_buf, mout_buf,
    xside, yside, vs_sem, vr_sem, xs_sem, xr_sem, bs_sem, br_sem, gxs_sem, gxr_sem, gbs_sem, gbr_sem, fs_sem, fr_sem,
):
    me, group, beside, across = partners()
    chunks, part, width = rows_buf.shape[0], rows_buf.shape[2], rows_buf.shape[3]
    units = w_gate.shape[1]
    heads_width = w_out.shape[0]
    far = lax.rem(beside + 2, 4)
    order = (me, across, beside, far)
    loads = [
        pltpu.make_async_copy(source, target, wsem.at[i])
        for i, (source, target) in enumerate(
            ((w_out_hbm, w_out), (w_gate_hbm, w_gate), (w_up_hbm, w_up), (w_down_hbm, w_down))
        )
    ]
    for load in loads:
        load.start()
    for ref in (gsd_ref, geg_ref, geu_ref, gso_ref, gsgu_ref, geo_ref, ged_ref):
        ref[...] = jnp.zeros_like(ref)
    greet(group, beside, across)

    def remote(source, target, ssem, rsem, other):
        return pltpu.make_async_remote_copy(
            src_ref=source, dst_ref=target, send_sem=ssem, recv_sem=rsem,
            device_id=(group, other), device_id_type=MESH_ID,
        )

    def gather_across(c):
        return remote(rows_buf.at[c, 0], rows_buf.at[c, 1], gxs_sem.at[c], gxr_sem.at[c], across)

    def gather_beside(c):
        return remote(rows_buf.at[c, 0], rows_buf.at[c, 2], gbs_sem.at[c], gbr_sem.at[c], beside)

    def gather_forward(c):
        return remote(rows_buf.at[c, 1], rows_buf.at[c, 3], fs_sem.at[c], fr_sem.at[c], beside)

    def reduce_beside(c):
        return remote(bsend.at[c], brecv.at[c], bs_sem.at[c], br_sem.at[c], beside)

    def reduce_across(c):
        main = pl.ds(0, width)
        return remote(
            xsend.at[c, :, main], xrecv.at[c, :, main], xs_sem.at[c], xr_sem.at[c], across
        )

    def side_across(c):
        return remote(xside.at[c], yside.at[c], vs_sem.at[c], vr_sem.at[c], across)

    def turned(value, high):
        value = jnp.pad(value, ((0, EXTRA - value.shape[0]), (0, EXTRA - value.shape[1])))
        return jnp.transpose(value)[:high]

    def store_partial(c, columns, value):
        low = value.astype(jnp.bfloat16)
        own_buf[c, :, columns] = low[:part]
        xsend[c, :, columns] = low[part : 2 * part]
        bsend[c, 0, :, columns] = low[2 * part : 3 * part]
        bsend[c, 1, :, columns] = low[3 * part :]

    def gathered(c):
        return rows_buf[c].reshape(4 * part, width)

    def forward_stage(c):
        gather_across(c).wait_recv()
        gather_forward(c).start()

    def pair_stage(c):
        reduce_beside(c).wait_recv()
        own_buf[c] = (
            own_buf[c].astype(jnp.float32) + brecv[c, 0].astype(jnp.float32)
        ).astype(jnp.bfloat16)
        xsend[c] = (
            xsend[c].astype(jnp.float32) + brecv[c, 1].astype(jnp.float32)
        ).astype(jnp.bfloat16)
        reduce_across(c).start()
        xside[c] = turned(xsend[c, :, width:].astype(jnp.float32), 32).astype(jnp.bfloat16)
        side_across(c).start()

    def totals(c):
        reduce_across(c).wait_recv()
        main = own_buf[c, :, :width].astype(jnp.float32) + xrecv[c, :, :width].astype(jnp.float32)
        side_across(c).wait_recv()
        side = own_buf[c, :, width : width + 32].astype(jnp.float32) + turned(
            yside[c].astype(jnp.float32), part
        )[:, :32]
        return main, side.astype(jnp.bfloat16)

    def own_rows(c):
        return pl.ds(pl.multiple_of(c * part, part), part)

    def save(number, c):
        source, target = ((out_ref, out_hbm), (hidden_buf, hgrad_hbm))[number]
        return pltpu.make_async_copy(
            source.at[own_rows(c), :], target.at[own_rows(c), :], save_sem.at[number, c]
        )

    def send_rows(c, value, again):
        if again:
            gather_across(c).wait_send()
            gather_beside(c).wait_send()
        rows_buf[c, 0] = value
        gather_across(c).start()
        gather_beside(c).start()

    def chunk_rows(c):
        return pl.ds(pl.multiple_of(c * 4 * part, 4 * part), 4 * part)

    def tiles(total, tile, body):
        def step(j, carry):
            body(pl.ds(pl.multiple_of(j * tile, tile), tile))
            return carry

        lax.fori_loop(0, total // tile, step, 0)

    def mixed_chunk(c):
        return jnp.concatenate([mixed_ref[o, c] for o in order], axis=0)

    def stage_mixer(c):
        @pl.when(c == 0)
        def _():
            loads[0].wait()

        rows = mixed_chunk(c)
        store_partial(c, slice(width, width + 16), mm_nt(rows, so_ref[...]))
        tiles(width, TILE, lambda cols: store_partial(c, cols, mm(rows, w_out[:, cols])))
        reduce_beside(c).start()

    def stage_hidden(c):
        main, side = totals(c)
        mid = side[:, :16]
        mout_buf[c] = mid
        mixer = main + mm(mid, eo_ref[...])
        mixer_buf[own_rows(c), :] = mixer
        factor = lax.rsqrt(jnp.mean(mixer * mixer, axis=1, keepdims=True) + epsilon)
        hidden = tokens_ref[own_rows(c), :].astype(jnp.float32) + mixer * factor * mgain_ref[...]
        hidden_buf[own_rows(c), :] = hidden
        send_rows(c, hidden.astype(jnp.bfloat16), False)

    def arrive(c):
        gather_beside(c).wait_recv()
        gather_forward(c).wait_recv()

    def stage_units(c):
        @pl.when(c == 0)
        def _():
            for load in loads[1:]:
                load.wait()

        arrive(c)
        mids = mm_nt(gathered(c), sgu_ref[...]).astype(jnp.bfloat16)
        mgu_buf[c] = mids

        def unit_tile(cols):
            rows = gathered(c)
            gate = mm(rows, w_gate[:, cols]) + mm(mids, eg_ref[:, cols])
            up = mm(rows, w_up[:, cols]) + mm(mids, eu_ref[:, cols])
            gate_buf[chunk_rows(c), cols] = gate.astype(jnp.bfloat16)
            up_buf[chunk_rows(c), cols] = up.astype(jnp.bfloat16)
            sig = 1.0 / (1.0 + jnp.exp(-gate))
            temp_a[:, cols] = (gate * sig * up).astype(jnp.bfloat16)

        tiles(units, TILE, unit_tile)
        gather_forward(c).wait_send()
        reduce_beside(c).wait_send()
        reduce_across(c).wait_send()
        side_across(c).wait_send()
        inner = temp_a[...]
        store_partial(c, slice(width, width + 16), mm_nt(inner, sd_ref[...]))
        tiles(width, 2 * TILE, lambda cols: store_partial(c, cols, mm(temp_a[...], w_down[:, cols])))
        reduce_beside(c).start()

    def norm_back_rows(values, gains, grads):
        factor = lax.rsqrt(jnp.mean(values * values, axis=1, keepdims=True) + epsilon)
        weighted = grads * gains
        return factor * weighted - values * (
            factor * factor * factor * jnp.mean(values * weighted, axis=1, keepdims=True)
        )

    def stage_feed(c):
        main, side = totals(c)
        mid = side[:, :16]
        feed = main + mm(mid, ed_ref[...])
        factor = lax.rsqrt(jnp.mean(feed * feed, axis=1, keepdims=True) + epsilon)
        gains = fgain_ref[...]
        out_ref[own_rows(c), :] = (hidden_buf[own_rows(c), :] + feed * factor * gains).astype(
            jnp.bfloat16
        )
        save(0, c).start()
        grad = norm_back_rows(feed, gains, cot_ref[own_rows(c), :].astype(jnp.float32))
        grad = grad.astype(jnp.bfloat16)
        send_rows(c, grad, True)
        ged_ref[...] += mm_tn(mid, grad)

    def stage_units_back(c):
        arrive(c)
        dmid = mm_nt(gathered(c), ed_ref[...]).astype(jnp.bfloat16)
        mids = mgu_buf[c]

        def unit_tile(cols):
            rows = gathered(c)
            inner_grad = mm_nt(rows, w_down[cols, :]) + mm(dmid, sd_ref[:, cols])
            gate = gate_buf[chunk_rows(c), cols].astype(jnp.float32)
            up = up_buf[chunk_rows(c), cols].astype(jnp.float32)
            sig = 1.0 / (1.0 + jnp.exp(-gate))
            silu = gate * sig
            gate_grad = (inner_grad * up * (sig + silu * (1.0 - sig))).astype(jnp.bfloat16)
            up_grad = (inner_grad * silu).astype(jnp.bfloat16)
            temp_a[:, cols] = gate_grad
            temp_b[:, cols] = up_grad
            gsd_ref[:, cols] += mm_tn(dmid, (silu * up).astype(jnp.bfloat16))
            geg_ref[:, cols] += mm_tn(mids, gate_grad)
            geu_ref[:, cols] += mm_tn(mids, up_grad)

        tiles(units, TILE, unit_tile)
        gather_forward(c).wait_send()
        reduce_beside(c).wait_send()
        reduce_across(c).wait_send()
        side_across(c).wait_send()
        store_partial(
            c,
            slice(width, width + 32),
            mm_nt(temp_a[...], eg_ref[...]) + mm_nt(temp_b[...], eu_ref[...]),
        )

        def width_tile(cols):
            store_partial(
                c, cols, mm_nt(temp_a[...], w_gate[cols, :]) + mm_nt(temp_b[...], w_up[cols, :])
            )

        tiles(width, TILE, width_tile)
        reduce_beside(c).start()

    def stage_mixer_grad(c):
        main, side = totals(c)
        grads = cot_ref[own_rows(c), :].astype(jnp.float32) + main + mm(side, sgu_ref[...])
        mixer_grad = norm_back_rows(mixer_buf[own_rows(c), :], mgain_ref[...], grads)
        mixer_grad = mixer_grad.astype(jnp.bfloat16)
        send_rows(c, mixer_grad, True)
        geo_ref[...] += mm_tn(mout_buf[c], mixer_grad)
        gsgu_ref[...] += mm_tn(side, hidden_buf[own_rows(c), :].astype(jnp.bfloat16))
        hidden_buf[own_rows(c), :] = grads
        save(1, c).start()

    def stage_mixed_grad(c):
        arrive(c)
        dmid = mm_nt(gathered(c), eo_ref[...]).astype(jnp.bfloat16)
        grad = (mm_nt(gathered(c), w_out[...]) + mm(dmid, so_ref[...])).astype(jnp.bfloat16)
        for i, o in enumerate(order):
            dmixed_ref[o, c] = grad[i * part : (i + 1) * part]
        gso_ref[...] += mm_tn(dmid, mixed_chunk(c))
        gather_forward(c).wait_send()
        gather_across(c).wait_send()
        gather_beside(c).wait_send()
        reduce_beside(c).wait_send()
        reduce_across(c).wait_send()
        side_across(c).wait_send()

    stages = {
        "S0": stage_mixer, "S1": stage_hidden, "S2": stage_units, "S3": stage_feed,
        "S4": stage_units_back, "S5": stage_mixer_grad, "S6": stage_mixed_grad,
        "P0": pair_stage, "P2": pair_stage, "P4": pair_stage,
        "F1": forward_stage, "F3": forward_stage, "F5": forward_stage,
    }

    packed = [
        sum(code << (6 * j) for j, code in enumerate(MIDDLE_ORDER[at : at + 5]))
        for at in range(0, len(MIDDLE_ORDER), 5)
    ]

    def step(i, carry):
        word = jnp.int32(packed[0])
        for k in range(1, len(packed)):
            word = jnp.where(i >= 5 * k, jnp.int32(packed[k]), word)
        place = lax.rem(i, 5)
        unit = jnp.int32(1)
        for k in range(1, 5):
            unit = jnp.where(place == k, jnp.int32(64**k), unit)
        code = lax.rem(lax.div(word, unit), 64)
        stage, c = lax.div(code, chunks), lax.rem(code, chunks)
        for k, name in enumerate(MIDDLE_STAGES):

            @pl.when(stage == k)
            def _():
                stages[name](c)

        return carry

    lax.fori_loop(0, len(MIDDLE_ORDER), step, 0)
    save_mixture = pltpu.make_async_copy(dmixed_ref, dmixed_hbm, save_sem.at[2, 0])
    save_mixture.start()
    for c in range(chunks):
        for number in range(2):
            save(number, c).wait()
    save_mixture.wait()


def middle(mixed, tokens, cot, w_out, w_gate, w_up, w_down, mgain, fgain, so, eo, sgu, eg, eu, sd, ed):
    rows, width = tokens.shape
    heads_width, units = w_out.shape[0], w_gate.shape[1]
    part = rows // CHUNKS
    whole_width = width + EXTRA
    vmem = pl.BlockSpec(memory_space=pltpu.VMEM)
    hbm = pl.BlockSpec(memory_space=pl.ANY)
    low, full = jnp.bfloat16, jnp.float32
    dma = pltpu.SemaphoreType.DMA((CHUNKS,))
    shape = jax.ShapeDtypeStruct
    flops = 2 * 4 * rows * width * (2 * heads_width + 6 * units)
    return pl.pallas_call(
        middle_body,
        in_specs=[vmem] * 3 + [hbm] * 4 + [vmem] * 9,
        out_specs=[hbm] * 3 + [vmem] * 7,
        out_shape=[
            shape((rows, width), low), shape((rows, width), full),
            shape((4, CHUNKS, part, heads_width), low),
            shape((16, units), full), shape((32, units), full), shape((32, units), full),
            shape((16, heads_width), full), shape((32, width), full), shape((16, width), full),
            shape((16, width), full),
        ],
        scratch_shapes=[
            pltpu.VMEM(w_out.shape, low), pltpu.VMEM(w_gate.shape, low),
            pltpu.VMEM(w_up.shape, low), pltpu.VMEM(w_down.shape, low),
            pltpu.SemaphoreType.DMA((4,)),
            pltpu.VMEM((rows, width), low), pltpu.VMEM((4, CHUNKS, part, heads_width), low),
            pltpu.SemaphoreType.DMA((3, CHUNKS)),
            pltpu.VMEM((CHUNKS, 4, part, width), low),
            pltpu.VMEM((CHUNKS, part, whole_width), low),
            pltpu.VMEM((CHUNKS, part, whole_width), low),
            pltpu.VMEM((CHUNKS, part, whole_width), low),
            pltpu.VMEM((CHUNKS, 2, part, whole_width), low),
            pltpu.VMEM((CHUNKS, 2, part, whole_width), low),
            pltpu.VMEM((4 * rows, units), low), pltpu.VMEM((4 * rows, units), low),
            pltpu.VMEM((4 * part, units), low), pltpu.VMEM((4 * part, units), low),
            pltpu.VMEM((CHUNKS, 4 * part, 32), low),
            pltpu.VMEM((rows, width), full), pltpu.VMEM((rows, width), full),
            pltpu.VMEM((CHUNKS, part, 16), low),
            pltpu.VMEM((CHUNKS, 32, EXTRA), low), pltpu.VMEM((CHUNKS, 32, EXTRA), low),
        ] + [dma] * 12,
        cost_estimate=pl.CostEstimate(
            flops=flops, bytes_accessed=2 * width * (heads_width + 3 * units), transcendentals=0
        ),
        compiler_params=pltpu.CompilerParams(
            collective_id=0, has_side_effects=True, vmem_limit_bytes=67043328
        ),
        name="mixer_to_feed",
    )(mixed.reshape(4, CHUNKS, part, heads_width), tokens, cot, w_out, w_gate, w_up, w_down,
      mgain, fgain, so, eo, sgu, eg, eu, sd, ed)


def probs_space(length, heads_width):
    rows = min(ATT_ROWS, length)
    blocks = length // rows
    longest = max(high - low for low, high in (key_window(b, rows) for b in range(blocks)))
    return (blocks, heads_width // HEAD_DIM, longest, rows)


def attention_scores(first, second, start, first_query, first_key, query_axis):
    scores = lax.dot_general(first, second, NT, preferred_element_type=jnp.float32)
    kpos = lax.broadcasted_iota(jnp.int32, scores.shape, 1 - query_axis) + first_key
    shape = [1, 1]
    shape[query_axis] = scores.shape[query_axis]
    qpos = lax.broadcasted_iota(jnp.int32, shape, query_axis) + first_query
    return jnp.where((kpos <= qpos) & (kpos >= start), scores, NEG)


def pick_body(
    at, seg_ref, qgain, kgain, mgain, fgain,
    sq, eq, sk, ek, sv, ev, so, eo, sg, eg, su, eu, sd, ed,
    shrink_out, eq_out, ek_out, ev_out, so_out, eo_out, sgu_out, eg_out, eu_out, sd_out, ed_out,
    qgain_out, kgain_out, mgain_out, fgain_out, start_row, set_out,
):
    rank = sq.shape[1]

    def scaled(ref):
        return (adapter_scale_factor * ref[at].astype(jnp.float32)).astype(jnp.bfloat16)

    for i, ref in enumerate((sq, sk, sv)):
        shrink_out[i * rank : (i + 1) * rank, :] = ref[at]
    for i, (ref, target) in enumerate(((eq, eq_out), (ek, ek_out), (ev, ev_out))):
        target[...] = jnp.zeros_like(target)
        target[i * rank : (i + 1) * rank, :] = scaled(ref)
    for i, (ref, target) in enumerate(((eg, eg_out), (eu, eu_out))):
        target[...] = jnp.zeros_like(target)
        target[i * rank : (i + 1) * rank, :] = scaled(ref)
    so_out[...] = so[at]
    sd_out[...] = sd[at]
    eo_out[...] = scaled(eo)
    ed_out[...] = scaled(ed)
    sgu_out[:rank, :] = sg[at]
    sgu_out[rank:, :] = su[at]
    for ref, target in ((qgain, qgain_out), (kgain, kgain_out), (mgain, mgain_out), (fgain, fgain_out)):
        target[...] = ref[...].astype(jnp.float32).reshape(target.shape)
    length = seg_ref.shape[1]
    row = seg_ref[...].astype(jnp.float32)
    col = jnp.transpose(jnp.broadcast_to(row, (HEAD_DIM, length)))[:, :1]
    start_row[...] = jnp.sum(
        jnp.where(col < row, 1.0, 0.0), axis=0, keepdims=True
    ).astype(jnp.int32)
    set_out[...] = jnp.full(set_out.shape, at, jnp.int32).astype(jnp.float32)


def front_body(
    set_ref, tokens_ref, wq_hbm, wk_hbm, wv_hbm, table_ref, seg_ref, qg_ref, kg_ref, mg_ref, fg_ref,
    *refs,
):
    adapters_hbm, refs = refs[:14], refs[14:]
    picked, refs = refs[:17], refs[17:]
    adapters, adapter_sem, refs = refs[-15:-1], refs[-1], refs[:-15]
    shrink_ref, eq_ref, ek_ref, ev_ref = picked[:4]
    qgain_ref, kgain_ref, start_ref = picked[11], picked[12], picked[15]
    front_steps(
        set_ref, tokens_ref, wq_hbm, wk_hbm, wv_hbm, table_ref,
        (seg_ref, qg_ref, kg_ref, mg_ref, fg_ref), adapters_hbm, adapters, adapter_sem, picked,
        shrink_ref, eq_ref, ek_ref, ev_ref, qgain_ref, kgain_ref, start_ref, *refs,
    )


def front_steps(
    set_ref, tokens_ref, wq_hbm, wk_hbm, wv_hbm, table_ref, small, adapters_hbm, adapters,
    adapter_sem, picked, shrink_ref, eq_ref, ek_ref, ev_ref, qgain_ref, kgain_ref, start_ref,
    mixed_hbm, qrot_hbm, krot_hbm, value_hbm, qproj_hbm, kproj_hbm, scale_hbm, mids_hbm, full_hbm,
    probs_hbm, probs_ref, mixed_ref, qrot_ref, krot_ref, value_ref, qproj_ref, kproj_ref, scale_ref, mids_ref, cos_ref, sin_ref,
    wq, wk, wv, wsem, full, lhs, squares, ex_send, ex_recv,
    xs_sem, xr_sem, fs_sem, fr_sem, bs_sem, br_sem, es_sem, er_sem, out_sem,
):
    me, group, beside, across = partners()
    far = lax.rem(beside + 2, 4)
    chunks, part, width = full.shape[1:]
    rows = chunks * part
    length = 4 * rows
    loads = [
        pltpu.make_async_copy(source, target, wsem.at[i])
        for i, (source, target) in enumerate(((wq_hbm, wq), (wk_hbm, wk), (wv_hbm, wv)))
    ]
    barrier = pltpu.get_barrier_semaphore()
    for other in (beside, across, far):
        pl.semaphore_signal(barrier, inc=1, device_id=(group, other), device_id_type=MESH_ID)
    fetches = [
        pltpu.make_async_copy(source, target, adapter_sem.at[i])
        for i, (source, target) in enumerate(zip(adapters_hbm, adapters))
    ]
    for load in (*fetches, *loads):
        load.start()
    pl.semaphore_wait(barrier, 3)

    def remote(source, target, ssem, rsem, other):
        return pltpu.make_async_remote_copy(
            src_ref=source, dst_ref=target, send_sem=ssem, recv_sem=rsem,
            device_id=(group, other), device_id_type=MESH_ID,
        )

    def send_across(c):
        return remote(tokens_ref.at[c], full.at[me, c], xs_sem.at[c], xr_sem.at[c], across)

    def forward(c):
        return remote(full.at[across, c], full.at[across, c], fs_sem.at[c], fr_sem.at[c], beside)

    to_beside = remote(tokens_ref, full.at[me], bs_sem, br_sem, beside)
    for c in range(chunks):
        send_across(c).start()
    to_beside.start()
    full[me] = tokens_ref[...]
    cos_ref[...] = table_ref[...]
    open_table(cos_ref, sin_ref)
    for fetch in fetches:
        fetch.wait()
    pick_body(set_ref[0], *small, *adapters, *picked)
    for load in loads:
        load.wait()
    pairs = chunks // 2
    half = rows // 2

    def block_step(b, carry):
        @pl.when(b == 0)
        def _():
            lhs[...] = tokens_ref[...].reshape(rows, width)

        @pl.when(b == 1)
        def _():
            to_beside.wait_recv()
            lhs[...] = full[beside].reshape(rows, width)

        @pl.when(b >= 2)
        def _():
            base = (b - 2) * pairs
            for j in range(pairs):
                send_across(base + j).wait_recv()
                forward(base + j).start()
            for j in range(pairs):
                lhs[j * part : (j + 1) * part] = full[across, base + j]
            for j in range(pairs):
                forward(base + j).wait_recv()
                lhs[half + j * part : half + (j + 1) * part] = full[far, base + j]

        mids = mm_nt(lhs[...], shrink_ref[...]).astype(jnp.bfloat16)
        query = mm(lhs[...], wq[...]) + mm(mids, eq_ref[...])
        key = mm(lhs[...], wk[...]) + mm(mids, ek_ref[...])
        value = (mm(lhs[...], wv[...]) + mm(mids, ev_ref[...])).astype(jnp.bfloat16)
        qsum = jnp.sum(query * query, axis=1, keepdims=True)
        ksum = jnp.sum(key * key, axis=1, keepdims=True)
        lane = lax.broadcasted_iota(jnp.int32, (rows, HEAD_DIM), 1)
        both = jnp.where(lane < 4, qsum, ksum)
        first = jnp.where(b == 0, me, jnp.where(b == 1, beside, across)) * rows
        second = jnp.where(b == 0, me, jnp.where(b == 1, beside, far)) * rows
        first = first + jnp.where(b >= 2, (b - 2) * half, 0)
        second = second + jnp.where(b >= 2, (b - 2) * half, half)
        for start, piece in ((first, slice(0, half)), (second, slice(half, rows))):
            there = pl.ds(pl.multiple_of(start, half), half)
            qproj_ref[there, :] = query[piece]
            kproj_ref[there, :] = key[piece]
            value_ref[there, :] = value[piece]
            mids_ref[there, :] = mids[piece]
            squares[there, :] = both[piece]
        return carry

    lax.fori_loop(0, 4, block_step, 0)
    saves = [
        pltpu.make_async_copy(source, target, out_sem.at[i])
        for i, (source, target) in enumerate(
            (
                (full, full_hbm), (value_ref, value_hbm), (qproj_ref, qproj_hbm),
                (kproj_ref, kproj_hbm), (mids_ref, mids_hbm), (scale_ref, scale_hbm),
                (qrot_ref, qrot_hbm), (krot_ref, krot_hbm), (mixed_ref, mixed_hbm),
                (probs_ref, probs_hbm),
            )
        )
    ]
    for save in saves[:5]:
        save.start()
    ex_send[...] = jnp.transpose(squares[...])[:8]
    swaps = [
        remote(ex_send, ex_recv.at[i], es_sem.at[i], er_sem.at[i], other)
        for i, other in enumerate((beside, across, far))
    ]
    for swap in swaps:
        swap.start()
    for swap in swaps:
        swap.wait_recv()
    total = ex_send[...] + ex_recv[0] + ex_recv[1] + ex_recv[2]
    factor = lax.rsqrt(total / (4 * wq.shape[1]) + epsilon)
    wide = jnp.concatenate(
        [
            jnp.broadcast_to(factor[:1], (HEAD_DIM // 2, length)),
            jnp.broadcast_to(factor[4:5], (HEAD_DIM // 2, length)),
        ],
        axis=0,
    )
    scale_ref[...] = jnp.transpose(wide)
    heads = wq.shape[1] // HEAD_DIM
    exponent = HEAD_DIM ** (-0.5) * LOG2E
    block_rows = min(ATT_ROWS, length)

    def turn_step(h, carry):
        cols = pl.ds(pl.multiple_of(h * HEAD_DIM, HEAD_DIM), HEAD_DIM)
        for source, lane, gain, target in (
            (qproj_ref, 0, qgain_ref, qrot_ref),
            (kproj_ref, HEAD_DIM // 2, kgain_ref, krot_ref),
        ):
            normed = source[:, cols] * scale_ref[:, lane : lane + 1] * gain[:, cols]
            turned = normed * cos_ref[...] + pltpu.roll(normed, HEAD_DIM // 2, 1) * sin_ref[...]
            target[:, cols] = turned.astype(jnp.bfloat16)
        return carry

    lax.fori_loop(0, heads, turn_step, 0)
    for save in saves[5:8]:
        save.start()

    def head_step(h, carry):
        cols = pl.ds(pl.multiple_of(h * HEAD_DIM, HEAD_DIM), HEAD_DIM)
        for block in range(length // block_rows):
            low, high = key_window(block, block_rows)
            here = pl.ds(block * block_rows, block_rows)
            keys = pl.ds(low, high - low)
            scores = attention_scores(
                krot_ref[keys, cols], qrot_ref[here, cols], start_ref[:, here],
                block * block_rows, low, 1,
            )
            top = jnp.max(scores, axis=0, keepdims=True)
            weights = jnp.exp2((scores - top) * exponent)
            total = jnp.sum(weights, axis=0, keepdims=True)
            probs = (weights * (1.0 / total)).astype(jnp.bfloat16)
            probs_ref[block, h, : high - low, :] = probs
            mixed_ref[here, cols] = mm_tn(probs, value_ref[keys, cols]).astype(jnp.bfloat16)
        return carry

    lax.fori_loop(0, heads, head_step, 0, unroll=2)
    for save in saves[8:]:
        save.start()
    for c in range(chunks):
        send_across(c).wait_send()
        forward(c).wait_send()
    to_beside.wait_send()
    for swap in swaps:
        swap.wait_send()
    for save in saves:
        save.wait()


def front(adapter_set, tokens, wq, wk, wv, table, segment_ids, gains, adapters):
    rows, width = tokens.shape
    heads_width = wq.shape[1]
    length = 4 * rows
    part = rows // CHUNKS
    rank = adapters[0].shape[1]
    units = adapters[9].shape[2]
    probs_shape = probs_space(length, heads_width)
    vmem = pl.BlockSpec(memory_space=pltpu.VMEM)
    hbm = pl.BlockSpec(memory_space=pl.ANY)
    low, full = jnp.bfloat16, jnp.float32
    shape = jax.ShapeDtypeStruct
    dma = pltpu.SemaphoreType.DMA
    return pl.pallas_call(
        front_body,
        in_specs=[pl.BlockSpec(memory_space=pltpu.SMEM), vmem] + [hbm] * 3 + [vmem] * 6 + [hbm] * 14,
        out_specs=[vmem] * 17 + [hbm] * 10,
        out_shape=[
            shape((3 * rank, width), low), shape((3 * rank, heads_width), low),
            shape((3 * rank, heads_width), low), shape((3 * rank, heads_width), low),
            shape((rank, heads_width), low), shape((rank, width), low), shape((2 * rank, width), low),
            shape((2 * rank, units), low), shape((2 * rank, units), low), shape((rank, units), low),
            shape((rank, width), low), shape((1, heads_width), full), shape((1, heads_width), full),
            shape((1, width), full), shape((1, width), full),
            shape((1, length), jnp.int32), shape((1, 128), full),
            shape((length, heads_width), low), shape((length, heads_width), low),
            shape((length, heads_width), low), shape((length, heads_width), low),
            shape((length, heads_width), full), shape((length, heads_width), full),
            shape((length, HEAD_DIM), full), shape((length, 3 * rank), low),
            shape((4, CHUNKS, part, width), low), shape(probs_shape, low),
        ],
        scratch_shapes=[pltpu.VMEM(probs_shape, low)]
        + [pltpu.VMEM((length, heads_width), low)] * 4
        + [pltpu.VMEM((length, heads_width), full)] * 2
        + [
            pltpu.VMEM((length, HEAD_DIM), full), pltpu.VMEM((length, 3 * rank), low),
            pltpu.VMEM(table.shape, full), pltpu.VMEM(table.shape, full),
            pltpu.VMEM(wq.shape, low), pltpu.VMEM(wk.shape, low), pltpu.VMEM(wv.shape, low),
            dma((3,)),
            pltpu.VMEM((4, CHUNKS, part, width), low), pltpu.VMEM((rows, width), low),
            pltpu.VMEM((length, HEAD_DIM), full), pltpu.VMEM((8, length), full),
            pltpu.VMEM((3, 8, length), full),
            dma((CHUNKS,)), dma((CHUNKS,)), dma((CHUNKS,)), dma((CHUNKS,)), dma, dma,
            dma((3,)), dma((3,)), dma((10,)),
        ] + [pltpu.VMEM(a.shape, low) for a in adapters] + [dma((14,))],
        cost_estimate=pl.CostEstimate(
            flops=2 * length * heads_width * (3 * width + 2 * length),
            bytes_accessed=2 * width * (3 * heads_width + length), transcendentals=0,
        ),
        compiler_params=pltpu.CompilerParams(
            collective_id=1, has_side_effects=True, vmem_limit_bytes=67043328
        ),
        name="gather_project_attend",
    )(adapter_set, tokens.reshape(CHUNKS, part, width), wq, wk, wv, table, segment_ids, *gains,
      *adapters)


def back_body(
    qrot_hbm, krot_hbm, value_hbm, dmixed_hbm, qproj_hbm, kproj_hbm, scale_hbm, qgain_ref,
    kgain_ref, table_hbm, probs_hbm, wq_hbm, wk_hbm, wv_hbm, shrink_ref,
    eq_ref, ek_ref, ev_ref, mids_ref, full_hbm, hgrad_hbm, set_ref,
    gso_ref, geg_ref, geu_ref, gsd_ref, gsgu_ref, geo_ref, ged_ref,
    tgrad_hbm, split_hbm, heads_hbm, shared_hbm, inward_hbm,
    wq, wk, wv, full, qrot_ref, krot_ref, value_ref, dmixed, qproj_ref, kproj_ref,
    scale_ref, cos_ref, sin_ref, hgrad_ref, probs_ref, probs_sem, wsem, save_sem,
    dq_buf, dk_buf, dv_buf, dq_low, dk_low, dv_low, sums_buf,
    split_send, heads_send, blocks, blocks_recv, blocks_xrecv, shared_send, inward_send,
    ex_send, ex_recv, dmid_send, dmid_recv, dmid_xsend, dmid_xrecv,
    own_buf, xsend, xrecv, bsend, brecv,
    es_sem, er_sem, xs_sem, xr_sem, bs_sem, br_sem, one_s, one_r,
    sp_s, sp_f, sp_r, hd_s, hd_r, sh_s, sh_r, in_s, in_r, local_sem,
):
    me, group, beside, across = partners()
    far = lax.rem(beside + 2, 4)
    order = (me, across, beside, far)
    groups = split_hbm.shape[0]
    chunks, part, width = own_buf.shape
    rows = chunks * part
    length = 4 * rows
    heads_width = wq.shape[1]
    units = geg_ref.shape[1]
    cols_each = blocks.shape[3]
    loads = [
        pltpu.make_async_copy(source, target, wsem.at[i])
        for i, (source, target) in enumerate(
            (
                (dmixed_hbm, dmixed), (qrot_hbm, qrot_ref),
                (krot_hbm, krot_ref), (value_hbm, value_ref),
                (table_hbm, cos_ref), (qproj_hbm, qproj_ref), (kproj_hbm, kproj_ref),
                (scale_hbm, scale_ref), (wq_hbm, wq), (wk_hbm, wk), (wv_hbm, wv),
                (hgrad_hbm, hgrad_ref), (full_hbm, full),
            )
        )
    ]
    probs_loads = [
        pltpu.make_async_copy(probs_hbm.at[i], probs_ref.at[i], probs_sem.at[i])
        for i in range(probs_hbm.shape[0])
    ]
    for load in (*loads[:6], *probs_loads, *loads[6:]):
        load.start()
    barrier = pltpu.get_barrier_semaphore()
    for other in (beside, across, far):
        pl.semaphore_signal(barrier, inc=1, device_id=(group, other), device_id_type=MESH_ID)

    def greet_group(j, carry):
        other = lax.rem(group + j, groups)
        pl.semaphore_signal(barrier, inc=1, device_id=(other, me), device_id_type=MESH_ID)
        return carry

    lax.fori_loop(1, groups, greet_group, 0)

    def remote(source, target, ssem, rsem, other):
        return pltpu.make_async_remote_copy(
            src_ref=source, dst_ref=target, send_sem=ssem, recv_sem=rsem,
            device_id=(group, other), device_id_type=MESH_ID,
        )

    def to_group(source, target, ssem, rsem, j):
        other = lax.rem(group + j, groups)
        return pltpu.make_async_remote_copy(
            src_ref=source(other), dst_ref=target.at[group], send_sem=ssem.at[j],
            recv_sem=rsem.at[group], device_id=(other, me), device_id_type=MESH_ID,
        )

    def from_group(source, target, ssem, rsem, j):
        sender = lax.rem(group + j, groups)
        return pltpu.make_async_remote_copy(
            src_ref=source(sender), dst_ref=target.at[sender], send_sem=ssem.at[j],
            recv_sem=rsem.at[sender], device_id=(sender, me), device_id_type=MESH_ID,
        )

    by_heads = (lambda other: heads_send, heads_hbm, hd_s, hd_r)
    shared = (lambda other: shared_send.at[other], shared_hbm, sh_s, sh_r)
    inward = (lambda other: inward_send.at[other, me], inward_hbm, in_s, in_r)
    exchanges = (None, by_heads, shared, inward)

    def start_exchange(number):
        exchange = exchanges[number]

        def one(j, carry):
            to_group(*exchange, j).start()
            return carry

        lax.fori_loop(1, groups, one, 0)
        pltpu.make_async_copy(
            exchange[0](group), exchange[1].at[group], local_sem.at[number]
        ).start()

    def end_exchange(number):
        exchange = exchanges[number]

        def one(j, carry):
            to_group(*exchange, j).wait_send()
            from_group(*exchange, j).wait_recv()
            return carry

        lax.fori_loop(1, groups, one, 0)
        pltpu.make_async_copy(
            exchange[0](group), exchange[1].at[group], local_sem.at[number]
        ).wait()

    neighbour = group + 1 - 2 * lax.rem(group, 2)

    def split_copy(source, slot, ssem, other):
        return pltpu.make_async_remote_copy(
            src_ref=source, dst_ref=split_hbm.at[slot], send_sem=ssem, recv_sem=sp_r.at[slot],
            device_id=(other, me), device_id_type=MESH_ID,
        )

    def split_direct(k):
        return split_copy(split_send, group, sp_s.at[2 * k], lax.rem(group + 2 * k, groups))

    def split_passed(k):
        slot = lax.rem(group + 2 * k, groups)
        return split_copy(split_hbm.at[slot], slot, sp_f.at[2 * k], neighbour)

    def split_arrival(slot):
        return split_copy(split_send, slot, sp_s.at[0], neighbour)

    split_near = split_copy(split_send, group, sp_s.at[0], neighbour)
    split_own = pltpu.make_async_copy(split_send, split_hbm.at[group], local_sem.at[0])

    def over_parity(body):
        def one(k, carry):
            body(k)
            return carry

        lax.fori_loop(1, groups // 2, one, 0)

    def start_split():
        over_parity(lambda k: split_direct(k).start())
        split_near.start()
        split_own.start()

    def pass_split(k):
        split_arrival(lax.rem(group + 2 * k, groups)).wait_recv()
        split_passed(k).start()

    def end_split_one(k):
        split_direct(k).wait_send()
        split_passed(k).wait_send()
        split_arrival(lax.rem(neighbour + 2 * k, groups)).wait_recv()

    def end_split():
        over_parity(end_split_one)
        split_near.wait_send()
        split_arrival(neighbour).wait_recv()
        split_own.wait()

    low = jnp.bfloat16
    heads = heads_width // HEAD_DIM
    inverse = HEAD_DIM ** (-0.5)
    for ref in (sums_buf, dk_buf, dv_buf):
        ref[...] = jnp.zeros_like(ref)
    block_rows = min(ATT_ROWS, length)

    def attend_back(block, first_query, first_key, size):
        here = pl.ds(first_query, block_rows)
        keys = pl.ds(first_key, size)

        def head_step(h, carry):
            cols = pl.ds(pl.multiple_of(h * HEAD_DIM, HEAD_DIM), HEAD_DIM)
            queries = qrot_ref[here, cols]
            key_rows = krot_ref[keys, cols]
            grads = dmixed[here, cols]
            prob_low = probs_ref[block, h, :size, :]
            probs = prob_low.astype(jnp.float32)
            prob_grad = mm_nt(value_ref[keys, cols], grads)
            weighted = probs * prob_grad
            delta = jnp.sum(weighted, axis=0, keepdims=True)
            score_grad = (weighted - probs * delta).astype(low)
            dv_buf[keys, cols] += mm(prob_low, grads)
            dk_buf[keys, cols] += mm(score_grad, queries)
            dq = mm_tn(score_grad, key_rows) * inverse
            dq = dq * cos_ref[here, :] - pltpu.roll(dq, HEAD_DIM // 2, 1) * sin_ref[here, :]
            dq = dq * qgain_ref[:, cols]
            dq_buf[here, cols] = dq
            sums_buf[0, here, :] += qproj_ref[here, cols] * dq
            return carry

        lax.fori_loop(0, heads, head_step, 0, unroll=2)

    pl.semaphore_wait(barrier, groups + 2)
    split_send[:, :units] = (adapter_scale_factor * geg_ref[:16]).astype(low)
    split_send[:, units : 2 * units] = (adapter_scale_factor * geu_ref[16:]).astype(low)
    split_send[:, 2 * units : 3 * units] = gsd_ref[...].astype(low)
    split_send[:, 3 * units : 3 * units + heads_width] = gso_ref[...].astype(low)
    split_send[:, 3 * units + heads_width :] = jnp.broadcast_to(set_ref[...], (16, 128)).astype(low)
    start_split()
    for t in range(4):
        for g in range(groups):
            at = slice((g * 4 + t) * cols_each, (g * 4 + t + 1) * cols_each)
            blocks[t, g, :16] = (adapter_scale_factor * geo_ref[:, at]).astype(low)
            blocks[t, g, 16:48] = gsgu_ref[:, at].astype(low)
            blocks[t, g, 48:] = (adapter_scale_factor * ged_ref[:, at]).astype(low)
    block_near = remote(blocks.at[beside], blocks_recv.at[0], one_s.at[0], one_r.at[0], beside)
    block_far = remote(blocks.at[far], blocks_recv.at[1], one_s.at[1], one_r.at[1], beside)
    block_across = remote(shared_send, blocks_xrecv, one_s.at[2], one_r.at[2], across)
    block_near.start()
    block_far.start()
    for load in loads[:6]:
        load.wait()
    open_table(cos_ref, sin_ref)

    for block in range(length // block_rows):
        first, last = key_window(block, block_rows)
        if True:
            probs_loads[block].wait()
            attend_back(block, block * block_rows, first, last - first)
        if block == 1:
            block_near.wait_recv()
            block_far.wait_recv()
            shared_send[...] = (
                blocks[across].astype(jnp.float32) + blocks_recv[1].astype(jnp.float32)
            ).astype(low)
            block_across.start()
        if block == length // block_rows - 1:
            block_across.wait()
            shared_send[...] = (
                blocks[me].astype(jnp.float32)
                + blocks_recv[0].astype(jnp.float32)
                + blocks_xrecv[...].astype(jnp.float32)
            ).astype(low)
            start_exchange(2)

    def head_end(h, carry):
        cols = pl.ds(pl.multiple_of(h * HEAD_DIM, HEAD_DIM), HEAD_DIM)
        dk = dk_buf[:, cols] * inverse
        dk = dk * cos_ref[...] - pltpu.roll(dk, HEAD_DIM // 2, 1) * sin_ref[...]
        dk = dk * kgain_ref[:, cols]
        dk_buf[:, cols] = dk
        sums_buf[1] += kproj_ref[:, cols] * dk
        dv_low[:, cols] = dv_buf[:, cols].astype(low)
        return carry

    for load in loads[6:]:
        load.wait()
    lax.fori_loop(0, heads, head_end, 0)

    ones = jnp.ones((8, HEAD_DIM), low)
    totals = []
    for i in range(2):
        high = sums_buf[i].astype(low)
        rest = (sums_buf[i] - high.astype(jnp.float32)).astype(low)
        totals.append(mm_nt(ones, high) + mm_nt(ones, rest))
    upper = lax.broadcasted_iota(jnp.int32, (8, length), 0) < 4
    ex_send[...] = jnp.where(upper, totals[0], totals[1])
    swaps = [
        remote(ex_send, ex_recv.at[i], es_sem.at[i], er_sem.at[i], other)
        for i, other in enumerate((beside, across, far))
    ]
    for swap in swaps:
        swap.start()
    for swap in swaps:
        swap.wait_recv()
    total = (ex_send[...] + ex_recv[0] + ex_recv[1] + ex_recv[2]) * (1.0 / (4 * heads_width))
    wide = jnp.concatenate(
        [
            jnp.broadcast_to(total[:1], (HEAD_DIM // 2, length)),
            jnp.broadcast_to(total[4:5], (HEAD_DIM // 2, length)),
        ],
        axis=0,
    )
    sums_buf[0] = jnp.transpose(wide)
    for dn, proj, target, at in (
        (dq_buf, qproj_ref, dq_low, 0), (dk_buf, kproj_ref, dk_low, HEAD_DIM // 2),
    ):
        scale = scale_ref[:, at : at + 1]
        means = sums_buf[0, :, at : at + 1]
        target[...] = (scale * dn[...] - proj[...] * (scale * scale * scale * means)).astype(low)

    dmid_near = remote(dmid_send, dmid_recv, one_s.at[3], one_r.at[3], beside)
    dmid_across = remote(dmid_xsend, dmid_xrecv, one_s.at[4], one_r.at[4], across)

    def reduce_beside(c):
        return remote(bsend.at[c], brecv.at[c], bs_sem.at[c], br_sem.at[c], beside)

    def reduce_across(c):
        return remote(xsend.at[c], xrecv.at[c], xs_sem.at[c], xr_sem.at[c], across)

    def chunk_of(buffer, c):
        return jnp.concatenate(
            [buffer[pl.ds(pl.multiple_of(o * rows + c * part, part), part), :] for o in order], axis=0
        )

    def stage_partial(c):
        parts = [chunk_of(buffer, c) for buffer in (dq_low, dk_low, dv_low)]
        tile = TILE

        def one(j, carry):
            at = pl.ds(pl.multiple_of(j * tile, tile), tile)
            value = (
                mm_nt(parts[0], wq[at, :]) + mm_nt(parts[1], wk[at, :]) + mm_nt(parts[2], wv[at, :])
            ).astype(low)
            own_buf[c, :, at] = value[:part]
            xsend[c, :, at] = value[part : 2 * part]
            bsend[c, 0, :, at] = value[2 * part : 3 * part]
            bsend[c, 1, :, at] = value[3 * part :]
            return carry

        lax.fori_loop(0, width // tile, one, 0)
        reduce_beside(c).start()

    def stage_pair(c):
        reduce_beside(c).wait_recv()
        xsend[c] = (xsend[c].astype(jnp.float32) + brecv[c, 1].astype(jnp.float32)).astype(low)
        reduce_across(c).start()
        own_buf[c] = (own_buf[c].astype(jnp.float32) + brecv[c, 0].astype(jnp.float32)).astype(low)

    def rank_sums_start():
        dmid_part = (
            mm_nt(eq_ref[...], dq_low[...]) + mm_nt(ek_ref[...], dk_low[...])
            + mm_nt(ev_ref[...], dv_low[...])
        )
        dmid_send[...] = dmid_part.astype(low)
        dmid_near.start()

    def rank_sums_cross():
        dmid_near.wait_recv()
        dmid_xsend[...] = (
            dmid_send[...].astype(jnp.float32) + dmid_recv[...].astype(jnp.float32)
        ).astype(low)
        dmid_across.start()

    def expand_gradients():
        mids = mids_ref[...]
        for i, buffer in enumerate((dq_low, dk_low, dv_low)):
            heads_send[:, i * heads_width : (i + 1) * heads_width] = (
                adapter_scale_factor * mm_tn(mids, buffer[...])[i * 16 : (i + 1) * 16]
            ).astype(low)
        start_exchange(1)

    def partial_step(i, carry):
        stage_partial(i)
        for k, extra in (
            (0, rank_sums_start), (1, rank_sums_cross), (1, lambda: over_parity(pass_split)),
        ):

            @pl.when(i == k)
            def _():
                extra()

        @pl.when(i == 2)
        def _():
            expand_gradients()

        stage_pair(i)
        return carry

    lax.fori_loop(0, chunks, partial_step, 0)
    dmid_across.wait_recv()
    dmid = (
        dmid_xsend[...].astype(jnp.float32) + dmid_xrecv[...].astype(jnp.float32)
    ).astype(low)
    inward_grad = mm(dmid, full[...])
    for t in range(4):
        for g in range(groups):
            at = slice((g * 4 + t) * cols_each, (g * 4 + t + 1) * cols_each)
            inward_send[g, t] = inward_grad[:, at].astype(low)
    start_exchange(3)
    dmid_across.wait_send()
    dmid_xsend[...] = dmid
    mine = pl.ds(pl.multiple_of(me * rows, rows), rows)
    hgrad_ref[...] += mm_tn(dmid_xsend[:, mine], shrink_ref[...])

    def own_rows(c):
        return pl.ds(pl.multiple_of(c * part, part), part)

    def save(c):
        return pltpu.make_async_copy(
            hgrad_ref.at[own_rows(c), :], tgrad_hbm.at[own_rows(c), :], save_sem.at[c]
        )

    def finish_step(c, carry):
        reduce_across(c).wait_recv()
        hgrad_ref[own_rows(c), :] += own_buf[c].astype(jnp.float32) + xrecv[c].astype(jnp.float32)
        save(c).start()
        return carry

    lax.fori_loop(0, chunks, finish_step, 0)
    for c in range(chunks):
        save(c).wait()
    for c in range(chunks):
        reduce_beside(c).wait_send()
        reduce_across(c).wait_send()
    for copy in (block_near, block_far, dmid_near, *swaps):
        copy.wait_send()
    end_split()
    for number in range(1, 4):
        end_exchange(number)


def back(
    qrot, krot, value, dmixed, qproj, kproj, scale, qgain, kgain, table, probs,
    wq, wk, wv, shrink, eq, ek, ev, mids, full, hgrad, chosen,
    gso, geg, geu, gsd, gsgu, geo, ged,
):
    rows, width = hgrad.shape
    heads_width, units = wq.shape[1], geg.shape[1]
    length = 4 * rows
    part = rows // CHUNKS
    groups = lax.axis_size("dp")
    cols_each = width // (4 * groups)
    split_width = 3 * units + heads_width + 128
    vmem = pl.BlockSpec(memory_space=pltpu.VMEM)
    hbm = pl.BlockSpec(memory_space=pl.ANY)
    low, f32 = jnp.bfloat16, jnp.float32
    shape = jax.ShapeDtypeStruct
    dma = pltpu.SemaphoreType.DMA
    buf = pltpu.VMEM
    return pl.pallas_call(
        back_body,
        in_specs=[hbm] * 7 + [vmem] * 2 + [hbm] * 5 + [vmem] * 5 + [hbm] * 2 + [vmem] * 8,
        out_specs=[hbm] * 5,
        out_shape=[
            shape((rows, width), f32),
            shape((groups, 16, split_width), low),
            shape((groups, 16, 3 * heads_width), low),
            shape((groups, 64, cols_each), low),
            shape((groups, 48, cols_each), low),
        ],
        scratch_shapes=[
            buf(wq.shape, low), buf(wk.shape, low), buf(wv.shape, low),
            buf(full.shape, low),
            buf(qrot.shape, low), buf(krot.shape, low), buf(value.shape, low), buf(dmixed.shape, low),
            buf(qproj.shape, f32), buf(kproj.shape, f32), buf(scale.shape, f32),
            buf(table.shape, f32), buf(table.shape, f32), buf(hgrad.shape, f32),
            buf(probs.shape, low), dma((probs.shape[0],)), dma((13,)), dma((CHUNKS,)),
            buf((length, heads_width), f32), buf((length, heads_width), f32),
            buf((length, heads_width), f32),
            buf((length, heads_width), low), buf((length, heads_width), low),
            buf((length, heads_width), low),
            buf((2, length, HEAD_DIM), f32),
            buf((16, split_width), low), buf((16, 3 * heads_width), low),
            buf((4, groups, 64, cols_each), low), buf((2, groups, 64, cols_each), low),
            buf((groups, 64, cols_each), low), buf((groups, 64, cols_each), low),
            buf((groups, 4, 48, cols_each), low),
            buf((8, length), f32), buf((3, 8, length), f32),
            buf((48, length), low), buf((48, length), low), buf((48, length), low),
            buf((48, length), low),
            buf((CHUNKS, part, width), low), buf((CHUNKS, part, width), low),
            buf((CHUNKS, part, width), low),
            buf((CHUNKS, 2, part, width), low), buf((CHUNKS, 2, part, width), low),
            dma((3,)), dma((3,)), dma((CHUNKS,)), dma((CHUNKS,)), dma((CHUNKS,)), dma((CHUNKS,)),
            dma((5,)), dma((5,)),
        ] + [dma((groups,))] * 9 + [dma((4,))],
        cost_estimate=pl.CostEstimate(
            flops=2 * length * heads_width * (3 * width + 5 * length),
            bytes_accessed=2 * width * (3 * heads_width + 3 * length), transcendentals=0,
        ),
        compiler_params=pltpu.CompilerParams(
            collective_id=2, has_side_effects=True, vmem_limit_bytes=67043328
        ),
        name="attention_back_to_tokens",
    )(qrot, krot, value, dmixed, qproj, kproj, scale, qgain, kgain, table, probs,
      wq, wk, wv, shrink, eq, ek, ev, mids, full, hgrad, chosen,
      gso, geg, geu, gsd, gsgu, geo, ged)


def finish_body(split_ref, heads_ref, shared_ref, inward_ref, block_ref, tokens_ref, *outs):
    block_out, tokens_out, *outs, which = outs
    groups = split_ref.shape[0]
    tag = split_ref.shape[2] - 128
    together = outs[0].shape[0]
    first = pl.program_id(0) * together

    @pl.when(first == 0)
    def _():
        for g in range(groups):
            which[g] = jnp.max(split_ref[g, :, tag:].astype(jnp.float32)).astype(jnp.int32)

    sq, eq, sk, ek, sv, ev, so, eo, sg, eg, su, eu, sd, ed = outs
    here = eq.shape[2]
    units = eg.shape[2]
    sources = []
    for i, target in enumerate((eq, ek, ev)):
        sources.append((target, lambda g, i=i: heads_ref[g, :, i * here : (i + 1) * here]))
    for i, target in enumerate((eg, eu, sd)):
        sources.append((target, lambda g, i=i: split_ref[g, :, i * units : (i + 1) * units]))
    sources.append((so, lambda g: split_ref[g, :, 3 * units : 3 * units + here]))
    for i, target in enumerate((sq, sk, sv)):
        sources.append((target, lambda g, i=i: inward_ref[g, i * 16 : (i + 1) * 16, :]))
    for i, target in enumerate((eo, sg, su, ed)):
        sources.append((target, lambda g, i=i: shared_ref[g, i * 16 : (i + 1) * 16, :]))
    for target, _ in sources:
        target[...] = jnp.zeros_like(target)

    def one(g, carry):
        at = which[g] - first

        @pl.when((at >= 0) & (at < together))
        def _():
            for target, source in sources:
                target[at] += source(g).astype(jnp.float32)

        return carry

    lax.fori_loop(0, groups, one, 0)
    block_out[...] = block_ref[...]
    tokens_out[...] = tokens_ref[...]


def finish(split, by_heads, shared, inward, block, tokens, sets, here, units):
    cols = shared.shape[2]
    rows, width = block.shape
    steps = min(FINISH_STEPS, sets)
    together = sets // steps
    part = rows // steps
    whole = lambda a: pl.BlockSpec(a.shape, lambda i: (0,) * a.ndim)
    strip = pl.BlockSpec((part, width), lambda i: (i, 0))
    widths = (cols, here, cols, here, cols, here, here, cols, cols, units, cols, units, units, cols)
    return pl.pallas_call(
        finish_body,
        grid=(steps,),
        in_specs=[whole(split), whole(by_heads), whole(shared), whole(inward), strip, strip],
        out_specs=[strip, strip] + [pl.BlockSpec((together, 16, w), lambda i: (i, 0, 0)) for w in widths],
        out_shape=[
            jax.ShapeDtypeStruct(block.shape, block.dtype),
            jax.ShapeDtypeStruct(tokens.shape, tokens.dtype),
        ] + [jax.ShapeDtypeStruct((sets, 16, w), jnp.float32) for w in widths],
        scratch_shapes=[pltpu.SMEM((split.shape[0],), jnp.int32)],
        compiler_params=pltpu.CompilerParams(vmem_limit_bytes=67043328),
        name="sum_by_set",
    )(split, by_heads, shared, inward, block, tokens)


def per_device(
    tokens,
    cotangent,
    segment_ids,
    adapter_set,
    w_query,
    w_key,
    w_value,
    w_out,
    w_gate,
    w_up,
    w_down,
    query_gain,
    key_gain,
    mixer_gain,
    feed_gain,
    shrink_query,
    expand_query,
    shrink_key,
    expand_key,
    shrink_value,
    expand_value,
    shrink_out,
    expand_out,
    shrink_gate,
    expand_gate,
    shrink_up,
    expand_up,
    shrink_down,
    expand_down,
):
    length = 4 * tokens.shape[0]
    table = jnp.asarray(rotary_constants(length, HEAD_DIM))
    (
        shrink_rows, expand_query_rows, expand_key_rows, expand_value_rows, out_shrink, out_expand,
        gate_up_shrink, gate_expand, up_expand, down_shrink, down_expand,
        query_gains, key_gains, mixer_gains, feed_gains, _, set_row,
        mixed, query_rot, key_rot, value_low, query_proj, key_proj, scales, qkv_middle, full_tokens,
        probs,
    ) = front(
        adapter_set, tokens, w_query, w_key, w_value, table, segment_ids,
        (query_gain, key_gain, mixer_gain, feed_gain),
        (
            shrink_query, expand_query, shrink_key, expand_key, shrink_value, expand_value,
            shrink_out, expand_out, shrink_gate, expand_gate, shrink_up, expand_up,
            shrink_down, expand_down,
        ),
    )
    (
        block_output, hidden_grad, mixed_grad, grad_down_shrink, gradient_gate_widened,
        gradient_up_widened, grad_out_shrink, owner_gate_up, owner_out, owner_down,
    ) = middle(
        mixed, tokens, cotangent, w_out, w_gate, w_up, w_down, mixer_gains, feed_gains,
        out_shrink, out_expand, gate_up_shrink, gate_expand, up_expand, down_shrink, down_expand,
    )
    token_grads, split, by_heads, shared, inward = back(
        query_rot, key_rot, value_low, mixed_grad.reshape(mixed.shape), query_proj, key_proj, scales,
        query_gains, key_gains, table, probs,
        w_query, w_key, w_value, shrink_rows, expand_query_rows, expand_key_rows, expand_value_rows,
        qkv_middle, full_tokens.reshape(length, -1), hidden_grad, set_row,
        grad_out_shrink, gradient_gate_widened, gradient_up_widened, grad_down_shrink,
        owner_gate_up, owner_out, owner_down,
    )
    return finish(
        split, by_heads, shared, inward, block_output, token_grads,
        shrink_query.shape[0], w_query.shape[1], w_gate.shape[1],
    )


def solution(mesh):
    in_specs = (
        P(("dp", "tensor"), None),
        P(("dp", "tensor"), None),
        P("dp", None),
        P("dp"),
        P(None, "tensor"),
        P(None, "tensor"),
        P(None, "tensor"),
        P("tensor", None),
        P(None, "tensor"),
        P(None, "tensor"),
        P("tensor", None),
        P("tensor"),
        P("tensor"),
        P(),
        P(),
        P(),
        P(None, None, "tensor"),
        P(),
        P(None, None, "tensor"),
        P(),
        P(None, None, "tensor"),
        P(None, None, "tensor"),
        P(),
        P(),
        P(None, None, "tensor"),
        P(),
        P(None, None, "tensor"),
        P(None, None, "tensor"),
        P(),
    )
    out_specs = (
        P(("dp", "tensor"), None),
        P(("dp", "tensor"), None),
        P(None, None, ("dp", "tensor")),
        P(None, None, "tensor"),
        P(None, None, ("dp", "tensor")),
        P(None, None, "tensor"),
        P(None, None, ("dp", "tensor")),
        P(None, None, "tensor"),
        P(None, None, "tensor"),
        P(None, None, ("dp", "tensor")),
        P(None, None, ("dp", "tensor")),
        P(None, None, "tensor"),
        P(None, None, ("dp", "tensor")),
        P(None, None, "tensor"),
        P(None, None, "tensor"),
        P(None, None, ("dp", "tensor")),
    )
    return jax.shard_map(
        per_device, mesh=mesh, in_specs=in_specs, out_specs=out_specs, check_vma=False
    )
```

```python
import functools
import jax
import jax.numpy as jnp
import numpy as np
from jax import lax
from jax.experimental import pallas as pl
from jax.experimental.pallas import tpu as pltpu
from jax.sharding import PartitionSpec as P

HEAD_DIM = 128
DOC_MOST = 512
ATT_ROWS = 256
rotary_base = 500000.0
NEG = -1e30
LOG2E = 1.4426950408889634


def rotary_constants(length, head_dim):
    half = head_dim // 2
    frequency = np.float32(rotary_base) ** (
        -(np.arange(half, dtype=np.float32) * np.float32(2.0) / np.float32(head_dim))
    )
    angles = np.arange(length, dtype=np.float32)[:, None] * frequency.astype(np.float32)[None, :]
    cosine = np.cos(angles.astype(np.float64)).astype(np.float32)
    sine = np.sin(angles.astype(np.float64)).astype(np.float32)
    return np.concatenate([cosine, sine], axis=1)


def open_table(cos_ref, sin_ref):
    table = cos_ref[...]
    turned = pltpu.roll(table, HEAD_DIM // 2, 1)
    low_half = lax.broadcasted_iota(jnp.int32, table.shape, 1) < HEAD_DIM // 2
    cos_ref[...] = jnp.where(low_half, table, turned)
    sin_ref[...] = jnp.where(low_half, -turned, table)


def key_window(block, rows):
    first = max(0, (block * rows - (DOC_MOST - 1)) // rows) * rows
    return first, (block + 1) * rows


epsilon = 1e-06
adapter_scale_factor = 0.5


CHUNKS = 4
FINISH_STEPS = 2
TILE = 1024
EXTRA = 128
NT = (((1,), (1,)), ((), ()))
TN = (((0,), (0,)), ((), ()))
MESH_ID = pl.DeviceIdType.MESH
MIDDLE_STAGES = ("S0", "P0", "S1", "F1", "S2", "P2", "S3", "F3", "S4", "P4", "S5", "F5", "S6")
MIDDLE_ORDER = (
    0, 1, 2, 4, 3, 5, 6, 7, 8, 9, 10, 11, 12,
    16, 13, 14, 17, 20, 18, 21, 15, 24, 19, 25, 22, 23,
    28, 32, 26, 29, 36, 33, 27, 30, 37, 34, 40, 31, 41,
    38, 35, 44, 45, 48, 39, 49, 42, 43, 46, 50, 47, 51,
)


def mm(left, right):
    return jnp.dot(left, right, preferred_element_type=jnp.float32)


def mm_nt(left, right):
    return lax.dot_general(left, right, NT, preferred_element_type=jnp.float32)


def mm_tn(left, right):
    return lax.dot_general(left, right, TN, preferred_element_type=jnp.float32)


def partners():
    me = lax.axis_index("tensor")
    group = lax.axis_index("dp")
    beside = me + 1 - 2 * lax.rem(me, 2)
    across = lax.rem(me + 2, 4)
    return me, group, beside, across


def greet(group, beside, across):
    barrier = pltpu.get_barrier_semaphore()
    for other in (beside, across):
        pl.semaphore_signal(barrier, inc=1, device_id=(group, other), device_id_type=MESH_ID)
    pl.semaphore_wait(barrier, 2)


def middle_body(
    mixed_ref, tokens_hbm, cot_hbm, w_out_hbm, w_gate_hbm, w_up_hbm, w_down_hbm,
    mgain_ref, fgain_ref, so_ref, eo_ref, sgu_ref, eg_ref, eu_ref, sd_ref, ed_ref,
    out_hbm, hgrad_hbm, dmixed_hbm, gsd_ref, geg_ref, geu_ref, gso_ref, gsgu_ref, geo_ref, ged_ref,
    w_out, w_gate, w_up, w_down, tokens_ref, cot_ref, wsem, out_ref, dmixed_ref, save_sem,
    rows_buf, own_buf, xsend, xrecv, bsend, brecv,
    gate_buf, up_buf, temp_a, temp_b, mgu_buf, mixer_buf, hidden_buf, mout_buf,
    xside, yside, vs_sem, vr_sem, xs_sem, xr_sem, bs_sem, br_sem, gxs_sem, gxr_sem, gbs_sem, gbr_sem, fs_sem, fr_sem,
):
    me, group, beside, across = partners()
    chunks, part, width = rows_buf.shape[0], rows_buf.shape[2], rows_buf.shape[3]
    units = w_gate.shape[1]
    heads_width = w_out.shape[0]
    far = lax.rem(beside + 2, 4)
    order = (me, across, beside, far)
    loads = [
        pltpu.make_async_copy(source, target, wsem.at[i])
        for i, (source, target) in enumerate(
            (
                (w_out_hbm, w_out), (tokens_hbm, tokens_ref), (w_gate_hbm, w_gate), (w_up_hbm, w_up),
                (w_down_hbm, w_down), (cot_hbm, cot_ref),
            )
        )
    ]
    for load in loads:
        load.start()
    for ref in (gsd_ref, geg_ref, geu_ref, gso_ref, gsgu_ref, geo_ref, ged_ref):
        ref[...] = jnp.zeros_like(ref)
    greet(group, beside, across)

    def remote(source, target, ssem, rsem, other):
        return pltpu.make_async_remote_copy(
            src_ref=source, dst_ref=target, send_sem=ssem, recv_sem=rsem,
            device_id=(group, other), device_id_type=MESH_ID,
        )

    def gather_across(c):
        return remote(rows_buf.at[c, 0], rows_buf.at[c, 1], gxs_sem.at[c], gxr_sem.at[c], across)

    def gather_beside(c):
        return remote(rows_buf.at[c, 0], rows_buf.at[c, 2], gbs_sem.at[c], gbr_sem.at[c], beside)

    def gather_forward(c):
        return remote(rows_buf.at[c, 1], rows_buf.at[c, 3], fs_sem.at[c], fr_sem.at[c], beside)

    def reduce_beside(c):
        return remote(bsend.at[c], brecv.at[c], bs_sem.at[c], br_sem.at[c], beside)

    def reduce_across(c):
        main = pl.ds(0, width)
        return remote(
            xsend.at[c, :, main], xrecv.at[c, :, main], xs_sem.at[c], xr_sem.at[c], across
        )

    def side_across(c):
        return remote(xside.at[c], yside.at[c], vs_sem.at[c], vr_sem.at[c], across)

    def turned(value, high):
        value = jnp.pad(value, ((0, EXTRA - value.shape[0]), (0, EXTRA - value.shape[1])))
        return jnp.transpose(value)[:high]

    def store_partial(c, columns, value):
        low = value.astype(jnp.bfloat16)
        own_buf[c, :, columns] = low[:part]
        xsend[c, :, columns] = low[part : 2 * part]
        bsend[c, 0, :, columns] = low[2 * part : 3 * part]
        bsend[c, 1, :, columns] = low[3 * part :]

    def gathered(c):
        return rows_buf[c].reshape(4 * part, width)

    def forward_stage(c):
        gather_across(c).wait_recv()
        gather_forward(c).start()

    def pair_stage(c):
        reduce_beside(c).wait_recv()
        own_buf[c] = (
            own_buf[c].astype(jnp.float32) + brecv[c, 0].astype(jnp.float32)
        ).astype(jnp.bfloat16)
        xsend[c] = (
            xsend[c].astype(jnp.float32) + brecv[c, 1].astype(jnp.float32)
        ).astype(jnp.bfloat16)
        reduce_across(c).start()
        xside[c] = turned(xsend[c, :, width:].astype(jnp.float32), 32).astype(jnp.bfloat16)
        side_across(c).start()

    def totals(c):
        reduce_across(c).wait_recv()
        main = own_buf[c, :, :width].astype(jnp.float32) + xrecv[c, :, :width].astype(jnp.float32)
        side_across(c).wait_recv()
        side = own_buf[c, :, width : width + 32].astype(jnp.float32) + turned(
            yside[c].astype(jnp.float32), part
        )[:, :32]
        return main, side.astype(jnp.bfloat16)

    def own_rows(c):
        return pl.ds(pl.multiple_of(c * part, part), part)

    def save(number, c):
        source, target = ((out_ref, out_hbm), (hidden_buf, hgrad_hbm))[number]
        return pltpu.make_async_copy(
            source.at[own_rows(c), :], target.at[own_rows(c), :], save_sem.at[number, c]
        )

    def send_rows(c, value, again):
        if again:
            gather_across(c).wait_send()
            gather_beside(c).wait_send()
        rows_buf[c, 0] = value
        gather_across(c).start()
        gather_beside(c).start()

    def chunk_rows(c):
        return pl.ds(pl.multiple_of(c * 4 * part, 4 * part), 4 * part)

    def tiles(total, tile, body):
        def step(j, carry):
            body(pl.ds(pl.multiple_of(j * tile, tile), tile))
            return carry

        lax.fori_loop(0, total // tile, step, 0)

    def mixed_chunk(c):
        return jnp.concatenate([mixed_ref[o, c] for o in order], axis=0)

    def stage_mixer(c):
        @pl.when(c == 0)
        def _():
            loads[0].wait()

        rows = mixed_chunk(c)
        store_partial(c, slice(width, width + 16), mm_nt(rows, so_ref[...]))
        tiles(width, TILE, lambda cols: store_partial(c, cols, mm(rows, w_out[:, cols])))
        reduce_beside(c).start()

    def stage_hidden(c):
        @pl.when(c == 0)
        def _():
            loads[1].wait()

        main, side = totals(c)
        mid = side[:, :16]
        mout_buf[c] = mid
        mixer = main + mm(mid, eo_ref[...])
        mixer_buf[own_rows(c), :] = mixer
        factor = lax.rsqrt(jnp.mean(mixer * mixer, axis=1, keepdims=True) + epsilon)
        hidden = tokens_ref[own_rows(c), :].astype(jnp.float32) + mixer * factor * mgain_ref[...]
        hidden_buf[own_rows(c), :] = hidden
        send_rows(c, hidden.astype(jnp.bfloat16), False)

    def arrive(c):
        gather_beside(c).wait_recv()
        gather_forward(c).wait_recv()

    def stage_units(c):
        @pl.when(c == 0)
        def _():
            for load in loads[2:]:
                load.wait()

        arrive(c)
        mids = mm_nt(gathered(c), sgu_ref[...]).astype(jnp.bfloat16)
        mgu_buf[c] = mids

        def unit_tile(cols):
            rows = gathered(c)
            gate = mm(rows, w_gate[:, cols]) + mm(mids, eg_ref[:, cols])
            up = mm(rows, w_up[:, cols]) + mm(mids, eu_ref[:, cols])
            gate_buf[chunk_rows(c), cols] = gate.astype(jnp.bfloat16)
            up_buf[chunk_rows(c), cols] = up.astype(jnp.bfloat16)
            sig = 1.0 / (1.0 + jnp.exp(-gate))
            temp_a[:, cols] = (gate * sig * up).astype(jnp.bfloat16)

        tiles(units, TILE, unit_tile)
        gather_forward(c).wait_send()
        reduce_beside(c).wait_send()
        reduce_across(c).wait_send()
        side_across(c).wait_send()
        inner = temp_a[...]
        store_partial(c, slice(width, width + 16), mm_nt(inner, sd_ref[...]))
        tiles(width, 2 * TILE, lambda cols: store_partial(c, cols, mm(temp_a[...], w_down[:, cols])))
        reduce_beside(c).start()

    def norm_back_rows(values, gains, grads):
        factor = lax.rsqrt(jnp.mean(values * values, axis=1, keepdims=True) + epsilon)
        weighted = grads * gains
        return factor * weighted - values * (
            factor * factor * factor * jnp.mean(values * weighted, axis=1, keepdims=True)
        )

    def stage_feed(c):
        main, side = totals(c)
        mid = side[:, :16]
        feed = main + mm(mid, ed_ref[...])
        factor = lax.rsqrt(jnp.mean(feed * feed, axis=1, keepdims=True) + epsilon)
        gains = fgain_ref[...]
        out_ref[own_rows(c), :] = (hidden_buf[own_rows(c), :] + feed * factor * gains).astype(
            jnp.bfloat16
        )
        save(0, c).start()
        grad = norm_back_rows(feed, gains, cot_ref[own_rows(c), :].astype(jnp.float32))
        grad = grad.astype(jnp.bfloat16)
        send_rows(c, grad, True)
        ged_ref[...] += mm_tn(mid, grad)

    def stage_units_back(c):
        arrive(c)
        dmid = mm_nt(gathered(c), ed_ref[...]).astype(jnp.bfloat16)
        mids = mgu_buf[c]

        def unit_tile(cols):
            rows = gathered(c)
            inner_grad = mm_nt(rows, w_down[cols, :]) + mm(dmid, sd_ref[:, cols])
            gate = gate_buf[chunk_rows(c), cols].astype(jnp.float32)
            up = up_buf[chunk_rows(c), cols].astype(jnp.float32)
            sig = 1.0 / (1.0 + jnp.exp(-gate))
            silu = gate * sig
            gate_grad = (inner_grad * up * (sig + silu * (1.0 - sig))).astype(jnp.bfloat16)
            up_grad = (inner_grad * silu).astype(jnp.bfloat16)
            temp_a[:, cols] = gate_grad
            temp_b[:, cols] = up_grad
            gsd_ref[:, cols] += mm_tn(dmid, (silu * up).astype(jnp.bfloat16))
            geg_ref[:, cols] += mm_tn(mids, gate_grad)
            geu_ref[:, cols] += mm_tn(mids, up_grad)

        tiles(units, TILE, unit_tile)
        gather_forward(c).wait_send()
        reduce_beside(c).wait_send()
        reduce_across(c).wait_send()
        side_across(c).wait_send()
        store_partial(
            c,
            slice(width, width + 32),
            mm_nt(temp_a[...], eg_ref[...]) + mm_nt(temp_b[...], eu_ref[...]),
        )

        def width_tile(cols):
            store_partial(
                c, cols, mm_nt(temp_a[...], w_gate[cols, :]) + mm_nt(temp_b[...], w_up[cols, :])
            )

        tiles(width, TILE, width_tile)
        reduce_beside(c).start()

    def stage_mixer_grad(c):
        main, side = totals(c)
        grads = cot_ref[own_rows(c), :].astype(jnp.float32) + main + mm(side, sgu_ref[...])
        mixer_grad = norm_back_rows(mixer_buf[own_rows(c), :], mgain_ref[...], grads)
        mixer_grad = mixer_grad.astype(jnp.bfloat16)
        send_rows(c, mixer_grad, True)
        geo_ref[...] += mm_tn(mout_buf[c], mixer_grad)
        gsgu_ref[...] += mm_tn(side, hidden_buf[own_rows(c), :].astype(jnp.bfloat16))
        hidden_buf[own_rows(c), :] = grads
        save(1, c).start()

    def stage_mixed_grad(c):
        arrive(c)
        dmid = mm_nt(gathered(c), eo_ref[...]).astype(jnp.bfloat16)
        grad = (mm_nt(gathered(c), w_out[...]) + mm(dmid, so_ref[...])).astype(jnp.bfloat16)
        for i, o in enumerate(order):
            dmixed_ref[o, c] = grad[i * part : (i + 1) * part]
        gso_ref[...] += mm_tn(dmid, mixed_chunk(c))
        gather_forward(c).wait_send()
        gather_across(c).wait_send()
        gather_beside(c).wait_send()
        reduce_beside(c).wait_send()
        reduce_across(c).wait_send()
        side_across(c).wait_send()

    stages = {
        "S0": stage_mixer, "S1": stage_hidden, "S2": stage_units, "S3": stage_feed,
        "S4": stage_units_back, "S5": stage_mixer_grad, "S6": stage_mixed_grad,
        "P0": pair_stage, "P2": pair_stage, "P4": pair_stage,
        "F1": forward_stage, "F3": forward_stage, "F5": forward_stage,
    }

    packed = [
        sum(code << (6 * j) for j, code in enumerate(MIDDLE_ORDER[at : at + 5]))
        for at in range(0, len(MIDDLE_ORDER), 5)
    ]

    def step(i, carry):
        word = jnp.int32(packed[0])
        for k in range(1, len(packed)):
            word = jnp.where(i >= 5 * k, jnp.int32(packed[k]), word)
        place = lax.rem(i, 5)
        unit = jnp.int32(1)
        for k in range(1, 5):
            unit = jnp.where(place == k, jnp.int32(64**k), unit)
        code = lax.rem(lax.div(word, unit), 64)
        stage, c = lax.div(code, chunks), lax.rem(code, chunks)
        for k, name in enumerate(MIDDLE_STAGES):

            @pl.when(stage == k)
            def _():
                stages[name](c)

        return carry

    lax.fori_loop(0, len(MIDDLE_ORDER), step, 0)
    save_mixture = pltpu.make_async_copy(dmixed_ref, dmixed_hbm, save_sem.at[2, 0])
    save_mixture.start()
    for c in range(chunks):
        for number in range(2):
            save(number, c).wait()
    save_mixture.wait()


def middle(mixed, tokens, cot, w_out, w_gate, w_up, w_down, mgain, fgain, so, eo, sgu, eg, eu, sd, ed):
    rows, width = tokens.shape
    heads_width, units = w_out.shape[0], w_gate.shape[1]
    part = rows // CHUNKS
    whole_width = width + EXTRA
    vmem = pl.BlockSpec(memory_space=pltpu.VMEM)
    hbm = pl.BlockSpec(memory_space=pl.ANY)
    low, full = jnp.bfloat16, jnp.float32
    dma = pltpu.SemaphoreType.DMA((CHUNKS,))
    shape = jax.ShapeDtypeStruct
    flops = 2 * 4 * rows * width * (2 * heads_width + 6 * units)
    return pl.pallas_call(
        middle_body,
        in_specs=[vmem] + [hbm] * 6 + [vmem] * 9,
        out_specs=[hbm] * 3 + [vmem] * 7,
        out_shape=[
            shape((rows, width), low), shape((rows, width), full),
            shape((4, CHUNKS, part, heads_width), low),
            shape((16, units), full), shape((32, units), full), shape((32, units), full),
            shape((16, heads_width), full), shape((32, width), full), shape((16, width), full),
            shape((16, width), full),
        ],
        scratch_shapes=[
            pltpu.VMEM(w_out.shape, low), pltpu.VMEM(w_gate.shape, low),
            pltpu.VMEM(w_up.shape, low), pltpu.VMEM(w_down.shape, low),
            pltpu.VMEM((rows, width), low), pltpu.VMEM((rows, width), low),
            pltpu.SemaphoreType.DMA((6,)),
            pltpu.VMEM((rows, width), low), pltpu.VMEM((4, CHUNKS, part, heads_width), low),
            pltpu.SemaphoreType.DMA((3, CHUNKS)),
            pltpu.VMEM((CHUNKS, 4, part, width), low),
            pltpu.VMEM((CHUNKS, part, whole_width), low),
            pltpu.VMEM((CHUNKS, part, whole_width), low),
            pltpu.VMEM((CHUNKS, part, whole_width), low),
            pltpu.VMEM((CHUNKS, 2, part, whole_width), low),
            pltpu.VMEM((CHUNKS, 2, part, whole_width), low),
            pltpu.VMEM((4 * rows, units), low), pltpu.VMEM((4 * rows, units), low),
            pltpu.VMEM((4 * part, units), low), pltpu.VMEM((4 * part, units), low),
            pltpu.VMEM((CHUNKS, 4 * part, 32), low),
            pltpu.VMEM((rows, width), full), pltpu.VMEM((rows, width), full),
            pltpu.VMEM((CHUNKS, part, 16), low),
            pltpu.VMEM((CHUNKS, 32, EXTRA), low), pltpu.VMEM((CHUNKS, 32, EXTRA), low),
        ] + [dma] * 12,
        cost_estimate=pl.CostEstimate(
            flops=flops, bytes_accessed=2 * width * (heads_width + 3 * units), transcendentals=0
        ),
        compiler_params=pltpu.CompilerParams(
            collective_id=0, has_side_effects=True, vmem_limit_bytes=67043328
        ),
        name="mixer_to_feed",
    )(mixed.reshape(4, CHUNKS, part, heads_width), tokens, cot, w_out, w_gate, w_up, w_down,
      mgain, fgain, so, eo, sgu, eg, eu, sd, ed)


def probs_space(length, heads_width):
    rows = min(ATT_ROWS, length)
    blocks = length // rows
    longest = max(high - low for low, high in (key_window(b, rows) for b in range(blocks)))
    return (blocks, heads_width // HEAD_DIM, longest, rows)


def attention_scores(first, second, start, first_query, first_key, query_axis):
    scores = lax.dot_general(first, second, NT, preferred_element_type=jnp.float32)
    kpos = lax.broadcasted_iota(jnp.int32, scores.shape, 1 - query_axis) + first_key
    shape = [1, 1]
    shape[query_axis] = scores.shape[query_axis]
    qpos = lax.broadcasted_iota(jnp.int32, shape, query_axis) + first_query
    return jnp.where((kpos <= qpos) & (kpos >= start), scores, NEG)


def pick_body(
    at, seg_ref, qgain, kgain, mgain, fgain,
    sq, eq, sk, ek, sv, ev, so, eo, sg, eg, su, eu, sd, ed,
    shrink_out, eq_out, ek_out, ev_out, so_out, eo_out, sgu_out, eg_out, eu_out, sd_out, ed_out,
    qgain_out, kgain_out, mgain_out, fgain_out, start_row, set_out,
):
    rank = sq.shape[1]

    def scaled(ref):
        return (adapter_scale_factor * ref[at].astype(jnp.float32)).astype(jnp.bfloat16)

    for i, ref in enumerate((sq, sk, sv)):
        shrink_out[i * rank : (i + 1) * rank, :] = ref[at]
    for i, (ref, target) in enumerate(((eq, eq_out), (ek, ek_out), (ev, ev_out))):
        target[...] = jnp.zeros_like(target)
        target[i * rank : (i + 1) * rank, :] = scaled(ref)
    for i, (ref, target) in enumerate(((eg, eg_out), (eu, eu_out))):
        target[...] = jnp.zeros_like(target)
        target[i * rank : (i + 1) * rank, :] = scaled(ref)
    so_out[...] = so[at]
    sd_out[...] = sd[at]
    eo_out[...] = scaled(eo)
    ed_out[...] = scaled(ed)
    sgu_out[:rank, :] = sg[at]
    sgu_out[rank:, :] = su[at]
    for ref, target in ((qgain, qgain_out), (kgain, kgain_out), (mgain, mgain_out), (fgain, fgain_out)):
        target[...] = ref[...].astype(jnp.float32).reshape(target.shape)
    length = seg_ref.shape[1]
    row = seg_ref[...].astype(jnp.float32)
    col = jnp.transpose(jnp.broadcast_to(row, (HEAD_DIM, length)))[:, :1]
    start_row[...] = jnp.sum(
        jnp.where(col < row, 1.0, 0.0), axis=0, keepdims=True
    ).astype(jnp.int32)
    set_out[...] = jnp.full(set_out.shape, at, jnp.int32).astype(jnp.float32)


def front_body(
    set_ref, tokens_ref, wq_hbm, wk_hbm, wv_hbm, table_ref, seg_ref, qg_ref, kg_ref, mg_ref, fg_ref,
    *refs,
):
    adapters_hbm, refs = refs[:14], refs[14:]
    picked, refs = refs[:17], refs[17:]
    adapters, adapter_sem, refs = refs[-15:-1], refs[-1], refs[:-15]
    shrink_ref, eq_ref, ek_ref, ev_ref = picked[:4]
    qgain_ref, kgain_ref, start_ref = picked[11], picked[12], picked[15]
    front_steps(
        set_ref, tokens_ref, wq_hbm, wk_hbm, wv_hbm, table_ref,
        (seg_ref, qg_ref, kg_ref, mg_ref, fg_ref), adapters_hbm, adapters, adapter_sem, picked,
        shrink_ref, eq_ref, ek_ref, ev_ref, qgain_ref, kgain_ref, start_ref, *refs,
    )


def front_steps(
    set_ref, tokens_ref, wq_hbm, wk_hbm, wv_hbm, table_ref, small, adapters_hbm, adapters,
    adapter_sem, picked, shrink_ref, eq_ref, ek_ref, ev_ref, qgain_ref, kgain_ref, start_ref,
    mixed_hbm, qrot_hbm, krot_hbm, value_hbm, qproj_hbm, kproj_hbm, scale_hbm, mids_hbm, full_hbm,
    probs_hbm, probs_ref, mixed_ref, qrot_ref, krot_ref, value_ref, qproj_ref, kproj_ref, scale_ref, mids_ref, cos_ref, sin_ref,
    wq, wk, wv, wsem, full, lhs, squares, ex_send, ex_recv,
    xs_sem, xr_sem, fs_sem, fr_sem, bs_sem, br_sem, es_sem, er_sem, out_sem,
):
    me, group, beside, across = partners()
    far = lax.rem(beside + 2, 4)
    chunks, part, width = full.shape[1:]
    rows = chunks * part
    length = 4 * rows
    loads = [
        pltpu.make_async_copy(source, target, wsem.at[i])
        for i, (source, target) in enumerate(((wq_hbm, wq), (wk_hbm, wk), (wv_hbm, wv)))
    ]
    barrier = pltpu.get_barrier_semaphore()
    for other in (beside, across, far):
        pl.semaphore_signal(barrier, inc=1, device_id=(group, other), device_id_type=MESH_ID)
    fetches = [
        pltpu.make_async_copy(source, target, adapter_sem.at[i])
        for i, (source, target) in enumerate(zip(adapters_hbm, adapters))
    ]
    for load in (*fetches, *loads):
        load.start()
    pl.semaphore_wait(barrier, 3)

    def remote(source, target, ssem, rsem, other):
        return pltpu.make_async_remote_copy(
            src_ref=source, dst_ref=target, send_sem=ssem, recv_sem=rsem,
            device_id=(group, other), device_id_type=MESH_ID,
        )

    def send_across(c):
        return remote(tokens_ref.at[c], full.at[me, c], xs_sem.at[c], xr_sem.at[c], across)

    def forward(c):
        return remote(full.at[across, c], full.at[across, c], fs_sem.at[c], fr_sem.at[c], beside)

    to_beside = remote(tokens_ref, full.at[me], bs_sem, br_sem, beside)
    for c in range(chunks):
        send_across(c).start()
    to_beside.start()
    full[me] = tokens_ref[...]
    cos_ref[...] = table_ref[...]
    open_table(cos_ref, sin_ref)
    for fetch in fetches:
        fetch.wait()
    pick_body(set_ref[0], *small, *adapters, *picked)
    for load in loads:
        load.wait()
    pairs = chunks // 2
    half = rows // 2

    def block_step(b, carry):
        @pl.when(b == 0)
        def _():
            lhs[...] = tokens_ref[...].reshape(rows, width)

        @pl.when(b == 1)
        def _():
            to_beside.wait_recv()
            lhs[...] = full[beside].reshape(rows, width)

        @pl.when(b >= 2)
        def _():
            base = (b - 2) * pairs
            for j in range(pairs):
                send_across(base + j).wait_recv()
                forward(base + j).start()
            for j in range(pairs):
                lhs[j * part : (j + 1) * part] = full[across, base + j]
            for j in range(pairs):
                forward(base + j).wait_recv()
                lhs[half + j * part : half + (j + 1) * part] = full[far, base + j]

        mids = mm_nt(lhs[...], shrink_ref[...]).astype(jnp.bfloat16)
        query = mm(lhs[...], wq[...]) + mm(mids, eq_ref[...])
        key = mm(lhs[...], wk[...]) + mm(mids, ek_ref[...])
        value = (mm(lhs[...], wv[...]) + mm(mids, ev_ref[...])).astype(jnp.bfloat16)
        qsum = jnp.sum(query * query, axis=1, keepdims=True)
        ksum = jnp.sum(key * key, axis=1, keepdims=True)
        lane = lax.broadcasted_iota(jnp.int32, (rows, HEAD_DIM), 1)
        both = jnp.where(lane < 4, qsum, ksum)
        first = jnp.where(b == 0, me, jnp.where(b == 1, beside, across)) * rows
        second = jnp.where(b == 0, me, jnp.where(b == 1, beside, far)) * rows
        first = first + jnp.where(b >= 2, (b - 2) * half, 0)
        second = second + jnp.where(b >= 2, (b - 2) * half, half)
        for start, piece in ((first, slice(0, half)), (second, slice(half, rows))):
            there = pl.ds(pl.multiple_of(start, half), half)
            qproj_ref[there, :] = query[piece]
            kproj_ref[there, :] = key[piece]
            value_ref[there, :] = value[piece]
            mids_ref[there, :] = mids[piece]
            squares[there, :] = both[piece]
        return carry

    lax.fori_loop(0, 4, block_step, 0)
    saves = [
        pltpu.make_async_copy(source, target, out_sem.at[i])
        for i, (source, target) in enumerate(
            (
                (full, full_hbm), (value_ref, value_hbm), (qproj_ref, qproj_hbm),
                (kproj_ref, kproj_hbm), (mids_ref, mids_hbm), (scale_ref, scale_hbm),
                (qrot_ref, qrot_hbm), (krot_ref, krot_hbm), (mixed_ref, mixed_hbm),
                (probs_ref, probs_hbm),
            )
        )
    ]
    for save in saves[:5]:
        save.start()
    ex_send[...] = jnp.transpose(squares[...])[:8]
    swaps = [
        remote(ex_send, ex_recv.at[i], es_sem.at[i], er_sem.at[i], other)
        for i, other in enumerate((beside, across, far))
    ]
    for swap in swaps:
        swap.start()
    for swap in swaps:
        swap.wait_recv()
    total = ex_send[...] + ex_recv[0] + ex_recv[1] + ex_recv[2]
    factor = lax.rsqrt(total / (4 * wq.shape[1]) + epsilon)
    wide = jnp.concatenate(
        [
            jnp.broadcast_to(factor[:1], (HEAD_DIM // 2, length)),
            jnp.broadcast_to(factor[4:5], (HEAD_DIM // 2, length)),
        ],
        axis=0,
    )
    scale_ref[...] = jnp.transpose(wide)
    heads = wq.shape[1] // HEAD_DIM
    exponent = HEAD_DIM ** (-0.5) * LOG2E
    block_rows = min(ATT_ROWS, length)

    def turn_step(h, carry):
        cols = pl.ds(pl.multiple_of(h * HEAD_DIM, HEAD_DIM), HEAD_DIM)
        for source, lane, gain, target in (
            (qproj_ref, 0, qgain_ref, qrot_ref),
            (kproj_ref, HEAD_DIM // 2, kgain_ref, krot_ref),
        ):
            normed = source[:, cols] * scale_ref[:, lane : lane + 1] * gain[:, cols]
            turned = normed * cos_ref[...] + pltpu.roll(normed, HEAD_DIM // 2, 1) * sin_ref[...]
            target[:, cols] = turned.astype(jnp.bfloat16)
        return carry

    lax.fori_loop(0, heads, turn_step, 0)
    for save in saves[5:8]:
        save.start()

    def head_step(h, carry):
        cols = pl.ds(pl.multiple_of(h * HEAD_DIM, HEAD_DIM), HEAD_DIM)
        for block in range(length // block_rows):
            low, high = key_window(block, block_rows)
            here = pl.ds(block * block_rows, block_rows)
            keys = pl.ds(low, high - low)
            scores = attention_scores(
                krot_ref[keys, cols], qrot_ref[here, cols], start_ref[:, here],
                block * block_rows, low, 1,
            )
            top = jnp.max(scores, axis=0, keepdims=True)
            weights = jnp.exp2((scores - top) * exponent)
            total = jnp.sum(weights, axis=0, keepdims=True)
            probs = (weights * (1.0 / total)).astype(jnp.bfloat16)
            probs_ref[block, h, : high - low, :] = probs
            mixed_ref[here, cols] = mm_tn(probs, value_ref[keys, cols]).astype(jnp.bfloat16)
        return carry

    lax.fori_loop(0, heads, head_step, 0, unroll=2)
    for save in saves[8:]:
        save.start()
    for c in range(chunks):
        send_across(c).wait_send()
        forward(c).wait_send()
    to_beside.wait_send()
    for swap in swaps:
        swap.wait_send()
    for save in saves:
        save.wait()


def front(adapter_set, tokens, wq, wk, wv, table, segment_ids, gains, adapters):
    rows, width = tokens.shape
    heads_width = wq.shape[1]
    length = 4 * rows
    part = rows // CHUNKS
    rank = adapters[0].shape[1]
    units = adapters[9].shape[2]
    probs_shape = probs_space(length, heads_width)
    vmem = pl.BlockSpec(memory_space=pltpu.VMEM)
    hbm = pl.BlockSpec(memory_space=pl.ANY)
    low, full = jnp.bfloat16, jnp.float32
    shape = jax.ShapeDtypeStruct
    dma = pltpu.SemaphoreType.DMA
    return pl.pallas_call(
        front_body,
        in_specs=[pl.BlockSpec(memory_space=pltpu.SMEM), vmem] + [hbm] * 3 + [vmem] * 6 + [hbm] * 14,
        out_specs=[vmem] * 17 + [hbm] * 10,
        out_shape=[
            shape((3 * rank, width), low), shape((3 * rank, heads_width), low),
            shape((3 * rank, heads_width), low), shape((3 * rank, heads_width), low),
            shape((rank, heads_width), low), shape((rank, width), low), shape((2 * rank, width), low),
            shape((2 * rank, units), low), shape((2 * rank, units), low), shape((rank, units), low),
            shape((rank, width), low), shape((1, heads_width), full), shape((1, heads_width), full),
            shape((1, width), full), shape((1, width), full),
            shape((1, length), jnp.int32), shape((1, 128), full),
            shape((length, heads_width), low), shape((length, heads_width), low),
            shape((length, heads_width), low), shape((length, heads_width), low),
            shape((length, heads_width), full), shape((length, heads_width), full),
            shape((length, HEAD_DIM), full), shape((length, 3 * rank), low),
            shape((4, CHUNKS, part, width), low), shape(probs_shape, low),
        ],
        scratch_shapes=[pltpu.VMEM(probs_shape, low)]
        + [pltpu.VMEM((length, heads_width), low)] * 4
        + [pltpu.VMEM((length, heads_width), full)] * 2
        + [
            pltpu.VMEM((length, HEAD_DIM), full), pltpu.VMEM((length, 3 * rank), low),
            pltpu.VMEM(table.shape, full), pltpu.VMEM(table.shape, full),
            pltpu.VMEM(wq.shape, low), pltpu.VMEM(wk.shape, low), pltpu.VMEM(wv.shape, low),
            dma((3,)),
            pltpu.VMEM((4, CHUNKS, part, width), low), pltpu.VMEM((rows, width), low),
            pltpu.VMEM((length, HEAD_DIM), full), pltpu.VMEM((8, length), full),
            pltpu.VMEM((3, 8, length), full),
            dma((CHUNKS,)), dma((CHUNKS,)), dma((CHUNKS,)), dma((CHUNKS,)), dma, dma,
            dma((3,)), dma((3,)), dma((10,)),
        ] + [pltpu.VMEM(a.shape, low) for a in adapters] + [dma((14,))],
        cost_estimate=pl.CostEstimate(
            flops=2 * length * heads_width * (3 * width + 2 * length),
            bytes_accessed=2 * width * (3 * heads_width + length), transcendentals=0,
        ),
        compiler_params=pltpu.CompilerParams(
            collective_id=1, has_side_effects=True, vmem_limit_bytes=67043328
        ),
        name="gather_project_attend",
    )(adapter_set, tokens.reshape(CHUNKS, part, width), wq, wk, wv, table, segment_ids, *gains,
      *adapters)


def back_body(
    qrot_hbm, krot_hbm, value_hbm, dmixed_hbm, qproj_hbm, kproj_hbm, scale_hbm, qgain_ref,
    kgain_ref, table_hbm, probs_hbm, wq_hbm, wk_hbm, wv_hbm, shrink_ref,
    eq_ref, ek_ref, ev_ref, mids_ref, full_hbm, hgrad_hbm, set_ref,
    gso_ref, geg_ref, geu_ref, gsd_ref, gsgu_ref, geo_ref, ged_ref,
    tgrad_hbm, split_hbm, heads_hbm, shared_hbm, inward_hbm,
    wq, wk, wv, full, qrot_ref, krot_ref, value_ref, dmixed, qproj_ref, kproj_ref,
    scale_ref, cos_ref, sin_ref, hgrad_ref, probs_ref, probs_sem, wsem, save_sem,
    dq_buf, dk_buf, dv_buf, dq_low, dk_low, dv_low, sums_buf,
    split_send, heads_send, blocks, blocks_recv, blocks_xrecv, shared_send, inward_send,
    ex_send, ex_recv, dmid_send, dmid_recv, dmid_xsend, dmid_xrecv,
    own_buf, xsend, xrecv, bsend, brecv,
    es_sem, er_sem, xs_sem, xr_sem, bs_sem, br_sem, one_s, one_r,
    sp_s, sp_f, sp_r, hd_s, hd_r, sh_s, sh_r, in_s, in_r, local_sem,
):
    me, group, beside, across = partners()
    far = lax.rem(beside + 2, 4)
    order = (me, across, beside, far)
    groups = split_hbm.shape[0]
    chunks, part, width = own_buf.shape
    rows = chunks * part
    length = 4 * rows
    heads_width = wq.shape[1]
    units = geg_ref.shape[1]
    cols_each = blocks.shape[3]
    loads = [
        pltpu.make_async_copy(source, target, wsem.at[i])
        for i, (source, target) in enumerate(
            (
                (dmixed_hbm, dmixed), (qrot_hbm, qrot_ref),
                (krot_hbm, krot_ref), (value_hbm, value_ref),
                (table_hbm, cos_ref), (qproj_hbm, qproj_ref), (kproj_hbm, kproj_ref),
                (scale_hbm, scale_ref), (wq_hbm, wq), (wk_hbm, wk), (wv_hbm, wv),
                (hgrad_hbm, hgrad_ref), (full_hbm, full),
            )
        )
    ]
    probs_loads = [
        pltpu.make_async_copy(probs_hbm.at[i], probs_ref.at[i], probs_sem.at[i])
        for i in range(probs_hbm.shape[0])
    ]
    for load in (*loads[:6], *probs_loads, *loads[6:]):
        load.start()
    barrier = pltpu.get_barrier_semaphore()
    for other in (beside, across, far):
        pl.semaphore_signal(barrier, inc=1, device_id=(group, other), device_id_type=MESH_ID)

    def greet_group(j, carry):
        other = lax.rem(group + j, groups)
        pl.semaphore_signal(barrier, inc=1, device_id=(other, me), device_id_type=MESH_ID)
        return carry

    lax.fori_loop(1, groups, greet_group, 0)

    def remote(source, target, ssem, rsem, other):
        return pltpu.make_async_remote_copy(
            src_ref=source, dst_ref=target, send_sem=ssem, recv_sem=rsem,
            device_id=(group, other), device_id_type=MESH_ID,
        )

    def to_group(source, target, ssem, rsem, j):
        other = lax.rem(group + j, groups)
        return pltpu.make_async_remote_copy(
            src_ref=source(other), dst_ref=target.at[group], send_sem=ssem.at[j],
            recv_sem=rsem.at[group], device_id=(other, me), device_id_type=MESH_ID,
        )

    def from_group(source, target, ssem, rsem, j):
        sender = lax.rem(group + j, groups)
        return pltpu.make_async_remote_copy(
            src_ref=source(sender), dst_ref=target.at[sender], send_sem=ssem.at[j],
            recv_sem=rsem.at[sender], device_id=(sender, me), device_id_type=MESH_ID,
        )

    by_heads = (lambda other: heads_send, heads_hbm, hd_s, hd_r)
    shared = (lambda other: shared_send.at[other], shared_hbm, sh_s, sh_r)
    inward = (lambda other: inward_send.at[other, me], inward_hbm, in_s, in_r)
    exchanges = (None, by_heads, shared, inward)

    def start_exchange(number):
        exchange = exchanges[number]

        def one(j, carry):
            to_group(*exchange, j).start()
            return carry

        lax.fori_loop(1, groups, one, 0)
        pltpu.make_async_copy(
            exchange[0](group), exchange[1].at[group], local_sem.at[number]
        ).start()

    def end_exchange(number):
        exchange = exchanges[number]

        def one(j, carry):
            to_group(*exchange, j).wait_send()
            from_group(*exchange, j).wait_recv()
            return carry

        lax.fori_loop(1, groups, one, 0)
        pltpu.make_async_copy(
            exchange[0](group), exchange[1].at[group], local_sem.at[number]
        ).wait()

    neighbour = group + 1 - 2 * lax.rem(group, 2)

    def split_copy(source, slot, ssem, other):
        return pltpu.make_async_remote_copy(
            src_ref=source, dst_ref=split_hbm.at[slot], send_sem=ssem, recv_sem=sp_r.at[slot],
            device_id=(other, me), device_id_type=MESH_ID,
        )

    def split_direct(k):
        return split_copy(split_send, group, sp_s.at[2 * k], lax.rem(group + 2 * k, groups))

    def split_passed(k):
        slot = lax.rem(group + 2 * k, groups)
        return split_copy(split_hbm.at[slot], slot, sp_f.at[2 * k], neighbour)

    def split_arrival(slot):
        return split_copy(split_send, slot, sp_s.at[0], neighbour)

    split_near = split_copy(split_send, group, sp_s.at[0], neighbour)
    split_own = pltpu.make_async_copy(split_send, split_hbm.at[group], local_sem.at[0])

    def over_parity(body):
        def one(k, carry):
            body(k)
            return carry

        lax.fori_loop(1, groups // 2, one, 0)

    def start_split():
        over_parity(lambda k: split_direct(k).start())
        split_near.start()
        split_own.start()

    def pass_split(k):
        split_arrival(lax.rem(group + 2 * k, groups)).wait_recv()
        split_passed(k).start()

    def end_split_one(k):
        split_direct(k).wait_send()
        split_passed(k).wait_send()
        split_arrival(lax.rem(neighbour + 2 * k, groups)).wait_recv()

    def end_split():
        over_parity(end_split_one)
        split_near.wait_send()
        split_arrival(neighbour).wait_recv()
        split_own.wait()

    low = jnp.bfloat16
    heads = heads_width // HEAD_DIM
    inverse = HEAD_DIM ** (-0.5)
    for ref in (sums_buf, dk_buf, dv_buf):
        ref[...] = jnp.zeros_like(ref)
    block_rows = min(ATT_ROWS, length)

    def attend_back(block, first_query, first_key, size):
        here = pl.ds(first_query, block_rows)
        keys = pl.ds(first_key, size)

        def head_step(h, carry):
            cols = pl.ds(pl.multiple_of(h * HEAD_DIM, HEAD_DIM), HEAD_DIM)
            queries = qrot_ref[here, cols]
            key_rows = krot_ref[keys, cols]
            grads = dmixed[here, cols]
            prob_low = probs_ref[block, h, :size, :]
            probs = prob_low.astype(jnp.float32)
            prob_grad = mm_nt(value_ref[keys, cols], grads)
            weighted = probs * prob_grad
            delta = jnp.sum(weighted, axis=0, keepdims=True)
            score_grad = (weighted - probs * delta).astype(low)
            dv_buf[keys, cols] += mm(prob_low, grads)
            dk_buf[keys, cols] += mm(score_grad, queries)
            dq = mm_tn(score_grad, key_rows) * inverse
            dq = dq * cos_ref[here, :] - pltpu.roll(dq, HEAD_DIM // 2, 1) * sin_ref[here, :]
            dq = dq * qgain_ref[:, cols]
            dq_buf[here, cols] = dq
            sums_buf[0, here, :] += qproj_ref[here, cols] * dq
            return carry

        lax.fori_loop(0, heads, head_step, 0, unroll=2)

    pl.semaphore_wait(barrier, groups + 2)
    split_send[:, :units] = (adapter_scale_factor * geg_ref[:16]).astype(low)
    split_send[:, units : 2 * units] = (adapter_scale_factor * geu_ref[16:]).astype(low)
    split_send[:, 2 * units : 3 * units] = gsd_ref[...].astype(low)
    split_send[:, 3 * units : 3 * units + heads_width] = gso_ref[...].astype(low)
    split_send[:, 3 * units + heads_width :] = jnp.broadcast_to(set_ref[...], (16, 128)).astype(low)
    start_split()
    for t in range(4):
        for g in range(groups):
            at = slice((g * 4 + t) * cols_each, (g * 4 + t + 1) * cols_each)
            blocks[t, g, :16] = (adapter_scale_factor * geo_ref[:, at]).astype(low)
            blocks[t, g, 16:48] = gsgu_ref[:, at].astype(low)
            blocks[t, g, 48:] = (adapter_scale_factor * ged_ref[:, at]).astype(low)
    block_near = remote(blocks.at[beside], blocks_recv.at[0], one_s.at[0], one_r.at[0], beside)
    block_far = remote(blocks.at[far], blocks_recv.at[1], one_s.at[1], one_r.at[1], beside)
    block_across = remote(shared_send, blocks_xrecv, one_s.at[2], one_r.at[2], across)
    block_near.start()
    block_far.start()
    for load in loads[:6]:
        load.wait()
    open_table(cos_ref, sin_ref)

    for block in range(length // block_rows):
        first, last = key_window(block, block_rows)
        if True:
            probs_loads[block].wait()
            attend_back(block, block * block_rows, first, last - first)
        if block == 1:
            block_near.wait_recv()
            block_far.wait_recv()
            shared_send[...] = (
                blocks[across].astype(jnp.float32) + blocks_recv[1].astype(jnp.float32)
            ).astype(low)
            block_across.start()
        if block == length // block_rows - 1:
            block_across.wait()
            shared_send[...] = (
                blocks[me].astype(jnp.float32)
                + blocks_recv[0].astype(jnp.float32)
                + blocks_xrecv[...].astype(jnp.float32)
            ).astype(low)
            start_exchange(2)

    def head_end(h, carry):
        cols = pl.ds(pl.multiple_of(h * HEAD_DIM, HEAD_DIM), HEAD_DIM)
        dk = dk_buf[:, cols] * inverse
        dk = dk * cos_ref[...] - pltpu.roll(dk, HEAD_DIM // 2, 1) * sin_ref[...]
        dk = dk * kgain_ref[:, cols]
        dk_buf[:, cols] = dk
        sums_buf[1] += kproj_ref[:, cols] * dk
        dv_low[:, cols] = dv_buf[:, cols].astype(low)
        return carry

    for load in loads[6:]:
        load.wait()
    lax.fori_loop(0, heads, head_end, 0)

    ones = jnp.ones((8, HEAD_DIM), low)
    totals = []
    for i in range(2):
        high = sums_buf[i].astype(low)
        rest = (sums_buf[i] - high.astype(jnp.float32)).astype(low)
        totals.append(mm_nt(ones, high) + mm_nt(ones, rest))
    upper = lax.broadcasted_iota(jnp.int32, (8, length), 0) < 4
    ex_send[...] = jnp.where(upper, totals[0], totals[1])
    swaps = [
        remote(ex_send, ex_recv.at[i], es_sem.at[i], er_sem.at[i], other)
        for i, other in enumerate((beside, across, far))
    ]
    for swap in swaps:
        swap.start()
    for swap in swaps:
        swap.wait_recv()
    total = (ex_send[...] + ex_recv[0] + ex_recv[1] + ex_recv[2]) * (1.0 / (4 * heads_width))
    wide = jnp.concatenate(
        [
            jnp.broadcast_to(total[:1], (HEAD_DIM // 2, length)),
            jnp.broadcast_to(total[4:5], (HEAD_DIM // 2, length)),
        ],
        axis=0,
    )
    sums_buf[0] = jnp.transpose(wide)
    for dn, proj, target, at in (
        (dq_buf, qproj_ref, dq_low, 0), (dk_buf, kproj_ref, dk_low, HEAD_DIM // 2),
    ):
        scale = scale_ref[:, at : at + 1]
        means = sums_buf[0, :, at : at + 1]
        target[...] = (scale * dn[...] - proj[...] * (scale * scale * scale * means)).astype(low)

    dmid_near = remote(dmid_send, dmid_recv, one_s.at[3], one_r.at[3], beside)
    dmid_across = remote(dmid_xsend, dmid_xrecv, one_s.at[4], one_r.at[4], across)

    def reduce_beside(c):
        return remote(bsend.at[c], brecv.at[c], bs_sem.at[c], br_sem.at[c], beside)

    def reduce_across(c):
        return remote(xsend.at[c], xrecv.at[c], xs_sem.at[c], xr_sem.at[c], across)

    def chunk_of(buffer, c):
        return jnp.concatenate(
            [buffer[pl.ds(pl.multiple_of(o * rows + c * part, part), part), :] for o in order], axis=0
        )

    def stage_partial(c):
        parts = [chunk_of(buffer, c) for buffer in (dq_low, dk_low, dv_low)]
        tile = 2 * TILE

        def one(j, carry):
            at = pl.ds(pl.multiple_of(j * tile, tile), tile)
            value = (
                mm_nt(parts[0], wq[at, :]) + mm_nt(parts[1], wk[at, :]) + mm_nt(parts[2], wv[at, :])
            ).astype(low)
            own_buf[c, :, at] = value[:part]
            xsend[c, :, at] = value[part : 2 * part]
            bsend[c, 0, :, at] = value[2 * part : 3 * part]
            bsend[c, 1, :, at] = value[3 * part :]
            return carry

        lax.fori_loop(0, width // tile, one, 0)
        reduce_beside(c).start()

    def stage_pair(c):
        reduce_beside(c).wait_recv()
        xsend[c] = (xsend[c].astype(jnp.float32) + brecv[c, 1].astype(jnp.float32)).astype(low)
        reduce_across(c).start()
        own_buf[c] = (own_buf[c].astype(jnp.float32) + brecv[c, 0].astype(jnp.float32)).astype(low)

    def rank_sums_start():
        dmid_part = (
            mm_nt(eq_ref[...], dq_low[...]) + mm_nt(ek_ref[...], dk_low[...])
            + mm_nt(ev_ref[...], dv_low[...])
        )
        dmid_send[...] = dmid_part.astype(low)
        dmid_near.start()

    def rank_sums_cross():
        dmid_near.wait_recv()
        dmid_xsend[...] = (
            dmid_send[...].astype(jnp.float32) + dmid_recv[...].astype(jnp.float32)
        ).astype(low)
        dmid_across.start()

    def expand_gradients():
        mids = mids_ref[...]
        for i, buffer in enumerate((dq_low, dk_low, dv_low)):
            heads_send[:, i * heads_width : (i + 1) * heads_width] = (
                adapter_scale_factor * mm_tn(mids, buffer[...])[i * 16 : (i + 1) * 16]
            ).astype(low)
        start_exchange(1)

    def partial_step(i, carry):
        stage_partial(i)
        for k, extra in (
            (0, rank_sums_start), (1, rank_sums_cross), (1, lambda: over_parity(pass_split)),
        ):

            @pl.when(i == k)
            def _():
                extra()

        @pl.when(i == 2)
        def _():
            expand_gradients()

        stage_pair(i)
        return carry

    lax.fori_loop(0, chunks, partial_step, 0)
    dmid_across.wait_recv()
    dmid = (
        dmid_xsend[...].astype(jnp.float32) + dmid_xrecv[...].astype(jnp.float32)
    ).astype(low)
    inward_grad = mm(dmid, full[...])
    for t in range(4):
        for g in range(groups):
            at = slice((g * 4 + t) * cols_each, (g * 4 + t + 1) * cols_each)
            inward_send[g, t] = inward_grad[:, at].astype(low)
    start_exchange(3)
    dmid_across.wait_send()
    dmid_xsend[...] = dmid
    mine = pl.ds(pl.multiple_of(me * rows, rows), rows)
    hgrad_ref[...] += mm_tn(dmid_xsend[:, mine], shrink_ref[...])

    def own_rows(c):
        return pl.ds(pl.multiple_of(c * part, part), part)

    def save(c):
        return pltpu.make_async_copy(
            hgrad_ref.at[own_rows(c), :], tgrad_hbm.at[own_rows(c), :], save_sem.at[c]
        )

    def finish_step(c, carry):
        reduce_across(c).wait_recv()
        hgrad_ref[own_rows(c), :] += own_buf[c].astype(jnp.float32) + xrecv[c].astype(jnp.float32)
        save(c).start()
        return carry

    lax.fori_loop(0, chunks, finish_step, 0)
    for c in range(chunks):
        save(c).wait()
    for c in range(chunks):
        reduce_beside(c).wait_send()
        reduce_across(c).wait_send()
    for copy in (block_near, block_far, dmid_near, *swaps):
        copy.wait_send()
    end_split()
    for number in range(1, 4):
        end_exchange(number)


def back(
    qrot, krot, value, dmixed, qproj, kproj, scale, qgain, kgain, table, probs,
    wq, wk, wv, shrink, eq, ek, ev, mids, full, hgrad, chosen,
    gso, geg, geu, gsd, gsgu, geo, ged,
):
    rows, width = hgrad.shape
    heads_width, units = wq.shape[1], geg.shape[1]
    length = 4 * rows
    part = rows // CHUNKS
    groups = lax.axis_size("dp")
    cols_each = width // (4 * groups)
    split_width = 3 * units + heads_width + 128
    vmem = pl.BlockSpec(memory_space=pltpu.VMEM)
    hbm = pl.BlockSpec(memory_space=pl.ANY)
    low, f32 = jnp.bfloat16, jnp.float32
    shape = jax.ShapeDtypeStruct
    dma = pltpu.SemaphoreType.DMA
    buf = pltpu.VMEM
    return pl.pallas_call(
        back_body,
        in_specs=[hbm] * 7 + [vmem] * 2 + [hbm] * 5 + [vmem] * 5 + [hbm] * 2 + [vmem] * 8,
        out_specs=[hbm] * 5,
        out_shape=[
            shape((rows, width), f32),
            shape((groups, 16, split_width), low),
            shape((groups, 16, 3 * heads_width), low),
            shape((groups, 64, cols_each), low),
            shape((groups, 48, cols_each), low),
        ],
        scratch_shapes=[
            buf(wq.shape, low), buf(wk.shape, low), buf(wv.shape, low),
            buf(full.shape, low),
            buf(qrot.shape, low), buf(krot.shape, low), buf(value.shape, low), buf(dmixed.shape, low),
            buf(qproj.shape, f32), buf(kproj.shape, f32), buf(scale.shape, f32),
            buf(table.shape, f32), buf(table.shape, f32), buf(hgrad.shape, f32),
            buf(probs.shape, low), dma((probs.shape[0],)), dma((13,)), dma((CHUNKS,)),
            buf((length, heads_width), f32), buf((length, heads_width), f32),
            buf((length, heads_width), f32),
            buf((length, heads_width), low), buf((length, heads_width), low),
            buf((length, heads_width), low),
            buf((2, length, HEAD_DIM), f32),
            buf((16, split_width), low), buf((16, 3 * heads_width), low),
            buf((4, groups, 64, cols_each), low), buf((2, groups, 64, cols_each), low),
            buf((groups, 64, cols_each), low), buf((groups, 64, cols_each), low),
            buf((groups, 4, 48, cols_each), low),
            buf((8, length), f32), buf((3, 8, length), f32),
            buf((48, length), low), buf((48, length), low), buf((48, length), low),
            buf((48, length), low),
            buf((CHUNKS, part, width), low), buf((CHUNKS, part, width), low),
            buf((CHUNKS, part, width), low),
            buf((CHUNKS, 2, part, width), low), buf((CHUNKS, 2, part, width), low),
            dma((3,)), dma((3,)), dma((CHUNKS,)), dma((CHUNKS,)), dma((CHUNKS,)), dma((CHUNKS,)),
            dma((5,)), dma((5,)),
        ] + [dma((groups,))] * 9 + [dma((4,))],
        cost_estimate=pl.CostEstimate(
            flops=2 * length * heads_width * (3 * width + 5 * length),
            bytes_accessed=2 * width * (3 * heads_width + 3 * length), transcendentals=0,
        ),
        compiler_params=pltpu.CompilerParams(
            collective_id=2, has_side_effects=True, vmem_limit_bytes=67043328
        ),
        name="attention_back_to_tokens",
    )(qrot, krot, value, dmixed, qproj, kproj, scale, qgain, kgain, table, probs,
      wq, wk, wv, shrink, eq, ek, ev, mids, full, hgrad, chosen,
      gso, geg, geu, gsd, gsgu, geo, ged)


def finish_body(split_ref, heads_ref, shared_ref, inward_ref, block_ref, tokens_ref, *outs):
    block_out, tokens_out, *outs, which = outs
    groups = split_ref.shape[0]
    tag = split_ref.shape[2] - 128
    together = outs[0].shape[0]
    first = pl.program_id(0) * together

    @pl.when(first == 0)
    def _():
        for g in range(groups):
            which[g] = jnp.max(split_ref[g, :, tag:].astype(jnp.float32)).astype(jnp.int32)

    sq, eq, sk, ek, sv, ev, so, eo, sg, eg, su, eu, sd, ed = outs
    here = eq.shape[2]
    units = eg.shape[2]
    sources = []
    for i, target in enumerate((eq, ek, ev)):
        sources.append((target, lambda g, i=i: heads_ref[g, :, i * here : (i + 1) * here]))
    for i, target in enumerate((eg, eu, sd)):
        sources.append((target, lambda g, i=i: split_ref[g, :, i * units : (i + 1) * units]))
    sources.append((so, lambda g: split_ref[g, :, 3 * units : 3 * units + here]))
    for i, target in enumerate((sq, sk, sv)):
        sources.append((target, lambda g, i=i: inward_ref[g, i * 16 : (i + 1) * 16, :]))
    for i, target in enumerate((eo, sg, su, ed)):
        sources.append((target, lambda g, i=i: shared_ref[g, i * 16 : (i + 1) * 16, :]))
    for target, _ in sources:
        target[...] = jnp.zeros_like(target)

    def one(g, carry):
        at = which[g] - first

        @pl.when((at >= 0) & (at < together))
        def _():
            for target, source in sources:
                target[at] += source(g).astype(jnp.float32)

        return carry

    lax.fori_loop(0, groups, one, 0)
    block_out[...] = block_ref[...]
    tokens_out[...] = tokens_ref[...]


def finish(split, by_heads, shared, inward, block, tokens, sets, here, units):
    cols = shared.shape[2]
    rows, width = block.shape
    steps = min(FINISH_STEPS, sets)
    together = sets // steps
    part = rows // steps
    whole = lambda a: pl.BlockSpec(a.shape, lambda i: (0,) * a.ndim)
    strip = pl.BlockSpec((part, width), lambda i: (i, 0))
    widths = (cols, here, cols, here, cols, here, here, cols, cols, units, cols, units, units, cols)
    return pl.pallas_call(
        finish_body,
        grid=(steps,),
        in_specs=[whole(split), whole(by_heads), whole(shared), whole(inward), strip, strip],
        out_specs=[strip, strip] + [pl.BlockSpec((together, 16, w), lambda i: (i, 0, 0)) for w in widths],
        out_shape=[
            jax.ShapeDtypeStruct(block.shape, block.dtype),
            jax.ShapeDtypeStruct(tokens.shape, tokens.dtype),
        ] + [jax.ShapeDtypeStruct((sets, 16, w), jnp.float32) for w in widths],
        scratch_shapes=[pltpu.SMEM((split.shape[0],), jnp.int32)],
        compiler_params=pltpu.CompilerParams(vmem_limit_bytes=67043328),
        name="sum_by_set",
    )(split, by_heads, shared, inward, block, tokens)


def per_device(
    tokens,
    cotangent,
    segment_ids,
    adapter_set,
    w_query,
    w_key,
    w_value,
    w_out,
    w_gate,
    w_up,
    w_down,
    query_gain,
    key_gain,
    mixer_gain,
    feed_gain,
    shrink_query,
    expand_query,
    shrink_key,
    expand_key,
    shrink_value,
    expand_value,
    shrink_out,
    expand_out,
    shrink_gate,
    expand_gate,
    shrink_up,
    expand_up,
    shrink_down,
    expand_down,
):
    length = 4 * tokens.shape[0]
    table = jnp.asarray(rotary_constants(length, HEAD_DIM))
    (
        shrink_rows, expand_query_rows, expand_key_rows, expand_value_rows, out_shrink, out_expand,
        gate_up_shrink, gate_expand, up_expand, down_shrink, down_expand,
        query_gains, key_gains, mixer_gains, feed_gains, _, set_row,
        mixed, query_rot, key_rot, value_low, query_proj, key_proj, scales, qkv_middle, full_tokens,
        probs,
    ) = front(
        adapter_set, tokens, w_query, w_key, w_value, table, segment_ids,
        (query_gain, key_gain, mixer_gain, feed_gain),
        (
            shrink_query, expand_query, shrink_key, expand_key, shrink_value, expand_value,
            shrink_out, expand_out, shrink_gate, expand_gate, shrink_up, expand_up,
            shrink_down, expand_down,
        ),
    )
    (
        block_output, hidden_grad, mixed_grad, grad_down_shrink, gradient_gate_widened,
        gradient_up_widened, grad_out_shrink, owner_gate_up, owner_out, owner_down,
    ) = middle(
        mixed, tokens, cotangent, w_out, w_gate, w_up, w_down, mixer_gains, feed_gains,
        out_shrink, out_expand, gate_up_shrink, gate_expand, up_expand, down_shrink, down_expand,
    )
    token_grads, split, by_heads, shared, inward = back(
        query_rot, key_rot, value_low, mixed_grad.reshape(mixed.shape), query_proj, key_proj, scales,
        query_gains, key_gains, table, probs,
        w_query, w_key, w_value, shrink_rows, expand_query_rows, expand_key_rows, expand_value_rows,
        qkv_middle, full_tokens.reshape(length, -1), hidden_grad, set_row,
        grad_out_shrink, gradient_gate_widened, gradient_up_widened, grad_down_shrink,
        owner_gate_up, owner_out, owner_down,
    )
    return finish(
        split, by_heads, shared, inward, block_output, token_grads,
        shrink_query.shape[0], w_query.shape[1], w_gate.shape[1],
    )


def solution(mesh):
    in_specs = (
        P(("dp", "tensor"), None),
        P(("dp", "tensor"), None),
        P("dp", None),
        P("dp"),
        P(None, "tensor"),
        P(None, "tensor"),
        P(None, "tensor"),
        P("tensor", None),
        P(None, "tensor"),
        P(None, "tensor"),
        P("tensor", None),
        P("tensor"),
        P("tensor"),
        P(),
        P(),
        P(),
        P(None, None, "tensor"),
        P(),
        P(None, None, "tensor"),
        P(),
        P(None, None, "tensor"),
        P(None, None, "tensor"),
        P(),
        P(),
        P(None, None, "tensor"),
        P(),
        P(None, None, "tensor"),
        P(None, None, "tensor"),
        P(),
    )
    out_specs = (
        P(("dp", "tensor"), None),
        P(("dp", "tensor"), None),
        P(None, None, ("dp", "tensor")),
        P(None, None, "tensor"),
        P(None, None, ("dp", "tensor")),
        P(None, None, "tensor"),
        P(None, None, ("dp", "tensor")),
        P(None, None, "tensor"),
        P(None, None, "tensor"),
        P(None, None, ("dp", "tensor")),
        P(None, None, ("dp", "tensor")),
        P(None, None, "tensor"),
        P(None, None, ("dp", "tensor")),
        P(None, None, "tensor"),
        P(None, None, "tensor"),
        P(None, None, ("dp", "tensor")),
    )
    return jax.shard_map(
        per_device, mesh=mesh, in_specs=in_specs, out_specs=out_specs, check_vma=False
    )
```
